32 devices in a mesh: dp: 8 (over y, x, core), seq: 4 (over z).
Axes of the slice: x: 2, y: 2, z: 4, core: 2. Of those that a mesh axis runs over, the one named last changes fastest.
Arguments:
- tokens: bfloat16 [16, 512, 2048], P('dp', 'seq'), may hold values from -6 to 6
- patches: bfloat16 [16, 512, 2048], P('dp', 'seq'), may hold values from -6 to 6
- seg_ids: int32 [16, 512], P('dp'), may hold values from 0 to 3, never falling along the last dimension, each value on 1 to 256 neighbouring positions
- seg_example: int32 [16, 4], P('dp'), may hold values from 0 to 1
- patch_owner: int32 [16, 512], P('dp'), may hold values from 0 to 1, as said below
- gain_self: bfloat16 [2048], P('dp'), may hold values from 0.5 to 1.5
- self_query: bfloat16 [2048, 2048], P('dp', 'seq'), may hold values from -0.125 to 0.125
- self_key: bfloat16 [2048, 2048], P('dp', 'seq'), may hold values from -0.125 to 0.125
- self_value: bfloat16 [2048, 2048], P('dp', 'seq'), may hold values from -0.125 to 0.125
- self_out: bfloat16 [2048, 2048], P('seq', 'dp'), may hold values from -0.375 to 0.375
- gain_cross: bfloat16 [2048], P('dp'), may hold values from 0.5 to 1.5
- cross_query: bfloat16 [2048, 2048], P('dp', 'seq'), may hold values from -0.125 to 0.125
- cross_key: bfloat16 [2048, 2048], P('dp', 'seq'), may hold values from -0.125 to 0.125
- cross_value: bfloat16 [2048, 2048], P('dp', 'seq'), may hold values from -0.125 to 0.125
- cross_out: bfloat16 [2048, 2048], P('seq', 'dp'), may hold values from -0.75 to 0.75
- gain_mlp: bfloat16 [2048], P('dp'), may hold values from 0.5 to 1.5
- mlp_gate: bfloat16 [2048, 5120], P('dp', 'seq'), may hold values from -0.125 to 0.125
- mlp_up: bfloat16 [2048, 5120], P('dp', 'seq'), may hold values from -0.125 to 0.125
- mlp_down: bfloat16 [5120, 2048], P('seq', 'dp'), may hold values from -0.078125 to 0.078125
- cotangent: bfloat16 [16, 512, 2048], P('dp', 'seq'), may hold values from -6 to 6
Outputs:
- output: bfloat16 [16, 512, 2048], P('dp', 'seq')
- grad_tokens: float32 [16, 512, 2048], P('dp', 'seq')
- grad_patches: float32 [16, 512, 2048], P('dp', 'seq')
- grad_gain_self: float32 [2048], P('dp')
- grad_self_query: float32 [2048, 2048], P('dp', 'seq')
- grad_self_key: float32 [2048, 2048], P('dp', 'seq')
- grad_self_value: float32 [2048, 2048], P('dp', 'seq')
- grad_self_out: float32 [2048, 2048], P('seq', 'dp')
- grad_gain_cross: float32 [2048], P('dp')
- grad_cross_query: float32 [2048, 2048], P('dp', 'seq')
- grad_cross_key: float32 [2048, 2048], P('dp', 'seq')
- grad_cross_value: float32 [2048, 2048], P('dp', 'seq')
- grad_cross_out: float32 [2048, 2048], P('seq', 'dp')
- grad_gain_mlp: float32 [2048], P('dp')
- grad_mlp_gate: float32 [2048, 5120], P('dp', 'seq')
- grad_mlp_up: float32 [2048, 5120], P('dp', 'seq')
- grad_mlp_down: float32 [5120, 2048], P('seq', 'dp')
The draws below stay inside these ranges and needn't reach their ends.
Inputs may be any that keep to these rules, and one draw needn't show every extreme that they name: `seg_ids`: within a row the segment numbers never fall and every one of the 4 segments is present. `patch_owner`: in every row each image number owns exactly 256 patch tokens, in any order.
All inputs are finite; a program needn't handle non-finite values.
Results may differ from the reference program's by a relative error of at most 0.025.
Values may be sent and summed in bfloat16 or wider, within the bound.
A program may use at most 256 MiB of HBM per device.

```python
import math
import jax
import jax.numpy as jnp
import numpy as np
from jax import lax

D = 2048
H = 16
HD = 128
FF = 5120
ROW = 512
NP = 256
EXR = 2
SEGS = 4
ROWS = 16
PATCH_ROW = 512
SEG_MOST = 256


def draw_patch_owner(key, part):
    row_keys = jax.random.split(key, ROWS)
    orders = jax.vmap(lambda row_key: jax.random.permutation(row_key, PATCH_ROW))(row_keys)
    return (orders // NP).astype(jnp.int32)


def with_ends(array, key, smallest, high):
    longest = array.shape.index(max(array.shape))
    spots = []
    for shift in (0, 1):
        where = [jax.random.randint(jax.random.fold_in(key, axis), (), 0, length) for axis, length in enumerate(array.shape)]
        where[longest] = (where[longest] + shift) % array.shape[longest]
        spots.append(tuple(where))
    return array.at[spots[0]].set(smallest).at[spots[1]].set(high)


def level_of(rng, shape, shards, smallest, largest):
    gain = 1.0
    for dim, shards_of in shards:
        steps = jax.random.uniform(jax.random.fold_in(jax.random.fold_in(rng, 6), dim), (shards_of,), jnp.float32, smallest / len(shards), largest / len(shards))
        gain = gain * jnp.repeat(jnp.exp(steps), shape[dim] // shards_of).reshape((-1,) + (1,) * (len(shape) - 1 - dim))
    return gain


def profile(count, total, limit, slope):
    portions = [(1 << 20) // math.isqrt(grade ** slope) + 1 for grade in range(2, count + 1)]
    surplus, given = total - limit - (count - 1), [1] * (count - 1)
    while surplus > 0:
        movable = [i for i in range(count - 1) if given[i] < limit]
        pool, remaining = sum([portions[i] for i in movable]), surplus
        for i in movable:
            addition = min(limit - given[i], max(1, remaining * portions[i] // pool), surplus)
            given[i] = given[i] + addition
            surplus = surplus - addition
    return np.array([limit] + given)


def ragged(stream_key, count, total, reach, lean):
    if count == 2:
        one = jax.random.randint(stream_key, (), max(1, total - reach), min(reach, total - 1) + 1)
        return jnp.stack([one, total - one])
    tallies = jnp.asarray(profile(count, total, reach, lean), jnp.int32)
    couples = (count - 1) // 2
    giver, receiver = tallies[1:1 + 2 * couples:2], tallies[2:2 + 2 * couples:2]
    margin = jnp.minimum(giver - 1, reach - receiver)
    moved = jax.random.randint(jax.random.fold_in(stream_key, 1), (couples,), 0, 1 << 20) % (margin + 1)
    tallies = tallies.at[1:1 + 2 * couples:2].set(giver - moved).at[2:2 + 2 * couples:2].set(receiver + moved)
    return tallies[jax.random.permutation(jax.random.fold_in(stream_key, 2), count)]


def bell_draw(key, extent, width, limit, cuts=(), kind=jnp.bfloat16):
    level = level_of(key, extent, cuts, -0.22, 0.18) if cuts else 1.0
    entries = jax.random.normal(key, extent, jnp.float32) * width * level
    return jnp.minimum(jnp.maximum(entries, -limit), limit).astype(kind)


def setup_inputs(seed: int = 0) -> dict:
    streams_of = jax.random.split(jax.random.key(seed), 21)
    tokens = bell_draw(streams_of[0], (ROWS, ROW, D), 1.0, 6.0, ((0, 8), (1, 4)))
    patches = bell_draw(streams_of[1], (ROWS, PATCH_ROW, D), 1.0, 6.0, ((0, 8), (1, 4)))
    seg_ids = jax.vmap(lambda own: jnp.searchsorted(jnp.cumsum(ragged(own, SEGS, ROW, SEG_MOST, 2)), jnp.arange(ROW), side="right"))(jax.random.split(streams_of[2], ROWS)).reshape((ROWS, ROW)).astype(jnp.int32)
    seg_example = with_ends(jax.random.randint(streams_of[3], (ROWS, SEGS), 0, EXR), jax.random.fold_in(streams_of[3], 1), 0, EXR - 1).astype(jnp.int32)
    patch_owner = draw_patch_owner(jax.random.fold_in(streams_of[20], 71), 0)
    gain_self = jnp.clip(1.0 + 0.1 * jax.random.normal(streams_of[5], (D,), jnp.float32), 0.5, 1.5).astype(jnp.bfloat16)
    self_query = bell_draw(streams_of[6], (D, D), D ** -0.5, 0.125, ((0, 8), (1, 4)))
    self_key = bell_draw(streams_of[7], (D, D), D ** -0.5, 0.125, ((0, 8), (1, 4)))
    self_value = bell_draw(streams_of[8], (D, D), D ** -0.5, 0.125, ((0, 8), (1, 4)))
    self_out = bell_draw(streams_of[9], (D, D), (D // 8) ** -0.5, 0.375, ((0, 4), (1, 8)))
    gain_cross = jnp.clip(1.0 + 0.1 * jax.random.normal(streams_of[10], (D,), jnp.float32), 0.5, 1.5).astype(jnp.bfloat16)
    cross_query = bell_draw(streams_of[11], (D, D), D ** -0.5, 0.125, ((0, 8), (1, 4)))
    cross_key = bell_draw(streams_of[12], (D, D), D ** -0.5, 0.125, ((0, 8), (1, 4)))
    cross_value = bell_draw(streams_of[13], (D, D), D ** -0.5, 0.125, ((0, 8), (1, 4)))
    cross_out = bell_draw(streams_of[14], (D, D), (D // 32) ** -0.5, 0.75, ((0, 4), (1, 8)))
    gain_mlp = jnp.clip(1.0 + 0.1 * jax.random.normal(streams_of[15], (D,), jnp.float32), 0.5, 1.5).astype(jnp.bfloat16)
    mlp_gate = bell_draw(streams_of[16], (D, FF), D ** -0.5, 0.125, ((0, 8), (1, 4)))
    mlp_up = bell_draw(streams_of[17], (D, FF), D ** -0.5, 0.125, ((0, 8), (1, 4)))
    mlp_down = bell_draw(streams_of[18], (FF, D), FF ** -0.5, 0.078125, ((0, 4), (1, 8)))
    cotangent = bell_draw(streams_of[19], (ROWS, ROW, D), 1.0, 6.0, ((0, 8), (1, 4)))
    return {"tokens": tokens, "patches": patches, "seg_ids": seg_ids, "seg_example": seg_example, "patch_owner": patch_owner, "gain_self": gain_self, "self_query": self_query, "self_key": self_key, "self_value": self_value, "self_out": self_out, "gain_cross": gain_cross, "cross_query": cross_query, "cross_key": cross_key, "cross_value": cross_value, "cross_out": cross_out, "gain_mlp": gain_mlp, "mlp_gate": mlp_gate, "mlp_up": mlp_up, "mlp_down": mlp_down, "cotangent": cotangent}


@jax.custom_vjp
def low(v):
    return lax.optimization_barrier(v.astype(jnp.bfloat16)).astype(jnp.float32)

@jax.custom_vjp
def low_back(v):
    return v

def low_keep(v):
    return (low(v), None)

def low_pass(kept, grad):
    return (grad,)

def back_keep(v):
    return (v, None)

def back_low(kept, grad):
    return (low(grad),)
low.defvjp(low_keep, low_pass)
low_back.defvjp(back_keep, back_low)
epsilon = 1e-06
masked_value = -1e+30
highest = lax.Precision.HIGHEST

def both_ways(values):
    return low_back(low(values))

def normalize(values, gain_vec):
    factor = lax.rsqrt(lax.optimization_barrier(jnp.mean(values * values, axis=-1, keepdims=True)) + epsilon)
    return values * factor * gain_vec

def product(left_side, right_side):
    return jnp.einsum('gtd,de->gte', left_side, right_side, precision=highest)

def attention(queries, key_rows, value_rows, allowed):
    count = queries.shape[0]
    length = queries.shape[1]
    queries = queries.reshape(count, length, H, HD)
    key_rows = key_rows.reshape(count, key_rows.shape[1], H, HD)
    value_rows = value_rows.reshape(count, value_rows.shape[1], H, HD)
    scores = low_back(jnp.einsum('gqhd,gkhd->ghqk', queries, key_rows, precision=highest) * HD ** (-0.5))
    scores = jnp.where(allowed[:, None] > 0, scores, masked_value)
    weights = low(jax.nn.softmax(scores, axis=-1))
    output = jnp.einsum('ghqk,gkhd->gqhd', weights, value_rows, precision=highest)
    return both_ways(output.reshape(count, length, H * HD))

def layer_block(params, row_block):
    gain_self, self_query, self_key, self_value, self_out, gain_cross, cross_query, cross_key, cross_value, cross_out, gain_mlp, mlp_gate, mlp_up, mlp_down = params
    tokens, patches, seg_ids, seg_example, patch_owner = row_block
    length = tokens.shape[1]
    positions = jnp.arange(length, dtype=jnp.int32)
    causal = positions[:, None] >= positions[None, :]
    self_mask = ((seg_ids[:, :, None] == seg_ids[:, None, :]) & causal[None]).astype(jnp.int32)
    onehot = (seg_ids[:, :, None] == jnp.arange(SEGS, dtype=jnp.int32)[None, None, :]).astype(jnp.int32)
    example_of = lax.optimization_barrier(jnp.sum(onehot * seg_example[:, None, :], axis=2))
    cross_mask = (example_of[:, :, None] == patch_owner[:, None, :]).astype(jnp.int32)
    normed = low(normalize(tokens, gain_self))
    attended = attention(both_ways(product(normed, self_query)), both_ways(product(normed, self_key)), both_ways(product(normed, self_value)), self_mask)
    after_self = tokens + low_back(product(attended, self_out))
    normed = low(normalize(after_self, gain_cross))
    mixed = attention(both_ways(product(normed, cross_query)), both_ways(product(patches, cross_key)), both_ways(product(patches, cross_value)), cross_mask)
    after_cross = after_self + low_back(product(mixed, cross_out))
    normed = low(normalize(after_cross, gain_mlp))
    gate_pre = low_back(product(normed, mlp_gate))
    upward = low_back(product(normed, mlp_up))
    hidden = low(jax.nn.gelu(gate_pre, approximate=True) * upward)
    return after_cross + low_back(product(hidden, mlp_down))

def reference(tokens, patches, seg_ids, seg_example, patch_owner, gain_self, self_query, self_key, self_value, self_out, gain_cross, cross_query, cross_key, cross_value, cross_out, gain_mlp, mlp_gate, mlp_up, mlp_down, cotangent):
    params = tuple((weight.astype(jnp.float32) for weight in (gain_self, self_query, self_key, self_value, self_out, gain_cross, cross_query, cross_key, cross_value, cross_out, gain_mlp, mlp_gate, mlp_up, mlp_down)))
    group_rows = math.gcd(ROWS, 8)

    def grouped(values):
        return values.reshape((ROWS // group_rows, group_rows) + values.shape[1:])
    int_parts = (grouped(seg_ids), grouped(seg_example), grouped(patch_owner))
    checked = jax.checkpoint(layer_block)

    def forward(weights, token_values, patch_values):

        def one_group(row_block):
            return checked(weights, row_block)
        return lax.map(one_group, (grouped(token_values), grouped(patch_values)) + int_parts)
    output, pullback = jax.vjp(forward, params, tokens.astype(jnp.float32), patches.astype(jnp.float32))
    grad_params, grad_tokens, grad_patches = pullback(grouped(cotangent.astype(jnp.float32)))
    return (output.reshape(ROWS, ROW, D).astype(jnp.bfloat16), grad_tokens.reshape(ROWS, ROW, D), grad_patches.reshape(ROWS, PATCH_ROW, D), grad_params[0], grad_params[1], grad_params[2], grad_params[3], grad_params[4], grad_params[5], grad_params[6], grad_params[7], grad_params[8], grad_params[9], grad_params[10], grad_params[11], grad_params[12], grad_params[13])
```

```python
import itertools

import jax
import jax.numpy as jnp
from jax import lax
from jax.sharding import Mesh
from jax.sharding import PartitionSpec as P

HD = 128


epsilon = 1e-06
masked_value = -1e30

AXES = ("chip", "core", "zh", "zp")


def moves(chips, source_of):
    pairs = []
    for chip, core, zh, zp in itertools.product(range(chips), range(2), range(2), range(2)):
        a, b, c, d = source_of(chip, core, zh, zp)
        pairs.append((((a * 2 + b) * 2 + c) * 2 + d, ((chip * 2 + core) * 2 + zh) * 2 + zp))
    return pairs


def permute(values, source_of):
    return lax.ppermute(values, AXES, moves(lax.axis_size("chip"), source_of))


def swapped(values):
    return permute(values, lambda chip, core, zh, zp: (chip, zh, core, zp))


def swapped_other(values):
    return permute(values, lambda chip, core, zh, zp: (chip, 1 - zh, core, zp))


def swapped_other_back(values):
    return permute(values, lambda chip, core, zh, zp: (chip, zh, 1 - core, zp))


def other_core(values):
    return permute(values, lambda chip, core, zh, zp: (chip, 1 - core, zh, zp))


def other_zp(values):
    return permute(values, lambda chip, core, zh, zp: (chip, core, zh, 1 - zp))


def spread(block):
    beside = other_zp(block)
    across = other_core(block)
    corner = other_core(beside)
    return jnp.concatenate([block, beside, across, corner], axis=1)


def collect(partial):
    half = partial.shape[1] // 2
    quarter = half // 2
    arrived = other_core(partial[:, half:].astype(jnp.bfloat16))
    kept = partial[:, :half] + arrived.astype(jnp.float32)
    landed = other_zp(kept[:, quarter:].astype(jnp.bfloat16))
    return kept[:, :quarter] + landed.astype(jnp.float32)


def relative(values):
    rows, length = values.shape
    cut = values.reshape(rows, 2, 2, length // 4)
    cut = jnp.where(lax.axis_index("core") == 1, cut[:, ::-1], cut)
    cut = jnp.where(lax.axis_index("zp") == 1, cut[:, :, ::-1], cut)
    return cut.reshape(rows, length)


def gather_weights(shards_of, axis):
    first = swapped(shards_of)
    second = swapped_other(shards_of)
    low = lax.axis_index("zh") == 0
    pair = jnp.concatenate(
        [jnp.where(low, first, second), jnp.where(low, second, first)], axis=axis
    )
    return lax.all_gather(pair, "chip", axis=axis, tiled=True)


def reduce_weights(grads, axis):
    part = lax.psum_scatter(
        grads.astype(jnp.bfloat16), "chip", scatter_dimension=axis, tiled=True
    )
    lower, upper = jnp.split(part, 2, axis=axis)
    low = lax.axis_index("zh") == 0
    first = swapped(jnp.where(low, lower, upper))
    second = swapped_other_back(jnp.where(low, upper, lower))
    return first.astype(jnp.float32) + second.astype(jnp.float32)


def normalize(values, gain_vec):
    factor = lax.rsqrt(jnp.mean(values * values, axis=-1, keepdims=True) + epsilon)
    return values * factor * gain_vec


def norm_back(values, gain_vec, gradient):
    normed_value, pullback = jax.vjp(lambda inputs: normalize(inputs, gain_vec), values)
    return pullback(gradient)[0]


def gain_part(values, gradient):
    factor = lax.rsqrt(jnp.mean(values * values, axis=-1, keepdims=True) + epsilon)
    return jnp.sum(gradient * values * factor, axis=(0, 1))


def project(left_side, right_side):
    return jnp.einsum("rtd,de->rte", left_side, right_side, preferred_element_type=jnp.float32)


def project_back(gradient, right_side):
    return jnp.einsum("rte,de->rtd", gradient, right_side, preferred_element_type=jnp.float32)


def weight_grad(left_side, gradient):
    return jnp.einsum("rtd,rte->de", left_side, gradient, preferred_element_type=jnp.float32)


def split_heads(values, head_count):
    return values.reshape(
        values.shape[0], values.shape[1], head_count, values.shape[2] // head_count
    )


def merge_heads(values):
    return values.reshape(values.shape[0], values.shape[1], values.shape[2] * values.shape[3])


def scores_of(queries, key_rows, allowed, score_scale):
    scores = (
        jnp.einsum("rqhd,rkhd->rhqk", queries, key_rows, preferred_element_type=jnp.float32)
        * score_scale
    )
    return jnp.where(allowed[:, None] > 0, scores, masked_value)


def attend(queries, key_rows, value_rows, allowed, score_scale):
    scores = scores_of(queries, key_rows, allowed, score_scale)
    peak_score = jnp.max(scores, axis=-1, keepdims=True)
    shifted = jnp.exp(scores - peak_score)
    denominator = jnp.sum(shifted, axis=-1, keepdims=True)
    weights = (shifted / denominator).astype(jnp.bfloat16)
    output = jnp.einsum("rhqk,rkhd->rqhd", weights, value_rows, preferred_element_type=jnp.float32)
    return (merge_heads(output).astype(jnp.bfloat16), peak_score + jnp.log(denominator))


def attend_back(queries, key_rows, value_rows, allowed, log_total, grad_out, score_scale):
    probability = jnp.exp(scores_of(queries, key_rows, allowed, score_scale) - log_total)
    grad_probs = jnp.einsum(
        "rqhd,rkhd->rhqk", grad_out, value_rows, preferred_element_type=jnp.float32
    )
    grad_values = jnp.einsum(
        "rhqk,rqhd->rkhd",
        probability.astype(jnp.bfloat16),
        grad_out,
        preferred_element_type=jnp.float32,
    )
    inner_sum = jnp.sum(probability * grad_probs, axis=-1, keepdims=True)
    grad_scores = (probability * (grad_probs - inner_sum)).astype(jnp.bfloat16)
    grad_queries = (
        jnp.einsum("rhqk,rkhd->rqhd", grad_scores, key_rows, preferred_element_type=jnp.float32)
        * score_scale
    )
    grad_keys = (
        jnp.einsum("rhqk,rqhd->rkhd", grad_scores, queries, preferred_element_type=jnp.float32)
        * score_scale
    )
    return (
        merge_heads(grad_queries).astype(jnp.bfloat16),
        merge_heads(grad_keys).astype(jnp.bfloat16),
        merge_heads(grad_values).astype(jnp.bfloat16),
    )


def gelu_tanh(values):
    return jax.nn.gelu(values, approximate=True)


def shards(
    tokens,
    patches,
    seg_ids,
    seg_example,
    patch_owner,
    gain_self,
    self_query,
    self_key,
    self_value,
    self_out,
    gain_cross,
    cross_query,
    cross_key,
    cross_value,
    cross_out,
    gain_mlp,
    mlp_gate,
    mlp_up,
    mlp_down,
    cotangent,
):
    head_count = self_query.shape[1] // HD
    score_scale = HD ** (-0.5)
    gains = lax.all_gather(
        jnp.stack([gain_self, gain_cross, gain_mlp]), ("chip", "core"), axis=1, tiled=True
    ).astype(jnp.float32)
    norm_one, norm_two, norm_three = gains[0], gains[1], gains[2]
    onehot = (
        seg_ids[:, :, None] == lax.iota(jnp.int32, seg_example.shape[1])[None, None, :]
    ).astype(jnp.int32)
    example_of = jnp.sum(onehot * seg_example[:, None, :], axis=2)
    marks = swapped(jnp.concatenate([seg_ids, example_of, patch_owner], axis=0))
    rows = seg_ids.shape[0]
    length = seg_ids.shape[1]
    seg_here = relative(marks[:rows])
    example_here = relative(marks[rows : 2 * rows])
    owner_here = relative(marks[2 * rows :])
    positions = relative(lax.broadcasted_iota(jnp.int32, (1, length), 1))
    causal = positions[:, :, None] >= positions[:, None, :]
    self_mask = ((seg_here[:, :, None] == seg_here[:, None, :]) & causal).astype(jnp.int32)
    cross_mask = (example_here[:, :, None] == owner_here[:, None, :]).astype(jnp.int32)

    local_tokens = swapped(tokens)
    self_in = gather_weights(jnp.stack([self_query, self_key, self_value]), 1)
    local_stream = local_tokens.astype(jnp.float32)
    normed_one = spread(normalize(local_stream, norm_one).astype(jnp.bfloat16))
    self_outw = gather_weights(self_out[None], 2)[0]
    patch_rows = spread(swapped(patches))
    cross_in = gather_weights(jnp.stack([cross_query, cross_key, cross_value]), 1)
    cross_outw = gather_weights(cross_out[None], 2)[0]
    mlp_in = gather_weights(jnp.stack([mlp_gate, mlp_up]), 1)
    mlp_downw = gather_weights(mlp_down[None], 2)[0]
    local_grad = swapped(cotangent)
    grad_rows = spread(local_grad)

    self_queries = split_heads(project(normed_one, self_in[0]).astype(jnp.bfloat16), head_count)
    self_keys = split_heads(project(normed_one, self_in[1]).astype(jnp.bfloat16), head_count)
    self_values = split_heads(project(normed_one, self_in[2]).astype(jnp.bfloat16), head_count)
    self_attended, self_total = attend(self_queries, self_keys, self_values, self_mask, score_scale)
    after_self = local_stream + collect(project(self_attended, self_outw))
    normed_two = spread(normalize(after_self, norm_two).astype(jnp.bfloat16))
    cross_queries = split_heads(project(normed_two, cross_in[0]).astype(jnp.bfloat16), head_count)
    cross_keys = split_heads(project(patch_rows, cross_in[1]).astype(jnp.bfloat16), head_count)
    cross_values = split_heads(project(patch_rows, cross_in[2]).astype(jnp.bfloat16), head_count)
    cross_mixed, cross_total = attend(
        cross_queries, cross_keys, cross_values, cross_mask, score_scale
    )
    after_cross = after_self + collect(project(cross_mixed, cross_outw))
    normed_three = spread(normalize(after_cross, norm_three).astype(jnp.bfloat16))
    gate_pre = project(normed_three, mlp_in[0])
    upward = project(normed_three, mlp_in[1])
    activated, gelu_pull = jax.vjp(gelu_tanh, gate_pre)
    hidden = (activated * upward).astype(jnp.bfloat16)
    result = collect(project(hidden, mlp_downw))
    output = swapped((after_cross + result).astype(jnp.bfloat16))

    grad_hidden = project_back(grad_rows, mlp_downw)
    grad_down_w = weight_grad(hidden, grad_rows)
    down_sum = reduce_weights(grad_down_w[None], 2)[0]
    grad_upward = (grad_hidden * activated).astype(jnp.bfloat16)
    grad_gate = gelu_pull(grad_hidden * upward)[0].astype(jnp.bfloat16)
    grad_norm_three = collect(
        project_back(grad_gate, mlp_in[0]) + project_back(grad_upward, mlp_in[1])
    )
    mlp_sums = reduce_weights(
        jnp.stack(
            [
                weight_grad(normed_three, grad_gate).astype(jnp.bfloat16),
                weight_grad(normed_three, grad_upward).astype(jnp.bfloat16),
            ]
        ),
        1,
    )
    part_three = gain_part(after_cross, grad_norm_three)
    grad_cross_stream = local_grad.astype(jnp.float32) + norm_back(
        after_cross, norm_three, grad_norm_three
    )
    cross_branch = spread(grad_cross_stream.astype(jnp.bfloat16))
    cross_out_sum = reduce_weights(weight_grad(cross_mixed, cross_branch)[None], 2)[0]
    grad_mixed = split_heads(
        project_back(cross_branch, cross_outw).astype(jnp.bfloat16), head_count
    )
    grad_cq, grad_ck, grad_cv = attend_back(
        cross_queries, cross_keys, cross_values, cross_mask, cross_total, grad_mixed, score_scale
    )
    cross_sums = reduce_weights(
        jnp.stack(
            [
                weight_grad(normed_two, grad_cq).astype(jnp.bfloat16),
                weight_grad(patch_rows, grad_ck).astype(jnp.bfloat16),
                weight_grad(patch_rows, grad_cv).astype(jnp.bfloat16),
            ]
        ),
        1,
    )
    grad_norm_two = collect(project_back(grad_cq, cross_in[0]))
    patch_part = collect(project_back(grad_ck, cross_in[1]) + project_back(grad_cv, cross_in[2]))
    grad_patches = swapped(patch_part.astype(jnp.bfloat16)).astype(jnp.float32)
    part_two = gain_part(after_self, grad_norm_two)
    grad_self_stream = grad_cross_stream + norm_back(after_self, norm_two, grad_norm_two)
    self_branch = spread(grad_self_stream.astype(jnp.bfloat16))
    self_out_sum = reduce_weights(weight_grad(self_attended, self_branch)[None], 2)[0]
    grad_attended = split_heads(
        project_back(self_branch, self_outw).astype(jnp.bfloat16), head_count
    )
    grad_sq, grad_sk, grad_sv = attend_back(
        self_queries, self_keys, self_values, self_mask, self_total, grad_attended, score_scale
    )
    self_sums = reduce_weights(
        jnp.stack(
            [
                weight_grad(normed_one, grad_sq).astype(jnp.bfloat16),
                weight_grad(normed_one, grad_sk).astype(jnp.bfloat16),
                weight_grad(normed_one, grad_sv).astype(jnp.bfloat16),
            ]
        ),
        1,
    )
    grad_norm_one = collect(
        project_back(grad_sq, self_in[0])
        + project_back(grad_sk, self_in[1])
        + project_back(grad_sv, self_in[2])
    )
    part_one = gain_part(local_stream, grad_norm_one)
    grad_local = grad_self_stream + norm_back(local_stream, norm_one, grad_norm_one)
    grad_tokens = swapped(grad_local.astype(jnp.bfloat16)).astype(jnp.float32)
    gain_sums = lax.psum(jnp.stack([part_one, part_two, part_three]), AXES)
    held = gain_self.shape[0]
    place = lax.axis_index(("chip", "core")) * held
    gain_sums = lax.dynamic_slice_in_dim(gain_sums, place, held, axis=1)
    return (
        output,
        grad_tokens,
        grad_patches,
        gain_sums[0],
        self_sums[0],
        self_sums[1],
        self_sums[2],
        self_out_sum,
        gain_sums[1],
        cross_sums[0],
        cross_sums[1],
        cross_sums[2],
        cross_out_sum,
        gain_sums[2],
        mlp_sums[0],
        mlp_sums[1],
        down_sum,
    )


def solution(mesh):
    devices = mesh.devices.reshape(mesh.shape["dp"] // 2, 2, 2, mesh.shape["seq"] // 2)
    fine = Mesh(devices, AXES)
    dp = ("chip", "core")
    seq = ("zh", "zp")
    stream = P(dp, seq, None)
    rows = P(dp, None)
    inward = P(dp, seq)
    outward = P(seq, dp)
    vector = P(dp)
    block = (vector, inward, inward, inward, outward)
    weights = block + block + (vector, inward, inward, outward)
    return jax.shard_map(
        shards,
        mesh=fine,
        in_specs=(stream, stream, rows, rows, rows) + weights + (stream,),
        out_specs=(stream, stream, stream) + weights,
        check_vma=False,
    )
```

```python
import itertools

import jax
import jax.numpy as jnp
from jax import lax
from jax.experimental import pallas as pl
from jax.experimental.pallas import tpu as pltpu
from jax.sharding import Mesh
from jax.sharding import PartitionSpec as P

HD = 128


epsilon = 1e-06
masked_value = -1e30

AXES = ("chip", "core", "zh", "zp")


def moves(chips, source_of):
    pairs = []
    for chip, core, zh, zp in itertools.product(range(chips), range(2), range(2), range(2)):
        a, b, c, d = source_of(chip, core, zh, zp)
        pairs.append((((a * 2 + b) * 2 + c) * 2 + d, ((chip * 2 + core) * 2 + zh) * 2 + zp))
    return pairs


def permute(values, source_of):
    return lax.ppermute(values, AXES, moves(lax.axis_size("chip"), source_of))


def swapped(values):
    return permute(values, lambda chip, core, zh, zp: (chip, zh, core, zp))


def swapped_other(values):
    return permute(values, lambda chip, core, zh, zp: (chip, 1 - zh, core, zp))


def swapped_other_back(values):
    return permute(values, lambda chip, core, zh, zp: (chip, zh, 1 - core, zp))


def other_core(values):
    return permute(values, lambda chip, core, zh, zp: (chip, 1 - core, zh, zp))


def other_zp(values):
    return permute(values, lambda chip, core, zh, zp: (chip, core, zh, 1 - zp))


def spread(block, *others):
    beside = other_zp(block)
    across = other_core(block)
    if others:
        beside, across = lax.optimization_barrier(((beside, across),) + others)[0]
    corner = other_core(beside)
    return jnp.concatenate([block, beside, across, corner], axis=1)


def collect_half(partial):
    half = partial.shape[1] // 2
    return partial[:, :half].astype(jnp.float32) + other_core(
        partial[:, half:]
    ).astype(jnp.float32)


def collect_rest(kept):
    quarter = kept.shape[1] // 2
    landed = other_zp(kept[:, quarter:].astype(jnp.bfloat16))
    return kept[:, :quarter] + landed.astype(jnp.float32)


def relative(values):
    rows, length = values.shape
    cut = values.reshape(rows, 2, 2, length // 4)
    cut = jnp.where(lax.axis_index("core") == 1, cut[:, ::-1], cut)
    cut = jnp.where(lax.axis_index("zp") == 1, cut[:, :, ::-1], cut)
    return cut.reshape(rows, length)


def after(values, *others):
    return lax.optimization_barrier((values,) + others)[0]


def exchange(shards_of):
    return swapped(shards_of), swapped_other(shards_of)


def pair_up(exchanged):
    first, second = exchanged
    low = lax.axis_index("zh") == 0
    return jnp.concatenate([jnp.where(low, first, second), jnp.where(low, second, first)], axis=0)


def gather_chips(pair):
    return lax.all_gather(pair, "chip", axis=0, tiled=True)


def scatter_chips(grads):
    return lax.psum_scatter(
        grads.astype(jnp.bfloat16), "chip", scatter_dimension=0, tiled=True
    )


def unpair(part):
    lower, upper = jnp.split(part, 2, axis=0)
    low = lax.axis_index("zh") == 0
    first = swapped(jnp.where(low, lower, upper))
    second = swapped_other_back(jnp.where(low, upper, lower))
    return first.astype(jnp.float32) + second.astype(jnp.float32)


def normalize(values, gain_vec):
    factor = lax.rsqrt(jnp.mean(values * values, axis=-1, keepdims=True) + epsilon)
    return values * factor * gain_vec


def norm_back(values, gain_vec, gradient):
    normed_value, pullback = jax.vjp(lambda inputs: normalize(inputs, gain_vec), values)
    return pullback(gradient)[0]


def gain_part(values, gradient):
    factor = lax.rsqrt(jnp.mean(values * values, axis=-1, keepdims=True) + epsilon)
    return jnp.sum(gradient * values * factor, axis=(0, 1))


MESH = pl.DeviceIdType.MESH
ANY = pl.BlockSpec(memory_space=pl.ANY)
VMEM = pl.BlockSpec(memory_space=pltpu.VMEM)
PARTS = 4


def across_plane(axis):
    chip = lax.axis_index("chip")
    x, y = chip % 2, chip // 2
    return y * 2 + 1 - x if axis == 0 else (1 - y) * 2 + x


def greet(everyone, plane=False):
    core, zh, zp = lax.axis_index("core"), lax.axis_index("zh"), lax.axis_index("zp")
    barrier = pltpu.get_barrier_semaphore()
    count = 0
    for a, b, c in itertools.product(range(2), range(2), range(2)):
        if (a, b, c) == (0, 0, 0) or (b and not everyone):
            continue
        pl.semaphore_signal(
            barrier,
            inc=1,
            device_id={"core": (core + a) % 2, "zh": (zh + b) % 2, "zp": (zp + c) % 2},
            device_id_type=MESH,
        )
        count += 1
    if plane:
        for axis in range(2):
            pl.semaphore_signal(
                barrier, inc=1, device_id={"chip": across_plane(axis)}, device_id_type=MESH
            )
            count += 1
    pl.semaphore_wait(barrier, count)


def to_core(src, dst, send, recv):
    return pltpu.make_async_remote_copy(
        src, dst, send, recv, device_id={"core": 1 - lax.axis_index("core")}, device_id_type=MESH
    )


def to_zp(src, dst, send, recv):
    return pltpu.make_async_remote_copy(
        src, dst, send, recv, device_id={"zp": 1 - lax.axis_index("zp")}, device_id_type=MESH
    )


def to_swapped(src, dst, send, recv):
    core, zh = lax.axis_index("core"), lax.axis_index("zh")
    return pltpu.make_async_remote_copy(
        src, dst, send, recv, device_id={"core": zh, "zh": core}, device_id_type=MESH
    )


class Exchange:
    def __init__(self, src, pair, sems):
        self.src, self.pair, self.sems = src, pair, sems
        self.core, self.zh = lax.axis_index("core"), lax.axis_index("zh")
        rows = src.shape[0]
        self.mine = pair.at[pl.ds(pl.multiple_of(self.core * rows, rows), rows)]
        self.slots = [pair.at[pl.ds(a * rows, rows)] for a in range(2)]

    def far(self):
        return pltpu.make_async_remote_copy(
            self.src,
            self.mine,
            self.sems.at[0],
            self.sems.at[2 + self.core],
            device_id={"core": self.zh, "zh": 1 - self.zh},
            device_id_type=MESH,
        )

    def near(self):
        return pltpu.make_async_remote_copy(
            self.src,
            self.mine,
            self.sems.at[1],
            self.sems.at[2 + self.core],
            device_id={"core": 1 - self.core},
            device_id_type=MESH,
        )

    def own(self):
        return pltpu.make_async_copy(self.src, self.mine, self.sems.at[2 + self.core])

    def start(self):
        self.far().start()

        @pl.when(self.core == self.zh)
        def _():
            self.own().start()

        @pl.when(self.core != self.zh)
        def _():
            self.near().start()

    def finish(self):
        self.far().wait_send()

        @pl.when(self.core != self.zh)
        def _():
            self.near().wait_send()

        for a in range(2):
            pltpu.make_async_copy(self.src, self.slots[a], self.sems.at[2 + a]).wait()


class Spread:
    def __init__(self, block, gathered, sems):
        self.block, self.gathered, self.sems = block, gathered, sems
        self.length = block.shape[1]
        self.step = 2 * self.length // PARTS

    def src(self, k):
        return self.block.at[k // (PARTS // 2), pl.ds(pl.multiple_of(k % (PARTS // 2) * self.step, self.step), self.step)]

    def dst(self, k, slot):
        return self.gathered.at[
            k // (PARTS // 2),
            pl.ds(
                pl.multiple_of(slot * self.length + k % (PARTS // 2) * self.step, self.step),
                self.step,
            ),
        ]

    def beside(self, k):
        return to_zp(self.src(k), self.dst(k, 1), self.sems.at[0, k], self.sems.at[1, k])

    def across(self, k):
        return to_core(self.src(k), self.dst(k, 2), self.sems.at[2, k], self.sems.at[3, k])

    def corner(self, k):
        return to_core(self.dst(k, 1), self.dst(k, 3), self.sems.at[4, k], self.sems.at[5, k])

    def own(self, k):
        return pltpu.make_async_copy(self.src(k), self.dst(k, 0), self.sems.at[6, k])

    def start(self, k):
        self.beside(k).start()
        self.across(k).start()
        self.own(k).start()

    def relay(self, k):
        self.beside(k).wait_recv()
        self.corner(k).start()

    def finish(self, k):
        self.beside(k).wait_send()
        self.across(k).wait()
        self.corner(k).wait()
        self.own(k).wait()


class Collect:
    def __init__(self, partial, arrived, outgoing, landed, sems):
        self.partial, self.arrived = partial, arrived
        self.outgoing, self.landed, self.sems = outgoing, landed, sems
        self.length = outgoing.shape[1]
        self.step = 2 * self.length // PARTS

    def at(self, ref, k, block):
        return ref.at[
            k // (PARTS // 2),
            pl.ds(
                pl.multiple_of(block * self.length + k % (PARTS // 2) * self.step, self.step),
                self.step,
            ),
        ]

    def crossing(self, k, block):
        return to_core(
            self.at(self.partial, k, 2 + block),
            self.at(self.arrived, k, block),
            self.sems.at[2 * block, k],
            self.sems.at[2 * block + 1, k],
        )

    def landing(self, k):
        return to_zp(
            self.at(self.outgoing, k, 0),
            self.at(self.landed, k, 0),
            self.sems.at[4, k],
            self.sems.at[5, k],
        )

    def start(self):
        for block in (1, 0):
            for k in range(PARTS):
                self.crossing(k, block).start()

    def forward(self, k):
        self.crossing(k, 1).wait_recv()
        self.at(self.outgoing, k, 0)[...] = (
            self.at(self.partial, k, 1)[...].astype(jnp.float32)
            + self.at(self.arrived, k, 1)[...].astype(jnp.float32)
        ).astype(jnp.bfloat16)
        self.landing(k).start()

    def total(self, k):
        self.crossing(k, 0).wait_recv()
        self.landing(k).wait_recv()
        return (
            self.at(self.partial, k, 0)[...].astype(jnp.float32)
            + self.at(self.arrived, k, 0)[...].astype(jnp.float32)
        ) + self.at(self.landed, k, 0)[...].astype(jnp.float32)

    def finish(self, k):
        self.crossing(k, 0).wait_send()
        self.crossing(k, 1).wait_send()
        self.landing(k).wait_send()


class Unpair:
    def __init__(self, part, terms, sems):
        self.part, self.terms, self.sems = part, terms, sems
        self.core, self.zh = lax.axis_index("core"), lax.axis_index("zh")
        self.rows = part.shape[0] // 2

    def piece(self, p):
        return self.part.at[pl.ds(p * self.rows, self.rows)]

    def remote(self, p):
        return pltpu.make_async_remote_copy(
            self.piece(p),
            self.terms.at[self.zh],
            self.sems.at[p],
            self.sems.at[2 + self.zh],
            device_id={"core": p, "zh": self.core},
            device_id_type=MESH,
        )

    def own(self, p):
        return pltpu.make_async_copy(
            self.piece(p), self.terms.at[self.zh], self.sems.at[2 + self.zh]
        )

    def stays(self, p):
        return jnp.logical_and(self.core == p, self.zh == p)

    def start(self):
        for p in range(2):

            @pl.when(self.stays(p))
            def _(p=p):
                self.own(p).start()

            @pl.when(jnp.logical_not(self.stays(p)))
            def _(p=p):
                self.remote(p).start()

    def finish(self):
        for p in range(2):

            @pl.when(jnp.logical_not(self.stays(p)))
            def _(p=p):
                self.remote(p).wait_send()

            pltpu.make_async_copy(
                self.piece(p), self.terms.at[p], self.sems.at[2 + p]
            ).wait()


class Swap:
    def __init__(self, block, target, sems):
        self.block, self.target, self.sems = block, target, sems
        self.swaps = lax.axis_index("core") != lax.axis_index("zh")
        self.step = 2 * block.shape[1] // PARTS

    def at(self, ref, k):
        return ref.at[
            k // (PARTS // 2), pl.ds(pl.multiple_of(k % (PARTS // 2) * self.step, self.step), self.step)
        ]

    def remote(self, k):
        return to_swapped(
            self.at(self.block, k), self.at(self.target, k), self.sems.at[0, k], self.sems.at[1, k]
        )

    def own(self, k):
        return pltpu.make_async_copy(self.at(self.block, k), self.at(self.target, k), self.sems.at[1, k])

    def start(self, k):
        @pl.when(self.swaps)
        def _():
            self.remote(k).start()

        @pl.when(jnp.logical_not(self.swaps))
        def _():
            self.own(k).start()

    def arrive(self, k):
        self.own(k).wait()

    def finish(self, k):
        @pl.when(self.swaps)
        def _():
            self.remote(k).wait_send()


def each(body):
    lax.fori_loop(0, PARTS, lambda k, carry: (body(k), carry)[1], 0)


def kernel_call(number, name, inputs, outs, scratch, body):
    names = list(inputs) + list(outs) + list(scratch)

    def kernel(*refs):
        body(dict(zip(names, refs)))

    results = pl.pallas_call(
        kernel,
        out_shape=tuple(shape for shape, _ in outs.values()),
        in_specs=[VMEM] * len(inputs),
        out_specs=tuple(spec for _, spec in outs.values()),
        scratch_shapes=list(scratch.values()),
        compiler_params=pltpu.CompilerParams(
            collective_id=number, has_side_effects=True, vmem_limit_bytes=56 * 1024 * 1024
        ),
        name=name,
    )(*inputs.values())
    return dict(zip(outs, results))


def collect_scratch(tag, rows, length, width):
    return {
        tag + "arrived": pltpu.VMEM((rows, 2 * length, width), jnp.bfloat16),
        tag + "outgoing": pltpu.VMEM((rows, length, width), jnp.bfloat16),
        tag + "landed": pltpu.VMEM((rows, length, width), jnp.bfloat16),
        tag + "collect_sems": pltpu.SemaphoreType.DMA((6, PARTS)),
    }


def collect_of(refs, tag, partial):
    return Collect(
        refs[partial],
        refs[tag + "arrived"],
        refs[tag + "outgoing"],
        refs[tag + "landed"],
        refs[tag + "collect_sems"],
    )


def shape_of(shape, dtype):
    return jax.ShapeDtypeStruct(shape, dtype)


def gathered_out(rows, length, width):
    return (shape_of((rows, 4 * length, width), jnp.bfloat16), ANY)


def pair_out(shard):
    return (shape_of((2 * shard.shape[0], shard.shape[1]), shard.dtype), ANY)


def terms_out(part):
    return (shape_of((2, part.shape[0] // 2, part.shape[1]), part.dtype), ANY)


class PlaneGather:
    def __init__(self, whole, columns, sems):
        self.whole, self.columns, self.sems = whole, columns, sems
        self.rows = whole.shape[0] // 4

    def half(self, chip, which):
        start, size = self.columns
        return self.whole.at[
            pl.ds(pl.multiple_of(chip * self.rows, self.rows), self.rows),
            pl.ds(start + which * (size // 2), size // 2),
        ]

    def own(self, axis, which):
        ref = self.half(lax.axis_index("chip"), which)
        return self.copy(ref, axis, 2 * axis + which)

    def passed(self, which):
        ref = self.half(across_plane(which), which)
        return self.copy(ref, 1 - which, 4 + which)

    def copy(self, ref, axis, number):
        return pltpu.make_async_remote_copy(
            ref,
            ref,
            self.sems.at[0, number],
            self.sems.at[1, number],
            device_id={"chip": across_plane(axis)},
            device_id_type=MESH,
        )

    def start(self):
        for axis in range(2):
            self.own(axis, axis).start()
        for axis in range(2):
            self.own(axis, 1 - axis).start()

    def relay(self):
        for which in range(2):
            self.own(which, which).wait_recv()
            self.passed(which).start()

    def finish(self):
        for axis in range(2):
            self.own(axis, axis).wait_send()
            self.own(axis, 1 - axis).wait()
            self.passed(axis).wait()


class SwapWhole:
    def __init__(self, array, target, sems):
        self.array, self.target, self.sems = array, target, sems
        self.swaps = lax.axis_index("core") != lax.axis_index("zh")

    def remote(self):
        return to_swapped(self.array, self.target, self.sems.at[0], self.sems.at[1])

    def own(self):
        return pltpu.make_async_copy(self.array, self.target, self.sems.at[1])

    def start(self):
        @pl.when(self.swaps)
        def _():
            self.remote().start()

        @pl.when(jnp.logical_not(self.swaps))
        def _():
            self.own().start()

    def finish(self):
        self.own().wait()

        @pl.when(self.swaps)
        def _():
            self.remote().wait_send()


def head(number, block, beside, marks, gain, first):
    rows, length, width = block.shape
    depth, size = first[0].shape
    in_plane = lax.axis_size("chip") == 4

    def body(refs):
        swap = Swap(refs["block"], refs["here"], refs["swap_sems"])
        marks_swap = SwapWhole(refs["marks"], refs["marks_here"], refs["marks_sems"])
        spread_work = Spread(refs["normed"], refs["gathered"], refs["spread_sems"])
        if in_plane:
            chip = lax.axis_index("chip")
            place = refs["whole"].at[pl.ds(pl.multiple_of(chip * 2 * depth, 2 * depth), 2 * depth)]
        else:
            place = refs["whole"]
        works = [
            Exchange(
                refs["first%d" % i],
                place.at[:, pl.ds(i * size, size)],
                refs["exchange_sems"].at[i],
            )
            for i in range(len(first))
        ]
        beside_swap = Swap(refs["beside"], refs["beside_here"], refs["beside_swap_sems"])
        beside_work = Spread(refs["beside_here"], refs["beside_gathered"], refs["beside_sems"])
        greet(True, in_plane)
        marks_swap.start()

        def norm_and_send(k):
            swap.arrive(k)
            values = swap.at(refs["here"], k)[...].astype(jnp.float32)
            spread_work.src(k)[...] = normalize(values, refs["gain"][...]).astype(jnp.bfloat16)
            spread_work.start(k)

        def pass_on(k):
            beside_swap.arrive(k)
            beside_work.start(k)

        planes = [
            PlaneGather(refs["whole"], (i * size, size), refs["plane_sems"].at[i])
            for i in range(len(first))
        ]
        last = len(works) - 1
        works[0].start()
        for i, work in enumerate(works):
            work.finish()
            if in_plane:
                planes[i].start()
            if i < last:
                works[i + 1].start()
            if i == 0:
                each(swap.start)
            if i == last - 1:
                each(beside_swap.start)
            if in_plane and i:
                planes[i - 1].relay()
            if i == 1:
                each(norm_and_send)
            if i == last:
                each(spread_work.relay)
        pass_on(0)
        pass_on(1)
        if in_plane:
            planes[last].relay()
        for k in range(2, PARTS):
            pass_on(k)
        each(beside_work.relay)
        each(beside_work.finish)
        each(beside_swap.finish)
        each(spread_work.finish)
        each(swap.finish)
        if in_plane:
            for plane in planes:
                plane.finish()
        marks_swap.finish()

    whole_rows = 8 * depth if in_plane else 2 * depth
    results = kernel_call(
        number,
        "head",
        {
            "block": block,
            "beside": beside,
            "marks": marks,
            "gain": gain[None],
            **{"first%d" % i: shard for i, shard in enumerate(first)},
        },
        {
            "here": (shape_of(block.shape, block.dtype), VMEM),
            "marks_here": (shape_of(marks.shape, marks.dtype), VMEM),
            "gathered": gathered_out(rows, length, width),
            "whole": (shape_of((whole_rows, len(first) * size), jnp.bfloat16), ANY),
            "beside_gathered": gathered_out(rows, length, width),
        },
        {
            "normed": pltpu.VMEM((rows, length, width), jnp.bfloat16),
            "spread_sems": pltpu.SemaphoreType.DMA((7, PARTS)),
            "swap_sems": pltpu.SemaphoreType.DMA((2, PARTS)),
            "beside_here": pltpu.VMEM((rows, length, width), jnp.bfloat16),
            "beside_sems": pltpu.SemaphoreType.DMA((7, PARTS)),
            "beside_swap_sems": pltpu.SemaphoreType.DMA((2, PARTS)),
            "marks_sems": pltpu.SemaphoreType.DMA((2,)),
            "exchange_sems": pltpu.SemaphoreType.DMA((len(first), 4)),
            "plane_sems": pltpu.SemaphoreType.DMA((len(first), 2, 6)),
        },
        body,
    )
    whole = results["whole"] if in_plane else gather_chips(results["whole"])
    return (
        results["here"],
        results["marks_here"],
        results["gathered"],
        whole,
        results["beside_gathered"],
    )


def turn_forward(number, partial, stream, gain):
    rows, length, width = stream.shape

    def body(refs):
        collect_work = collect_of(refs, "", "partial")
        spread_work = Spread(refs["normed"], refs["gathered"], refs["spread_sems"])
        greet(False)
        collect_work.start()
        each(collect_work.forward)

        def norm_and_send(k):
            values = collect_work.at(refs["stream"], k, 0)[...].astype(
                jnp.float32
            ) + collect_work.total(k)
            collect_work.at(refs["after"], k, 0)[...] = values
            spread_work.src(k)[...] = normalize(values, refs["gain"][...]).astype(jnp.bfloat16)
            spread_work.start(k)

        each(norm_and_send)
        each(spread_work.relay)
        each(spread_work.finish)
        each(collect_work.finish)

    results = kernel_call(
        number,
        "turn_forward",
        {"partial": partial, "stream": stream, "gain": gain[None]},
        {
            "after": (shape_of(stream.shape, jnp.float32), VMEM),
            "gathered": gathered_out(rows, length, width),
        },
        {
            **collect_scratch("", rows, length, width),
            "normed": pltpu.VMEM((rows, length, width), jnp.bfloat16),
            "spread_sems": pltpu.SemaphoreType.DMA((7, PARTS)),
        },
        body,
    )
    return results["after"], results["gathered"]


def norm_slope(values, gain, gradient):
    factor = lax.rsqrt(jnp.mean(values * values, axis=-1, keepdims=True) + epsilon)
    scaled = gain * gradient
    inner = jnp.mean(scaled * values, axis=-1, keepdims=True)
    return factor * scaled - values * (factor * factor * factor * inner), gradient * values * factor


def turn_back(number, partial, values, stream, gain, *parts):
    rows, length, width = values.shape

    def body(refs):
        collect_work = collect_of(refs, "", "partial")
        spread_work = Spread(refs["branch"], refs["gathered"], refs["spread_sems"])
        works = [
            Unpair(refs["part%d" % i], refs["terms%d" % i], refs["unpair_sems"].at[i])
            for i in range(len(parts))
        ]
        greet(bool(parts))
        collect_work.start()
        each(collect_work.forward)
        refs["gain_sum"][...] = jnp.zeros_like(refs["gain_sum"])

        def slope_and_send(k):
            slope, terms = norm_slope(
                collect_work.at(refs["values"], k, 0)[...].astype(jnp.float32),
                refs["gain"][...],
                collect_work.total(k),
            )
            sums = collect_work.at(refs["stream"], k, 0)[...].astype(jnp.float32) + slope
            collect_work.at(refs["after"], k, 0)[...] = sums
            spread_work.src(k)[...] = sums.astype(jnp.bfloat16)
            spread_work.start(k)
            refs["gain_sum"][...] += jnp.sum(terms, axis=0, keepdims=True)

        for work in works:
            work.start()
        each(slope_and_send)
        each(spread_work.relay)
        each(spread_work.finish)
        each(collect_work.finish)
        for work in works:
            work.finish()

    results = kernel_call(
        number,
        "turn_back",
        {
            "partial": partial,
            "values": values,
            "stream": stream,
            "gain": gain[None],
            **{"part%d" % i: part for i, part in enumerate(parts)},
        },
        {
            "after": (shape_of(values.shape, jnp.float32), VMEM),
            "gathered": gathered_out(rows, length, width),
            "gain_sum": (shape_of((1, width), jnp.float32), VMEM),
            **{"terms%d" % i: terms_out(part) for i, part in enumerate(parts)},
        },
        {
            **collect_scratch("", rows, length, width),
            "branch": pltpu.VMEM((rows, length, width), jnp.bfloat16),
            "spread_sems": pltpu.SemaphoreType.DMA((7, PARTS)),
            "unpair_sems": pltpu.SemaphoreType.DMA((max(1, len(parts)), 4)),
        },
        body,
    )
    return (results["after"], results["gathered"], results["gain_sum"]) + tuple(
        results["terms%d" % i] for i in range(len(parts))
    )


def leave(number, partial, values, stream, gain, *parts):
    rows, length, width = values.shape

    def body(refs):
        collect_work = collect_of(refs, "", "partial")
        swap = Swap(refs["leaving"], refs["out"], refs["swap_sems"])
        works = [
            Unpair(refs["part%d" % i], refs["terms%d" % i], refs["unpair_sems"].at[i])
            for i in range(len(parts))
        ]
        greet(True)
        collect_work.start()
        each(collect_work.forward)
        for work in works:
            work.start()
        refs["gain_sum"][...] = jnp.zeros_like(refs["gain_sum"])

        def slope_and_send(k):
            slope, terms = norm_slope(
                collect_work.at(refs["values"], k, 0)[...].astype(jnp.float32),
                refs["gain"][...],
                collect_work.total(k),
            )
            sums = collect_work.at(refs["stream"], k, 0)[...] + slope
            swap.at(refs["leaving"], k)[...] = sums.astype(jnp.bfloat16)
            swap.start(k)
            refs["gain_sum"][...] += jnp.sum(terms, axis=0, keepdims=True)

        each(slope_and_send)
        each(swap.arrive)
        each(swap.finish)
        each(collect_work.finish)
        for work in works:
            work.finish()

    results = kernel_call(
        number,
        "leave",
        {
            "partial": partial,
            "values": values,
            "stream": stream,
            "gain": gain[None],
            **{"part%d" % i: part for i, part in enumerate(parts)},
        },
        {
            "out": (shape_of(values.shape, jnp.bfloat16), ANY),
            "gain_sum": (shape_of((1, width), jnp.float32), VMEM),
            **{"terms%d" % i: terms_out(part) for i, part in enumerate(parts)},
        },
        {
            **collect_scratch("", rows, length, width),
            "leaving": pltpu.VMEM((rows, length, width), jnp.bfloat16),
            "swap_sems": pltpu.SemaphoreType.DMA((2, PARTS)),
            "unpair_sems": pltpu.SemaphoreType.DMA((max(1, len(parts)), 4)),
        },
        body,
    )
    return (results["out"], results["gain_sum"]) + tuple(
        results["terms%d" % i] for i in range(len(parts))
    )


def return_weights(number, gain_sums, *parts):
    chips = lax.axis_size("chip")
    steps = 3 + chips.bit_length() - 1

    def body(refs):
        works = [
            Unpair(refs["part%d" % i], refs["terms%d" % i], refs["sems"].at[i])
            for i in range(len(parts))
        ]
        core, zh, zp = (lax.axis_index(axis) for axis in ("core", "zh", "zp"))
        chip = lax.axis_index("chip")
        partners = [{"core": 1 - core}, {"zp": 1 - zp}, {"zh": 1 - zh}]
        for bit in range(chips.bit_length() - 1):
            size = 2**bit
            partners.append({"chip": chip + size - 2 * size * (chip // size % 2)})
        barrier = pltpu.get_barrier_semaphore()
        count = 0
        for a, b, c in itertools.product(range(2), range(2), range(2)):
            if (a, b, c) == (0, 0, 0):
                continue
            pl.semaphore_signal(
                barrier,
                inc=1,
                device_id={"core": (core + a) % 2, "zh": (zh + b) % 2, "zp": (zp + c) % 2},
                device_id_type=MESH,
            )
            count += 1
        for partner in partners[3:]:
            pl.semaphore_signal(barrier, inc=1, device_id=partner, device_id_type=MESH)
            count += 1
        pl.semaphore_wait(barrier, count)

        sums = refs["gain_sums"][...]
        for step in range(steps):
            refs["given"][step] = sums
            copy = pltpu.make_async_remote_copy(
                refs["given"].at[step],
                refs["taken"].at[step],
                refs["gain_sems"].at[0, step],
                refs["gain_sems"].at[1, step],
                device_id=partners[step],
                device_id_type=MESH,
            )
            copy.start()
            if step == 0:
                for work in works:
                    work.start()
            copy.wait()
            sums = sums + refs["taken"][step]
        refs["totals"][...] = sums
        for work in works:
            work.finish()

    shape = gain_sums.shape
    results = kernel_call(
        number,
        "return_weights",
        {"gain_sums": gain_sums, **{"part%d" % i: part for i, part in enumerate(parts)}},
        {
            "totals": (shape_of(shape, jnp.float32), VMEM),
            **{"terms%d" % i: terms_out(part) for i, part in enumerate(parts)},
        },
        {
            "given": pltpu.VMEM((steps,) + shape, jnp.float32),
            "taken": pltpu.VMEM((steps,) + shape, jnp.float32),
            "gain_sems": pltpu.SemaphoreType.DMA((2, steps)),
            "sems": pltpu.SemaphoreType.DMA((len(parts), 4)),
        },
        body,
    )
    return (results["totals"],) + tuple(results["terms%d" % i] for i in range(len(parts)))


def summed(terms):
    return terms[0].astype(jnp.float32) + terms[1].astype(jnp.float32)


def project(left_side, right_side):
    return jnp.einsum("rtd,de->rte", left_side, right_side, preferred_element_type=jnp.float32)


def project_back(gradient, right_side):
    return jnp.einsum("rte,de->rtd", gradient, right_side, preferred_element_type=jnp.float32)


def weight_grad(left_side, gradient):
    return jnp.einsum("rtd,rte->de", left_side, gradient, preferred_element_type=jnp.float32)


def split_heads(values, head_count):
    return values.reshape(
        values.shape[0], values.shape[1], head_count, values.shape[2] // head_count
    )


def merge_heads(values):
    return values.reshape(values.shape[0], values.shape[1], values.shape[2] * values.shape[3])


def scores_of(queries, key_rows, allowed, score_scale):
    scores = (
        jnp.einsum("rqhd,rkhd->rhqk", queries, key_rows, preferred_element_type=jnp.float32)
        * score_scale
    )
    return jnp.where(allowed[:, None] > 0, scores, masked_value)


def attend(queries, key_rows, value_rows, allowed, score_scale):
    scores = scores_of(queries, key_rows, allowed, score_scale)
    peak_score = jnp.max(scores, axis=-1, keepdims=True)
    shifted = jnp.exp(scores - peak_score)
    denominator = jnp.sum(shifted, axis=-1, keepdims=True)
    weights = (shifted / denominator).astype(jnp.bfloat16)
    output = jnp.einsum("rhqk,rkhd->rqhd", weights, value_rows, preferred_element_type=jnp.float32)
    return (merge_heads(output).astype(jnp.bfloat16), peak_score + jnp.log(denominator))


def attend_back(queries, key_rows, value_rows, allowed, log_total, grad_out, score_scale):
    probability = jnp.exp(scores_of(queries, key_rows, allowed, score_scale) - log_total)
    grad_probs = jnp.einsum(
        "rqhd,rkhd->rhqk", grad_out, value_rows, preferred_element_type=jnp.float32
    )
    grad_values = jnp.einsum(
        "rhqk,rqhd->rkhd",
        probability.astype(jnp.bfloat16),
        grad_out,
        preferred_element_type=jnp.float32,
    )
    inner_sum = jnp.sum(probability * grad_probs, axis=-1, keepdims=True)
    grad_scores = (probability * (grad_probs - inner_sum)).astype(jnp.bfloat16)
    grad_queries = (
        jnp.einsum("rhqk,rkhd->rqhd", grad_scores, key_rows, preferred_element_type=jnp.float32)
        * score_scale
    )
    grad_keys = (
        jnp.einsum("rhqk,rqhd->rkhd", grad_scores, queries, preferred_element_type=jnp.float32)
        * score_scale
    )
    return (
        merge_heads(grad_queries).astype(jnp.bfloat16),
        merge_heads(grad_keys).astype(jnp.bfloat16),
        merge_heads(grad_values).astype(jnp.bfloat16),
    )


def gelu_tanh(values):
    return jax.nn.gelu(values, approximate=True)


def shards(
    tokens,
    patches,
    seg_ids,
    seg_example,
    patch_owner,
    gain_self,
    self_query,
    self_key,
    self_value,
    self_out,
    gain_cross,
    cross_query,
    cross_key,
    cross_value,
    cross_out,
    gain_mlp,
    mlp_gate,
    mlp_up,
    mlp_down,
    cotangent,
):
    head_count = self_query.shape[1] // HD
    score_scale = HD ** (-0.5)
    gains = lax.all_gather(
        jnp.stack([gain_self, gain_cross, gain_mlp]), ("chip", "core"), axis=1, tiled=True
    ).astype(jnp.float32)
    norm_one, norm_two, norm_three = gains[0], gains[1], gains[2]
    onehot = (
        seg_ids[:, :, None] == lax.iota(jnp.int32, seg_example.shape[1])[None, None, :]
    ).astype(jnp.int32)
    example_of = jnp.sum(onehot * seg_example[:, None, :], axis=2)
    marks = jnp.concatenate([seg_ids, example_of, patch_owner], axis=0)
    rows = seg_ids.shape[0]
    length = seg_ids.shape[1]
    wide = self_query.shape[1]
    hidden_wide = mlp_gate.shape[1]
    local_tokens, marks, normed_one, self_w, patch_rows = head(
        0, tokens, patches, marks, norm_one, (self_query, self_key, self_value, self_out.T)
    )
    cross_moved = exchange(
        after(
            jnp.concatenate([cross_key, cross_value, cross_query, cross_out.T], axis=1), normed_one
        )
    )
    seg_here = relative(marks[:rows])
    example_here = relative(marks[rows : 2 * rows])
    owner_here = relative(marks[2 * rows :])
    positions = relative(lax.broadcasted_iota(jnp.int32, (1, length), 1))
    causal = positions[:, :, None] >= positions[:, None, :]
    self_mask = ((seg_here[:, :, None] == seg_here[:, None, :]) & causal).astype(jnp.int32)
    cross_mask = (example_here[:, :, None] == owner_here[:, None, :]).astype(jnp.int32)
    self_qkv = project(normed_one, self_w[:, : 3 * wide]).astype(jnp.bfloat16)
    self_outw = self_w[:, 3 * wide :]
    self_queries = split_heads(self_qkv[..., :wide], head_count)
    self_keys = split_heads(self_qkv[..., wide : 2 * wide], head_count)
    self_values = split_heads(self_qkv[..., 2 * wide :], head_count)
    self_attended, self_total = attend(self_queries, self_keys, self_values, self_mask, score_scale)
    self_partial = project_back(self_attended, self_outw).astype(jnp.bfloat16)
    cross_pair = pair_up(after(cross_moved, self_partial))
    cross_w = gather_chips(cross_pair)
    cross_kv = cross_w[:, : 2 * wide]
    cross_q = cross_w[:, 2 * wide : 3 * wide]
    cross_outw = cross_w[:, 3 * wide :]
    mlp_moved = exchange(after(jnp.concatenate([mlp_gate, mlp_up], axis=1), cross_pair))
    after_self, normed_two = turn_forward(
        2, after(self_partial, cross_pair), local_tokens, norm_two
    )
    mlp_pair = pair_up(after(mlp_moved, after_self))
    mlp_in = gather_chips(mlp_pair)
    normed_two = after(normed_two, mlp_pair)
    down_moved = exchange(after(mlp_down.T, mlp_pair))
    local_grad = swapped(after(cotangent, mlp_pair))
    cross_kv_rows = project(patch_rows, cross_kv).astype(jnp.bfloat16)
    cross_queries = split_heads(project(normed_two, cross_q).astype(jnp.bfloat16), head_count)
    cross_keys = split_heads(cross_kv_rows[..., :wide], head_count)
    cross_values = split_heads(cross_kv_rows[..., wide:], head_count)
    cross_mixed, cross_total = attend(
        cross_queries, cross_keys, cross_values, cross_mask, score_scale
    )
    cross_partial = project_back(cross_mixed, cross_outw).astype(jnp.bfloat16)
    down_pair = pair_up(after(down_moved, cross_partial))
    mlp_downw = gather_chips(down_pair)
    after_cross, normed_three = turn_forward(
        3, after(cross_partial, down_pair), after_self, norm_three
    )
    both = project(normed_three, mlp_in)
    grad_rows = spread(after(local_grad, normed_three), both)
    gate_pre = both[..., :hidden_wide]
    upward = both[..., hidden_wide:]
    activated, gelu_pull = jax.vjp(gelu_tanh, gate_pre)
    hidden = (activated * upward).astype(jnp.bfloat16)

    grad_down_w = weight_grad(grad_rows, hidden).astype(jnp.bfloat16)
    down_part = scatter_chips(grad_down_w)
    grad_hidden = project(after(grad_rows, grad_down_w), mlp_downw)
    grad_upward = (grad_hidden * activated).astype(jnp.bfloat16)
    grad_gate = gelu_pull(grad_hidden * upward)[0].astype(jnp.bfloat16)
    grad_both = jnp.concatenate([grad_gate, grad_upward], axis=2)
    partial_three = project_back(grad_both, mlp_in).astype(jnp.bfloat16)
    grad_mlp_w = weight_grad(normed_three, grad_both).astype(jnp.bfloat16)
    mlp_part = scatter_chips(grad_mlp_w)
    result_partial = project_back(hidden, mlp_downw).astype(jnp.bfloat16)
    partial_three, result_partial = lax.optimization_barrier(
        (after(partial_three, grad_mlp_w), result_partial)
    )
    grad_cross_stream, cross_branch, part_three = turn_back(
        4, partial_three, after_cross, local_grad, norm_three
    )
    result_kept = collect_half(after(result_partial, cross_branch))
    grad_mixed = project(cross_branch, cross_outw).astype(jnp.bfloat16)
    grad_mixed, result_kept = lax.optimization_barrier((grad_mixed, result_kept))
    result = collect_rest(result_kept)
    grad_cq, grad_ck, grad_cv = attend_back(
        cross_queries,
        cross_keys,
        cross_values,
        cross_mask,
        cross_total,
        split_heads(grad_mixed, head_count),
        score_scale,
    )
    grad_cq, result = lax.optimization_barrier(
        (grad_cq, (after_cross + result).astype(jnp.bfloat16))
    )
    output = swapped(result)
    partial_two = project_back(grad_cq, cross_q).astype(jnp.bfloat16)
    grad_ckv = jnp.concatenate([grad_ck, grad_cv], axis=2)
    cross_grads = jnp.concatenate(
        [
            weight_grad(patch_rows, grad_ckv).astype(jnp.bfloat16),
            weight_grad(normed_two, grad_cq).astype(jnp.bfloat16),
            weight_grad(cross_branch, cross_mixed).astype(jnp.bfloat16),
        ],
        axis=1,
    )
    cross_part = scatter_chips(cross_grads)
    partial_two, output = lax.optimization_barrier((after(partial_two, cross_grads), output))
    grad_self_stream, self_branch, part_two, down_terms, mlp_terms = turn_back(
        5, partial_two, after_self, grad_cross_stream, norm_two, down_part, mlp_part
    )
    down_sum = summed(down_terms).T
    mlp_sum = summed(mlp_terms)
    patch_kept = collect_half(project_back(after(grad_ckv, self_branch), cross_kv).astype(jnp.bfloat16))
    grad_attended = project(self_branch, self_outw).astype(jnp.bfloat16)
    grad_attended, patch_kept = lax.optimization_barrier((grad_attended, patch_kept))
    cross_sum = unpair(after(cross_part, self_branch))
    patch_part = collect_rest(patch_kept)
    grad_self_out = weight_grad(after(self_branch, grad_attended), self_attended).astype(
        jnp.bfloat16
    )
    grad_qkv = jnp.concatenate(
        attend_back(
            self_queries,
            self_keys,
            self_values,
            self_mask,
            self_total,
            split_heads(grad_attended, head_count),
            score_scale,
        ),
        axis=2,
    )
    grad_qkv, patch_part = lax.optimization_barrier(
        (after(grad_qkv, grad_self_out), patch_part.astype(jnp.bfloat16))
    )
    grad_patches = swapped(patch_part)
    self_out_part = scatter_chips(grad_self_out)
    grad_self_in = weight_grad(normed_one, grad_qkv).astype(jnp.bfloat16)
    self_part = scatter_chips(grad_self_in)
    partial_one = project_back(after(grad_qkv, grad_self_in), self_w[:, : 3 * wide]).astype(
        jnp.bfloat16
    )
    partial_one, grad_patches, cross_sum = lax.optimization_barrier(
        (partial_one, grad_patches, cross_sum)
    )
    grad_tokens, part_one, self_out_terms = leave(
        6, partial_one, local_tokens, grad_self_stream, norm_one, self_out_part
    )
    gain_sums, self_terms = return_weights(
        7, jnp.concatenate([part_one, part_two, part_three]), self_part
    )
    held = gain_self.shape[0]
    place = lax.axis_index(("chip", "core")) * held
    gain_sums = lax.dynamic_slice_in_dim(gain_sums, place, held, axis=1)
    self_sum = summed(self_terms)
    return (
        output,
        grad_tokens.astype(jnp.float32),
        grad_patches.astype(jnp.float32),
        gain_sums[0],
        self_sum[:, :wide],
        self_sum[:, wide : 2 * wide],
        self_sum[:, 2 * wide :],
        summed(self_out_terms).T,
        gain_sums[1],
        cross_sum[:, 2 * wide : 3 * wide],
        cross_sum[:, :wide],
        cross_sum[:, wide : 2 * wide],
        cross_sum[:, 3 * wide :].T,
        gain_sums[2],
        mlp_sum[:, :hidden_wide],
        mlp_sum[:, hidden_wide:],
        down_sum,
    )


def solution(mesh):
    devices = mesh.devices.reshape(mesh.shape["dp"] // 2, 2, 2, mesh.shape["seq"] // 2)
    fine = Mesh(devices, AXES)
    dp = ("chip", "core")
    seq = ("zh", "zp")
    stream = P(dp, seq, None)
    rows = P(dp, None)
    inward = P(dp, seq)
    outward = P(seq, dp)
    vector = P(dp)
    block = (vector, inward, inward, inward, outward)
    weights = block + block + (vector, inward, inward, outward)
    return jax.shard_map(
        shards,
        mesh=fine,
        in_specs=(stream, stream, rows, rows, rows) + weights + (stream,),
        out_specs=(stream, stream, stream) + weights,
        check_vma=False,
    )
```

```python
import itertools

import jax
import jax.numpy as jnp
from jax import lax
from jax.experimental import pallas as pl
from jax.experimental.pallas import tpu as pltpu
from jax.sharding import Mesh
from jax.sharding import PartitionSpec as P

HD = 128


epsilon = 1e-06
masked_value = -1e30

AXES = ("chip", "core", "zh", "zp")


def moves(chips, source_of):
    pairs = []
    for chip, core, zh, zp in itertools.product(range(chips), range(2), range(2), range(2)):
        a, b, c, d = source_of(chip, core, zh, zp)
        pairs.append((((a * 2 + b) * 2 + c) * 2 + d, ((chip * 2 + core) * 2 + zh) * 2 + zp))
    return pairs


def permute(values, source_of):
    return lax.ppermute(values, AXES, moves(lax.axis_size("chip"), source_of))


def swapped(values):
    return permute(values, lambda chip, core, zh, zp: (chip, zh, core, zp))


def swapped_other(values):
    return permute(values, lambda chip, core, zh, zp: (chip, 1 - zh, core, zp))


def other_core(values):
    return permute(values, lambda chip, core, zh, zp: (chip, 1 - core, zh, zp))


def other_zp(values):
    return permute(values, lambda chip, core, zh, zp: (chip, core, zh, 1 - zp))


def spread(block, *others):
    beside = other_zp(block)
    across = other_core(block)
    if others:
        beside, across = lax.optimization_barrier(((beside, across),) + others)[0]
    corner = other_core(beside)
    return jnp.concatenate([block, beside, across, corner], axis=1)


def relative(values):
    rows, length = values.shape
    cut = values.reshape(rows, 2, 2, length // 4)
    cut = jnp.where(lax.axis_index("core") == 1, cut[:, ::-1], cut)
    cut = jnp.where(lax.axis_index("zp") == 1, cut[:, :, ::-1], cut)
    return cut.reshape(rows, length)


def after(values, *others):
    return lax.optimization_barrier((values,) + others)[0]


def exchange(shards_of):
    return swapped(shards_of), swapped_other(shards_of)


def pair_up(exchanged):
    first, second = exchanged
    low = lax.axis_index("zh") == 0
    return jnp.concatenate([jnp.where(low, first, second), jnp.where(low, second, first)], axis=0)


def gather_chips(pair):
    return lax.all_gather(pair, "chip", axis=0, tiled=True)


def scatter_chips(grads):
    return lax.psum_scatter(
        grads.astype(jnp.bfloat16), "chip", scatter_dimension=0, tiled=True
    )


def normalize(values, gain_vec):
    factor = lax.rsqrt(jnp.mean(values * values, axis=-1, keepdims=True) + epsilon)
    return values * factor * gain_vec


def norm_back(values, gain_vec, gradient):
    normed_value, pullback = jax.vjp(lambda inputs: normalize(inputs, gain_vec), values)
    return pullback(gradient)[0]


def gain_part(values, gradient):
    factor = lax.rsqrt(jnp.mean(values * values, axis=-1, keepdims=True) + epsilon)
    return jnp.sum(gradient * values * factor, axis=(0, 1))


MESH = pl.DeviceIdType.MESH
ANY = pl.BlockSpec(memory_space=pl.ANY)
VMEM = pl.BlockSpec(memory_space=pltpu.VMEM)
PARTS = 4


def across_plane(axis):
    chip = lax.axis_index("chip")
    x, y = chip % 2, chip // 2
    return y * 2 + 1 - x if axis == 0 else (1 - y) * 2 + x


def greet(everyone, plane=False):
    core, zh, zp = lax.axis_index("core"), lax.axis_index("zh"), lax.axis_index("zp")
    barrier = pltpu.get_barrier_semaphore()
    count = 0
    for a, b, c in itertools.product(range(2), range(2), range(2)):
        if (a, b, c) == (0, 0, 0) or (b and not everyone):
            continue
        pl.semaphore_signal(
            barrier,
            inc=1,
            device_id={"core": (core + a) % 2, "zh": (zh + b) % 2, "zp": (zp + c) % 2},
            device_id_type=MESH,
        )
        count += 1
    if plane:
        chips = lax.axis_size("chip")
        for a, b in itertools.product(range(1, chips), range(2)):
            pl.semaphore_signal(
                barrier,
                inc=1,
                device_id={
                    "chip": (lax.axis_index("chip") + a) % chips,
                    "core": (core + b) % 2,
                },
                device_id_type=MESH,
            )
            count += 1
    pl.semaphore_wait(barrier, count)


def to_core(src, dst, send, recv):
    return pltpu.make_async_remote_copy(
        src, dst, send, recv, device_id={"core": 1 - lax.axis_index("core")}, device_id_type=MESH
    )


def to_zp(src, dst, send, recv):
    return pltpu.make_async_remote_copy(
        src, dst, send, recv, device_id={"zp": 1 - lax.axis_index("zp")}, device_id_type=MESH
    )


def to_swapped(src, dst, send, recv):
    core, zh = lax.axis_index("core"), lax.axis_index("zh")
    return pltpu.make_async_remote_copy(
        src, dst, send, recv, device_id={"core": zh, "zh": core}, device_id_type=MESH
    )


class Exchange:
    def __init__(self, src, pair, sems):
        self.src, self.pair, self.sems = src, pair, sems
        self.core, self.zh = lax.axis_index("core"), lax.axis_index("zh")
        rows = src.shape[0]
        self.mine = pair.at[pl.ds(pl.multiple_of(self.core * rows, rows), rows)]
        self.slots = [pair.at[pl.ds(a * rows, rows)] for a in range(2)]

    def far(self):
        return pltpu.make_async_remote_copy(
            self.src,
            self.mine,
            self.sems.at[0],
            self.sems.at[2 + self.core],
            device_id={"core": self.zh, "zh": 1 - self.zh},
            device_id_type=MESH,
        )

    def near(self):
        return pltpu.make_async_remote_copy(
            self.src,
            self.mine,
            self.sems.at[1],
            self.sems.at[2 + self.core],
            device_id={"core": 1 - self.core},
            device_id_type=MESH,
        )

    def own(self):
        return pltpu.make_async_copy(self.src, self.mine, self.sems.at[2 + self.core])

    def start(self):
        self.far().start()

        @pl.when(self.core == self.zh)
        def _():
            self.own().start()

        @pl.when(self.core != self.zh)
        def _():
            self.near().start()

    def finish(self):
        self.far().wait_send()

        @pl.when(self.core != self.zh)
        def _():
            self.near().wait_send()

        for a in range(2):
            pltpu.make_async_copy(self.src, self.slots[a], self.sems.at[2 + a]).wait()


class Spread:
    def __init__(self, block, gathered, sems):
        self.block, self.gathered, self.sems = block, gathered, sems
        self.length = block.shape[1]
        self.step = 2 * self.length // PARTS

    def src(self, k):
        return self.block.at[k // (PARTS // 2), pl.ds(pl.multiple_of(k % (PARTS // 2) * self.step, self.step), self.step)]

    def dst(self, k, slot):
        return self.gathered.at[
            k // (PARTS // 2),
            pl.ds(
                pl.multiple_of(slot * self.length + k % (PARTS // 2) * self.step, self.step),
                self.step,
            ),
        ]

    def beside(self, k):
        return to_zp(self.src(k), self.dst(k, 1), self.sems.at[0, k], self.sems.at[1, k])

    def across(self, k):
        return to_core(self.src(k), self.dst(k, 2), self.sems.at[2, k], self.sems.at[3, k])

    def corner(self, k):
        return to_core(self.dst(k, 1), self.dst(k, 3), self.sems.at[4, k], self.sems.at[5, k])

    def own(self, k):
        return pltpu.make_async_copy(self.src(k), self.dst(k, 0), self.sems.at[6, k])

    def start(self, k):
        self.beside(k).start()
        self.across(k).start()
        self.own(k).start()

    def relay(self, k):
        self.beside(k).wait_recv()
        self.corner(k).start()

    def finish(self, k):
        self.beside(k).wait_send()
        self.across(k).wait()
        self.corner(k).wait()
        self.own(k).wait()


class Collect:
    def __init__(self, partial, arrived, outgoing, landed, sems):
        self.partial, self.arrived = partial, arrived
        self.outgoing, self.landed, self.sems = outgoing, landed, sems
        self.length = outgoing.shape[1]
        self.step = 2 * self.length // PARTS

    def at(self, ref, k, block):
        return ref.at[
            k // (PARTS // 2),
            pl.ds(
                pl.multiple_of(block * self.length + k % (PARTS // 2) * self.step, self.step),
                self.step,
            ),
        ]

    def crossing(self, k, block):
        return to_core(
            self.at(self.partial, k, 2 + block),
            self.at(self.arrived, k, block),
            self.sems.at[2 * block, k],
            self.sems.at[2 * block + 1, k],
        )

    def landing(self, k):
        return to_zp(
            self.at(self.outgoing, k, 0),
            self.at(self.landed, k, 0),
            self.sems.at[4, k],
            self.sems.at[5, k],
        )

    def start(self):
        for block in (1, 0):
            for k in range(PARTS):
                self.crossing(k, block).start()

    def forward(self, k):
        self.crossing(k, 1).wait_recv()
        self.at(self.outgoing, k, 0)[...] = (
            self.at(self.partial, k, 1)[...].astype(jnp.float32)
            + self.at(self.arrived, k, 1)[...].astype(jnp.float32)
        ).astype(jnp.bfloat16)
        self.landing(k).start()

    def total(self, k):
        self.crossing(k, 0).wait_recv()
        self.landing(k).wait_recv()
        return (
            self.at(self.partial, k, 0)[...].astype(jnp.float32)
            + self.at(self.arrived, k, 0)[...].astype(jnp.float32)
        ) + self.at(self.landed, k, 0)[...].astype(jnp.float32)

    def finish(self, k):
        self.crossing(k, 0).wait_send()
        self.crossing(k, 1).wait_send()
        self.landing(k).wait_send()


class Unpair:
    def __init__(self, part, terms, sems):
        self.part, self.terms, self.sems = part, terms, sems
        self.core, self.zh = lax.axis_index("core"), lax.axis_index("zh")
        self.rows = part.shape[0] // 2

    def piece(self, p):
        return self.part.at[pl.ds(p * self.rows, self.rows)]

    def remote(self, p):
        return pltpu.make_async_remote_copy(
            self.piece(p),
            self.terms.at[self.zh],
            self.sems.at[p],
            self.sems.at[2 + self.zh],
            device_id={"core": p, "zh": self.core},
            device_id_type=MESH,
        )

    def own(self, p):
        return pltpu.make_async_copy(
            self.piece(p), self.terms.at[self.zh], self.sems.at[2 + self.zh]
        )

    def stays(self, p):
        return jnp.logical_and(self.core == p, self.zh == p)

    def start(self):
        for p in range(2):

            @pl.when(self.stays(p))
            def _(p=p):
                self.own(p).start()

            @pl.when(jnp.logical_not(self.stays(p)))
            def _(p=p):
                self.remote(p).start()

    def finish(self):
        for p in range(2):

            @pl.when(jnp.logical_not(self.stays(p)))
            def _(p=p):
                self.remote(p).wait_send()

            pltpu.make_async_copy(
                self.piece(p), self.terms.at[p], self.sems.at[2 + p]
            ).wait()


class Swap:
    def __init__(self, block, target, sems):
        self.block, self.target, self.sems = block, target, sems
        self.swaps = lax.axis_index("core") != lax.axis_index("zh")
        self.step = 2 * block.shape[1] // PARTS

    def at(self, ref, k):
        return ref.at[
            k // (PARTS // 2), pl.ds(pl.multiple_of(k % (PARTS // 2) * self.step, self.step), self.step)
        ]

    def remote(self, k):
        return to_swapped(
            self.at(self.block, k), self.at(self.target, k), self.sems.at[0, k], self.sems.at[1, k]
        )

    def own(self, k):
        return pltpu.make_async_copy(self.at(self.block, k), self.at(self.target, k), self.sems.at[1, k])

    def start(self, k):
        @pl.when(self.swaps)
        def _():
            self.remote(k).start()

        @pl.when(jnp.logical_not(self.swaps))
        def _():
            self.own(k).start()

    def arrive(self, k):
        self.own(k).wait()

    def finish(self, k):
        @pl.when(self.swaps)
        def _():
            self.remote(k).wait_send()


def each(body):
    lax.fori_loop(0, PARTS, lambda k, carry: (body(k), carry)[1], 0)


def kernel_call(number, name, inputs, outs, scratch, body):
    names = list(inputs) + list(outs) + list(scratch)

    def kernel(*refs):
        body(dict(zip(names, refs)))

    results = pl.pallas_call(
        kernel,
        out_shape=tuple(shape for shape, _ in outs.values()),
        in_specs=[VMEM] * len(inputs),
        out_specs=tuple(spec for _, spec in outs.values()),
        scratch_shapes=list(scratch.values()),
        compiler_params=pltpu.CompilerParams(
            collective_id=number, has_side_effects=True, vmem_limit_bytes=61 * 1024 * 1024
        ),
        name=name,
    )(*inputs.values())
    return dict(zip(outs, results))


def collect_scratch(tag, rows, length, width):
    return {
        tag + "arrived": pltpu.VMEM((rows, 2 * length, width), jnp.bfloat16),
        tag + "outgoing": pltpu.VMEM((rows, length, width), jnp.bfloat16),
        tag + "landed": pltpu.VMEM((rows, length, width), jnp.bfloat16),
        tag + "collect_sems": pltpu.SemaphoreType.DMA((6, PARTS)),
    }


def collect_of(refs, tag, partial):
    return Collect(
        refs[partial],
        refs[tag + "arrived"],
        refs[tag + "outgoing"],
        refs[tag + "landed"],
        refs[tag + "collect_sems"],
    )


def shape_of(shape, dtype):
    return jax.ShapeDtypeStruct(shape, dtype)


def gathered_out(rows, length, width):
    return (shape_of((rows, 4 * length, width), jnp.bfloat16), ANY)


def pair_out(shard):
    return (shape_of((2 * shard.shape[0], shard.shape[1]), shard.dtype), ANY)


def terms_out(part):
    return (shape_of((2, part.shape[0] // 2, part.shape[1]), part.dtype), ANY)


class PlaneGather:
    def __init__(self, whole, columns, sems):
        self.whole, self.columns, self.sems = whole, columns, sems
        self.rows = whole.shape[0] // 4

    def half(self, chip, which):
        start, size = self.columns
        return self.whole.at[
            pl.ds(pl.multiple_of(chip * self.rows, self.rows), self.rows),
            pl.ds(start + which * (size // 2), size // 2),
        ]

    def own(self, axis, which):
        ref = self.half(lax.axis_index("chip"), which)
        return self.copy(ref, axis, 2 * axis + which)

    def passed(self, which):
        ref = self.half(across_plane(which), which)
        return self.copy(ref, 1 - which, 4 + which)

    def copy(self, ref, axis, number):
        return pltpu.make_async_remote_copy(
            ref,
            ref,
            self.sems.at[0, number],
            self.sems.at[1, number],
            device_id={"chip": across_plane(axis)},
            device_id_type=MESH,
        )

    def start(self):
        for axis in range(2):
            self.own(axis, axis).start()
        for axis in range(2):
            self.own(axis, 1 - axis).start()

    def relay(self):
        for which in range(2):
            self.own(which, which).wait_recv()
            self.passed(which).start()

    def finish(self):
        for axis in range(2):
            self.own(axis, axis).wait_send()
            self.own(axis, 1 - axis).wait()
            self.passed(axis).wait()


class SwapWhole:
    def __init__(self, array, target, sems):
        self.array, self.target, self.sems = array, target, sems
        self.swaps = lax.axis_index("core") != lax.axis_index("zh")

    def remote(self):
        return to_swapped(self.array, self.target, self.sems.at[0], self.sems.at[1])

    def own(self):
        return pltpu.make_async_copy(self.array, self.target, self.sems.at[1])

    def start(self):
        @pl.when(self.swaps)
        def _():
            self.remote().start()

        @pl.when(jnp.logical_not(self.swaps))
        def _():
            self.own().start()

    def finish(self):
        self.own().wait()

        @pl.when(self.swaps)
        def _():
            self.remote().wait_send()


class GainGather:
    def __init__(self, own, slots, whole, sems):
        self.own, self.slots, self.whole, self.sems = own, slots, whole, sems
        self.chips = lax.axis_size("chip")
        self.chip, self.core = lax.axis_index("chip"), lax.axis_index("core")

    def others(self):
        for number in range(1, 2 * self.chips):
            yield number, (self.chip + number // 2) % self.chips, (self.core + number % 2) % 2

    def send(self, number, chip, core):
        return pltpu.make_async_remote_copy(
            self.own,
            self.slots.at[self.chip * 2 + self.core],
            self.sems.at[0, number],
            self.sems.at[1, self.chip * 2 + self.core],
            device_id={"chip": chip, "core": core},
            device_id_type=MESH,
        )

    def start(self):
        for other in self.others():
            self.send(*other).start()
        self.slots.at[self.chip * 2 + self.core][...] = self.own[...]

    def finish(self):
        for number, chip, core in self.others():
            self.send(number, chip, core).wait_send()
            place = chip * 2 + core
            pltpu.make_async_copy(self.own, self.slots.at[place], self.sems.at[1, place]).wait()
        held = self.own.shape[1]
        for place in range(2 * self.chips):
            self.whole[:, place * held : (place + 1) * held] = self.slots[place]


def head(number, block, beside, marks, gains, first, second):
    rows, length, width = block.shape
    depth, size = first[0].shape
    chips = lax.axis_size("chip")
    in_plane = chips == 4
    if not in_plane:
        gains = lax.all_gather(gains, ("chip", "core"), axis=1, tiled=True)

    def body(refs):
        swap = Swap(refs["block"], refs["here"], refs["swap_sems"])
        marks_swap = SwapWhole(refs["marks"], refs["marks_here"], refs["marks_sems"])
        spread_work = Spread(refs["normed"], refs["gathered"], refs["spread_sems"])
        if in_plane:
            chip = lax.axis_index("chip")
            place = refs["whole"].at[pl.ds(pl.multiple_of(chip * 2 * depth, 2 * depth), 2 * depth)]
            gain_work = GainGather(
                refs["gains"], refs["gain_slots"], refs["gains_whole"], refs["gain_sems"]
            )
        else:
            place = refs["whole"]
        works = [
            Exchange(
                refs["first%d" % i],
                place.at[:, pl.ds(i * size, size)],
                refs["exchange_sems"].at[i],
            )
            for i in range(len(first))
        ]
        beside_swap = Swap(refs["beside"], refs["beside_here"], refs["beside_swap_sems"])
        beside_work = Spread(refs["beside_here"], refs["beside_gathered"], refs["beside_sems"])
        later = [
            Exchange(
                refs["second%d" % i],
                refs["pair"].at[:, pl.ds(i * size, size)],
                refs["exchange_sems"].at[len(first) + i],
            )
            for i in range(len(second))
        ]
        greet(True, in_plane)
        marks_swap.start()

        def norm_and_send(k):
            swap.arrive(k)
            values = swap.at(refs["here"], k)[...].astype(jnp.float32)
            spread_work.src(k)[...] = normalize(values, refs["gains_whole"][0:1, :]).astype(
                jnp.bfloat16
            )
            spread_work.start(k)

        planes = [
            PlaneGather(refs["whole"], (i * size, size), refs["plane_sems"].at[i])
            for i in range(len(first))
        ]
        last = len(works) - 1
        works[0].start()
        if in_plane:
            gain_work.start()
            gain_work.finish()
        else:
            refs["gains_whole"][...] = refs["gains"][...]
        for i, work in enumerate(works):
            work.finish()
            if in_plane:
                planes[i].start()
            if i < last:
                works[i + 1].start()
            if i == 0:
                each(swap.start)
            if i == last - 1:
                each(beside_swap.start)
            if in_plane and i:
                planes[i - 1].relay()
            if i == 1:
                each(norm_and_send)
            if i == last:
                each(spread_work.relay)

        def pass_on(k):
            beside_swap.arrive(k)
            beside_work.start(k)

        later[0].start()
        pass_on(0)
        pass_on(1)
        if in_plane:
            planes[last].relay()
        for k in range(2, PARTS):
            pass_on(k)
        for i, work in enumerate(later):
            if i + 1 < len(later):
                later[i + 1].start()
            if i == 1:
                each(beside_work.relay)
            work.finish()
        each(beside_work.finish)
        each(beside_swap.finish)
        each(spread_work.finish)
        each(swap.finish)
        if in_plane:
            for plane in planes:
                plane.finish()
        marks_swap.finish()

    whole_rows = 8 * depth if in_plane else 2 * depth
    results = kernel_call(
        number,
        "head",
        {
            "block": block,
            "beside": beside,
            "marks": marks,
            "gains": gains,
            **{"first%d" % i: shard for i, shard in enumerate(first)},
            **{"second%d" % i: shard for i, shard in enumerate(second)},
        },
        {
            "here": (shape_of(block.shape, block.dtype), VMEM),
            "marks_here": (shape_of(marks.shape, marks.dtype), VMEM),
            "gains_whole": (shape_of((gains.shape[0], width), jnp.float32), VMEM),
            "gathered": gathered_out(rows, length, width),
            "whole": (shape_of((whole_rows, len(first) * size), jnp.bfloat16), ANY),
            "beside_gathered": gathered_out(rows, length, width),
            "pair": (shape_of((2 * depth, len(second) * size), jnp.bfloat16), ANY),
        },
        {
            "normed": pltpu.VMEM((rows, length, width), jnp.bfloat16),
            "spread_sems": pltpu.SemaphoreType.DMA((7, PARTS)),
            "swap_sems": pltpu.SemaphoreType.DMA((2, PARTS)),
            "beside_here": pltpu.VMEM((rows, length, width), jnp.bfloat16),
            "beside_sems": pltpu.SemaphoreType.DMA((7, PARTS)),
            "beside_swap_sems": pltpu.SemaphoreType.DMA((2, PARTS)),
            "marks_sems": pltpu.SemaphoreType.DMA((2,)),
            "exchange_sems": pltpu.SemaphoreType.DMA((len(first) + len(second), 4)),
            "plane_sems": pltpu.SemaphoreType.DMA((len(first), 2, 6)),
            "gain_slots": pltpu.VMEM((2 * chips,) + gains.shape, jnp.float32),
            "gain_sems": pltpu.SemaphoreType.DMA((2, 2 * chips)),
        },
        body,
    )
    whole = results["whole"] if in_plane else gather_chips(results["whole"])
    return (
        results["here"],
        results["marks_here"],
        results["gains_whole"],
        results["gathered"],
        results["beside_gathered"],
        whole,
        results["pair"],
    )


def turn_forward(number, partial, stream, gain):
    rows, length, width = stream.shape

    def body(refs):
        collect_work = collect_of(refs, "", "partial")
        spread_work = Spread(refs["normed"], refs["gathered"], refs["spread_sems"])
        greet(False)
        collect_work.start()
        each(collect_work.forward)

        def norm_and_send(k):
            values = collect_work.at(refs["stream"], k, 0)[...].astype(
                jnp.float32
            ) + collect_work.total(k)
            collect_work.at(refs["after"], k, 0)[...] = values
            spread_work.src(k)[...] = normalize(values, refs["gain"][...]).astype(jnp.bfloat16)
            spread_work.start(k)

        each(norm_and_send)
        each(spread_work.relay)
        each(spread_work.finish)
        each(collect_work.finish)

    results = kernel_call(
        number,
        "turn_forward",
        {"partial": partial, "stream": stream, "gain": gain[None]},
        {
            "after": (shape_of(stream.shape, jnp.float32), VMEM),
            "gathered": gathered_out(rows, length, width),
        },
        {
            **collect_scratch("", rows, length, width),
            "normed": pltpu.VMEM((rows, length, width), jnp.bfloat16),
            "spread_sems": pltpu.SemaphoreType.DMA((7, PARTS)),
        },
        body,
    )
    return results["after"], results["gathered"]


class WeightGradFill:
    def __init__(self, tag, left, right):
        self.tag = tag
        depth, columns = left.shape[1], right.shape[1]
        self.size = 256
        self.tiles = depth // self.size
        self.inputs = {tag + "left": left, tag + "right": right}
        self.outs = {tag + "out": (shape_of((depth, columns), jnp.bfloat16), ANY)}
        self.scratch = {
            tag + "stage": pltpu.VMEM((2, self.size, columns), jnp.bfloat16),
            tag + "sems": pltpu.SemaphoreType.DMA((2,)),
        }

    def at(self, i):
        return pl.ds(pl.multiple_of(i * self.size, self.size), self.size)

    def copy(self, refs, i):
        return pltpu.make_async_copy(
            refs[self.tag + "stage"].at[i % 2],
            refs[self.tag + "out"].at[self.at(i)],
            refs[self.tag + "sems"].at[i % 2],
        )

    def tile(self, refs, i):
        @pl.when(i >= 2)
        def _():
            self.copy(refs, i - 2).wait()

        refs[self.tag + "stage"].at[i % 2][...] = down(
            refs[self.tag + "left"].at[:, self.at(i)][...], refs[self.tag + "right"][...]
        ).astype(jnp.bfloat16)
        self.copy(refs, i).start()

    def end(self, refs):
        for i in (self.tiles - 2, self.tiles - 1):
            self.copy(refs, i).wait()


class ProductFill:
    def __init__(self, tag, left, right, columns):
        self.tag, self.columns = tag, columns
        rows = left.shape[0]
        self.size = 256
        self.tiles = rows // self.size
        self.inputs = {tag + "left": left, tag + "right": right}
        self.outs = {tag + "out": (shape_of((rows, right.shape[0]), jnp.bfloat16), VMEM)}
        self.scratch = {}

    def tile(self, refs, i):
        at = pl.ds(pl.multiple_of(i * self.size, self.size), self.size)
        start, width = self.columns
        refs[self.tag + "out"].at[at][...] = across(
            refs[self.tag + "left"].at[at][...],
            refs[self.tag + "right"].at[:, pl.ds(start, width)][...],
        ).astype(jnp.bfloat16)

    def end(self, refs):
        pass


def fill_in(refs, fill, part, parts):
    if fill is not None:
        first, last = fill.tiles * part // parts, fill.tiles * (part + 1) // parts
        lax.fori_loop(first, last, lambda i, carry: (fill.tile(refs, i), carry)[1], 0)


def norm_slope(values, gain, gradient):
    factor = lax.rsqrt(jnp.mean(values * values, axis=-1, keepdims=True) + epsilon)
    scaled = gain * gradient
    inner = jnp.mean(scaled * values, axis=-1, keepdims=True)
    return factor * scaled - values * (factor * factor * factor * inner), gradient * values * factor


def turn_back(number, partial, values, stream, gain, fills, *parts):
    rows, length, width = values.shape
    first, second = (tuple(fills) + (None, None))[:2]

    def body(refs):
        collect_work = collect_of(refs, "", "partial")
        spread_work = Spread(refs["branch"], refs["gathered"], refs["spread_sems"])
        works = [
            Unpair(refs["part%d" % i], refs["terms%d" % i], refs["unpair_sems"].at[i])
            for i in range(len(parts))
        ]
        greet(bool(parts))
        collect_work.start()
        each(collect_work.forward)
        refs["gain_sum"][...] = jnp.zeros_like(refs["gain_sum"])

        def slope_and_send(k):
            slope, terms = norm_slope(
                collect_work.at(refs["values"], k, 0)[...].astype(jnp.float32),
                refs["gain"][...],
                collect_work.total(k),
            )
            sums = collect_work.at(refs["stream"], k, 0)[...].astype(jnp.float32) + slope
            collect_work.at(refs["after"], k, 0)[...] = sums
            spread_work.src(k)[...] = sums.astype(jnp.bfloat16)
            spread_work.start(k)
            refs["gain_sum"][...] += jnp.sum(terms, axis=0, keepdims=True)

        for work in works:
            work.start()
        if first is None:
            each(slope_and_send)
        else:
            for k in range(PARTS):
                fill_in(refs, first, k, PARTS)
                slope_and_send(k)
        fill_in(refs, second, 0, 1)
        each(spread_work.relay)
        each(spread_work.finish)
        each(collect_work.finish)
        for work in works:
            work.finish()
        for fill in fills:
            fill.end(refs)

    extra = {"inputs": {}, "outs": {}, "scratch": {}}
    for fill in fills:
        for kind, found in extra.items():
            found.update(getattr(fill, kind))
    results = kernel_call(
        number,
        "turn_back",
        {
            "partial": partial,
            "values": values,
            "stream": stream,
            "gain": gain[None],
            **{"part%d" % i: part for i, part in enumerate(parts)},
            **extra["inputs"],
        },
        {
            "after": (shape_of(values.shape, jnp.float32), VMEM),
            "gathered": gathered_out(rows, length, width),
            "gain_sum": (shape_of((1, width), jnp.float32), VMEM),
            **{"terms%d" % i: terms_out(part) for i, part in enumerate(parts)},
            **extra["outs"],
        },
        {
            **collect_scratch("", rows, length, width),
            "branch": pltpu.VMEM((rows, length, width), jnp.bfloat16),
            "spread_sems": pltpu.SemaphoreType.DMA((7, PARTS)),
            "unpair_sems": pltpu.SemaphoreType.DMA((max(1, len(parts)), 4)),
            **extra["scratch"],
        },
        body,
    )
    return (
        (results["after"], results["gathered"], results["gain_sum"])
        + tuple(results["terms%d" % i] for i in range(len(parts)))
        + tuple(results[name] for fill in fills for name in fill.outs)
    )


class OutWork:
    def __init__(self, collect_work, swap, base):
        self.collect_work, self.swap, self.base = collect_work, swap, base

    def begin(self):
        self.collect_work.start()

    def forward(self):
        each(self.collect_work.forward)

    def leave_part(self, k):
        total = self.collect_work.total(k)
        if self.base is not None:
            total = total + self.swap.at(self.base, k)[...]
        self.swap.at(self.swap.block, k)[...] = total.astype(jnp.bfloat16)
        self.swap.start(k)

    def end(self):
        each(self.swap.arrive)
        each(self.swap.finish)
        each(self.collect_work.finish)


def head_at(ref, r, h, offset):
    return ref.at[r, :, pl.ds(pl.multiple_of(offset + h * HD, HD), HD)]


def across(left, right):
    return lax.dot_general(
        left, right, (((1,), (1,)), ((), ())), preferred_element_type=jnp.float32
    )


def down(left, right):
    return lax.dot_general(
        left, right, (((0,), (0,)), ((), ())), preferred_element_type=jnp.float32
    )


def masked_probability(refs, r, queries, key_rows):
    scores = across(queries, key_rows) * HD ** (-0.5)
    allowed = jnp.logical_and(
        refs["query_mark"][r] == refs["key_mark"][r],
        refs["query_place"][...] >= refs["key_place"][...],
    )
    scores = jnp.where(allowed, scores, masked_value)
    shifted = jnp.exp(scores - jnp.max(scores, axis=-1, keepdims=True))
    return shifted / jnp.sum(shifted, axis=-1, keepdims=True)


def rows_of(ref, t, size):
    per_row = ref.shape[1] // size
    return ref.at[t // per_row, pl.ds(pl.multiple_of(t % per_row * size, size), size)]


def attention_back(
    number, branch, weights, places, queries, pairs, marks, lefts, attended, out, part
):
    query_place, pair_place, out_place = places
    (query_array, query_at), (pair_array, pair_at) = queries, pairs
    same = query_array is pair_array
    rows, length, width = branch.shape
    wide = weights.shape[1] // 4
    heads = wide // HD
    block = (rows, length // 4, width)
    flat = (rows * length, width)
    inputs = {
        "branch": branch,
        "weights": weights,
        "queries": query_array,
        "query_mark": marks[0],
        "key_mark": marks[1],
        "query_place": marks[2],
        "key_place": marks[3],
        "left0": lefts[0].reshape(flat),
        "part": part,
    }
    if not same:
        inputs["pairs"] = pair_array
        inputs["left1"] = lefts[1].reshape(flat)
    if attended is not None:
        inputs["attended"] = attended.reshape(rows * length, wide)
    if out is not None:
        inputs["partial"] = out[0]
        if out[1] is not None:
            inputs["base"] = out[1]
    grad_columns = wide * (4 if attended is not None else 3)
    outs = {
        "input_partial": (shape_of((rows, length, width), jnp.bfloat16), VMEM),
        "weight_grads": (shape_of((width, grad_columns), jnp.bfloat16), ANY),
        "terms": terms_out(part),
    }
    scratch = {
        "grad_out": pltpu.VMEM((rows, length, wide), jnp.bfloat16),
        "stage": pltpu.VMEM((2, 256, grad_columns), jnp.bfloat16),
        "stage_sems": pltpu.SemaphoreType.DMA((2,)),
        "unpair_sems": pltpu.SemaphoreType.DMA((4,)),
    }
    if out is not None:
        outs["out"] = (shape_of(block, jnp.bfloat16), ANY)
        scratch.update(collect_scratch("", *block))
        scratch["leaving"] = pltpu.VMEM(block, jnp.bfloat16)
        scratch["swap_sems"] = pltpu.SemaphoreType.DMA((2, PARTS))
    if same:
        scratch["grad_all"] = pltpu.VMEM((rows, length, 3 * wide), jnp.bfloat16)
    else:
        scratch["grad_queries"] = pltpu.VMEM((rows, length, wide), jnp.bfloat16)
        outs["grad_pairs"] = (shape_of((rows, length, 2 * wide), jnp.bfloat16), VMEM)
    scale = HD ** (-0.5)
    total = rows * heads
    size = 256

    def body(refs):
        unpair = Unpair(refs["part"], refs["terms"], refs["unpair_sems"])
        out_work = None
        if out is not None:
            out_work = OutWork(
                collect_of(refs, "", "partial"),
                Swap(refs["leaving"], refs["out"], refs["swap_sems"]),
                refs.get("base"),
            )
        grad_queries = refs["grad_all"] if same else refs["grad_queries"]
        grad_pairs = refs["grad_all"] if same else refs["grad_pairs"]
        pair_refs = refs["queries"] if same else refs["pairs"]
        pair_out = wide if same else 0

        def form_grad_out(t):
            rows_of(refs["grad_out"], t, size)[...] = jnp.dot(
                rows_of(refs["branch"], t, size)[...],
                refs["weights"].at[:, pl.ds(out_place, wide)][...],
                preferred_element_type=jnp.float32,
            ).astype(jnp.bfloat16)

        def one(i):
            r, h = i // heads, i % heads
            queries_here = head_at(refs["queries"], r, h, query_at)[...]
            key_rows = head_at(pair_refs, r, h, pair_at)[...]
            value_rows = head_at(pair_refs, r, h, pair_at + wide)[...]
            grad_here = head_at(refs["grad_out"], r, h, 0)[...]
            probability = masked_probability(refs, r, queries_here, key_rows)
            grad_values = down(probability.astype(jnp.bfloat16), grad_here)
            grad_probs = across(grad_here, value_rows)
            inner = jnp.sum(probability * grad_probs, axis=-1, keepdims=True)
            grad_scores = (probability * (grad_probs - inner)).astype(jnp.bfloat16)
            query_terms = jnp.dot(grad_scores, key_rows, preferred_element_type=jnp.float32)
            key_terms = down(grad_scores, queries_here)
            head_at(grad_queries, r, h, 0)[...] = (query_terms * scale).astype(jnp.bfloat16)
            head_at(grad_pairs, r, h, pair_out)[...] = (key_terms * scale).astype(jnp.bfloat16)
            head_at(grad_pairs, r, h, pair_out + wide)[...] = grad_values.astype(jnp.bfloat16)

        def form_partial(t):
            columns = (query_place, 3 * wide if same else wide)
            rows_of(refs["input_partial"], t, size)[...] = across(
                rows_of(grad_queries, t, size)[...],
                refs["weights"].at[:, pl.ds(*columns)][...],
            ).astype(jnp.bfloat16)

        def written(i):
            return pltpu.make_async_copy(
                refs["stage"].at[i % 2],
                refs["weight_grads"].at[pl.ds(pl.multiple_of(i * size, size), size)],
                refs["stage_sems"].at[i % 2],
            )

        def form_grads(i):
            @pl.when(i >= 2)
            def _():
                written(i - 2).wait()

            at = pl.ds(pl.multiple_of(i * size, size), size)
            stage = refs["stage"].at[i % 2]

            def put(place, left, right):
                terms = right[...].reshape(rows * length, right.shape[-1])
                stage[:, place : place + right.shape[-1]] = down(left, terms).astype(jnp.bfloat16)

            put(query_place, refs["left0"].at[:, at][...], grad_queries)
            if not same:
                put(pair_place, refs["left1"].at[:, at][...], grad_pairs)
            if attended is not None:
                here = refs["branch"].at[:, :, at][...].reshape(rows * length, size)
                stage[:, out_place : out_place + wide] = down(here, refs["attended"][...]).astype(
                    jnp.bfloat16
                )
            written(i).start()

        def loop(count, work, stops=()):
            def step(i, carry):
                work(i)
                if out_work is not None:
                    for stop, k in stops:

                        @pl.when(i == stop)
                        def _(k=k):
                            out_work.leave_part(k)

                return carry

            lax.fori_loop(0, count, step, 0)

        greet(True)
        if out_work is not None:
            out_work.begin()
        loop(rows * length // size, form_grad_out)
        if out_work is not None:
            out_work.forward()
        unpair.start()
        loop(total, one, ((total // 2, 0), (total - 2, 1), (total - 1, 2)))
        loop(width // size, form_grads, ((2, 3),))
        loop(rows * length // size, form_partial)
        if out_work is not None:
            out_work.end()
        unpair.finish()
        for i in (width // size - 2, width // size - 1):
            written(i).wait()

    results = kernel_call(number, "attention_back", inputs, outs, scratch, body)
    return (
        results["input_partial"],
        results["weight_grads"],
        results["terms"],
        results.get("grad_pairs"),
        results.get("out"),
    )


class PlaneScatter:
    def __init__(self, grads, columns, taken, passing, crossed, part, sems):
        self.grads, self.columns, self.taken, self.passing = grads, columns, taken, passing
        self.crossed, self.part, self.sems = crossed, part, sems
        self.rows = grads.shape[0] // 4
        self.me = lax.axis_index("chip")

    def terms(self, chip, which):
        start, size = self.columns
        return self.grads.at[
            pl.ds(pl.multiple_of(chip * self.rows, self.rows), self.rows),
            pl.ds(start + which * (size // 2), size // 2),
        ]

    def copy(self, src, dst, axis, number):
        return pltpu.make_async_remote_copy(
            src,
            dst,
            self.sems.at[0, number],
            self.sems.at[1, number],
            device_id={"chip": across_plane(axis)},
            device_id_type=MESH,
        )

    def first(self, which, block):
        chip = 3 - self.me if block else across_plane(which)
        return self.copy(
            self.terms(chip, which), self.taken.at[which, block], which, 2 * which + block
        )

    def second(self, which):
        return self.copy(
            self.passing.at[which], self.crossed.at[which], 1 - which, 4 + which
        )

    def start(self):
        for block in (1, 0):
            for which in range(2):
                self.first(which, block).start()

    def pass_on(self):
        for which in range(2):
            self.first(which, 1).wait_recv()
            self.passing.at[which][...] = (
                self.terms(across_plane(1 - which), which)[...].astype(jnp.float32)
                + self.taken.at[which, 1][...].astype(jnp.float32)
            ).astype(jnp.bfloat16)
            self.second(which).start()

    def total(self):
        half = self.columns[1] // 2
        for which in range(2):
            self.first(which, 0).wait_recv()
            self.second(which).wait_recv()
            self.part.at[:, pl.ds(which * half, half)][...] = (
                self.terms(self.me, which)[...].astype(jnp.float32)
                + self.taken.at[which, 0][...].astype(jnp.float32)
                + self.crossed.at[which][...].astype(jnp.float32)
            ).astype(jnp.bfloat16)

    def finish(self):
        for which in range(2):
            for block in range(2):
                self.first(which, block).wait_send()
            self.second(which).wait_send()


def sum_everywhere(given, taken, sems, totals):
    chips = lax.axis_size("chip")
    core, zh, zp, chip = (lax.axis_index(axis) for axis in ("core", "zh", "zp", "chip"))
    partners = [{"core": 1 - core}, {"zp": 1 - zp}, {"zh": 1 - zh}]
    for bit in range(chips.bit_length() - 1):
        size = 2**bit
        partners.append({"chip": chip + size - 2 * size * (chip // size % 2)})
    sums = given[0]
    for step, partner in enumerate(partners):
        if step:
            given[step] = sums
        copy = pltpu.make_async_remote_copy(
            given.at[step],
            taken.at[step],
            sems.at[0, step],
            sems.at[1, step],
            device_id=partner,
            device_id_type=MESH,
        )
        copy.start()
        copy.wait()
        sums = sums + taken[step]
    totals[...] = sums


def leave(number, partial, values, stream, gain, gain_sums, grads, part):
    rows, length, width = values.shape
    chips = lax.axis_size("chip")
    in_plane = chips == 4
    steps = 3 + chips.bit_length() - 1
    if not in_plane:
        grads = scatter_chips(grads)
    owned = grads.shape[0] // (4 if in_plane else 1)
    columns = grads.shape[1]
    size = 512
    pieces = columns // size if in_plane else 0

    def body(refs):
        collect_work = collect_of(refs, "", "partial")
        swap = Swap(refs["leaving"], refs["out"], refs["swap_sems"])
        unpair = Unpair(refs["part"], refs["terms"], refs["unpair_sems"])
        if in_plane:
            scatters = [
                PlaneScatter(
                    refs["grads"],
                    (p * size, size),
                    refs["taken"].at[p],
                    refs["passing"].at[p],
                    refs["crossed"].at[p],
                    refs["summed"].at[p],
                    refs["plane_sems"].at[p],
                )
                for p in range(pieces)
            ]
            returns = [
                Unpair(
                    refs["summed"].at[p],
                    refs["grad_terms"].at[:, :, pl.ds(p * size, size)],
                    refs["return_sems"].at[p],
                )
                for p in range(pieces)
            ]
        else:
            scatters = []
            returns = [Unpair(refs["grads"], refs["grad_terms"], refs["return_sems"].at[0])]
        greet(True, True)
        for scatter in scatters:
            scatter.start()
        collect_work.start()
        each(collect_work.forward)
        unpair.start()
        if not in_plane:
            returns[0].start()
        refs["given"].at[0][1:3] = refs["gain_sums"][...]
        refs["gain_sum"][...] = jnp.zeros_like(refs["gain_sum"])

        def slope_and_send(k):
            slope, terms = norm_slope(
                collect_work.at(refs["values"], k, 0)[...].astype(jnp.float32),
                refs["gain"][...],
                collect_work.total(k),
            )
            sums = collect_work.at(refs["stream"], k, 0)[...] + slope
            swap.at(refs["leaving"], k)[...] = sums.astype(jnp.bfloat16)
            swap.start(k)
            refs["gain_sum"][...] += jnp.sum(terms, axis=0, keepdims=True)

        for k in range(PARTS):
            slope_and_send(k)
            if k < len(scatters):
                scatters[k].pass_on()
        for scatter in scatters[PARTS:]:
            scatter.pass_on()
        for scatter, back in zip(scatters, returns):
            scatter.total()
            back.start()
        refs["given"].at[0][0:1] = refs["gain_sum"][...]
        sum_everywhere(refs["given"], refs["got"], refs["gain_sems"], refs["totals"])
        each(swap.arrive)
        each(swap.finish)
        each(collect_work.finish)
        unpair.finish()
        for scatter in scatters:
            scatter.finish()
        for back in returns:
            back.finish()

    scratch = {
        **collect_scratch("", rows, length, width),
        "leaving": pltpu.VMEM((rows, length, width), jnp.bfloat16),
        "swap_sems": pltpu.SemaphoreType.DMA((2, PARTS)),
        "unpair_sems": pltpu.SemaphoreType.DMA((4,)),
        "return_sems": pltpu.SemaphoreType.DMA((max(1, pieces), 4)),
        "gain_sum": pltpu.VMEM((1, width), jnp.float32),
        "given": pltpu.VMEM((steps, 3, width), jnp.float32),
        "got": pltpu.VMEM((steps, 3, width), jnp.float32),
        "gain_sems": pltpu.SemaphoreType.DMA((2, steps)),
    }
    if in_plane:
        scratch["taken"] = pltpu.VMEM((pieces, 2, 2, owned, size // 2), jnp.bfloat16)
        scratch["passing"] = pltpu.VMEM((pieces, 2, owned, size // 2), jnp.bfloat16)
        scratch["crossed"] = pltpu.VMEM((pieces, 2, owned, size // 2), jnp.bfloat16)
        scratch["summed"] = pltpu.VMEM((pieces, owned, size), jnp.bfloat16)
        scratch["plane_sems"] = pltpu.SemaphoreType.DMA((pieces, 2, 6))
    results = kernel_call(
        number,
        "leave",
        {
            "partial": partial,
            "values": values,
            "stream": stream,
            "gain": gain[None],
            "gain_sums": gain_sums,
            "grads": grads,
            "part": part,
        },
        {
            "out": (shape_of(values.shape, jnp.bfloat16), ANY),
            "totals": (shape_of((3, width), jnp.float32), VMEM),
            "terms": terms_out(part),
            "grad_terms": (shape_of((2, owned // 2, columns), jnp.bfloat16), ANY),
        },
        scratch,
        body,
    )
    return results["out"], results["totals"], results["terms"], results["grad_terms"]


def summed(terms):
    return terms[0].astype(jnp.float32) + terms[1].astype(jnp.float32)


def project(left_side, right_side):
    return jnp.einsum("rtd,de->rte", left_side, right_side, preferred_element_type=jnp.float32)


def project_back(gradient, right_side):
    return jnp.einsum("rte,de->rtd", gradient, right_side, preferred_element_type=jnp.float32)


def weight_grad(left_side, gradient):
    return jnp.einsum("rtd,rte->de", left_side, gradient, preferred_element_type=jnp.float32)


def split_heads(values, head_count):
    return values.reshape(
        values.shape[0], values.shape[1], head_count, values.shape[2] // head_count
    )


def merge_heads(values):
    return values.reshape(values.shape[0], values.shape[1], values.shape[2] * values.shape[3])


def scores_of(queries, key_rows, allowed, score_scale):
    scores = (
        jnp.einsum("rqhd,rkhd->rhqk", queries, key_rows, preferred_element_type=jnp.float32)
        * score_scale
    )
    return jnp.where(allowed[:, None] > 0, scores, masked_value)


def attend(queries, key_rows, value_rows, allowed, score_scale):
    scores = scores_of(queries, key_rows, allowed, score_scale)
    peak_score = jnp.max(scores, axis=-1, keepdims=True)
    shifted = jnp.exp(scores - peak_score)
    denominator = jnp.sum(shifted, axis=-1, keepdims=True)
    weights = (shifted / denominator).astype(jnp.bfloat16)
    output = jnp.einsum("rhqk,rkhd->rqhd", weights, value_rows, preferred_element_type=jnp.float32)
    return merge_heads(output).astype(jnp.bfloat16)


def gelu_tanh(values):
    return jax.nn.gelu(values, approximate=True)


def shards(
    tokens,
    patches,
    seg_ids,
    seg_example,
    patch_owner,
    gain_self,
    self_query,
    self_key,
    self_value,
    self_out,
    gain_cross,
    cross_query,
    cross_key,
    cross_value,
    cross_out,
    gain_mlp,
    mlp_gate,
    mlp_up,
    mlp_down,
    cotangent,
):
    head_count = self_query.shape[1] // HD
    score_scale = HD ** (-0.5)
    gains = jnp.stack([gain_self, gain_cross, gain_mlp]).astype(jnp.float32)
    onehot = (
        seg_ids[:, :, None] == lax.iota(jnp.int32, seg_example.shape[1])[None, None, :]
    ).astype(jnp.int32)
    example_of = jnp.sum(onehot * seg_example[:, None, :], axis=2)
    marks = jnp.concatenate([seg_ids, example_of, patch_owner], axis=0)
    rows = seg_ids.shape[0]
    length = seg_ids.shape[1]
    wide = self_query.shape[1]
    hidden_wide = mlp_gate.shape[1]
    local_tokens, marks, gains, normed_one, patch_rows, self_w, cross_pair = head(
        0,
        tokens,
        patches,
        marks,
        gains,
        (self_query, self_key, self_value, self_out.T),
        (cross_key, cross_value, cross_query, cross_out.T),
    )
    norm_one, norm_two, norm_three = gains[0], gains[1], gains[2]
    cross_w = gather_chips(cross_pair)
    cross_kv = cross_w[:, : 2 * wide]
    cross_q = cross_w[:, 2 * wide : 3 * wide]
    cross_outw = cross_w[:, 3 * wide :]
    mlp_moved = exchange(after(jnp.concatenate([mlp_gate, mlp_up], axis=1), normed_one))
    seg_here = relative(marks[:rows])
    example_here = relative(marks[rows : 2 * rows])
    owner_here = relative(marks[2 * rows :])
    positions = relative(lax.broadcasted_iota(jnp.int32, (1, length), 1))
    causal = positions[:, :, None] >= positions[:, None, :]
    self_mask = ((seg_here[:, :, None] == seg_here[:, None, :]) & causal).astype(jnp.int32)
    cross_mask = (example_here[:, :, None] == owner_here[:, None, :]).astype(jnp.int32)
    self_marks = (
        seg_here[:, :, None],
        seg_here[:, None, :],
        positions.reshape(length, 1),
        positions.reshape(1, length),
    )
    cross_marks = (
        example_here[:, :, None],
        owner_here[:, None, :],
        jnp.zeros((length, 1), jnp.int32),
        jnp.zeros((1, length), jnp.int32),
    )
    self_qkv = project(normed_one, self_w[:, : 3 * wide]).astype(jnp.bfloat16)
    self_outw = self_w[:, 3 * wide :]
    self_queries = split_heads(self_qkv[..., :wide], head_count)
    self_keys = split_heads(self_qkv[..., wide : 2 * wide], head_count)
    self_values = split_heads(self_qkv[..., 2 * wide :], head_count)
    self_attended = attend(self_queries, self_keys, self_values, self_mask, score_scale)
    self_partial = project_back(self_attended, self_outw).astype(jnp.bfloat16)
    after_self, normed_two = turn_forward(1, self_partial, local_tokens, norm_two)
    mlp_pair = pair_up(after(mlp_moved, after_self))
    mlp_in = gather_chips(mlp_pair)
    normed_two = after(normed_two, mlp_pair)
    down_moved = exchange(after(mlp_down.T, mlp_pair))
    local_grad = swapped(after(cotangent, mlp_pair))
    cross_kv_rows = project(patch_rows, cross_kv).astype(jnp.bfloat16)
    cross_query_rows = project(normed_two, cross_q).astype(jnp.bfloat16)
    cross_queries = split_heads(cross_query_rows, head_count)
    cross_keys = split_heads(cross_kv_rows[..., :wide], head_count)
    cross_values = split_heads(cross_kv_rows[..., wide:], head_count)
    cross_mixed = attend(cross_queries, cross_keys, cross_values, cross_mask, score_scale)
    cross_partial = project_back(cross_mixed, cross_outw).astype(jnp.bfloat16)
    down_pair = pair_up(after(down_moved, cross_partial))
    mlp_downw = gather_chips(down_pair)
    after_cross, normed_three = turn_forward(
        2, after(cross_partial, down_pair), after_self, norm_three
    )
    both = project(normed_three, mlp_in)
    grad_rows = spread(after(local_grad, normed_three), both)
    gate_pre = both[..., :hidden_wide]
    upward = both[..., hidden_wide:]
    activated, gelu_pull = jax.vjp(gelu_tanh, gate_pre)
    hidden = (activated * upward).astype(jnp.bfloat16)

    grad_down_w = weight_grad(grad_rows, hidden).astype(jnp.bfloat16)
    down_part = scatter_chips(grad_down_w)
    grad_hidden = project(after(grad_rows, grad_down_w), mlp_downw)
    grad_upward = (grad_hidden * activated).astype(jnp.bfloat16)
    grad_gate = gelu_pull(grad_hidden * upward)[0].astype(jnp.bfloat16)
    grad_both = jnp.concatenate([grad_gate, grad_upward], axis=2)
    partial_three = project_back(grad_both, mlp_in).astype(jnp.bfloat16)
    tokens_here = rows * length
    grad_mlp_w = weight_grad(normed_three, grad_both).astype(jnp.bfloat16)
    mlp_part = scatter_chips(grad_mlp_w)
    grad_cross_stream, cross_branch, part_three, result_partial = turn_back(
        3,
        after(partial_three, grad_mlp_w),
        after_cross,
        local_grad,
        norm_three,
        (ProductFill("result_", hidden.reshape(tokens_here, -1), mlp_downw, (0, hidden_wide)),),
    )
    partial_two, cross_grads, down_terms, grad_ckv, output = attention_back(
        4,
        cross_branch,
        cross_w,
        (2 * wide, 0, 3 * wide),
        (cross_query_rows, 0),
        (cross_kv_rows, 0),
        cross_marks,
        (normed_two, patch_rows),
        cross_mixed,
        (result_partial.reshape(rows, length, -1), after_cross),
        down_part,
    )
    down_sum = summed(down_terms).T
    cross_part = scatter_chips(cross_grads)
    grad_self_stream, self_branch, part_two, mlp_terms, patch_partial = turn_back(
        5,
        partial_two,
        after_self,
        grad_cross_stream,
        norm_two,
        (ProductFill("patch_", grad_ckv.reshape(tokens_here, -1), cross_w, (0, 2 * wide)),),
        mlp_part,
    )
    mlp_sum = summed(mlp_terms)
    grad_self_out = weight_grad(self_branch, self_attended).astype(jnp.bfloat16)
    self_out_part = scatter_chips(grad_self_out)
    partial_one, grad_self_in, cross_terms, _, grad_patches = attention_back(
        6,
        after(self_branch, grad_self_out),
        self_w,
        (0, wide, 3 * wide),
        (self_qkv, 0),
        (self_qkv, wide),
        self_marks,
        (normed_one, normed_one),
        None,
        (patch_partial.reshape(rows, length, -1), None),
        cross_part,
    )
    cross_sum = summed(cross_terms)
    grad_tokens, gain_sums, self_out_terms, self_terms = leave(
        7,
        partial_one,
        local_tokens,
        grad_self_stream,
        norm_one,
        jnp.concatenate([part_two, part_three]),
        grad_self_in,
        self_out_part,
    )
    held = gain_self.shape[0]
    place = lax.axis_index(("chip", "core")) * held
    gain_sums = lax.dynamic_slice_in_dim(gain_sums, place, held, axis=1)
    self_sum = summed(self_terms)
    return (
        output,
        grad_tokens.astype(jnp.float32),
        grad_patches.astype(jnp.float32),
        gain_sums[0],
        self_sum[:, :wide],
        self_sum[:, wide : 2 * wide],
        self_sum[:, 2 * wide :],
        summed(self_out_terms).T,
        gain_sums[1],
        cross_sum[:, 2 * wide : 3 * wide],
        cross_sum[:, :wide],
        cross_sum[:, wide : 2 * wide],
        cross_sum[:, 3 * wide :].T,
        gain_sums[2],
        mlp_sum[:, :hidden_wide],
        mlp_sum[:, hidden_wide:],
        down_sum,
    )


def solution(mesh):
    devices = mesh.devices.reshape(mesh.shape["dp"] // 2, 2, 2, mesh.shape["seq"] // 2)
    fine = Mesh(devices, AXES)
    dp = ("chip", "core")
    seq = ("zh", "zp")
    stream = P(dp, seq, None)
    rows = P(dp, None)
    inward = P(dp, seq)
    outward = P(seq, dp)
    vector = P(dp)
    block = (vector, inward, inward, inward, outward)
    weights = block + block + (vector, inward, inward, outward)
    return jax.shard_map(
        shards,
        mesh=fine,
        in_specs=(stream, stream, rows, rows, rows) + weights + (stream,),
        out_specs=(stream, stream, stream) + weights,
        check_vma=False,
    )
```

```python
import itertools

import jax
import jax.numpy as jnp
from jax import lax
from jax.experimental import pallas as pl
from jax.experimental.pallas import tpu as pltpu
from jax.sharding import Mesh
from jax.sharding import PartitionSpec as P

HD = 128


epsilon = 1e-06
masked_value = -1e30

AXES = ("chip", "core", "zh", "zp")


def moves(chips, source_of):
    pairs = []
    for chip, core, zh, zp in itertools.product(range(chips), range(2), range(2), range(2)):
        a, b, c, d = source_of(chip, core, zh, zp)
        pairs.append((((a * 2 + b) * 2 + c) * 2 + d, ((chip * 2 + core) * 2 + zh) * 2 + zp))
    return pairs


def permute(values, source_of):
    return lax.ppermute(values, AXES, moves(lax.axis_size("chip"), source_of))


def swapped(values):
    return permute(values, lambda chip, core, zh, zp: (chip, zh, core, zp))


def swapped_other(values):
    return permute(values, lambda chip, core, zh, zp: (chip, 1 - zh, core, zp))


def relative(values):
    rows, length = values.shape
    cut = values.reshape(rows, 2, 2, length // 4)
    cut = jnp.where(lax.axis_index("core") == 1, cut[:, ::-1], cut)
    cut = jnp.where(lax.axis_index("zp") == 1, cut[:, :, ::-1], cut)
    return cut.reshape(rows, length)


def after(values, *others):
    return lax.optimization_barrier((values,) + others)[0]


def exchange(shards_of):
    return swapped(shards_of), swapped_other(shards_of)


def pair_up(exchanged):
    first, second = exchanged
    low = lax.axis_index("zh") == 0
    return jnp.concatenate([jnp.where(low, first, second), jnp.where(low, second, first)], axis=0)


def gather_chips(pair):
    return lax.all_gather(pair, "chip", axis=0, tiled=True)


def scatter_chips(grads):
    return lax.psum_scatter(
        grads.astype(jnp.bfloat16), "chip", scatter_dimension=0, tiled=True
    )


def normalize(values, gain_vec):
    factor = lax.rsqrt(jnp.mean(values * values, axis=-1, keepdims=True) + epsilon)
    return values * factor * gain_vec


def norm_back(values, gain_vec, gradient):
    normed_value, pullback = jax.vjp(lambda inputs: normalize(inputs, gain_vec), values)
    return pullback(gradient)[0]


def gain_part(values, gradient):
    factor = lax.rsqrt(jnp.mean(values * values, axis=-1, keepdims=True) + epsilon)
    return jnp.sum(gradient * values * factor, axis=(0, 1))


MESH = pl.DeviceIdType.MESH
ANY = pl.BlockSpec(memory_space=pl.ANY)
VMEM = pl.BlockSpec(memory_space=pltpu.VMEM)
PARTS = 4


def across_plane(axis):
    chip = lax.axis_index("chip")
    x, y = chip % 2, chip // 2
    return y * 2 + 1 - x if axis == 0 else (1 - y) * 2 + x


def greet(everyone, plane=False):
    core, zh, zp = lax.axis_index("core"), lax.axis_index("zh"), lax.axis_index("zp")
    barrier = pltpu.get_barrier_semaphore()
    count = 0
    for a, b, c in itertools.product(range(2), range(2), range(2)):
        if (a, b, c) == (0, 0, 0) or (b and not everyone):
            continue
        pl.semaphore_signal(
            barrier,
            inc=1,
            device_id={"core": (core + a) % 2, "zh": (zh + b) % 2, "zp": (zp + c) % 2},
            device_id_type=MESH,
        )
        count += 1
    if plane:
        chips = lax.axis_size("chip")
        for a, b in itertools.product(range(1, chips), range(2)):
            pl.semaphore_signal(
                barrier,
                inc=1,
                device_id={
                    "chip": (lax.axis_index("chip") + a) % chips,
                    "core": (core + b) % 2,
                },
                device_id_type=MESH,
            )
            count += 1
    pl.semaphore_wait(barrier, count)


def to_core(src, dst, send, recv):
    return pltpu.make_async_remote_copy(
        src, dst, send, recv, device_id={"core": 1 - lax.axis_index("core")}, device_id_type=MESH
    )


def to_zp(src, dst, send, recv):
    return pltpu.make_async_remote_copy(
        src, dst, send, recv, device_id={"zp": 1 - lax.axis_index("zp")}, device_id_type=MESH
    )


def to_swapped(src, dst, send, recv):
    core, zh = lax.axis_index("core"), lax.axis_index("zh")
    return pltpu.make_async_remote_copy(
        src, dst, send, recv, device_id={"core": zh, "zh": core}, device_id_type=MESH
    )


class Exchange:
    def __init__(self, src, pair, sems):
        self.src, self.pair, self.sems = src, pair, sems
        self.core, self.zh = lax.axis_index("core"), lax.axis_index("zh")
        rows = src.shape[0]
        self.mine = pair.at[pl.ds(pl.multiple_of(self.core * rows, rows), rows)]
        self.slots = [pair.at[pl.ds(a * rows, rows)] for a in range(2)]

    def far(self):
        return pltpu.make_async_remote_copy(
            self.src,
            self.mine,
            self.sems.at[0],
            self.sems.at[2 + self.core],
            device_id={"core": self.zh, "zh": 1 - self.zh},
            device_id_type=MESH,
        )

    def near(self):
        return pltpu.make_async_remote_copy(
            self.src,
            self.mine,
            self.sems.at[1],
            self.sems.at[2 + self.core],
            device_id={"core": 1 - self.core},
            device_id_type=MESH,
        )

    def own(self):
        return pltpu.make_async_copy(self.src, self.mine, self.sems.at[2 + self.core])

    def start(self):
        self.far().start()

        @pl.when(self.core == self.zh)
        def _():
            self.own().start()

        @pl.when(self.core != self.zh)
        def _():
            self.near().start()

    def finish(self):
        self.far().wait_send()

        @pl.when(self.core != self.zh)
        def _():
            self.near().wait_send()

        for a in range(2):
            pltpu.make_async_copy(self.src, self.slots[a], self.sems.at[2 + a]).wait()


class Spread:
    def __init__(self, block, gathered, sems):
        self.block, self.gathered, self.sems = block, gathered, sems
        self.length = block.shape[1]
        self.step = 2 * self.length // PARTS

    def src(self, k):
        return self.block.at[k // (PARTS // 2), pl.ds(pl.multiple_of(k % (PARTS // 2) * self.step, self.step), self.step)]

    def dst(self, k, slot):
        return self.gathered.at[
            k // (PARTS // 2),
            pl.ds(
                pl.multiple_of(slot * self.length + k % (PARTS // 2) * self.step, self.step),
                self.step,
            ),
        ]

    def beside(self, k):
        return to_zp(self.src(k), self.dst(k, 1), self.sems.at[0, k], self.sems.at[1, k])

    def across(self, k):
        return to_core(self.src(k), self.dst(k, 2), self.sems.at[2, k], self.sems.at[3, k])

    def corner(self, k):
        return to_core(self.dst(k, 1), self.dst(k, 3), self.sems.at[4, k], self.sems.at[5, k])

    def own(self, k):
        return pltpu.make_async_copy(self.src(k), self.dst(k, 0), self.sems.at[6, k])

    def start(self, k):
        self.beside(k).start()
        self.across(k).start()
        self.own(k).start()

    def relay(self, k):
        self.beside(k).wait_recv()
        self.corner(k).start()

    def finish(self, k):
        self.beside(k).wait_send()
        self.across(k).wait()
        self.corner(k).wait()
        self.own(k).wait()


class Collect:
    def __init__(self, partial, arrived, outgoing, landed, sems):
        self.partial, self.arrived = partial, arrived
        self.outgoing, self.landed, self.sems = outgoing, landed, sems
        self.length = outgoing.shape[1]
        self.step = 2 * self.length // PARTS

    def at(self, ref, k, block):
        return ref.at[
            k // (PARTS // 2),
            pl.ds(
                pl.multiple_of(block * self.length + k % (PARTS // 2) * self.step, self.step),
                self.step,
            ),
        ]

    def crossing(self, k, block):
        return to_core(
            self.at(self.partial, k, 2 + block),
            self.at(self.arrived, k, block),
            self.sems.at[2 * block, k],
            self.sems.at[2 * block + 1, k],
        )

    def landing(self, k):
        return to_zp(
            self.at(self.outgoing, k, 0),
            self.at(self.landed, k, 0),
            self.sems.at[4, k],
            self.sems.at[5, k],
        )

    def start(self):
        for block in (1, 0):
            self.start_block(block)

    def start_block(self, block):
        for k in range(PARTS):
            self.crossing(k, block).start()

    def forward(self, k):
        self.crossing(k, 1).wait_recv()
        self.at(self.outgoing, k, 0)[...] = (
            self.at(self.partial, k, 1)[...].astype(jnp.float32)
            + self.at(self.arrived, k, 1)[...].astype(jnp.float32)
        ).astype(jnp.bfloat16)
        self.landing(k).start()

    def total(self, k):
        self.crossing(k, 0).wait_recv()
        self.landing(k).wait_recv()
        return (
            self.at(self.partial, k, 0)[...].astype(jnp.float32)
            + self.at(self.arrived, k, 0)[...].astype(jnp.float32)
        ) + self.at(self.landed, k, 0)[...].astype(jnp.float32)

    def finish(self, k):
        self.crossing(k, 0).wait_send()
        self.crossing(k, 1).wait_send()
        self.landing(k).wait_send()


class Unpair:
    def __init__(self, part, terms, sems):
        self.part, self.terms, self.sems = part, terms, sems
        self.core, self.zh = lax.axis_index("core"), lax.axis_index("zh")
        self.rows = part.shape[0] // 2

    def piece(self, p):
        return self.part.at[pl.ds(p * self.rows, self.rows)]

    def remote(self, p):
        return pltpu.make_async_remote_copy(
            self.piece(p),
            self.terms.at[self.zh],
            self.sems.at[p],
            self.sems.at[2 + self.zh],
            device_id={"core": p, "zh": self.core},
            device_id_type=MESH,
        )

    def own(self, p):
        return pltpu.make_async_copy(
            self.piece(p), self.terms.at[self.zh], self.sems.at[2 + self.zh]
        )

    def stays(self, p):
        return jnp.logical_and(self.core == p, self.zh == p)

    def start(self):
        for p in range(2):

            @pl.when(self.stays(p))
            def _(p=p):
                self.own(p).start()

            @pl.when(jnp.logical_not(self.stays(p)))
            def _(p=p):
                self.remote(p).start()

    def finish(self):
        for p in range(2):

            @pl.when(jnp.logical_not(self.stays(p)))
            def _(p=p):
                self.remote(p).wait_send()

            pltpu.make_async_copy(
                self.piece(p), self.terms.at[p], self.sems.at[2 + p]
            ).wait()


class Swap:
    def __init__(self, block, target, sems):
        self.block, self.target, self.sems = block, target, sems
        self.swaps = lax.axis_index("core") != lax.axis_index("zh")
        self.step = 2 * block.shape[1] // PARTS

    def at(self, ref, k):
        return ref.at[
            k // (PARTS // 2), pl.ds(pl.multiple_of(k % (PARTS // 2) * self.step, self.step), self.step)
        ]

    def remote(self, k):
        return to_swapped(
            self.at(self.block, k), self.at(self.target, k), self.sems.at[0, k], self.sems.at[1, k]
        )

    def own(self, k):
        return pltpu.make_async_copy(self.at(self.block, k), self.at(self.target, k), self.sems.at[1, k])

    def start(self, k):
        @pl.when(self.swaps)
        def _():
            self.remote(k).start()

        @pl.when(jnp.logical_not(self.swaps))
        def _():
            self.own(k).start()

    def arrive(self, k):
        self.own(k).wait()

    def finish(self, k):
        @pl.when(self.swaps)
        def _():
            self.remote(k).wait_send()


def each(body):
    lax.fori_loop(0, PARTS, lambda k, carry: (body(k), carry)[1], 0)


def kernel_call(number, name, inputs, outs, scratch, body):
    names = list(inputs) + list(outs) + list(scratch)

    def kernel(*refs):
        body(dict(zip(names, refs)))

    results = pl.pallas_call(
        kernel,
        out_shape=tuple(shape for shape, _ in outs.values()),
        in_specs=[VMEM] * len(inputs),
        out_specs=tuple(spec for _, spec in outs.values()),
        scratch_shapes=list(scratch.values()),
        compiler_params=pltpu.CompilerParams(
            collective_id=number,
            has_side_effects=number is not None,
            vmem_limit_bytes=61 * 1024 * 1024,
        ),
        name=name,
    )(*inputs.values())
    return dict(zip(outs, results))


def collect_scratch(tag, rows, length, width):
    return {
        tag + "arrived": pltpu.VMEM((rows, 2 * length, width), jnp.bfloat16),
        tag + "outgoing": pltpu.VMEM((rows, length, width), jnp.bfloat16),
        tag + "landed": pltpu.VMEM((rows, length, width), jnp.bfloat16),
        tag + "collect_sems": pltpu.SemaphoreType.DMA((6, PARTS)),
    }


def collect_of(refs, tag, partial):
    return Collect(
        refs[partial],
        refs[tag + "arrived"],
        refs[tag + "outgoing"],
        refs[tag + "landed"],
        refs[tag + "collect_sems"],
    )


def shape_of(shape, dtype):
    return jax.ShapeDtypeStruct(shape, dtype)


def gathered_out(rows, length, width):
    return (shape_of((rows, 4 * length, width), jnp.bfloat16), ANY)


def pair_out(shard):
    return (shape_of((2 * shard.shape[0], shard.shape[1]), shard.dtype), ANY)


def terms_out(part):
    return (shape_of((2, part.shape[0] // 2, part.shape[1]), part.dtype), ANY)


class PlaneGather:
    def __init__(self, whole, columns, sems):
        self.whole, self.columns, self.sems = whole, columns, sems
        self.rows = whole.shape[0] // 4

    def half(self, chip, which):
        start, size = self.columns
        return self.whole.at[
            pl.ds(pl.multiple_of(chip * self.rows, self.rows), self.rows),
            pl.ds(start + which * (size // 2), size // 2),
        ]

    def own(self, axis, which):
        ref = self.half(lax.axis_index("chip"), which)
        return self.copy(ref, axis, 2 * axis + which)

    def passed(self, which):
        ref = self.half(across_plane(which), which)
        return self.copy(ref, 1 - which, 4 + which)

    def copy(self, ref, axis, number):
        return pltpu.make_async_remote_copy(
            ref,
            ref,
            self.sems.at[0, number],
            self.sems.at[1, number],
            device_id={"chip": across_plane(axis)},
            device_id_type=MESH,
        )

    def start(self):
        for axis in range(2):
            self.own(axis, axis).start()
        for axis in range(2):
            self.own(axis, 1 - axis).start()

    def relay(self):
        for which in range(2):
            self.own(which, which).wait_recv()
            self.passed(which).start()

    def finish(self):
        for axis in range(2):
            self.own(axis, axis).wait_send()
            self.own(axis, 1 - axis).wait()
            self.passed(axis).wait()


class SwapWhole:
    def __init__(self, array, target, sems):
        self.array, self.target, self.sems = array, target, sems
        self.swaps = lax.axis_index("core") != lax.axis_index("zh")

    def remote(self):
        return to_swapped(self.array, self.target, self.sems.at[0], self.sems.at[1])

    def own(self):
        return pltpu.make_async_copy(self.array, self.target, self.sems.at[1])

    def start(self):
        @pl.when(self.swaps)
        def _():
            self.remote().start()

        @pl.when(jnp.logical_not(self.swaps))
        def _():
            self.own().start()

    def finish(self):
        self.own().wait()

        @pl.when(self.swaps)
        def _():
            self.remote().wait_send()


class GainGather:
    def __init__(self, own, slots, whole, sems):
        self.own, self.slots, self.whole, self.sems = own, slots, whole, sems
        self.chips = lax.axis_size("chip")
        self.chip, self.core = lax.axis_index("chip"), lax.axis_index("core")

    def others(self):
        for number in range(1, 2 * self.chips):
            yield number, (self.chip + number // 2) % self.chips, (self.core + number % 2) % 2

    def send(self, number, chip, core):
        return pltpu.make_async_remote_copy(
            self.own,
            self.slots.at[self.chip * 2 + self.core],
            self.sems.at[0, number],
            self.sems.at[1, self.chip * 2 + self.core],
            device_id={"chip": chip, "core": core},
            device_id_type=MESH,
        )

    def start(self):
        for other in self.others():
            self.send(*other).start()
        self.slots.at[self.chip * 2 + self.core][...] = self.own[...]

    def finish(self):
        for number, chip, core in self.others():
            self.send(number, chip, core).wait_send()
            place = chip * 2 + core
            pltpu.make_async_copy(self.own, self.slots.at[place], self.sems.at[1, place]).wait()
        held = self.own.shape[1]
        for place in range(2 * self.chips):
            self.whole[:, place * held : (place + 1) * held] = self.slots[place]


def head(number, block, beside, marks, gains, first, second):
    rows, length, width = block.shape
    depth, size = first[0].shape
    chips = lax.axis_size("chip")
    in_plane = chips == 4
    if not in_plane:
        gains = lax.all_gather(gains, ("chip", "core"), axis=1, tiled=True)

    def body(refs):
        swap = Swap(refs["block"], refs["here"], refs["swap_sems"])
        marks_swap = SwapWhole(refs["marks"], refs["marks_here"], refs["marks_sems"])
        spread_work = Spread(refs["normed"], refs["gathered"], refs["spread_sems"])
        if in_plane:
            chip = lax.axis_index("chip")
            place = refs["whole"].at[pl.ds(pl.multiple_of(chip * 2 * depth, 2 * depth), 2 * depth)]
            gain_work = GainGather(
                refs["gains"], refs["gain_slots"], refs["gains_whole"], refs["gain_sems"]
            )
        else:
            place = refs["whole"]
        works = [
            Exchange(
                refs["first%d" % i],
                place.at[:, pl.ds(i * size, size)],
                refs["exchange_sems"].at[i],
            )
            for i in range(len(first))
        ]
        beside_swap = Swap(refs["beside"], refs["beside_here"], refs["beside_swap_sems"])
        beside_work = Spread(refs["beside_here"], refs["beside_gathered"], refs["beside_sems"])
        later = [
            Exchange(
                refs["second%d" % i],
                refs["pair"].at[:, pl.ds(i * size, size)],
                refs["exchange_sems"].at[len(first) + i],
            )
            for i in range(len(second))
        ]
        greet(True, in_plane)
        marks_swap.start()

        def norm_and_send(k):
            swap.arrive(k)
            values = swap.at(refs["here"], k)[...].astype(jnp.float32)
            spread_work.src(k)[...] = normalize(values, refs["gains_whole"][0:1, :]).astype(
                jnp.bfloat16
            )
            spread_work.start(k)

        planes = [
            PlaneGather(refs["whole"], (i * size, size), refs["plane_sems"].at[i])
            for i in range(len(first))
        ]
        last = len(works) - 1
        works[0].start()
        if in_plane:
            gain_work.start()
            gain_work.finish()
        else:
            refs["gains_whole"][...] = refs["gains"][...]
        for i, work in enumerate(works):
            work.finish()
            if in_plane:
                planes[i].start()
            if i < last:
                works[i + 1].start()
            if i == 0:
                each(swap.start)
            if i == last - 1:
                each(beside_swap.start)
            if in_plane and i:
                planes[i - 1].relay()
            if i == 1:
                each(norm_and_send)
            if i == last:
                each(spread_work.relay)

        def pass_on(k):
            beside_swap.arrive(k)
            beside_work.start(k)

        later[0].start()
        pass_on(0)
        pass_on(1)
        if in_plane:
            planes[last].relay()
        for k in range(2, PARTS):
            pass_on(k)
        for i, work in enumerate(later):
            if i + 1 < len(later):
                later[i + 1].start()
            if i == 1:
                each(beside_work.relay)
            work.finish()
        each(beside_work.finish)
        each(beside_swap.finish)
        each(spread_work.finish)
        each(swap.finish)
        if in_plane:
            for plane in planes:
                plane.finish()
        marks_swap.finish()

    whole_rows = 8 * depth if in_plane else 2 * depth
    results = kernel_call(
        number,
        "head",
        {
            "block": block,
            "beside": beside,
            "marks": marks,
            "gains": gains,
            **{"first%d" % i: shard for i, shard in enumerate(first)},
            **{"second%d" % i: shard for i, shard in enumerate(second)},
        },
        {
            "here": (shape_of(block.shape, block.dtype), VMEM),
            "marks_here": (shape_of(marks.shape, marks.dtype), VMEM),
            "gains_whole": (shape_of((gains.shape[0], width), jnp.float32), VMEM),
            "gathered": gathered_out(rows, length, width),
            "whole": (shape_of((whole_rows, len(first) * size), jnp.bfloat16), ANY),
            "beside_gathered": gathered_out(rows, length, width),
            "pair": (shape_of((2 * depth, len(second) * size), jnp.bfloat16), ANY),
        },
        {
            "normed": pltpu.VMEM((rows, length, width), jnp.bfloat16),
            "spread_sems": pltpu.SemaphoreType.DMA((7, PARTS)),
            "swap_sems": pltpu.SemaphoreType.DMA((2, PARTS)),
            "beside_here": pltpu.VMEM((rows, length, width), jnp.bfloat16),
            "beside_sems": pltpu.SemaphoreType.DMA((7, PARTS)),
            "beside_swap_sems": pltpu.SemaphoreType.DMA((2, PARTS)),
            "marks_sems": pltpu.SemaphoreType.DMA((2,)),
            "exchange_sems": pltpu.SemaphoreType.DMA((len(first) + len(second), 4)),
            "plane_sems": pltpu.SemaphoreType.DMA((len(first), 2, 6)),
            "gain_slots": pltpu.VMEM((2 * chips,) + gains.shape, jnp.float32),
            "gain_sems": pltpu.SemaphoreType.DMA((2, 2 * chips)),
        },
        body,
    )
    whole = results["whole"] if in_plane else gather_chips(results["whole"])
    return (
        results["here"],
        results["marks_here"],
        results["gains_whole"],
        results["gathered"],
        results["beside_gathered"],
        whole,
        results["pair"],
    )


class WeightGradFill:
    def __init__(self, tag, left, right):
        self.tag = tag
        depth, columns = left.shape[1], right.shape[1]
        self.size = 256
        self.tiles = depth // self.size
        self.inputs = {tag + "left": left, tag + "right": right}
        self.outs = {tag + "out": (shape_of((depth, columns), jnp.bfloat16), ANY)}
        self.scratch = {
            tag + "stage": pltpu.VMEM((2, self.size, columns), jnp.bfloat16),
            tag + "sems": pltpu.SemaphoreType.DMA((2,)),
        }

    def at(self, i):
        return pl.ds(pl.multiple_of(i * self.size, self.size), self.size)

    def copy(self, refs, i):
        return pltpu.make_async_copy(
            refs[self.tag + "stage"].at[i % 2],
            refs[self.tag + "out"].at[self.at(i)],
            refs[self.tag + "sems"].at[i % 2],
        )

    def tile(self, refs, i):
        @pl.when(i >= 2)
        def _():
            self.copy(refs, i - 2).wait()

        refs[self.tag + "stage"].at[i % 2][...] = down(
            refs[self.tag + "left"].at[:, self.at(i)][...], refs[self.tag + "right"][...]
        ).astype(jnp.bfloat16)
        self.copy(refs, i).start()

    def end(self, refs):
        for i in (self.tiles - 2, self.tiles - 1):
            self.copy(refs, i).wait()


class ProductFill:
    def __init__(self, tag, left, right, columns):
        self.tag, self.columns = tag, columns
        rows = left.shape[0]
        self.size = 256
        self.tiles = rows // self.size
        self.inputs = {tag + "left": left, tag + "right": right}
        self.outs = {tag + "out": (shape_of((rows, right.shape[0]), jnp.bfloat16), VMEM)}
        self.scratch = {}

    def tile(self, refs, i):
        at = pl.ds(pl.multiple_of(i * self.size, self.size), self.size)
        start, width = self.columns
        refs[self.tag + "out"].at[at][...] = across(
            refs[self.tag + "left"].at[at][...],
            refs[self.tag + "right"].at[:, pl.ds(start, width)][...],
        ).astype(jnp.bfloat16)

    def end(self, refs):
        pass


def fill_in(refs, fill, part, parts):
    if fill is not None:
        first, last = fill.tiles * part // parts, fill.tiles * (part + 1) // parts
        lax.fori_loop(first, last, lambda i, carry: (fill.tile(refs, i), carry)[1], 0)


def norm_slope(values, gain, gradient):
    factor = lax.rsqrt(jnp.mean(values * values, axis=-1, keepdims=True) + epsilon)
    scaled = gain * gradient
    inner = jnp.mean(scaled * values, axis=-1, keepdims=True)
    return factor * scaled - values * (factor * factor * factor * inner), gradient * values * factor


def turn_back(number, partial, values, stream, gain, fills, *parts):
    rows, length, width = values.shape
    first, second = (tuple(fills) + (None, None))[:2]

    def body(refs):
        collect_work = collect_of(refs, "", "partial")
        spread_work = Spread(refs["branch"], refs["gathered"], refs["spread_sems"])
        works = [
            Unpair(refs["part%d" % i], refs["terms%d" % i], refs["unpair_sems"].at[i])
            for i in range(len(parts))
        ]
        greet(bool(parts))
        for work in works:
            work.start()
        collect_work.start()
        each(collect_work.forward)
        refs["gain_sum"][...] = jnp.zeros_like(refs["gain_sum"])

        def slope_and_send(k):
            slope, terms = norm_slope(
                collect_work.at(refs["values"], k, 0)[...].astype(jnp.float32),
                refs["gain"][...],
                collect_work.total(k),
            )
            sums = collect_work.at(refs["stream"], k, 0)[...].astype(jnp.float32) + slope
            collect_work.at(refs["after"], k, 0)[...] = sums
            spread_work.src(k)[...] = sums.astype(jnp.bfloat16)
            spread_work.start(k)
            refs["gain_sum"][...] += jnp.sum(terms, axis=0, keepdims=True)

        if first is None:
            each(slope_and_send)
        else:
            for k in range(PARTS):
                fill_in(refs, first, k, PARTS)
                slope_and_send(k)
        fill_in(refs, second, 0, 1)
        each(spread_work.relay)
        each(spread_work.finish)
        each(collect_work.finish)
        for work in works:
            work.finish()
        for fill in fills:
            fill.end(refs)

    extra = {"inputs": {}, "outs": {}, "scratch": {}}
    for fill in fills:
        for kind, found in extra.items():
            found.update(getattr(fill, kind))
    results = kernel_call(
        number,
        "turn_back",
        {
            "partial": partial,
            "values": values,
            "stream": stream,
            "gain": gain[None],
            **{"part%d" % i: part for i, part in enumerate(parts)},
            **extra["inputs"],
        },
        {
            "after": (shape_of(values.shape, jnp.float32), VMEM),
            "gathered": gathered_out(rows, length, width),
            "gain_sum": (shape_of((1, width), jnp.float32), VMEM),
            **{"terms%d" % i: terms_out(part) for i, part in enumerate(parts)},
            **extra["outs"],
        },
        {
            **collect_scratch("", rows, length, width),
            "branch": pltpu.VMEM((rows, length, width), jnp.bfloat16),
            "spread_sems": pltpu.SemaphoreType.DMA((7, PARTS)),
            "unpair_sems": pltpu.SemaphoreType.DMA((max(1, len(parts)), 4)),
            **extra["scratch"],
        },
        body,
    )
    return (
        (results["after"], results["gathered"], results["gain_sum"])
        + tuple(results["terms%d" % i] for i in range(len(parts)))
        + tuple(results[name] for fill in fills for name in fill.outs)
    )


class OutWork:
    def __init__(self, collect_work, swap, base):
        self.collect_work, self.swap, self.base = collect_work, swap, base

    def begin(self):
        self.collect_work.start()

    def forward(self):
        each(self.collect_work.forward)

    def leave_part(self, k):
        total = self.collect_work.total(k)
        if self.base is not None:
            total = total + self.swap.at(self.base, k)[...]
        self.swap.at(self.swap.block, k)[...] = total.astype(jnp.bfloat16)
        self.swap.start(k)

    def end(self):
        each(self.swap.arrive)
        each(self.swap.finish)
        each(self.collect_work.finish)


def head_at(ref, r, h, offset):
    return ref.at[r, :, pl.ds(pl.multiple_of(offset + h * HD, HD), HD)]


def across(left, right):
    return lax.dot_general(
        left, right, (((1,), (1,)), ((), ())), preferred_element_type=jnp.float32
    )


def down(left, right):
    return lax.dot_general(
        left, right, (((0,), (0,)), ((), ())), preferred_element_type=jnp.float32
    )


def masked_probability(refs, r, queries, key_rows):
    scores = across(queries, key_rows) * HD ** (-0.5)
    allowed = jnp.logical_and(
        refs["query_mark"][r] == refs["key_mark"][r],
        refs["query_place"][...] >= refs["key_place"][...],
    )
    scores = jnp.where(allowed, scores, masked_value)
    shifted = jnp.exp(scores - jnp.max(scores, axis=-1, keepdims=True))
    return shifted / jnp.sum(shifted, axis=-1, keepdims=True)


def rows_of(ref, t, size):
    per_row = ref.shape[1] // size
    return ref.at[t // per_row, pl.ds(pl.multiple_of(t % per_row * size, size), size)]


def attention_back(
    number, branch, weights, places, queries, pairs, marks, lefts, attended, out, part
):
    query_place, pair_place, out_place = places
    (query_array, query_at), (pair_array, pair_at) = queries, pairs
    same = query_array is pair_array
    rows, length, width = branch.shape
    wide = weights.shape[1] // 4
    heads = wide // HD
    block = (rows, length // 4, width)
    flat = (rows * length, width)
    inputs = {
        "branch": branch,
        "weights": weights,
        "queries": query_array,
        "query_mark": marks[0],
        "key_mark": marks[1],
        "query_place": marks[2],
        "key_place": marks[3],
        "left0": lefts[0].reshape(flat),
        "part": part,
    }
    if not same:
        inputs["pairs"] = pair_array
        inputs["left1"] = lefts[1].reshape(flat)
    if attended is not None:
        inputs["attended"] = attended.reshape(rows * length, wide)
    if out is not None:
        inputs["partial"] = out[0]
        if out[1] is not None:
            inputs["base"] = out[1]
    grad_columns = wide * (4 if attended is not None else 3)
    outs = {
        "input_partial": (shape_of((rows, length, width), jnp.bfloat16), VMEM),
        "weight_grads": (shape_of((width, grad_columns), jnp.bfloat16), ANY),
        "terms": terms_out(part),
    }
    scratch = {
        "grad_out": pltpu.VMEM((rows, length, wide), jnp.bfloat16),
        "stage": pltpu.VMEM((2, 256, grad_columns), jnp.bfloat16),
        "stage_sems": pltpu.SemaphoreType.DMA((2,)),
        "unpair_sems": pltpu.SemaphoreType.DMA((4,)),
    }
    if out is not None:
        outs["out"] = (shape_of(block, jnp.bfloat16), ANY)
        scratch.update(collect_scratch("", *block))
        scratch["leaving"] = pltpu.VMEM(block, jnp.bfloat16)
        scratch["swap_sems"] = pltpu.SemaphoreType.DMA((2, PARTS))
    if same:
        scratch["grad_all"] = pltpu.VMEM((rows, length, 3 * wide), jnp.bfloat16)
    else:
        scratch["grad_queries"] = pltpu.VMEM((rows, length, wide), jnp.bfloat16)
        outs["grad_pairs"] = (shape_of((rows, length, 2 * wide), jnp.bfloat16), VMEM)
    scale = HD ** (-0.5)
    total = rows * heads
    size = 256

    def body(refs):
        unpair = Unpair(refs["part"], refs["terms"], refs["unpair_sems"])
        out_work = None
        if out is not None:
            out_work = OutWork(
                collect_of(refs, "", "partial"),
                Swap(refs["leaving"], refs["out"], refs["swap_sems"]),
                refs.get("base"),
            )
        grad_queries = refs["grad_all"] if same else refs["grad_queries"]
        grad_pairs = refs["grad_all"] if same else refs["grad_pairs"]
        pair_refs = refs["queries"] if same else refs["pairs"]
        pair_out = wide if same else 0

        def form_grad_out(t):
            rows_of(refs["grad_out"], t, size)[...] = jnp.dot(
                rows_of(refs["branch"], t, size)[...],
                refs["weights"].at[:, pl.ds(out_place, wide)][...],
                preferred_element_type=jnp.float32,
            ).astype(jnp.bfloat16)

        def one(i):
            r, h = i // heads, i % heads
            queries_here = head_at(refs["queries"], r, h, query_at)[...]
            key_rows = head_at(pair_refs, r, h, pair_at)[...]
            value_rows = head_at(pair_refs, r, h, pair_at + wide)[...]
            grad_here = head_at(refs["grad_out"], r, h, 0)[...]
            probability = masked_probability(refs, r, queries_here, key_rows)
            grad_values = down(probability.astype(jnp.bfloat16), grad_here)
            grad_probs = across(grad_here, value_rows)
            inner = jnp.sum(probability * grad_probs, axis=-1, keepdims=True)
            grad_scores = (probability * (grad_probs - inner)).astype(jnp.bfloat16)
            query_terms = jnp.dot(grad_scores, key_rows, preferred_element_type=jnp.float32)
            key_terms = down(grad_scores, queries_here)
            head_at(grad_queries, r, h, 0)[...] = (query_terms * scale).astype(jnp.bfloat16)
            head_at(grad_pairs, r, h, pair_out)[...] = (key_terms * scale).astype(jnp.bfloat16)
            head_at(grad_pairs, r, h, pair_out + wide)[...] = grad_values.astype(jnp.bfloat16)

        def form_partial(t):
            columns = (query_place, 3 * wide if same else wide)
            rows_of(refs["input_partial"], t, size)[...] = across(
                rows_of(grad_queries, t, size)[...],
                refs["weights"].at[:, pl.ds(*columns)][...],
            ).astype(jnp.bfloat16)

        def written(i):
            return pltpu.make_async_copy(
                refs["stage"].at[i % 2],
                refs["weight_grads"].at[pl.ds(pl.multiple_of(i * size, size), size)],
                refs["stage_sems"].at[i % 2],
            )

        def form_grads(i):
            @pl.when(i >= 2)
            def _():
                written(i - 2).wait()

            at = pl.ds(pl.multiple_of(i * size, size), size)
            stage = refs["stage"].at[i % 2]

            def put(place, left, right):
                terms = right[...].reshape(rows * length, right.shape[-1])
                stage[:, place : place + right.shape[-1]] = down(left, terms).astype(jnp.bfloat16)

            put(query_place, refs["left0"].at[:, at][...], grad_queries)
            if not same:
                put(pair_place, refs["left1"].at[:, at][...], grad_pairs)
            if attended is not None:
                here = refs["branch"].at[:, :, at][...].reshape(rows * length, size)
                stage[:, out_place : out_place + wide] = down(here, refs["attended"][...]).astype(
                    jnp.bfloat16
                )
            written(i).start()

        def loop(count, work, stops=()):
            def step(i, carry):
                work(i)
                if out_work is not None:
                    for stop, k in stops:

                        @pl.when(i == stop)
                        def _(k=k):
                            out_work.leave_part(k)

                return carry

            lax.fori_loop(0, count, step, 0)

        greet(True)
        unpair.start()
        if out_work is not None:
            out_work.begin()
        loop(rows * length // size, form_grad_out)
        if out_work is not None:
            out_work.forward()
        loop(total, one, ((total - 1, 0),))
        loop(width // size, form_grads, ((1, 1), (3, 2), (5, 3)))
        loop(rows * length // size, form_partial)
        if out_work is not None:
            out_work.end()
        unpair.finish()
        for i in (width // size - 2, width // size - 1):
            written(i).wait()

    results = kernel_call(number, "attention_back", inputs, outs, scratch, body)
    return (
        results["input_partial"],
        results["weight_grads"],
        results["terms"],
        results.get("grad_pairs"),
        results.get("out"),
    )


def attention_turn(number, lefts, weights, places, marks, stream, gain, done=None, beside=None):
    query_place, pair_place, out_place = places
    same = lefts[0] is lefts[1]
    rows, length, width = lefts[0].shape
    wide = weights.shape[1] // 4
    heads = wide // HD
    quarter = length // 4
    size = 256
    inputs = {"weights": weights}
    outs, scratch = {}, {}
    if done is None:
        inputs.update(
            {
                "left0": lefts[0],
                "query_mark": marks[0],
                "key_mark": marks[1],
                "query_place": marks[2],
                "key_place": marks[3],
            }
        )
        outs["queries"] = (
            shape_of((rows, length, wide * (3 if same else 1)), jnp.bfloat16),
            VMEM,
        )
        outs["attended"] = (shape_of((rows, length, wide), jnp.bfloat16), VMEM)
        if not same:
            inputs["left1"] = lefts[1]
            outs["pairs"] = (shape_of((rows, length, 2 * wide), jnp.bfloat16), VMEM)
    else:
        inputs["attended"] = done
    if stream is not None:
        inputs["stream"] = stream
        inputs["gain"] = gain[None]
        outs["after"] = (shape_of(stream.shape, jnp.float32), VMEM)
        outs["gathered"] = gathered_out(rows, quarter, width)
        scratch.update(
            {
                **collect_scratch("", rows, quarter, width),
                "partial": pltpu.VMEM((rows, length, width), jnp.bfloat16),
                "normed": pltpu.VMEM((rows, quarter, width), jnp.bfloat16),
                "spread_sems": pltpu.SemaphoreType.DMA((7, PARTS)),
            }
        )
    if beside is not None:
        inputs["beside"] = beside
        outs["beside_gathered"] = gathered_out(rows, quarter, width)
        outs["beside_here"] = (shape_of((rows, quarter, width), jnp.bfloat16), VMEM)
        scratch["beside_sems"] = pltpu.SemaphoreType.DMA((7, PARTS))
        scratch["beside_swap_sems"] = pltpu.SemaphoreType.DMA((2, PARTS))

    def body(refs):
        if stream is not None:
            collect_work = collect_of(refs, "", "partial")
            spread_work = Spread(refs["normed"], refs["gathered"], refs["spread_sems"])
        if beside is not None:
            swap = Swap(refs["beside"], refs["beside_here"], refs["beside_swap_sems"])
            beside_work = Spread(
                refs["beside_here"], refs["beside_gathered"], refs["beside_sems"]
            )
        if done is None:
            pair_refs = refs["queries"] if same else refs["pairs"]
        pair_at = wide if same else 0

        def loop(count, work):
            lax.fori_loop(0, count, lambda i, carry: (work(i), carry)[1], 0)

        def form(left, place, columns, target):
            def tile(t):
                rows_of(target, t, size)[...] = jnp.dot(
                    rows_of(left, t, size)[...],
                    refs["weights"].at[:, pl.ds(place, columns)][...],
                    preferred_element_type=jnp.float32,
                ).astype(jnp.bfloat16)

            loop(rows * length // size, tile)

        def one(i):
            r, h = i // heads, i % heads
            probability = masked_probability(
                refs,
                r,
                head_at(refs["queries"], r, h, 0)[...],
                head_at(pair_refs, r, h, pair_at)[...],
            ).astype(jnp.bfloat16)
            head_at(refs["attended"], r, h, 0)[...] = jnp.dot(
                probability,
                head_at(pair_refs, r, h, pair_at + wide)[...],
                preferred_element_type=jnp.float32,
            ).astype(jnp.bfloat16)

        def form_block(block):
            def tile(r):
                at = pl.ds(block * quarter, quarter)
                refs["partial"].at[r, at][...] = across(
                    refs["attended"].at[r, at][...],
                    refs["weights"].at[:, pl.ds(out_place, wide)][...],
                ).astype(jnp.bfloat16)

            loop(rows, tile)

        def norm_and_send(k):
            values = collect_work.at(refs["stream"], k, 0)[...].astype(
                jnp.float32
            ) + collect_work.total(k)
            collect_work.at(refs["after"], k, 0)[...] = values
            spread_work.src(k)[...] = normalize(values, refs["gain"][...]).astype(jnp.bfloat16)
            spread_work.start(k)

        def pass_on(first, last):
            if beside is not None:
                for k in range(first, last):
                    swap.arrive(k)
                    beside_work.start(k)

        if number is not None:
            greet(beside is not None)
        if beside is not None:
            each(swap.start)
        if done is None:
            if same:
                form(refs["left0"], query_place, 3 * wide, refs["queries"])
            else:
                form(refs["left1"], pair_place, 2 * wide, refs["pairs"])
                pass_on(0, 1)
                form(refs["left0"], query_place, wide, refs["queries"])
            pass_on(0 if same else 1, 2)
            loop(rows * heads, one)
        pass_on(0 if done is not None else 2, PARTS)
        if stream is not None:
            for block in (3, 2):
                form_block(block)
                collect_work.start_block(block - 2)
            form_block(1)
            each(collect_work.forward)
            form_block(0)
            if beside is not None:
                each(beside_work.relay)
            each(norm_and_send)
            each(spread_work.relay)
            each(spread_work.finish)
            each(collect_work.finish)
        elif beside is not None:
            each(beside_work.relay)
        if beside is not None:
            each(beside_work.finish)
            each(swap.finish)

    results = kernel_call(number, "attention_turn", inputs, outs, scratch, body)
    return tuple(
        results.get(name)
        for name in (
            "queries",
            "pairs",
            "attended",
            "after",
            "gathered",
            "beside_here",
            "beside_gathered",
        )
    )


class PlaneScatter:
    def __init__(self, grads, columns, taken, passing, crossed, part, sems):
        self.grads, self.columns, self.taken, self.passing = grads, columns, taken, passing
        self.crossed, self.part, self.sems = crossed, part, sems
        self.rows = grads.shape[0] // 4
        self.me = lax.axis_index("chip")

    def terms(self, chip, which):
        start, size = self.columns
        return self.grads.at[
            pl.ds(pl.multiple_of(chip * self.rows, self.rows), self.rows),
            pl.ds(start + which * (size // 2), size // 2),
        ]

    def copy(self, src, dst, axis, number):
        return pltpu.make_async_remote_copy(
            src,
            dst,
            self.sems.at[0, number],
            self.sems.at[1, number],
            device_id={"chip": across_plane(axis)},
            device_id_type=MESH,
        )

    def first(self, which, block):
        chip = 3 - self.me if block else across_plane(which)
        return self.copy(
            self.terms(chip, which), self.taken.at[which, block], which, 2 * which + block
        )

    def second(self, which):
        return self.copy(
            self.passing.at[which], self.crossed.at[which], 1 - which, 4 + which
        )

    def start(self):
        for block in (1, 0):
            for which in range(2):
                self.first(which, block).start()

    def pass_on(self, following):
        for which in range(2):
            self.first(which, 1).wait_recv()
        if following is not None:
            following.start()
        for which in range(2):
            self.passing.at[which][...] = (
                self.terms(across_plane(1 - which), which)[...].astype(jnp.float32)
                + self.taken.at[which, 1][...].astype(jnp.float32)
            ).astype(jnp.bfloat16)
            self.second(which).start()

    def total(self):
        half = self.columns[1] // 2
        for which in range(2):
            self.first(which, 0).wait_recv()
            self.second(which).wait_recv()
            self.part.at[:, pl.ds(which * half, half)][...] = (
                self.terms(self.me, which)[...].astype(jnp.float32)
                + self.taken.at[which, 0][...].astype(jnp.float32)
                + self.crossed.at[which][...].astype(jnp.float32)
            ).astype(jnp.bfloat16)

    def finish(self):
        for which in range(2):
            for block in range(2):
                self.first(which, block).wait_send()
            self.second(which).wait_send()


def sum_everywhere(given, taken, sems, totals):
    chips = lax.axis_size("chip")
    core, zh, zp, chip = (lax.axis_index(axis) for axis in ("core", "zh", "zp", "chip"))
    partners = [{"core": 1 - core}, {"zp": 1 - zp}, {"zh": 1 - zh}]
    for bit in range(chips.bit_length() - 1):
        size = 2**bit
        partners.append({"chip": chip + size - 2 * size * (chip // size % 2)})
    sums = given[0]
    for step, partner in enumerate(partners):
        if step:
            given[step] = sums
        copy = pltpu.make_async_remote_copy(
            given.at[step],
            taken.at[step],
            sems.at[0, step],
            sems.at[1, step],
            device_id=partner,
            device_id_type=MESH,
        )
        copy.start()
        copy.wait()
        sums = sums + taken[step]
    totals[...] = sums


def leave(number, partial, values, stream, gain, gain_sums, grads, part):
    rows, length, width = values.shape
    chips = lax.axis_size("chip")
    in_plane = chips == 4
    steps = 3 + chips.bit_length() - 1
    if not in_plane:
        grads = scatter_chips(grads)
    owned = grads.shape[0] // (4 if in_plane else 1)
    columns = grads.shape[1]
    size = 512
    pieces = columns // size if in_plane else 0

    def body(refs):
        collect_work = collect_of(refs, "", "partial")
        swap = Swap(refs["leaving"], refs["out"], refs["swap_sems"])
        unpair = Unpair(refs["part"], refs["terms"], refs["unpair_sems"])
        if in_plane:
            scatters = [
                PlaneScatter(
                    refs["grads"],
                    (p * size, size),
                    refs["taken"].at[p],
                    refs["passing"].at[p],
                    refs["crossed"].at[p],
                    refs["summed"].at[p],
                    refs["plane_sems"].at[p],
                )
                for p in range(pieces)
            ]
            returns = [
                Unpair(
                    refs["summed"].at[p],
                    refs["grad_terms"].at[:, :, pl.ds(p * size, size)],
                    refs["return_sems"].at[p],
                )
                for p in range(pieces)
            ]
        else:
            scatters = []
            returns = [Unpair(refs["grads"], refs["grad_terms"], refs["return_sems"].at[0])]
        greet(True, True)
        unpair.start()
        if scatters:
            scatters[0].start()
        collect_work.start()
        each(collect_work.forward)
        if not in_plane:
            returns[0].start()
        refs["given"].at[0][1:3] = refs["gain_sums"][...]
        refs["gain_sum"][...] = jnp.zeros_like(refs["gain_sum"])

        def slope_and_send(k):
            slope, terms = norm_slope(
                collect_work.at(refs["values"], k, 0)[...].astype(jnp.float32),
                refs["gain"][...],
                collect_work.total(k),
            )
            sums = collect_work.at(refs["stream"], k, 0)[...] + slope
            swap.at(refs["leaving"], k)[...] = sums.astype(jnp.bfloat16)
            swap.start(k)
            refs["gain_sum"][...] += jnp.sum(terms, axis=0, keepdims=True)

        turns = max(PARTS, len(scatters) + 1)
        for k in range(turns):
            if k < PARTS:
                slope_and_send(k)
            if k < len(scatters):
                scatters[k].pass_on(scatters[k + 1] if k + 1 < len(scatters) else None)
            if 0 < k <= len(scatters):
                scatters[k - 1].total()
                returns[k - 1].start()
        refs["given"].at[0][0:1] = refs["gain_sum"][...]
        sum_everywhere(refs["given"], refs["got"], refs["gain_sems"], refs["totals"])
        each(swap.arrive)
        each(swap.finish)
        each(collect_work.finish)
        unpair.finish()
        for scatter in scatters:
            scatter.finish()
        for back in returns:
            back.finish()

    scratch = {
        **collect_scratch("", rows, length, width),
        "leaving": pltpu.VMEM((rows, length, width), jnp.bfloat16),
        "swap_sems": pltpu.SemaphoreType.DMA((2, PARTS)),
        "unpair_sems": pltpu.SemaphoreType.DMA((4,)),
        "return_sems": pltpu.SemaphoreType.DMA((max(1, pieces), 4)),
        "gain_sum": pltpu.VMEM((1, width), jnp.float32),
        "given": pltpu.VMEM((steps, 3, width), jnp.float32),
        "got": pltpu.VMEM((steps, 3, width), jnp.float32),
        "gain_sems": pltpu.SemaphoreType.DMA((2, steps)),
    }
    if in_plane:
        scratch["taken"] = pltpu.VMEM((pieces, 2, 2, owned, size // 2), jnp.bfloat16)
        scratch["passing"] = pltpu.VMEM((pieces, 2, owned, size // 2), jnp.bfloat16)
        scratch["crossed"] = pltpu.VMEM((pieces, 2, owned, size // 2), jnp.bfloat16)
        scratch["summed"] = pltpu.VMEM((pieces, owned, size), jnp.bfloat16)
        scratch["plane_sems"] = pltpu.SemaphoreType.DMA((pieces, 2, 6))
    results = kernel_call(
        number,
        "leave",
        {
            "partial": partial,
            "values": values,
            "stream": stream,
            "gain": gain[None],
            "gain_sums": gain_sums,
            "grads": grads,
            "part": part,
        },
        {
            "out": (shape_of(values.shape, jnp.bfloat16), ANY),
            "totals": (shape_of((3, width), jnp.float32), VMEM),
            "terms": terms_out(part),
            "grad_terms": (shape_of((2, owned // 2, columns), jnp.bfloat16), ANY),
        },
        scratch,
        body,
    )
    return results["out"], results["totals"], results["terms"], results["grad_terms"]


def summed(terms):
    return terms[0].astype(jnp.float32) + terms[1].astype(jnp.float32)


def project(left_side, right_side):
    return jnp.einsum("rtd,de->rte", left_side, right_side, preferred_element_type=jnp.float32)


def project_back(gradient, right_side):
    return jnp.einsum("rte,de->rtd", gradient, right_side, preferred_element_type=jnp.float32)


def weight_grad(left_side, gradient):
    return jnp.einsum("rtd,rte->de", left_side, gradient, preferred_element_type=jnp.float32)


def gelu_tanh(values):
    return jax.nn.gelu(values, approximate=True)


def shards(
    tokens,
    patches,
    seg_ids,
    seg_example,
    patch_owner,
    gain_self,
    self_query,
    self_key,
    self_value,
    self_out,
    gain_cross,
    cross_query,
    cross_key,
    cross_value,
    cross_out,
    gain_mlp,
    mlp_gate,
    mlp_up,
    mlp_down,
    cotangent,
):
    gains = jnp.stack([gain_self, gain_cross, gain_mlp]).astype(jnp.float32)
    onehot = (
        seg_ids[:, :, None] == lax.iota(jnp.int32, seg_example.shape[1])[None, None, :]
    ).astype(jnp.int32)
    example_of = jnp.sum(onehot * seg_example[:, None, :], axis=2)
    marks = jnp.concatenate([seg_ids, example_of, patch_owner], axis=0)
    rows = seg_ids.shape[0]
    length = seg_ids.shape[1]
    wide = self_query.shape[1]
    hidden_wide = mlp_gate.shape[1]
    local_tokens, marks, gains, normed_one, patch_rows, self_w, cross_pair = head(
        0,
        tokens,
        patches,
        marks,
        gains,
        (self_query, self_key, self_value, self_out.T),
        (cross_key, cross_value, cross_query, cross_out.T),
    )
    norm_one, norm_two, norm_three = gains[0], gains[1], gains[2]
    cross_w = gather_chips(cross_pair)
    mlp_moved = exchange(after(jnp.concatenate([mlp_gate, mlp_up], axis=1), normed_one))
    seg_here = relative(marks[:rows])
    example_here = relative(marks[rows : 2 * rows])
    owner_here = relative(marks[2 * rows :])
    positions = relative(lax.broadcasted_iota(jnp.int32, (1, length), 1))
    self_marks = (
        seg_here[:, :, None],
        seg_here[:, None, :],
        positions.reshape(length, 1),
        positions.reshape(1, length),
    )
    cross_marks = (
        example_here[:, :, None],
        owner_here[:, None, :],
        jnp.zeros((length, 1), jnp.int32),
        jnp.zeros((1, length), jnp.int32),
    )
    self_places = (0, wide, 3 * wide)
    self_lefts = (normed_one, normed_one)
    self_qkv, _, self_attended, _, _, _, _ = attention_turn(
        None, self_lefts, self_w, self_places, self_marks, None, None
    )
    mlp_pair = pair_up(after(mlp_moved, self_attended))
    mlp_in = gather_chips(mlp_pair)
    down_moved = exchange(after(mlp_down.T, mlp_pair))
    _, _, _, after_self, normed_two, _, _ = attention_turn(
        1,
        self_lefts,
        self_w,
        self_places,
        self_marks,
        local_tokens,
        norm_two,
        after(self_attended, mlp_pair),
    )
    down_pair = pair_up(after(down_moved, after_self))
    mlp_downw = gather_chips(down_pair)
    (
        cross_query_rows,
        cross_kv_rows,
        cross_mixed,
        after_cross,
        normed_three,
        local_grad,
        grad_rows,
    ) = attention_turn(
        2,
        (after(normed_two, down_pair), patch_rows),
        cross_w,
        (2 * wide, 0, 3 * wide),
        cross_marks,
        after_self,
        norm_three,
        None,
        cotangent,
    )
    both = project(normed_three, mlp_in)
    gate_pre = both[..., :hidden_wide]
    upward = both[..., hidden_wide:]
    activated, gelu_pull = jax.vjp(gelu_tanh, gate_pre)
    hidden = (activated * upward).astype(jnp.bfloat16)

    grad_down_w = weight_grad(grad_rows, hidden).astype(jnp.bfloat16)
    down_part = scatter_chips(grad_down_w)
    grad_hidden = project(after(grad_rows, grad_down_w), mlp_downw)
    grad_upward = (grad_hidden * activated).astype(jnp.bfloat16)
    grad_gate = gelu_pull(grad_hidden * upward)[0].astype(jnp.bfloat16)
    grad_both = jnp.concatenate([grad_gate, grad_upward], axis=2)
    partial_three = project_back(grad_both, mlp_in).astype(jnp.bfloat16)
    tokens_here = rows * length
    grad_mlp_w = weight_grad(normed_three, grad_both).astype(jnp.bfloat16)
    mlp_part = scatter_chips(grad_mlp_w)
    grad_cross_stream, cross_branch, part_three, result_partial = turn_back(
        3,
        after(partial_three, grad_mlp_w),
        after_cross,
        local_grad,
        norm_three,
        (ProductFill("result_", hidden.reshape(tokens_here, -1), mlp_downw, (0, hidden_wide)),),
    )
    partial_two, cross_grads, down_terms, grad_ckv, output = attention_back(
        4,
        cross_branch,
        cross_w,
        (2 * wide, 0, 3 * wide),
        (cross_query_rows, 0),
        (cross_kv_rows, 0),
        cross_marks,
        (normed_two, patch_rows),
        cross_mixed,
        (result_partial.reshape(rows, length, -1), after_cross),
        down_part,
    )
    down_sum = summed(down_terms).T
    cross_part = scatter_chips(cross_grads)
    grad_self_stream, self_branch, part_two, mlp_terms, patch_partial = turn_back(
        5,
        partial_two,
        after_self,
        grad_cross_stream,
        norm_two,
        (ProductFill("patch_", grad_ckv.reshape(tokens_here, -1), cross_w, (0, 2 * wide)),),
        mlp_part,
    )
    mlp_sum = summed(mlp_terms)
    grad_self_out = weight_grad(self_branch, self_attended).astype(jnp.bfloat16)
    self_out_part = scatter_chips(grad_self_out)
    partial_one, grad_self_in, cross_terms, _, grad_patches = attention_back(
        6,
        after(self_branch, grad_self_out),
        self_w,
        (0, wide, 3 * wide),
        (self_qkv, 0),
        (self_qkv, wide),
        self_marks,
        (normed_one, normed_one),
        None,
        (patch_partial.reshape(rows, length, -1), None),
        cross_part,
    )
    cross_sum = summed(cross_terms)
    grad_tokens, gain_sums, self_out_terms, self_terms = leave(
        7,
        partial_one,
        local_tokens,
        grad_self_stream,
        norm_one,
        jnp.concatenate([part_two, part_three]),
        grad_self_in,
        self_out_part,
    )
    held = gain_self.shape[0]
    place = lax.axis_index(("chip", "core")) * held
    gain_sums = lax.dynamic_slice_in_dim(gain_sums, place, held, axis=1)
    self_sum = summed(self_terms)
    return (
        output,
        grad_tokens.astype(jnp.float32),
        grad_patches.astype(jnp.float32),
        gain_sums[0],
        self_sum[:, :wide],
        self_sum[:, wide : 2 * wide],
        self_sum[:, 2 * wide :],
        summed(self_out_terms).T,
        gain_sums[1],
        cross_sum[:, 2 * wide : 3 * wide],
        cross_sum[:, :wide],
        cross_sum[:, wide : 2 * wide],
        cross_sum[:, 3 * wide :].T,
        gain_sums[2],
        mlp_sum[:, :hidden_wide],
        mlp_sum[:, hidden_wide:],
        down_sum,
    )


def solution(mesh):
    devices = mesh.devices.reshape(mesh.shape["dp"] // 2, 2, 2, mesh.shape["seq"] // 2)
    fine = Mesh(devices, AXES)
    dp = ("chip", "core")
    seq = ("zh", "zp")
    stream = P(dp, seq, None)
    rows = P(dp, None)
    inward = P(dp, seq)
    outward = P(seq, dp)
    vector = P(dp)
    block = (vector, inward, inward, inward, outward)
    weights = block + block + (vector, inward, inward, outward)
    return jax.shard_map(
        shards,
        mesh=fine,
        in_specs=(stream, stream, rows, rows, rows) + weights + (stream,),
        out_specs=(stream, stream, stream) + weights,
        check_vma=False,
    )
```

```python
import itertools

import jax
import jax.numpy as jnp
from jax import lax
from jax.experimental import pallas as pl
from jax.experimental.pallas import tpu as pltpu
from jax.sharding import Mesh
from jax.sharding import PartitionSpec as P

HD = 128


epsilon = 1e-06
masked_value = -1e30

AXES = ("chip", "core", "zh", "zp")


def moves(chips, source_of):
    pairs = []
    for chip, core, zh, zp in itertools.product(range(chips), range(2), range(2), range(2)):
        a, b, c, d = source_of(chip, core, zh, zp)
        pairs.append((((a * 2 + b) * 2 + c) * 2 + d, ((chip * 2 + core) * 2 + zh) * 2 + zp))
    return pairs


def permute(values, source_of):
    return lax.ppermute(values, AXES, moves(lax.axis_size("chip"), source_of))


def swapped(values):
    return permute(values, lambda chip, core, zh, zp: (chip, zh, core, zp))


def swapped_other(values):
    return permute(values, lambda chip, core, zh, zp: (chip, 1 - zh, core, zp))


def relative(values):
    rows, length = values.shape
    cut = values.reshape(rows, 2, 2, length // 4)
    cut = jnp.where(lax.axis_index("core") == 1, cut[:, ::-1], cut)
    cut = jnp.where(lax.axis_index("zp") == 1, cut[:, :, ::-1], cut)
    return cut.reshape(rows, length)


def after(values, *others):
    return lax.optimization_barrier((values,) + others)[0]


def exchange(shards_of):
    return swapped(shards_of), swapped_other(shards_of)


def pair_up(exchanged):
    first, second = exchanged
    low = lax.axis_index("zh") == 0
    return jnp.concatenate([jnp.where(low, first, second), jnp.where(low, second, first)], axis=0)


def gather_chips(pair):
    return lax.all_gather(pair, "chip", axis=0, tiled=True)


def scatter_chips(grads):
    return lax.psum_scatter(
        grads.astype(jnp.bfloat16), "chip", scatter_dimension=0, tiled=True
    )


def normalize(values, gain_vec):
    factor = lax.rsqrt(jnp.mean(values * values, axis=-1, keepdims=True) + epsilon)
    return values * factor * gain_vec


def norm_back(values, gain_vec, gradient):
    normed_value, pullback = jax.vjp(lambda inputs: normalize(inputs, gain_vec), values)
    return pullback(gradient)[0]


def gain_part(values, gradient):
    factor = lax.rsqrt(jnp.mean(values * values, axis=-1, keepdims=True) + epsilon)
    return jnp.sum(gradient * values * factor, axis=(0, 1))


MESH = pl.DeviceIdType.MESH
ANY = pl.BlockSpec(memory_space=pl.ANY)
VMEM = pl.BlockSpec(memory_space=pltpu.VMEM)
PARTS = 4


def across_plane(axis):
    chip = lax.axis_index("chip")
    x, y = chip % 2, chip // 2
    return y * 2 + 1 - x if axis == 0 else (1 - y) * 2 + x


def greet(everyone, plane=False):
    core, zh, zp = lax.axis_index("core"), lax.axis_index("zh"), lax.axis_index("zp")
    barrier = pltpu.get_barrier_semaphore()
    count = 0
    for a, b, c in itertools.product(range(2), range(2), range(2)):
        if (a, b, c) == (0, 0, 0) or (b and not everyone):
            continue
        pl.semaphore_signal(
            barrier,
            inc=1,
            device_id={"core": (core + a) % 2, "zh": (zh + b) % 2, "zp": (zp + c) % 2},
            device_id_type=MESH,
        )
        count += 1
    if plane:
        chips = lax.axis_size("chip")
        for a, b in itertools.product(range(1, chips), range(2)):
            pl.semaphore_signal(
                barrier,
                inc=1,
                device_id={
                    "chip": (lax.axis_index("chip") + a) % chips,
                    "core": (core + b) % 2,
                },
                device_id_type=MESH,
            )
            count += 1
    pl.semaphore_wait(barrier, count)


def to_core(src, dst, send, recv):
    return pltpu.make_async_remote_copy(
        src, dst, send, recv, device_id={"core": 1 - lax.axis_index("core")}, device_id_type=MESH
    )


def to_zp(src, dst, send, recv):
    return pltpu.make_async_remote_copy(
        src, dst, send, recv, device_id={"zp": 1 - lax.axis_index("zp")}, device_id_type=MESH
    )


def to_swapped(src, dst, send, recv):
    core, zh = lax.axis_index("core"), lax.axis_index("zh")
    return pltpu.make_async_remote_copy(
        src, dst, send, recv, device_id={"core": zh, "zh": core}, device_id_type=MESH
    )


class Exchange:
    def __init__(self, src, pair, sems):
        self.src, self.pair, self.sems = src, pair, sems
        self.core, self.zh = lax.axis_index("core"), lax.axis_index("zh")
        rows = src.shape[0]
        self.mine = pair.at[pl.ds(pl.multiple_of(self.core * rows, rows), rows)]
        self.slots = [pair.at[pl.ds(a * rows, rows)] for a in range(2)]

    def far(self):
        return pltpu.make_async_remote_copy(
            self.src,
            self.mine,
            self.sems.at[0],
            self.sems.at[2 + self.core],
            device_id={"core": self.zh, "zh": 1 - self.zh},
            device_id_type=MESH,
        )

    def near(self):
        return pltpu.make_async_remote_copy(
            self.src,
            self.mine,
            self.sems.at[1],
            self.sems.at[2 + self.core],
            device_id={"core": 1 - self.core},
            device_id_type=MESH,
        )

    def own(self):
        return pltpu.make_async_copy(self.src, self.mine, self.sems.at[2 + self.core])

    def start(self):
        self.far().start()

        @pl.when(self.core == self.zh)
        def _():
            self.own().start()

        @pl.when(self.core != self.zh)
        def _():
            self.near().start()

    def finish(self):
        self.far().wait_send()

        @pl.when(self.core != self.zh)
        def _():
            self.near().wait_send()

        for a in range(2):
            pltpu.make_async_copy(self.src, self.slots[a], self.sems.at[2 + a]).wait()


class Spread:
    def __init__(self, block, gathered, sems):
        self.block, self.gathered, self.sems = block, gathered, sems
        self.length = block.shape[1]
        self.step = 2 * self.length // PARTS

    def src(self, k):
        return self.block.at[k // (PARTS // 2), pl.ds(pl.multiple_of(k % (PARTS // 2) * self.step, self.step), self.step)]

    def dst(self, k, slot):
        return self.gathered.at[
            k // (PARTS // 2),
            pl.ds(
                pl.multiple_of(slot * self.length + k % (PARTS // 2) * self.step, self.step),
                self.step,
            ),
        ]

    def beside(self, k):
        return to_zp(self.src(k), self.dst(k, 1), self.sems.at[0, k], self.sems.at[1, k])

    def across(self, k):
        return to_core(self.src(k), self.dst(k, 2), self.sems.at[2, k], self.sems.at[3, k])

    def corner(self, k):
        return to_core(self.dst(k, 1), self.dst(k, 3), self.sems.at[4, k], self.sems.at[5, k])

    def own(self, k):
        return pltpu.make_async_copy(self.src(k), self.dst(k, 0), self.sems.at[6, k])

    def start(self, k):
        self.beside(k).start()
        self.across(k).start()
        self.own(k).start()

    def relay(self, k):
        self.beside(k).wait_recv()
        self.corner(k).start()

    def finish(self, k):
        self.beside(k).wait_send()
        self.across(k).wait()
        self.corner(k).wait()
        self.own(k).wait()


class Collect:
    def __init__(self, partial, arrived, outgoing, landed, sems):
        self.partial, self.arrived = partial, arrived
        self.outgoing, self.landed, self.sems = outgoing, landed, sems
        self.length = outgoing.shape[1]
        self.step = 2 * self.length // PARTS

    def at(self, ref, k, block):
        return ref.at[
            k // (PARTS // 2),
            pl.ds(
                pl.multiple_of(block * self.length + k % (PARTS // 2) * self.step, self.step),
                self.step,
            ),
        ]

    def crossing(self, k, block):
        return to_core(
            self.at(self.partial, k, 2 + block),
            self.at(self.arrived, k, block),
            self.sems.at[2 * block, k],
            self.sems.at[2 * block + 1, k],
        )

    def landing(self, k):
        return to_zp(
            self.at(self.outgoing, k, 0),
            self.at(self.landed, k, 0),
            self.sems.at[4, k],
            self.sems.at[5, k],
        )

    def start(self):
        for block in (1, 0):
            self.start_block(block)

    def start_block(self, block):
        for k in range(PARTS):
            self.crossing(k, block).start()

    def forward(self, k):
        self.crossing(k, 1).wait_recv()
        self.at(self.outgoing, k, 0)[...] = (
            self.at(self.partial, k, 1)[...].astype(jnp.float32)
            + self.at(self.arrived, k, 1)[...].astype(jnp.float32)
        ).astype(jnp.bfloat16)
        self.landing(k).start()

    def total(self, k):
        self.crossing(k, 0).wait_recv()
        self.landing(k).wait_recv()
        return (
            self.at(self.partial, k, 0)[...].astype(jnp.float32)
            + self.at(self.arrived, k, 0)[...].astype(jnp.float32)
        ) + self.at(self.landed, k, 0)[...].astype(jnp.float32)

    def finish(self, k):
        self.crossing(k, 0).wait_send()
        self.crossing(k, 1).wait_send()
        self.landing(k).wait_send()


class Unpair:
    def __init__(self, part, terms, sems):
        self.part, self.terms, self.sems = part, terms, sems
        self.core, self.zh = lax.axis_index("core"), lax.axis_index("zh")
        self.rows = part.shape[0] // 2

    def piece(self, p):
        return self.part.at[pl.ds(p * self.rows, self.rows)]

    def remote(self, p):
        return pltpu.make_async_remote_copy(
            self.piece(p),
            self.terms.at[self.zh],
            self.sems.at[p],
            self.sems.at[2 + self.zh],
            device_id={"core": p, "zh": self.core},
            device_id_type=MESH,
        )

    def own(self, p):
        return pltpu.make_async_copy(
            self.piece(p), self.terms.at[self.zh], self.sems.at[2 + self.zh]
        )

    def stays(self, p):
        return jnp.logical_and(self.core == p, self.zh == p)

    def start(self):
        for p in range(2):

            @pl.when(self.stays(p))
            def _(p=p):
                self.own(p).start()

            @pl.when(jnp.logical_not(self.stays(p)))
            def _(p=p):
                self.remote(p).start()

    def finish(self):
        for p in range(2):

            @pl.when(jnp.logical_not(self.stays(p)))
            def _(p=p):
                self.remote(p).wait_send()

            pltpu.make_async_copy(
                self.piece(p), self.terms.at[p], self.sems.at[2 + p]
            ).wait()


class Swap:
    def __init__(self, block, target, sems):
        self.block, self.target, self.sems = block, target, sems
        self.swaps = lax.axis_index("core") != lax.axis_index("zh")
        self.step = 2 * block.shape[1] // PARTS

    def at(self, ref, k):
        return ref.at[
            k // (PARTS // 2), pl.ds(pl.multiple_of(k % (PARTS // 2) * self.step, self.step), self.step)
        ]

    def remote(self, k):
        return to_swapped(
            self.at(self.block, k), self.at(self.target, k), self.sems.at[0, k], self.sems.at[1, k]
        )

    def own(self, k):
        return pltpu.make_async_copy(self.at(self.block, k), self.at(self.target, k), self.sems.at[1, k])

    def start(self, k):
        @pl.when(self.swaps)
        def _():
            self.remote(k).start()

        @pl.when(jnp.logical_not(self.swaps))
        def _():
            self.own(k).start()

    def arrive(self, k):
        self.own(k).wait()

    def finish(self, k):
        @pl.when(self.swaps)
        def _():
            self.remote(k).wait_send()


def each(body):
    lax.fori_loop(0, PARTS, lambda k, carry: (body(k), carry)[1], 0)


class Moves:
    def __init__(self, loads, stores):
        self.loads, self.stores, self.waited, self.going = loads, stores, set(), []

    def start(self, *names):
        for name in names:
            if name in self.loads:
                self.loads[name].start()

    def ready(self, *names):
        for name in names:
            if name in self.loads and name not in self.waited:
                self.waited.add(name)
                self.loads[name].wait()

    def store(self, *names):
        for name in names:
            if name in self.stores:
                self.stores[name].start()
                self.going.append(name)

    def end(self):
        for name in self.going:
            self.stores[name].wait()


def kernel_call(number, name, inputs, outs, scratch, body, lazy=(), eager=()):
    lazy = [key for key in lazy if key in inputs]
    eager = [key for key in eager if key in outs]
    scratch = dict(scratch)
    for key in lazy:
        scratch["lazy_" + key] = pltpu.VMEM(inputs[key].shape, inputs[key].dtype)
    for key in eager:
        scratch["eager_" + key] = pltpu.VMEM(outs[key][0].shape, outs[key][0].dtype)
    scratch["move_sems"] = pltpu.SemaphoreType.DMA((max(1, len(lazy) + len(eager)),))
    names = list(inputs) + list(outs) + list(scratch)

    def kernel(*given):
        refs = dict(zip(names, given))
        sems = refs["move_sems"]
        loads, stores = {}, {}
        for number, key in enumerate(lazy):
            here = refs["lazy_" + key]
            loads[key] = pltpu.make_async_copy(refs[key], here, sems.at[number])
            refs[key] = here
        for number, key in enumerate(eager):
            here = refs["eager_" + key]
            stores[key] = pltpu.make_async_copy(here, refs[key], sems.at[len(lazy) + number])
            refs[key] = here
        body(refs, Moves(loads, stores))

    results = pl.pallas_call(
        kernel,
        out_shape=tuple(shape for shape, _ in outs.values()),
        in_specs=[ANY if key in lazy else VMEM for key in inputs],
        out_specs=tuple(ANY if key in eager else spec for key, (_, spec) in outs.items()),
        scratch_shapes=list(scratch.values()),
        compiler_params=pltpu.CompilerParams(
            collective_id=number,
            has_side_effects=number is not None,
            vmem_limit_bytes=61 * 1024 * 1024,
        ),
        name=name,
    )(*inputs.values())
    return dict(zip(outs, results))


def collect_scratch(tag, rows, length, width):
    return {
        tag + "arrived": pltpu.VMEM((rows, 2 * length, width), jnp.bfloat16),
        tag + "outgoing": pltpu.VMEM((rows, length, width), jnp.bfloat16),
        tag + "landed": pltpu.VMEM((rows, length, width), jnp.bfloat16),
        tag + "collect_sems": pltpu.SemaphoreType.DMA((6, PARTS)),
    }


def collect_of(refs, tag, partial):
    return Collect(
        refs[partial],
        refs[tag + "arrived"],
        refs[tag + "outgoing"],
        refs[tag + "landed"],
        refs[tag + "collect_sems"],
    )


def shape_of(shape, dtype):
    return jax.ShapeDtypeStruct(shape, dtype)


def gathered_out(rows, length, width):
    return (shape_of((rows, 4 * length, width), jnp.bfloat16), ANY)


def pair_out(shard):
    return (shape_of((2 * shard.shape[0], shard.shape[1]), shard.dtype), ANY)


def terms_out(part):
    return (shape_of((2, part.shape[0] // 2, part.shape[1]), part.dtype), ANY)


class PlaneGather:
    def __init__(self, whole, columns, sems):
        self.whole, self.columns, self.sems = whole, columns, sems
        self.rows = whole.shape[0] // 4

    def half(self, chip, which):
        start, size = self.columns
        return self.whole.at[
            pl.ds(pl.multiple_of(chip * self.rows, self.rows), self.rows),
            pl.ds(start + which * (size // 2), size // 2),
        ]

    def own(self, axis, which):
        ref = self.half(lax.axis_index("chip"), which)
        return self.copy(ref, axis, 2 * axis + which)

    def passed(self, which):
        ref = self.half(across_plane(which), which)
        return self.copy(ref, 1 - which, 4 + which)

    def copy(self, ref, axis, number):
        return pltpu.make_async_remote_copy(
            ref,
            ref,
            self.sems.at[0, number],
            self.sems.at[1, number],
            device_id={"chip": across_plane(axis)},
            device_id_type=MESH,
        )

    def start(self):
        for axis in range(2):
            self.own(axis, axis).start()
        for axis in range(2):
            self.own(axis, 1 - axis).start()

    def relay(self):
        for which in range(2):
            self.own(which, which).wait_recv()
            self.passed(which).start()

    def finish(self):
        for axis in range(2):
            self.own(axis, axis).wait_send()
            self.own(axis, 1 - axis).wait()
            self.passed(axis).wait()


class SwapWhole:
    def __init__(self, array, target, sems):
        self.array, self.target, self.sems = array, target, sems
        self.swaps = lax.axis_index("core") != lax.axis_index("zh")

    def remote(self):
        return to_swapped(self.array, self.target, self.sems.at[0], self.sems.at[1])

    def own(self):
        return pltpu.make_async_copy(self.array, self.target, self.sems.at[1])

    def start(self):
        @pl.when(self.swaps)
        def _():
            self.remote().start()

        @pl.when(jnp.logical_not(self.swaps))
        def _():
            self.own().start()

    def finish(self):
        self.own().wait()

        @pl.when(self.swaps)
        def _():
            self.remote().wait_send()


class GainGather:
    def __init__(self, own, slots, whole, sems):
        self.own, self.slots, self.whole, self.sems = own, slots, whole, sems
        self.chips = lax.axis_size("chip")
        self.chip, self.core = lax.axis_index("chip"), lax.axis_index("core")

    def others(self):
        for number in range(1, 2 * self.chips):
            yield number, (self.chip + number // 2) % self.chips, (self.core + number % 2) % 2

    def send(self, number, chip, core):
        return pltpu.make_async_remote_copy(
            self.own,
            self.slots.at[self.chip * 2 + self.core],
            self.sems.at[0, number],
            self.sems.at[1, self.chip * 2 + self.core],
            device_id={"chip": chip, "core": core},
            device_id_type=MESH,
        )

    def start(self):
        for other in self.others():
            self.send(*other).start()
        self.slots.at[self.chip * 2 + self.core][...] = self.own[...]

    def finish(self):
        for number, chip, core in self.others():
            self.send(number, chip, core).wait_send()
            place = chip * 2 + core
            pltpu.make_async_copy(self.own, self.slots.at[place], self.sems.at[1, place]).wait()
        held = self.own.shape[1]
        for place in range(2 * self.chips):
            self.whole[:, place * held : (place + 1) * held] = self.slots[place]


def head(number, block, beside, marks, gains, first, second):
    rows, length, width = block.shape
    depth, size = first[0].shape
    chips = lax.axis_size("chip")
    in_plane = chips == 4
    if not in_plane:
        gains = lax.all_gather(gains, ("chip", "core"), axis=1, tiled=True)

    def body(refs, moves):
        swap = Swap(refs["block"], refs["here"], refs["swap_sems"])
        marks_swap = SwapWhole(refs["marks"], refs["marks_here"], refs["marks_sems"])
        spread_work = Spread(refs["normed"], refs["gathered"], refs["spread_sems"])
        if in_plane:
            chip = lax.axis_index("chip")
            place = refs["whole"].at[pl.ds(pl.multiple_of(chip * 2 * depth, 2 * depth), 2 * depth)]
            gain_work = GainGather(
                refs["gains"], refs["gain_slots"], refs["gains_whole"], refs["gain_sems"]
            )
        else:
            place = refs["whole"]
        works = [
            Exchange(
                refs["first%d" % i],
                place.at[:, pl.ds(i * size, size)],
                refs["exchange_sems"].at[i],
            )
            for i in range(len(first))
        ]
        beside_swap = Swap(refs["beside"], refs["beside_here"], refs["beside_swap_sems"])
        beside_work = Spread(refs["beside_here"], refs["beside_gathered"], refs["beside_sems"])
        later = [
            Exchange(
                refs["second%d" % i],
                refs["pair"].at[:, pl.ds(i * size, size)],
                refs["exchange_sems"].at[len(first) + i],
            )
            for i in range(len(second))
        ]
        greet(True, in_plane)
        marks_swap.start()

        def norm_and_send(k):
            swap.arrive(k)
            values = swap.at(refs["here"], k)[...].astype(jnp.float32)
            spread_work.src(k)[...] = normalize(values, refs["gains_whole"][0:1, :]).astype(
                jnp.bfloat16
            )
            spread_work.start(k)

        planes = [
            PlaneGather(refs["whole"], (i * size, size), refs["plane_sems"].at[i])
            for i in range(len(first))
        ]
        last = len(works) - 1
        works[0].start()
        if in_plane:
            gain_work.start()
            gain_work.finish()
        else:
            refs["gains_whole"][...] = refs["gains"][...]
        for i, work in enumerate(works):
            work.finish()
            if in_plane:
                planes[i].start()
            if i < last:
                works[i + 1].start()
            if i == 0:
                each(swap.start)
            if i == last - 1:
                each(beside_swap.start)
            if in_plane and i:
                planes[i - 1].relay()
            if i == 1:
                each(norm_and_send)
            if i == last:
                each(spread_work.relay)

        def pass_on(k):
            beside_swap.arrive(k)
            beside_work.start(k)

        later[0].start()
        pass_on(0)
        pass_on(1)
        if in_plane:
            planes[last].relay()
        for k in range(2, PARTS):
            pass_on(k)
        for i, work in enumerate(later):
            if i + 1 < len(later):
                later[i + 1].start()
            if i == 1:
                each(beside_work.relay)
            work.finish()
        each(beside_work.finish)
        each(beside_swap.finish)
        each(spread_work.finish)
        each(swap.finish)
        if in_plane:
            for plane in planes:
                plane.finish()
        marks_swap.finish()

    whole_rows = 8 * depth if in_plane else 2 * depth
    results = kernel_call(
        number,
        "head",
        {
            "block": block,
            "beside": beside,
            "marks": marks,
            "gains": gains,
            **{"first%d" % i: shard for i, shard in enumerate(first)},
            **{"second%d" % i: shard for i, shard in enumerate(second)},
        },
        {
            "here": (shape_of(block.shape, block.dtype), VMEM),
            "marks_here": (shape_of(marks.shape, marks.dtype), VMEM),
            "gains_whole": (shape_of((gains.shape[0], width), jnp.float32), VMEM),
            "gathered": gathered_out(rows, length, width),
            "whole": (shape_of((whole_rows, len(first) * size), jnp.bfloat16), ANY),
            "beside_gathered": gathered_out(rows, length, width),
            "pair": (shape_of((2 * depth, len(second) * size), jnp.bfloat16), ANY),
        },
        {
            "normed": pltpu.VMEM((rows, length, width), jnp.bfloat16),
            "spread_sems": pltpu.SemaphoreType.DMA((7, PARTS)),
            "swap_sems": pltpu.SemaphoreType.DMA((2, PARTS)),
            "beside_here": pltpu.VMEM((rows, length, width), jnp.bfloat16),
            "beside_sems": pltpu.SemaphoreType.DMA((7, PARTS)),
            "beside_swap_sems": pltpu.SemaphoreType.DMA((2, PARTS)),
            "marks_sems": pltpu.SemaphoreType.DMA((2,)),
            "exchange_sems": pltpu.SemaphoreType.DMA((len(first) + len(second), 4)),
            "plane_sems": pltpu.SemaphoreType.DMA((len(first), 2, 6)),
            "gain_slots": pltpu.VMEM((2 * chips,) + gains.shape, jnp.float32),
            "gain_sems": pltpu.SemaphoreType.DMA((2, 2 * chips)),
        },
        body,
    )
    whole = results["whole"] if in_plane else gather_chips(results["whole"])
    return (
        results["here"],
        results["marks_here"],
        results["gains_whole"],
        results["gathered"],
        results["beside_gathered"],
        whole,
        results["pair"],
    )


class WeightGradFill:
    def __init__(self, tag, left, right):
        self.tag = tag
        depth, columns = left.shape[1], right.shape[1]
        self.size = 256
        self.tiles = depth // self.size
        self.inputs = {tag + "left": left, tag + "right": right}
        self.outs = {tag + "out": (shape_of((depth, columns), jnp.bfloat16), ANY)}
        self.scratch = {
            tag + "stage": pltpu.VMEM((2, self.size, columns), jnp.bfloat16),
            tag + "sems": pltpu.SemaphoreType.DMA((2,)),
        }

    def at(self, i):
        return pl.ds(pl.multiple_of(i * self.size, self.size), self.size)

    def copy(self, refs, i):
        return pltpu.make_async_copy(
            refs[self.tag + "stage"].at[i % 2],
            refs[self.tag + "out"].at[self.at(i)],
            refs[self.tag + "sems"].at[i % 2],
        )

    def tile(self, refs, i):
        @pl.when(i >= 2)
        def _():
            self.copy(refs, i - 2).wait()

        refs[self.tag + "stage"].at[i % 2][...] = down(
            refs[self.tag + "left"].at[:, self.at(i)][...], refs[self.tag + "right"][...]
        ).astype(jnp.bfloat16)
        self.copy(refs, i).start()

    def end(self, refs):
        for i in (self.tiles - 2, self.tiles - 1):
            self.copy(refs, i).wait()


class ProductFill:
    def __init__(self, tag, left, right, columns):
        self.tag, self.columns = tag, columns
        rows = left.shape[0]
        self.size = 256
        self.tiles = rows // self.size
        self.inputs = {tag + "left": left, tag + "right": right}
        self.outs = {tag + "out": (shape_of((rows, right.shape[0]), jnp.bfloat16), VMEM)}
        self.scratch = {}

    def tile(self, refs, i):
        at = pl.ds(pl.multiple_of(i * self.size, self.size), self.size)
        start, width = self.columns
        refs[self.tag + "out"].at[at][...] = across(
            refs[self.tag + "left"].at[at][...],
            refs[self.tag + "right"].at[:, pl.ds(start, width)][...],
        ).astype(jnp.bfloat16)

    def end(self, refs):
        pass


def fill_in(refs, fill, part, parts):
    if fill is not None:
        first, last = fill.tiles * part // parts, fill.tiles * (part + 1) // parts
        lax.fori_loop(first, last, lambda i, carry: (fill.tile(refs, i), carry)[1], 0)


def norm_slope(values, gain, gradient):
    factor = lax.rsqrt(jnp.mean(values * values, axis=-1, keepdims=True) + epsilon)
    scaled = gain * gradient
    inner = jnp.mean(scaled * values, axis=-1, keepdims=True)
    return factor * scaled - values * (factor * factor * factor * inner), gradient * values * factor


def turn_back(number, partial, values, stream, gain, fills, *parts):
    rows, length, width = values.shape
    first, second = (tuple(fills) + (None, None))[:2]

    def body(refs, moves):
        collect_work = collect_of(refs, "", "partial")
        spread_work = Spread(refs["branch"], refs["gathered"], refs["spread_sems"])
        works = [
            Unpair(refs["part%d" % i], refs["terms%d" % i], refs["unpair_sems"].at[i])
            for i in range(len(parts))
        ]
        part_names = ["part%d" % i for i in range(len(parts))]
        fill_names = [[*fill.inputs] for fill in fills]
        moves.start(*part_names, "partial", "values", "stream", *sum(fill_names, []))
        greet(bool(parts))
        moves.ready(*part_names)
        for work in works:
            work.start()
        moves.ready("partial")
        collect_work.start()
        each(collect_work.forward)
        refs["gain_sum"][...] = jnp.zeros_like(refs["gain_sum"])

        def slope_and_send(k):
            slope, terms = norm_slope(
                collect_work.at(refs["values"], k, 0)[...].astype(jnp.float32),
                refs["gain"][...],
                collect_work.total(k),
            )
            sums = collect_work.at(refs["stream"], k, 0)[...].astype(jnp.float32) + slope
            collect_work.at(refs["after"], k, 0)[...] = sums
            spread_work.src(k)[...] = sums.astype(jnp.bfloat16)
            spread_work.start(k)
            refs["gain_sum"][...] += jnp.sum(terms, axis=0, keepdims=True)

        moves.ready("values", "stream")
        moves.ready(*sum(fill_names[:1], []))
        if first is None:
            each(slope_and_send)
        else:
            for k in range(PARTS):
                fill_in(refs, first, k, PARTS)
                slope_and_send(k)
        moves.store("after")
        for fill in fills[:1]:
            moves.store(*fill.outs)
        moves.ready(*sum(fill_names[1:], []))
        fill_in(refs, second, 0, 1)
        for fill in fills[1:]:
            moves.store(*fill.outs)
        each(spread_work.relay)
        each(spread_work.finish)
        each(collect_work.finish)
        for work in works:
            work.finish()
        for fill in fills:
            fill.end(refs)
        moves.end()

    extra = {"inputs": {}, "outs": {}, "scratch": {}}
    for fill in fills:
        for kind, found in extra.items():
            found.update(getattr(fill, kind))
    results = kernel_call(
        number,
        "turn_back",
        {
            "partial": partial,
            "values": values,
            "stream": stream,
            "gain": gain[None],
            **{"part%d" % i: part for i, part in enumerate(parts)},
            **extra["inputs"],
        },
        {
            "after": (shape_of(values.shape, jnp.float32), VMEM),
            "gathered": gathered_out(rows, length, width),
            "gain_sum": (shape_of((1, width), jnp.float32), VMEM),
            **{"terms%d" % i: terms_out(part) for i, part in enumerate(parts)},
            **extra["outs"],
        },
        {
            **collect_scratch("", rows, length, width),
            "branch": pltpu.VMEM((rows, length, width), jnp.bfloat16),
            "spread_sems": pltpu.SemaphoreType.DMA((7, PARTS)),
            "unpair_sems": pltpu.SemaphoreType.DMA((max(1, len(parts)), 4)),
            **extra["scratch"],
        },
        body,
        lazy=("partial", "values", "stream")
        + tuple("part%d" % i for i in range(len(parts)))
        + tuple(extra["inputs"]),
        eager=("after",)
        + tuple(name for name, (_, spec) in extra["outs"].items() if spec is VMEM),
    )
    return (
        (results["after"], results["gathered"], results["gain_sum"])
        + tuple(results["terms%d" % i] for i in range(len(parts)))
        + tuple(results[name] for fill in fills for name in fill.outs)
    )


class OutWork:
    def __init__(self, collect_work, swap, base):
        self.collect_work, self.swap, self.base = collect_work, swap, base

    def begin(self):
        self.collect_work.start()

    def forward(self):
        each(self.collect_work.forward)

    def leave_part(self, k):
        total = self.collect_work.total(k)
        if self.base is not None:
            total = total + self.swap.at(self.base, k)[...]
        self.swap.at(self.swap.block, k)[...] = total.astype(jnp.bfloat16)
        self.swap.start(k)

    def end(self):
        each(self.swap.arrive)
        each(self.swap.finish)
        each(self.collect_work.finish)


def head_at(ref, r, h, offset):
    return ref.at[r, :, pl.ds(pl.multiple_of(offset + h * HD, HD), HD)]


def across(left, right):
    return lax.dot_general(
        left, right, (((1,), (1,)), ((), ())), preferred_element_type=jnp.float32
    )


def down(left, right):
    return lax.dot_general(
        left, right, (((0,), (0,)), ((), ())), preferred_element_type=jnp.float32
    )


def masked_probability(refs, r, queries, key_rows):
    scores = across(queries, key_rows) * HD ** (-0.5)
    allowed = jnp.logical_and(
        refs["query_mark"][r] == refs["key_mark"][r],
        refs["query_place"][...] >= refs["key_place"][...],
    )
    scores = jnp.where(allowed, scores, masked_value)
    shifted = jnp.exp(scores - jnp.max(scores, axis=-1, keepdims=True))
    return shifted / jnp.sum(shifted, axis=-1, keepdims=True)


def rows_of(ref, t, size):
    per_row = ref.shape[1] // size
    return ref.at[t // per_row, pl.ds(pl.multiple_of(t % per_row * size, size), size)]


def attention_back(
    number, branch, weights, places, queries, pairs, marks, lefts, attended, out, part
):
    query_place, pair_place, out_place = places
    (query_array, query_at), (pair_array, pair_at) = queries, pairs
    same = query_array is pair_array
    rows, length, width = branch.shape
    wide = weights.shape[1] // 4
    heads = wide // HD
    block = (rows, length // 4, width)
    flat = (rows * length, width)
    inputs = {
        "branch": branch,
        "weights": weights,
        "queries": query_array,
        "query_mark": marks[0],
        "key_mark": marks[1],
        "query_place": marks[2],
        "key_place": marks[3],
        "left0": lefts[0].reshape(flat),
        "part": part,
    }
    if not same:
        inputs["pairs"] = pair_array
        inputs["left1"] = lefts[1].reshape(flat)
    if attended is not None:
        inputs["attended"] = attended.reshape(rows * length, wide)
    if out is not None:
        inputs["partial"] = out[0]
        if out[1] is not None:
            inputs["base"] = out[1]
    grad_columns = wide * (4 if attended is not None else 3)
    outs = {
        "input_partial": (shape_of((rows, length, width), jnp.bfloat16), VMEM),
        "weight_grads": (shape_of((width, grad_columns), jnp.bfloat16), ANY),
        "terms": terms_out(part),
    }
    scratch = {
        "grad_out": pltpu.VMEM((rows, length, wide), jnp.bfloat16),
        "stage": pltpu.VMEM((2, 256, grad_columns), jnp.bfloat16),
        "stage_sems": pltpu.SemaphoreType.DMA((2,)),
        "unpair_sems": pltpu.SemaphoreType.DMA((4,)),
    }
    if out is not None:
        outs["out"] = (shape_of(block, jnp.bfloat16), ANY)
        scratch.update(collect_scratch("", *block))
        scratch["leaving"] = pltpu.VMEM(block, jnp.bfloat16)
        scratch["swap_sems"] = pltpu.SemaphoreType.DMA((2, PARTS))
    if same:
        scratch["grad_all"] = pltpu.VMEM((rows, length, 3 * wide), jnp.bfloat16)
    else:
        scratch["grad_queries"] = pltpu.VMEM((rows, length, wide), jnp.bfloat16)
        outs["grad_pairs"] = (shape_of((rows, length, 2 * wide), jnp.bfloat16), VMEM)
    scale = HD ** (-0.5)
    total = rows * heads
    size = 256

    def body(refs, moves):
        unpair = Unpair(refs["part"], refs["terms"], refs["unpair_sems"])
        out_work = None
        if out is not None:
            out_work = OutWork(
                collect_of(refs, "", "partial"),
                Swap(refs["leaving"], refs["out"], refs["swap_sems"]),
                refs.get("base"),
            )
        grad_queries = refs["grad_all"] if same else refs["grad_queries"]
        grad_pairs = refs["grad_all"] if same else refs["grad_pairs"]
        pair_refs = refs["queries"] if same else refs["pairs"]
        pair_out = wide if same else 0

        def form_grad_out(t):
            rows_of(refs["grad_out"], t, size)[...] = jnp.dot(
                rows_of(refs["branch"], t, size)[...],
                refs["weights"].at[:, pl.ds(out_place, wide)][...],
                preferred_element_type=jnp.float32,
            ).astype(jnp.bfloat16)

        def one(i):
            r, h = i // heads, i % heads
            queries_here = head_at(refs["queries"], r, h, query_at)[...]
            key_rows = head_at(pair_refs, r, h, pair_at)[...]
            value_rows = head_at(pair_refs, r, h, pair_at + wide)[...]
            grad_here = head_at(refs["grad_out"], r, h, 0)[...]
            probability = masked_probability(refs, r, queries_here, key_rows)
            grad_values = down(probability.astype(jnp.bfloat16), grad_here)
            grad_probs = across(grad_here, value_rows)
            inner = jnp.sum(probability * grad_probs, axis=-1, keepdims=True)
            grad_scores = (probability * (grad_probs - inner)).astype(jnp.bfloat16)
            query_terms = jnp.dot(grad_scores, key_rows, preferred_element_type=jnp.float32)
            key_terms = down(grad_scores, queries_here)
            head_at(grad_queries, r, h, 0)[...] = (query_terms * scale).astype(jnp.bfloat16)
            head_at(grad_pairs, r, h, pair_out)[...] = (key_terms * scale).astype(jnp.bfloat16)
            head_at(grad_pairs, r, h, pair_out + wide)[...] = grad_values.astype(jnp.bfloat16)

        def form_partial(t):
            columns = (query_place, 3 * wide if same else wide)
            rows_of(refs["input_partial"], t, size)[...] = across(
                rows_of(grad_queries, t, size)[...],
                refs["weights"].at[:, pl.ds(*columns)][...],
            ).astype(jnp.bfloat16)

        def written(i):
            return pltpu.make_async_copy(
                refs["stage"].at[i % 2],
                refs["weight_grads"].at[pl.ds(pl.multiple_of(i * size, size), size)],
                refs["stage_sems"].at[i % 2],
            )

        def form_grads(i):
            @pl.when(i >= 2)
            def _():
                written(i - 2).wait()

            at = pl.ds(pl.multiple_of(i * size, size), size)
            stage = refs["stage"].at[i % 2]

            def put(place, left, right):
                terms = right[...].reshape(rows * length, right.shape[-1])
                stage[:, place : place + right.shape[-1]] = down(left, terms).astype(jnp.bfloat16)

            put(query_place, refs["left0"].at[:, at][...], grad_queries)
            if not same:
                put(pair_place, refs["left1"].at[:, at][...], grad_pairs)
            if attended is not None:
                here = refs["branch"].at[:, :, at][...].reshape(rows * length, size)
                stage[:, out_place : out_place + wide] = down(here, refs["attended"][...]).astype(
                    jnp.bfloat16
                )
            written(i).start()

        def loop(count, work, stops=()):
            def step(i, carry):
                work(i)
                if out_work is not None:
                    for stop, k in stops:

                        @pl.when(i == stop)
                        def _(k=k):
                            out_work.leave_part(k)

                return carry

            lax.fori_loop(0, count, step, 0)

        moves.start("part", "partial", "branch", "weights", "queries", "pairs", "base")
        moves.start("left0", "left1", "attended")
        greet(True)
        moves.ready("part")
        unpair.start()
        moves.ready("partial")
        if out_work is not None:
            out_work.begin()
        moves.ready("branch", "weights")
        loop(rows * length // size, form_grad_out)
        if out_work is not None:
            out_work.forward()
        moves.ready("queries", "pairs", "base")
        loop(total, one, ((total - 1, 0),))
        moves.store("grad_pairs")
        moves.ready("left0", "left1", "attended")
        loop(width // size, form_grads, ((1, 1), (3, 2), (5, 3)))
        loop(rows * length // size, form_partial)
        moves.store("input_partial")
        if out_work is not None:
            out_work.end()
        unpair.finish()
        for i in (width // size - 2, width // size - 1):
            written(i).wait()
        moves.end()

    big = ("part", "partial", "branch", "weights", "queries", "pairs", "base")
    results = kernel_call(
        number,
        "attention_back",
        inputs,
        outs,
        scratch,
        body,
        lazy=big + ("left0", "left1", "attended"),
        eager=("grad_pairs", "input_partial"),
    )
    return (
        results["input_partial"],
        results["weight_grads"],
        results["terms"],
        results.get("grad_pairs"),
        results.get("out"),
    )


def attention_turn(number, lefts, weights, places, marks, stream, gain, done=None, beside=None):
    query_place, pair_place, out_place = places
    same = lefts[0] is lefts[1]
    rows, length, width = lefts[0].shape
    wide = weights.shape[1] // 4
    heads = wide // HD
    quarter = length // 4
    size = 256
    inputs = {"weights": weights}
    outs, scratch = {}, {}
    if done is None:
        inputs.update(
            {
                "left0": lefts[0],
                "query_mark": marks[0],
                "key_mark": marks[1],
                "query_place": marks[2],
                "key_place": marks[3],
            }
        )
        outs["queries"] = (
            shape_of((rows, length, wide * (3 if same else 1)), jnp.bfloat16),
            VMEM,
        )
        outs["attended"] = (shape_of((rows, length, wide), jnp.bfloat16), VMEM)
        if not same:
            inputs["left1"] = lefts[1]
            outs["pairs"] = (shape_of((rows, length, 2 * wide), jnp.bfloat16), VMEM)
    else:
        inputs["attended"] = done
    if stream is not None:
        inputs["stream"] = stream
        inputs["gain"] = gain[None]
        outs["after"] = (shape_of(stream.shape, jnp.float32), VMEM)
        outs["gathered"] = gathered_out(rows, quarter, width)
        scratch.update(
            {
                **collect_scratch("", rows, quarter, width),
                "partial": pltpu.VMEM((rows, length, width), jnp.bfloat16),
                "normed": pltpu.VMEM((rows, quarter, width), jnp.bfloat16),
                "spread_sems": pltpu.SemaphoreType.DMA((7, PARTS)),
            }
        )
    if beside is not None:
        inputs["beside"] = beside
        outs["beside_gathered"] = gathered_out(rows, quarter, width)
        outs["beside_here"] = (shape_of((rows, quarter, width), jnp.bfloat16), VMEM)
        scratch["beside_sems"] = pltpu.SemaphoreType.DMA((7, PARTS))
        scratch["beside_swap_sems"] = pltpu.SemaphoreType.DMA((2, PARTS))

    def body(refs, moves):
        if stream is not None:
            collect_work = collect_of(refs, "", "partial")
            spread_work = Spread(refs["normed"], refs["gathered"], refs["spread_sems"])
        if beside is not None:
            swap = Swap(refs["beside"], refs["beside_here"], refs["beside_swap_sems"])
            beside_work = Spread(
                refs["beside_here"], refs["beside_gathered"], refs["beside_sems"]
            )
        if done is None:
            pair_refs = refs["queries"] if same else refs["pairs"]
        pair_at = wide if same else 0

        def loop(count, work):
            lax.fori_loop(0, count, lambda i, carry: (work(i), carry)[1], 0)

        def form(left, place, columns, target):
            def tile(t):
                rows_of(target, t, size)[...] = jnp.dot(
                    rows_of(left, t, size)[...],
                    refs["weights"].at[:, pl.ds(place, columns)][...],
                    preferred_element_type=jnp.float32,
                ).astype(jnp.bfloat16)

            loop(rows * length // size, tile)

        def one(i):
            r, h = i // heads, i % heads
            probability = masked_probability(
                refs,
                r,
                head_at(refs["queries"], r, h, 0)[...],
                head_at(pair_refs, r, h, pair_at)[...],
            ).astype(jnp.bfloat16)
            head_at(refs["attended"], r, h, 0)[...] = jnp.dot(
                probability,
                head_at(pair_refs, r, h, pair_at + wide)[...],
                preferred_element_type=jnp.float32,
            ).astype(jnp.bfloat16)

        def form_block(block):
            def tile(r):
                at = pl.ds(block * quarter, quarter)
                refs["partial"].at[r, at][...] = across(
                    refs["attended"].at[r, at][...],
                    refs["weights"].at[:, pl.ds(out_place, wide)][...],
                ).astype(jnp.bfloat16)

            loop(rows, tile)

        def norm_and_send(k):
            values = collect_work.at(refs["stream"], k, 0)[...].astype(
                jnp.float32
            ) + collect_work.total(k)
            collect_work.at(refs["after"], k, 0)[...] = values
            spread_work.src(k)[...] = normalize(values, refs["gain"][...]).astype(jnp.bfloat16)
            spread_work.start(k)

        def pass_on(first, last):
            if beside is not None:
                for k in range(first, last):
                    swap.arrive(k)
                    beside_work.start(k)

        moves.start("beside", "left1", "weights", "left0", "attended", "stream")
        if number is not None:
            greet(beside is not None)
        moves.ready("beside")
        if beside is not None:
            each(swap.start)
        moves.ready("left1", "weights")
        if done is None:
            if same:
                moves.ready("left0")
                form(refs["left0"], query_place, 3 * wide, refs["queries"])
            else:
                form(refs["left1"], pair_place, 2 * wide, refs["pairs"])
                pass_on(0, 1)
                moves.ready("left0")
                form(refs["left0"], query_place, wide, refs["queries"])
            pass_on(0 if same else 1, 2)
            moves.store("queries", "pairs")
            loop(rows * heads, one)
            moves.store("attended")
        pass_on(0 if done is not None else 2, PARTS)
        moves.store("beside_here")
        moves.ready("attended", "stream")
        if stream is not None:
            for block in (3, 2):
                form_block(block)
                collect_work.start_block(block - 2)
            form_block(1)
            each(collect_work.forward)
            form_block(0)
            if beside is not None:
                each(beside_work.relay)
            each(norm_and_send)
            moves.store("after")
            each(spread_work.relay)
            each(spread_work.finish)
            each(collect_work.finish)
        elif beside is not None:
            each(beside_work.relay)
        if beside is not None:
            each(beside_work.finish)
            each(swap.finish)
        moves.end()

    results = kernel_call(
        number,
        "attention_turn",
        inputs,
        outs,
        scratch,
        body,
        lazy=("beside", "left1", "weights", "left0", "attended", "stream"),
        eager=("queries", "pairs", "attended", "after", "beside_here"),
    )
    return tuple(
        results.get(name)
        for name in (
            "queries",
            "pairs",
            "attended",
            "after",
            "gathered",
            "beside_here",
            "beside_gathered",
        )
    )


class PlaneScatter:
    def __init__(self, grads, columns, taken, passing, crossed, part, sems):
        self.grads, self.columns, self.taken, self.passing = grads, columns, taken, passing
        self.crossed, self.part, self.sems = crossed, part, sems
        self.rows = grads.shape[0] // 4
        self.me = lax.axis_index("chip")

    def terms(self, chip, which):
        start, size = self.columns
        return self.grads.at[
            pl.ds(pl.multiple_of(chip * self.rows, self.rows), self.rows),
            pl.ds(start + which * (size // 2), size // 2),
        ]

    def copy(self, src, dst, axis, number):
        return pltpu.make_async_remote_copy(
            src,
            dst,
            self.sems.at[0, number],
            self.sems.at[1, number],
            device_id={"chip": across_plane(axis)},
            device_id_type=MESH,
        )

    def first(self, which, block):
        chip = 3 - self.me if block else across_plane(which)
        return self.copy(
            self.terms(chip, which), self.taken.at[which, block], which, 2 * which + block
        )

    def second(self, which):
        return self.copy(
            self.passing.at[which], self.crossed.at[which], 1 - which, 4 + which
        )

    def start(self):
        for block in (1, 0):
            for which in range(2):
                self.first(which, block).start()

    def pass_on(self, following):
        for which in range(2):
            self.first(which, 1).wait_recv()
        if following is not None:
            following.start()
        for which in range(2):
            self.passing.at[which][...] = (
                self.terms(across_plane(1 - which), which)[...].astype(jnp.float32)
                + self.taken.at[which, 1][...].astype(jnp.float32)
            ).astype(jnp.bfloat16)
            self.second(which).start()

    def total(self):
        half = self.columns[1] // 2
        for which in range(2):
            self.first(which, 0).wait_recv()
            self.second(which).wait_recv()
            self.part.at[:, pl.ds(which * half, half)][...] = (
                self.terms(self.me, which)[...].astype(jnp.float32)
                + self.taken.at[which, 0][...].astype(jnp.float32)
                + self.crossed.at[which][...].astype(jnp.float32)
            ).astype(jnp.bfloat16)

    def finish(self):
        for which in range(2):
            for block in range(2):
                self.first(which, block).wait_send()
            self.second(which).wait_send()


def sum_everywhere(given, taken, sems, totals):
    chips = lax.axis_size("chip")
    core, zh, zp, chip = (lax.axis_index(axis) for axis in ("core", "zh", "zp", "chip"))
    partners = [{"core": 1 - core}, {"zp": 1 - zp}, {"zh": 1 - zh}]
    for bit in range(chips.bit_length() - 1):
        size = 2**bit
        partners.append({"chip": chip + size - 2 * size * (chip // size % 2)})
    sums = given[0]
    for step, partner in enumerate(partners):
        if step:
            given[step] = sums
        copy = pltpu.make_async_remote_copy(
            given.at[step],
            taken.at[step],
            sems.at[0, step],
            sems.at[1, step],
            device_id=partner,
            device_id_type=MESH,
        )
        copy.start()
        copy.wait()
        sums = sums + taken[step]
    totals[...] = sums


def leave(number, partial, values, stream, gain, gain_sums, grads, part):
    rows, length, width = values.shape
    chips = lax.axis_size("chip")
    in_plane = chips == 4
    steps = 3 + chips.bit_length() - 1
    if not in_plane:
        grads = scatter_chips(grads)
    owned = grads.shape[0] // (4 if in_plane else 1)
    columns = grads.shape[1]
    size = 512
    pieces = columns // size if in_plane else 0

    def body(refs, moves):
        collect_work = collect_of(refs, "", "partial")
        swap = Swap(refs["leaving"], refs["out"], refs["swap_sems"])
        unpair = Unpair(refs["part"], refs["terms"], refs["unpair_sems"])
        if in_plane:
            scatters = [
                PlaneScatter(
                    refs["grads"],
                    (p * size, size),
                    refs["taken"].at[p],
                    refs["passing"].at[p],
                    refs["crossed"].at[p],
                    refs["summed"].at[p],
                    refs["plane_sems"].at[p],
                )
                for p in range(pieces)
            ]
            returns = [
                Unpair(
                    refs["summed"].at[p],
                    refs["grad_terms"].at[:, :, pl.ds(p * size, size)],
                    refs["return_sems"].at[p],
                )
                for p in range(pieces)
            ]
        else:
            scatters = []
            returns = [Unpair(refs["grads"], refs["grad_terms"], refs["return_sems"].at[0])]
        moves.start("part", "grads", "partial", "values", "stream")
        greet(True, True)
        moves.ready("part")
        unpair.start()
        moves.ready("partial")
        collect_work.start()
        moves.ready("grads")
        if scatters:
            scatters[0].start()
        each(collect_work.forward)
        if not in_plane:
            returns[0].start()
        moves.ready("values", "stream")
        refs["given"].at[0][1:3] = refs["gain_sums"][...]
        refs["gain_sum"][...] = jnp.zeros_like(refs["gain_sum"])

        def slope_and_send(k):
            slope, terms = norm_slope(
                collect_work.at(refs["values"], k, 0)[...].astype(jnp.float32),
                refs["gain"][...],
                collect_work.total(k),
            )
            sums = collect_work.at(refs["stream"], k, 0)[...] + slope
            swap.at(refs["leaving"], k)[...] = sums.astype(jnp.bfloat16)
            swap.start(k)
            refs["gain_sum"][...] += jnp.sum(terms, axis=0, keepdims=True)

        turns = max(PARTS, len(scatters) + 1)
        for k in range(turns):
            if k < PARTS:
                slope_and_send(k)
            if k < len(scatters):
                scatters[k].pass_on(scatters[k + 1] if k + 1 < len(scatters) else None)
            if 0 < k <= len(scatters):
                scatters[k - 1].total()
                returns[k - 1].start()
        refs["given"].at[0][0:1] = refs["gain_sum"][...]
        sum_everywhere(refs["given"], refs["got"], refs["gain_sems"], refs["totals"])
        each(swap.arrive)
        each(swap.finish)
        each(collect_work.finish)
        unpair.finish()
        for scatter in scatters:
            scatter.finish()
        for back in returns:
            back.finish()

    scratch = {
        **collect_scratch("", rows, length, width),
        "leaving": pltpu.VMEM((rows, length, width), jnp.bfloat16),
        "swap_sems": pltpu.SemaphoreType.DMA((2, PARTS)),
        "unpair_sems": pltpu.SemaphoreType.DMA((4,)),
        "return_sems": pltpu.SemaphoreType.DMA((max(1, pieces), 4)),
        "gain_sum": pltpu.VMEM((1, width), jnp.float32),
        "given": pltpu.VMEM((steps, 3, width), jnp.float32),
        "got": pltpu.VMEM((steps, 3, width), jnp.float32),
        "gain_sems": pltpu.SemaphoreType.DMA((2, steps)),
    }
    if in_plane:
        scratch["taken"] = pltpu.VMEM((pieces, 2, 2, owned, size // 2), jnp.bfloat16)
        scratch["passing"] = pltpu.VMEM((pieces, 2, owned, size // 2), jnp.bfloat16)
        scratch["crossed"] = pltpu.VMEM((pieces, 2, owned, size // 2), jnp.bfloat16)
        scratch["summed"] = pltpu.VMEM((pieces, owned, size), jnp.bfloat16)
        scratch["plane_sems"] = pltpu.SemaphoreType.DMA((pieces, 2, 6))
    results = kernel_call(
        number,
        "leave",
        {
            "partial": partial,
            "values": values,
            "stream": stream,
            "gain": gain[None],
            "gain_sums": gain_sums,
            "grads": grads,
            "part": part,
        },
        {
            "out": (shape_of(values.shape, jnp.bfloat16), ANY),
            "totals": (shape_of((3, width), jnp.float32), VMEM),
            "terms": terms_out(part),
            "grad_terms": (shape_of((2, owned // 2, columns), jnp.bfloat16), ANY),
        },
        scratch,
        body,
        lazy=("part", "grads", "partial", "values", "stream"),
    )
    return results["out"], results["totals"], results["terms"], results["grad_terms"]


def summed(terms):
    return terms[0].astype(jnp.float32) + terms[1].astype(jnp.float32)


def project(left_side, right_side):
    return jnp.einsum("rtd,de->rte", left_side, right_side, preferred_element_type=jnp.float32)


def project_back(gradient, right_side):
    return jnp.einsum("rte,de->rtd", gradient, right_side, preferred_element_type=jnp.float32)


def weight_grad(left_side, gradient):
    return jnp.einsum("rtd,rte->de", left_side, gradient, preferred_element_type=jnp.float32)


def gelu_tanh(values):
    return jax.nn.gelu(values, approximate=True)


def shards(
    tokens,
    patches,
    seg_ids,
    seg_example,
    patch_owner,
    gain_self,
    self_query,
    self_key,
    self_value,
    self_out,
    gain_cross,
    cross_query,
    cross_key,
    cross_value,
    cross_out,
    gain_mlp,
    mlp_gate,
    mlp_up,
    mlp_down,
    cotangent,
):
    gains = jnp.stack([gain_self, gain_cross, gain_mlp]).astype(jnp.float32)
    onehot = (
        seg_ids[:, :, None] == lax.iota(jnp.int32, seg_example.shape[1])[None, None, :]
    ).astype(jnp.int32)
    example_of = jnp.sum(onehot * seg_example[:, None, :], axis=2)
    marks = jnp.concatenate([seg_ids, example_of, patch_owner], axis=0)
    rows = seg_ids.shape[0]
    length = seg_ids.shape[1]
    wide = self_query.shape[1]
    hidden_wide = mlp_gate.shape[1]
    local_tokens, marks, gains, normed_one, patch_rows, self_w, cross_pair = head(
        0,
        tokens,
        patches,
        marks,
        gains,
        (self_query, self_key, self_value, self_out.T),
        (cross_key, cross_value, cross_query, cross_out.T),
    )
    norm_one, norm_two, norm_three = gains[0], gains[1], gains[2]
    cross_w = gather_chips(cross_pair)
    mlp_moved = exchange(after(jnp.concatenate([mlp_gate, mlp_up], axis=1), normed_one))
    seg_here = relative(marks[:rows])
    example_here = relative(marks[rows : 2 * rows])
    owner_here = relative(marks[2 * rows :])
    positions = relative(lax.broadcasted_iota(jnp.int32, (1, length), 1))
    self_marks = (
        seg_here[:, :, None],
        seg_here[:, None, :],
        positions.reshape(length, 1),
        positions.reshape(1, length),
    )
    cross_marks = (
        example_here[:, :, None],
        owner_here[:, None, :],
        jnp.zeros((length, 1), jnp.int32),
        jnp.zeros((1, length), jnp.int32),
    )
    self_places = (0, wide, 3 * wide)
    self_lefts = (normed_one, normed_one)
    self_qkv, _, self_attended, _, _, _, _ = attention_turn(
        None, self_lefts, self_w, self_places, self_marks, None, None
    )
    mlp_pair = pair_up(after(mlp_moved, self_attended))
    mlp_in = gather_chips(mlp_pair)
    down_moved = exchange(after(mlp_down.T, mlp_pair))
    _, _, _, after_self, normed_two, _, _ = attention_turn(
        1,
        self_lefts,
        self_w,
        self_places,
        self_marks,
        local_tokens,
        norm_two,
        after(self_attended, mlp_pair),
    )
    down_pair = pair_up(after(down_moved, after_self))
    mlp_downw = gather_chips(down_pair)
    (
        cross_query_rows,
        cross_kv_rows,
        cross_mixed,
        after_cross,
        normed_three,
        local_grad,
        grad_rows,
    ) = attention_turn(
        2,
        (after(normed_two, down_pair), patch_rows),
        cross_w,
        (2 * wide, 0, 3 * wide),
        cross_marks,
        after_self,
        norm_three,
        None,
        cotangent,
    )
    both = project(normed_three, mlp_in)
    gate_pre = both[..., :hidden_wide]
    upward = both[..., hidden_wide:]
    activated, gelu_pull = jax.vjp(gelu_tanh, gate_pre)
    hidden = (activated * upward).astype(jnp.bfloat16)

    grad_down_w = weight_grad(grad_rows, hidden).astype(jnp.bfloat16)
    down_part = scatter_chips(grad_down_w)
    grad_hidden = project(after(grad_rows, grad_down_w), mlp_downw)
    grad_upward = (grad_hidden * activated).astype(jnp.bfloat16)
    grad_gate = gelu_pull(grad_hidden * upward)[0].astype(jnp.bfloat16)
    grad_both = jnp.concatenate([grad_gate, grad_upward], axis=2)
    partial_three = project_back(grad_both, mlp_in).astype(jnp.bfloat16)
    tokens_here = rows * length
    grad_mlp_w = weight_grad(normed_three, grad_both).astype(jnp.bfloat16)
    mlp_part = scatter_chips(grad_mlp_w)
    grad_cross_stream, cross_branch, part_three, result_partial = turn_back(
        3,
        after(partial_three, grad_mlp_w),
        after_cross,
        local_grad,
        norm_three,
        (ProductFill("result_", hidden.reshape(tokens_here, -1), mlp_downw, (0, hidden_wide)),),
    )
    partial_two, cross_grads, down_terms, grad_ckv, output = attention_back(
        4,
        cross_branch,
        cross_w,
        (2 * wide, 0, 3 * wide),
        (cross_query_rows, 0),
        (cross_kv_rows, 0),
        cross_marks,
        (normed_two, patch_rows),
        cross_mixed,
        (result_partial.reshape(rows, length, -1), after_cross),
        down_part,
    )
    down_sum = summed(down_terms).T
    cross_part = scatter_chips(cross_grads)
    grad_self_stream, self_branch, part_two, mlp_terms, patch_partial = turn_back(
        5,
        partial_two,
        after_self,
        grad_cross_stream,
        norm_two,
        (ProductFill("patch_", grad_ckv.reshape(tokens_here, -1), cross_w, (0, 2 * wide)),),
        mlp_part,
    )
    mlp_sum = summed(mlp_terms)
    grad_self_out = weight_grad(self_branch, self_attended).astype(jnp.bfloat16)
    self_out_part = scatter_chips(grad_self_out)
    partial_one, grad_self_in, cross_terms, _, grad_patches = attention_back(
        6,
        after(self_branch, grad_self_out),
        self_w,
        (0, wide, 3 * wide),
        (self_qkv, 0),
        (self_qkv, wide),
        self_marks,
        (normed_one, normed_one),
        None,
        (patch_partial.reshape(rows, length, -1), None),
        cross_part,
    )
    cross_sum = summed(cross_terms)
    grad_tokens, gain_sums, self_out_terms, self_terms = leave(
        7,
        partial_one,
        local_tokens,
        grad_self_stream,
        norm_one,
        jnp.concatenate([part_two, part_three]),
        grad_self_in,
        self_out_part,
    )
    held = gain_self.shape[0]
    place = lax.axis_index(("chip", "core")) * held
    gain_sums = lax.dynamic_slice_in_dim(gain_sums, place, held, axis=1)
    self_sum = summed(self_terms)
    return (
        output,
        grad_tokens.astype(jnp.float32),
        grad_patches.astype(jnp.float32),
        gain_sums[0],
        self_sum[:, :wide],
        self_sum[:, wide : 2 * wide],
        self_sum[:, 2 * wide :],
        summed(self_out_terms).T,
        gain_sums[1],
        cross_sum[:, 2 * wide : 3 * wide],
        cross_sum[:, :wide],
        cross_sum[:, wide : 2 * wide],
        cross_sum[:, 3 * wide :].T,
        gain_sums[2],
        mlp_sum[:, :hidden_wide],
        mlp_sum[:, hidden_wide:],
        down_sum,
    )


def solution(mesh):
    devices = mesh.devices.reshape(mesh.shape["dp"] // 2, 2, 2, mesh.shape["seq"] // 2)
    fine = Mesh(devices, AXES)
    dp = ("chip", "core")
    seq = ("zh", "zp")
    stream = P(dp, seq, None)
    rows = P(dp, None)
    inward = P(dp, seq)
    outward = P(seq, dp)
    vector = P(dp)
    block = (vector, inward, inward, inward, outward)
    weights = block + block + (vector, inward, inward, outward)
    return jax.shard_map(
        shards,
        mesh=fine,
        in_specs=(stream, stream, rows, rows, rows) + weights + (stream,),
        out_specs=(stream, stream, stream) + weights,
        check_vma=False,
    )
```

```python
import itertools

import jax
import jax.numpy as jnp
from jax import lax
from jax.experimental import pallas as pl
from jax.experimental.pallas import tpu as pltpu
from jax.sharding import Mesh
from jax.sharding import PartitionSpec as P

HD = 128


epsilon = 1e-06
masked_value = -1e30

AXES = ("chip", "core", "zh", "zp")


def moves(chips, source_of):
    pairs = []
    for chip, core, zh, zp in itertools.product(range(chips), range(2), range(2), range(2)):
        a, b, c, d = source_of(chip, core, zh, zp)
        pairs.append((((a * 2 + b) * 2 + c) * 2 + d, ((chip * 2 + core) * 2 + zh) * 2 + zp))
    return pairs


def permute(values, source_of):
    return lax.ppermute(values, AXES, moves(lax.axis_size("chip"), source_of))


def swapped(values):
    return permute(values, lambda chip, core, zh, zp: (chip, zh, core, zp))


def swapped_other(values):
    return permute(values, lambda chip, core, zh, zp: (chip, 1 - zh, core, zp))


def relative(values):
    rows, length = values.shape
    cut = values.reshape(rows, 2, 2, length // 4)
    cut = jnp.where(lax.axis_index("core") == 1, cut[:, ::-1], cut)
    cut = jnp.where(lax.axis_index("zp") == 1, cut[:, :, ::-1], cut)
    return cut.reshape(rows, length)


def after(values, *others):
    return lax.optimization_barrier((values,) + others)[0]


def exchange(shards_of):
    return swapped(shards_of), swapped_other(shards_of)


def pair_up(exchanged):
    first, second = exchanged
    low = lax.axis_index("zh") == 0
    return jnp.concatenate([jnp.where(low, first, second), jnp.where(low, second, first)], axis=0)


def gather_chips(pair):
    return lax.all_gather(pair, "chip", axis=0, tiled=True)


def scatter_chips(grads):
    return lax.psum_scatter(
        grads.astype(jnp.bfloat16), "chip", scatter_dimension=0, tiled=True
    )


def normalize(values, gain_vec):
    factor = lax.rsqrt(jnp.mean(values * values, axis=-1, keepdims=True) + epsilon)
    return values * factor * gain_vec


def norm_back(values, gain_vec, gradient):
    normed_value, pullback = jax.vjp(lambda inputs: normalize(inputs, gain_vec), values)
    return pullback(gradient)[0]


def gain_part(values, gradient):
    factor = lax.rsqrt(jnp.mean(values * values, axis=-1, keepdims=True) + epsilon)
    return jnp.sum(gradient * values * factor, axis=(0, 1))


MESH = pl.DeviceIdType.MESH
ANY = pl.BlockSpec(memory_space=pl.ANY)
VMEM = pl.BlockSpec(memory_space=pltpu.VMEM)
PARTS = 4


def across_plane(axis):
    chip = lax.axis_index("chip")
    x, y = chip % 2, chip // 2
    return y * 2 + 1 - x if axis == 0 else (1 - y) * 2 + x


def greet(everyone, plane=False):
    core, zh, zp = lax.axis_index("core"), lax.axis_index("zh"), lax.axis_index("zp")
    barrier = pltpu.get_barrier_semaphore()
    count = 0
    for a, b, c in itertools.product(range(2), range(2), range(2)):
        if (a, b, c) == (0, 0, 0) or (b and not everyone):
            continue
        pl.semaphore_signal(
            barrier,
            inc=1,
            device_id={"core": (core + a) % 2, "zh": (zh + b) % 2, "zp": (zp + c) % 2},
            device_id_type=MESH,
        )
        count += 1
    if plane:
        chips = lax.axis_size("chip")
        for a, b in itertools.product(range(1, chips), range(2)):
            pl.semaphore_signal(
                barrier,
                inc=1,
                device_id={
                    "chip": (lax.axis_index("chip") + a) % chips,
                    "core": (core + b) % 2,
                },
                device_id_type=MESH,
            )
            count += 1
    pl.semaphore_wait(barrier, count)


def to_core(src, dst, send, recv):
    return pltpu.make_async_remote_copy(
        src, dst, send, recv, device_id={"core": 1 - lax.axis_index("core")}, device_id_type=MESH
    )


def to_zp(src, dst, send, recv):
    return pltpu.make_async_remote_copy(
        src, dst, send, recv, device_id={"zp": 1 - lax.axis_index("zp")}, device_id_type=MESH
    )


def to_swapped(src, dst, send, recv):
    core, zh = lax.axis_index("core"), lax.axis_index("zh")
    return pltpu.make_async_remote_copy(
        src, dst, send, recv, device_id={"core": zh, "zh": core}, device_id_type=MESH
    )


class Exchange:
    def __init__(self, src, pair, sems):
        self.src, self.pair, self.sems = src, pair, sems
        self.core, self.zh = lax.axis_index("core"), lax.axis_index("zh")
        rows = src.shape[0]
        self.mine = pair.at[pl.ds(pl.multiple_of(self.core * rows, rows), rows)]
        self.slots = [pair.at[pl.ds(a * rows, rows)] for a in range(2)]

    def far(self):
        return pltpu.make_async_remote_copy(
            self.src,
            self.mine,
            self.sems.at[0],
            self.sems.at[2 + self.core],
            device_id={"core": self.zh, "zh": 1 - self.zh},
            device_id_type=MESH,
        )

    def near(self):
        return pltpu.make_async_remote_copy(
            self.src,
            self.mine,
            self.sems.at[1],
            self.sems.at[2 + self.core],
            device_id={"core": 1 - self.core},
            device_id_type=MESH,
        )

    def own(self):
        return pltpu.make_async_copy(self.src, self.mine, self.sems.at[2 + self.core])

    def start(self):
        self.far().start()

        @pl.when(self.core == self.zh)
        def _():
            self.own().start()

        @pl.when(self.core != self.zh)
        def _():
            self.near().start()

    def finish(self):
        self.far().wait_send()

        @pl.when(self.core != self.zh)
        def _():
            self.near().wait_send()

        for a in range(2):
            pltpu.make_async_copy(self.src, self.slots[a], self.sems.at[2 + a]).wait()


class Spread:
    def __init__(self, block, gathered, sems):
        self.block, self.gathered, self.sems = block, gathered, sems
        self.length = block.shape[1]
        self.step = 2 * self.length // PARTS

    def src(self, k):
        return self.block.at[k // (PARTS // 2), pl.ds(pl.multiple_of(k % (PARTS // 2) * self.step, self.step), self.step)]

    def dst(self, k, slot):
        return self.gathered.at[
            k // (PARTS // 2),
            pl.ds(
                pl.multiple_of(slot * self.length + k % (PARTS // 2) * self.step, self.step),
                self.step,
            ),
        ]

    def beside(self, k):
        return to_zp(self.src(k), self.dst(k, 1), self.sems.at[0, k], self.sems.at[1, k])

    def across(self, k):
        return to_core(self.src(k), self.dst(k, 2), self.sems.at[2, k], self.sems.at[3, k])

    def corner(self, k):
        return to_core(self.dst(k, 1), self.dst(k, 3), self.sems.at[4, k], self.sems.at[5, k])

    def own(self, k):
        return pltpu.make_async_copy(self.src(k), self.dst(k, 0), self.sems.at[6, k])

    def start(self, k):
        self.beside(k).start()
        self.across(k).start()
        self.own(k).start()

    def relay(self, k):
        self.beside(k).wait_recv()
        self.corner(k).start()

    def finish(self, k):
        self.beside(k).wait_send()
        self.across(k).wait()
        self.corner(k).wait()
        self.own(k).wait()


class Collect:
    def __init__(self, partial, arrived, outgoing, landed, sems):
        self.partial, self.arrived = partial, arrived
        self.outgoing, self.landed, self.sems = outgoing, landed, sems
        self.length = outgoing.shape[1]
        self.step = 2 * self.length // PARTS

    def at(self, ref, k, block):
        return ref.at[
            k // (PARTS // 2),
            pl.ds(
                pl.multiple_of(block * self.length + k % (PARTS // 2) * self.step, self.step),
                self.step,
            ),
        ]

    def crossing(self, k, block):
        return to_core(
            self.at(self.partial, k, 2 + block),
            self.at(self.arrived, k, block),
            self.sems.at[2 * block, k],
            self.sems.at[2 * block + 1, k],
        )

    def landing(self, k):
        return to_zp(
            self.at(self.outgoing, k, 0),
            self.at(self.landed, k, 0),
            self.sems.at[4, k],
            self.sems.at[5, k],
        )

    def start(self):
        for block in (1, 0):
            self.start_block(block)

    def start_block(self, block):
        for k in range(PARTS):
            self.crossing(k, block).start()

    def forward(self, k):
        self.crossing(k, 1).wait_recv()
        self.at(self.outgoing, k, 0)[...] = (
            self.at(self.partial, k, 1)[...].astype(jnp.float32)
            + self.at(self.arrived, k, 1)[...].astype(jnp.float32)
        ).astype(jnp.bfloat16)
        self.landing(k).start()

    def total(self, k):
        self.crossing(k, 0).wait_recv()
        self.landing(k).wait_recv()
        return (
            self.at(self.partial, k, 0)[...].astype(jnp.float32)
            + self.at(self.arrived, k, 0)[...].astype(jnp.float32)
        ) + self.at(self.landed, k, 0)[...].astype(jnp.float32)

    def finish(self, k):
        self.crossing(k, 0).wait_send()
        self.crossing(k, 1).wait_send()
        self.landing(k).wait_send()


class Unpair:
    def __init__(self, part, terms, sems):
        self.part, self.terms, self.sems = part, terms, sems
        self.core, self.zh = lax.axis_index("core"), lax.axis_index("zh")
        self.rows = part.shape[0] // 2

    def piece(self, p):
        return self.part.at[pl.ds(p * self.rows, self.rows)]

    def remote(self, p):
        return pltpu.make_async_remote_copy(
            self.piece(p),
            self.terms.at[self.zh],
            self.sems.at[p],
            self.sems.at[2 + self.zh],
            device_id={"core": p, "zh": self.core},
            device_id_type=MESH,
        )

    def own(self, p):
        return pltpu.make_async_copy(
            self.piece(p), self.terms.at[self.zh], self.sems.at[2 + self.zh]
        )

    def stays(self, p):
        return jnp.logical_and(self.core == p, self.zh == p)

    def start(self):
        for p in range(2):

            @pl.when(self.stays(p))
            def _(p=p):
                self.own(p).start()

            @pl.when(jnp.logical_not(self.stays(p)))
            def _(p=p):
                self.remote(p).start()

    def finish(self):
        for p in range(2):

            @pl.when(jnp.logical_not(self.stays(p)))
            def _(p=p):
                self.remote(p).wait_send()

            pltpu.make_async_copy(
                self.piece(p), self.terms.at[p], self.sems.at[2 + p]
            ).wait()


class Swap:
    def __init__(self, block, target, sems):
        self.block, self.target, self.sems = block, target, sems
        self.swaps = lax.axis_index("core") != lax.axis_index("zh")
        self.step = 2 * block.shape[1] // PARTS

    def at(self, ref, k):
        return ref.at[
            k // (PARTS // 2), pl.ds(pl.multiple_of(k % (PARTS // 2) * self.step, self.step), self.step)
        ]

    def remote(self, k):
        return to_swapped(
            self.at(self.block, k), self.at(self.target, k), self.sems.at[0, k], self.sems.at[1, k]
        )

    def own(self, k):
        return pltpu.make_async_copy(self.at(self.block, k), self.at(self.target, k), self.sems.at[1, k])

    def start(self, k):
        @pl.when(self.swaps)
        def _():
            self.remote(k).start()

        @pl.when(jnp.logical_not(self.swaps))
        def _():
            self.own(k).start()

    def arrive(self, k):
        self.own(k).wait()

    def finish(self, k):
        @pl.when(self.swaps)
        def _():
            self.remote(k).wait_send()


def each(body):
    lax.fori_loop(0, PARTS, lambda k, carry: (body(k), carry)[1], 0)


class Moves:
    def __init__(self, loads, stores):
        self.loads, self.stores, self.waited, self.going = loads, stores, set(), []

    def start(self, *names):
        for name in names:
            if name in self.loads:
                self.loads[name].start()

    def ready(self, *names):
        for name in names:
            if name in self.loads and name not in self.waited:
                self.waited.add(name)
                self.loads[name].wait()

    def store(self, *names):
        for name in names:
            if name in self.stores:
                self.stores[name].start()
                self.going.append(name)

    def end(self):
        for name in self.going:
            self.stores[name].wait()


def kernel_call(number, name, inputs, outs, scratch, body, lazy=(), eager=(), columns=None):
    columns = columns or {}
    lazy = [key for key in lazy if key in inputs]
    eager = [key for key in eager if key in outs]
    scratch = dict(scratch)
    for key in lazy:
        shape = inputs[key].shape
        if key in columns:
            shape = (shape[0], columns[key][1])
        scratch["lazy_" + key] = pltpu.VMEM(shape, inputs[key].dtype)
    for key in eager:
        scratch["eager_" + key] = pltpu.VMEM(outs[key][0].shape, outs[key][0].dtype)
    scratch["move_sems"] = pltpu.SemaphoreType.DMA((max(1, len(lazy) + len(eager)),))
    names = list(inputs) + list(outs) + list(scratch)

    def kernel(*given):
        refs = dict(zip(names, given))
        sems = refs["move_sems"]
        loads, stores = {}, {}
        for number, key in enumerate(lazy):
            here, source = refs["lazy_" + key], refs[key]
            if key in columns:
                source = source.at[:, pl.ds(*columns[key])]
            loads[key] = pltpu.make_async_copy(source, here, sems.at[number])
            refs[key] = here
        for number, key in enumerate(eager):
            here = refs["eager_" + key]
            stores[key] = pltpu.make_async_copy(here, refs[key], sems.at[len(lazy) + number])
            refs[key] = here
        body(refs, Moves(loads, stores))

    results = pl.pallas_call(
        kernel,
        out_shape=tuple(shape for shape, _ in outs.values()),
        in_specs=[ANY if key in lazy else VMEM for key in inputs],
        out_specs=tuple(ANY if key in eager else spec for key, (_, spec) in outs.items()),
        scratch_shapes=list(scratch.values()),
        compiler_params=pltpu.CompilerParams(
            collective_id=number,
            has_side_effects=number is not None,
            vmem_limit_bytes=61 * 1024 * 1024,
        ),
        name=name,
    )(*inputs.values())
    return dict(zip(outs, results))


def collect_scratch(tag, rows, length, width):
    return {
        tag + "arrived": pltpu.VMEM((rows, 2 * length, width), jnp.bfloat16),
        tag + "outgoing": pltpu.VMEM((rows, length, width), jnp.bfloat16),
        tag + "landed": pltpu.VMEM((rows, length, width), jnp.bfloat16),
        tag + "collect_sems": pltpu.SemaphoreType.DMA((6, PARTS)),
    }


def collect_of(refs, tag, partial):
    return Collect(
        refs[partial],
        refs[tag + "arrived"],
        refs[tag + "outgoing"],
        refs[tag + "landed"],
        refs[tag + "collect_sems"],
    )


def shape_of(shape, dtype):
    return jax.ShapeDtypeStruct(shape, dtype)


def gathered_out(rows, length, width):
    return (shape_of((rows, 4 * length, width), jnp.bfloat16), ANY)


def pair_out(shard):
    return (shape_of((2 * shard.shape[0], shard.shape[1]), shard.dtype), ANY)


def terms_out(part):
    return (shape_of((2, part.shape[0] // 2, part.shape[1]), part.dtype), ANY)


class PlaneGather:
    def __init__(self, whole, columns, sems):
        self.whole, self.columns, self.sems = whole, columns, sems
        self.rows = whole.shape[0] // 4

    def half(self, chip, which):
        start, size = self.columns
        return self.whole.at[
            pl.ds(pl.multiple_of(chip * self.rows, self.rows), self.rows),
            pl.ds(start + which * (size // 2), size // 2),
        ]

    def own(self, axis, which):
        ref = self.half(lax.axis_index("chip"), which)
        return self.copy(ref, axis, 2 * axis + which)

    def passed(self, which):
        ref = self.half(across_plane(which), which)
        return self.copy(ref, 1 - which, 4 + which)

    def copy(self, ref, axis, number):
        return pltpu.make_async_remote_copy(
            ref,
            ref,
            self.sems.at[0, number],
            self.sems.at[1, number],
            device_id={"chip": across_plane(axis)},
            device_id_type=MESH,
        )

    def start(self):
        for axis in range(2):
            self.own(axis, axis).start()
        for axis in range(2):
            self.own(axis, 1 - axis).start()

    def relay(self):
        for which in range(2):
            self.own(which, which).wait_recv()
            self.passed(which).start()

    def finish(self):
        for axis in range(2):
            self.own(axis, axis).wait_send()
            self.own(axis, 1 - axis).wait()
            self.passed(axis).wait()


class SwapWhole:
    def __init__(self, array, target, sems):
        self.array, self.target, self.sems = array, target, sems
        self.swaps = lax.axis_index("core") != lax.axis_index("zh")

    def remote(self):
        return to_swapped(self.array, self.target, self.sems.at[0], self.sems.at[1])

    def own(self):
        return pltpu.make_async_copy(self.array, self.target, self.sems.at[1])

    def start(self):
        @pl.when(self.swaps)
        def _():
            self.remote().start()

        @pl.when(jnp.logical_not(self.swaps))
        def _():
            self.own().start()

    def finish(self):
        self.own().wait()

        @pl.when(self.swaps)
        def _():
            self.remote().wait_send()


class GainGather:
    def __init__(self, own, slots, whole, sems):
        self.own, self.slots, self.whole, self.sems = own, slots, whole, sems
        self.chips = lax.axis_size("chip")
        self.chip, self.core = lax.axis_index("chip"), lax.axis_index("core")

    def others(self):
        for number in range(1, 2 * self.chips):
            yield number, (self.chip + number // 2) % self.chips, (self.core + number % 2) % 2

    def send(self, number, chip, core):
        return pltpu.make_async_remote_copy(
            self.own,
            self.slots.at[self.chip * 2 + self.core],
            self.sems.at[0, number],
            self.sems.at[1, self.chip * 2 + self.core],
            device_id={"chip": chip, "core": core},
            device_id_type=MESH,
        )

    def start(self):
        for other in self.others():
            self.send(*other).start()
        self.slots.at[self.chip * 2 + self.core][...] = self.own[...]

    def finish(self):
        for number, chip, core in self.others():
            self.send(number, chip, core).wait_send()
            place = chip * 2 + core
            pltpu.make_async_copy(self.own, self.slots.at[place], self.sems.at[1, place]).wait()
        held = self.own.shape[1]
        for place in range(2 * self.chips):
            self.whole[:, place * held : (place + 1) * held] = self.slots[place]


def head(number, block, beside, marks, gains, first, second):
    rows, length, width = block.shape
    depth, size = first[0].shape
    chips = lax.axis_size("chip")
    in_plane = chips == 4
    if not in_plane:
        gains = lax.all_gather(gains, ("chip", "core"), axis=1, tiled=True)

    def body(refs, moves):
        swap = Swap(refs["block"], refs["here"], refs["swap_sems"])
        marks_swap = SwapWhole(refs["marks"], refs["marks_here"], refs["marks_sems"])
        spread_work = Spread(refs["normed"], refs["gathered"], refs["spread_sems"])
        if in_plane:
            chip = lax.axis_index("chip")
            place = refs["whole"].at[pl.ds(pl.multiple_of(chip * 2 * depth, 2 * depth), 2 * depth)]
            gain_work = GainGather(
                refs["gains"], refs["gain_slots"], refs["gains_whole"], refs["gain_sems"]
            )
        else:
            place = refs["whole"]
        works = [
            Exchange(
                refs["first%d" % i],
                place.at[:, pl.ds(i * size, size)],
                refs["exchange_sems"].at[i],
            )
            for i in range(len(first))
        ]
        beside_swap = Swap(refs["beside"], refs["beside_here"], refs["beside_swap_sems"])
        beside_work = Spread(refs["beside_here"], refs["beside_gathered"], refs["beside_sems"])
        later = [
            Exchange(
                refs["second%d" % i],
                refs["pair"].at[:, pl.ds(i * size, size)],
                refs["exchange_sems"].at[len(first) + i],
            )
            for i in range(len(second))
        ]
        greet(True, in_plane)
        marks_swap.start()

        def norm_and_send(k):
            swap.arrive(k)
            values = swap.at(refs["here"], k)[...].astype(jnp.float32)
            spread_work.src(k)[...] = normalize(values, refs["gains_whole"][0:1, :]).astype(
                jnp.bfloat16
            )
            spread_work.start(k)

        planes = [
            PlaneGather(refs["whole"], (i * size, size), refs["plane_sems"].at[i])
            for i in range(len(first))
        ]
        last = len(works) - 1
        works[0].start()
        if in_plane:
            gain_work.start()
            gain_work.finish()
        else:
            refs["gains_whole"][...] = refs["gains"][...]
        for i, work in enumerate(works):
            work.finish()
            if in_plane:
                planes[i].start()
            if i < last:
                works[i + 1].start()
            if i == 0:
                each(swap.start)
            if i == last - 1:
                each(beside_swap.start)
            if in_plane and i:
                planes[i - 1].relay()
            if i == 1:
                each(norm_and_send)
            if i == last:
                each(spread_work.relay)

        def pass_on(k):
            beside_swap.arrive(k)
            beside_work.start(k)

        later[0].start()
        pass_on(0)
        pass_on(1)
        if in_plane:
            planes[last].relay()
        for k in range(2, PARTS):
            pass_on(k)
        for i, work in enumerate(later):
            if i + 1 < len(later):
                later[i + 1].start()
            if i == 1:
                each(beside_work.relay)
            work.finish()
        each(beside_work.finish)
        each(beside_swap.finish)
        each(spread_work.finish)
        each(swap.finish)
        if in_plane:
            for plane in planes:
                plane.finish()
        marks_swap.finish()

    whole_rows = 8 * depth if in_plane else 2 * depth
    results = kernel_call(
        number,
        "head",
        {
            "block": block,
            "beside": beside,
            "marks": marks,
            "gains": gains,
            **{"first%d" % i: shard for i, shard in enumerate(first)},
            **{"second%d" % i: shard for i, shard in enumerate(second)},
        },
        {
            "here": (shape_of(block.shape, block.dtype), VMEM),
            "marks_here": (shape_of(marks.shape, marks.dtype), VMEM),
            "gains_whole": (shape_of((gains.shape[0], width), jnp.float32), VMEM),
            "gathered": gathered_out(rows, length, width),
            "whole": (shape_of((whole_rows, len(first) * size), jnp.bfloat16), ANY),
            "beside_gathered": gathered_out(rows, length, width),
            "pair": (shape_of((2 * depth, len(second) * size), jnp.bfloat16), ANY),
        },
        {
            "normed": pltpu.VMEM((rows, length, width), jnp.bfloat16),
            "spread_sems": pltpu.SemaphoreType.DMA((7, PARTS)),
            "swap_sems": pltpu.SemaphoreType.DMA((2, PARTS)),
            "beside_here": pltpu.VMEM((rows, length, width), jnp.bfloat16),
            "beside_sems": pltpu.SemaphoreType.DMA((7, PARTS)),
            "beside_swap_sems": pltpu.SemaphoreType.DMA((2, PARTS)),
            "marks_sems": pltpu.SemaphoreType.DMA((2,)),
            "exchange_sems": pltpu.SemaphoreType.DMA((len(first) + len(second), 4)),
            "plane_sems": pltpu.SemaphoreType.DMA((len(first), 2, 6)),
            "gain_slots": pltpu.VMEM((2 * chips,) + gains.shape, jnp.float32),
            "gain_sems": pltpu.SemaphoreType.DMA((2, 2 * chips)),
        },
        body,
    )
    whole = results["whole"] if in_plane else gather_chips(results["whole"])
    return (
        results["here"],
        results["marks_here"],
        results["gains_whole"],
        results["gathered"],
        results["beside_gathered"],
        whole,
        results["pair"],
    )


class ProductFill:
    def __init__(self, tag, left, right, columns):
        self.tag = tag
        self.columns = {tag + "right": columns}
        rows = left.shape[0]
        self.size = 256
        self.tiles = rows // self.size
        self.inputs = {tag + "left": left, tag + "right": right}
        self.outs = {tag + "out": (shape_of((rows, right.shape[0]), jnp.bfloat16), VMEM)}
        self.scratch = {}

    def tile(self, refs, i):
        at = pl.ds(pl.multiple_of(i * self.size, self.size), self.size)
        refs[self.tag + "out"].at[at][...] = across(
            refs[self.tag + "left"].at[at][...],
            refs[self.tag + "right"][...],
        ).astype(jnp.bfloat16)

    def end(self, refs):
        pass


def fill_in(refs, fill, part, parts):
    if fill is not None:
        first, last = fill.tiles * part // parts, fill.tiles * (part + 1) // parts
        lax.fori_loop(first, last, lambda i, carry: (fill.tile(refs, i), carry)[1], 0)


def norm_slope(values, gain, gradient):
    factor = lax.rsqrt(jnp.mean(values * values, axis=-1, keepdims=True) + epsilon)
    scaled = gain * gradient
    inner = jnp.mean(scaled * values, axis=-1, keepdims=True)
    return factor * scaled - values * (factor * factor * factor * inner), gradient * values * factor


def turn_back(number, partial, values, stream, gain, fills, *parts):
    rows, length, width = values.shape
    first, second = (tuple(fills) + (None, None))[:2]

    def body(refs, moves):
        collect_work = collect_of(refs, "", "partial")
        spread_work = Spread(refs["branch"], refs["gathered"], refs["spread_sems"])
        works = [
            Unpair(refs["part%d" % i], refs["terms%d" % i], refs["unpair_sems"].at[i])
            for i in range(len(parts))
        ]
        part_names = ["part%d" % i for i in range(len(parts))]
        fill_names = [[*fill.inputs] for fill in fills]
        moves.start(*part_names, "partial", "values", "stream", *sum(fill_names, []))
        greet(bool(parts))
        moves.ready(*part_names)
        for work in works:
            work.start()
        moves.ready("partial")
        collect_work.start()
        each(collect_work.forward)
        refs["gain_sum"][...] = jnp.zeros_like(refs["gain_sum"])

        def slope_and_send(k):
            slope, terms = norm_slope(
                collect_work.at(refs["values"], k, 0)[...].astype(jnp.float32),
                refs["gain"][...],
                collect_work.total(k),
            )
            sums = collect_work.at(refs["stream"], k, 0)[...].astype(jnp.float32) + slope
            collect_work.at(refs["after"], k, 0)[...] = sums
            spread_work.src(k)[...] = sums.astype(jnp.bfloat16)
            spread_work.start(k)
            refs["gain_sum"][...] += jnp.sum(terms, axis=0, keepdims=True)

        moves.ready("values", "stream")
        moves.ready(*sum(fill_names[:1], []))
        if first is None:
            each(slope_and_send)
        else:
            for k in range(PARTS):
                fill_in(refs, first, k, PARTS)
                slope_and_send(k)
        moves.store("after")
        for fill in fills[:1]:
            moves.store(*fill.outs)
        moves.ready(*sum(fill_names[1:], []))
        fill_in(refs, second, 0, 1)
        for fill in fills[1:]:
            moves.store(*fill.outs)
        each(spread_work.relay)
        each(spread_work.finish)
        each(collect_work.finish)
        for work in works:
            work.finish()
        for fill in fills:
            fill.end(refs)
        moves.end()

    extra = {"inputs": {}, "outs": {}, "scratch": {}}
    for fill in fills:
        for kind, found in extra.items():
            found.update(getattr(fill, kind))
    results = kernel_call(
        number,
        "turn_back",
        {
            "partial": partial,
            "values": values,
            "stream": stream,
            "gain": gain[None],
            **{"part%d" % i: part for i, part in enumerate(parts)},
            **extra["inputs"],
        },
        {
            "after": (shape_of(values.shape, jnp.float32), VMEM),
            "gathered": gathered_out(rows, length, width),
            "gain_sum": (shape_of((1, width), jnp.float32), VMEM),
            **{"terms%d" % i: terms_out(part) for i, part in enumerate(parts)},
            **extra["outs"],
        },
        {
            **collect_scratch("", rows, length, width),
            "branch": pltpu.VMEM((rows, length, width), jnp.bfloat16),
            "spread_sems": pltpu.SemaphoreType.DMA((7, PARTS)),
            "unpair_sems": pltpu.SemaphoreType.DMA((max(1, len(parts)), 4)),
            **extra["scratch"],
        },
        body,
        lazy=("partial", "values", "stream")
        + tuple("part%d" % i for i in range(len(parts)))
        + tuple(extra["inputs"]),
        eager=("after",)
        + tuple(name for name, (_, spec) in extra["outs"].items() if spec is VMEM),
        columns={key: found for fill in fills for key, found in fill.columns.items()},
    )
    return (
        (results["after"], results["gathered"], results["gain_sum"])
        + tuple(results["terms%d" % i] for i in range(len(parts)))
        + tuple(results[name] for fill in fills for name in fill.outs)
    )


class OutWork:
    def __init__(self, collect_work, swap, base):
        self.collect_work, self.swap, self.base = collect_work, swap, base

    def begin(self):
        self.collect_work.start()

    def forward(self):
        each(self.collect_work.forward)

    def leave_part(self, k):
        total = self.collect_work.total(k)
        if self.base is not None:
            total = total + self.swap.at(self.base, k)[...]
        self.swap.at(self.swap.block, k)[...] = total.astype(jnp.bfloat16)
        self.swap.start(k)

    def end(self):
        each(self.swap.arrive)
        each(self.swap.finish)
        each(self.collect_work.finish)


def head_at(ref, r, h, offset):
    return ref.at[r, :, pl.ds(pl.multiple_of(offset + h * HD, HD), HD)]


def across(left, right):
    return lax.dot_general(
        left, right, (((1,), (1,)), ((), ())), preferred_element_type=jnp.float32
    )


def down(left, right):
    return lax.dot_general(
        left, right, (((0,), (0,)), ((), ())), preferred_element_type=jnp.float32
    )


def masked_probability(refs, r, queries, key_rows):
    scores = across(queries, key_rows) * HD ** (-0.5)
    allowed = jnp.logical_and(
        refs["query_mark"][r] == refs["key_mark"][r],
        refs["query_place"][...] >= refs["key_place"][...],
    )
    scores = jnp.where(allowed, scores, masked_value)
    shifted = jnp.exp(scores - jnp.max(scores, axis=-1, keepdims=True))
    return shifted / jnp.sum(shifted, axis=-1, keepdims=True)


def rows_of(ref, t, size):
    per_row = ref.shape[1] // size
    return ref.at[t // per_row, pl.ds(pl.multiple_of(t % per_row * size, size), size)]


def attention_back(
    number, branch, weights, places, queries, pairs, marks, lefts, attended, out, part
):
    query_place, pair_place, out_place = places
    (query_array, query_at), (pair_array, pair_at) = queries, pairs
    same = query_array is pair_array
    rows, length, width = branch.shape
    wide = weights.shape[1] // 4
    heads = wide // HD
    block = (rows, length // 4, width)
    flat = (rows * length, width)
    inputs = {
        "branch": branch,
        "weights": weights,
        "queries": query_array,
        "query_mark": marks[0],
        "key_mark": marks[1],
        "query_place": marks[2],
        "key_place": marks[3],
        "left0": lefts[0].reshape(flat),
        "part": part,
    }
    if not same:
        inputs["pairs"] = pair_array
        inputs["left1"] = lefts[1].reshape(flat)
    if attended is not None:
        inputs["attended"] = attended.reshape(rows * length, wide)
    if out is not None:
        inputs["partial"] = out[0]
        if out[1] is not None:
            inputs["base"] = out[1]
    grad_columns = wide * (4 if attended is not None else 3)
    outs = {
        "input_partial": (shape_of((rows, length, width), jnp.bfloat16), VMEM),
        "weight_grads": (shape_of((width, grad_columns), jnp.bfloat16), ANY),
        "terms": terms_out(part),
    }
    scratch = {
        "grad_out": pltpu.VMEM((rows, length, wide), jnp.bfloat16),
        "stage": pltpu.VMEM((2, 256, grad_columns), jnp.bfloat16),
        "stage_sems": pltpu.SemaphoreType.DMA((2,)),
        "unpair_sems": pltpu.SemaphoreType.DMA((4,)),
    }
    if out is not None:
        outs["out"] = (shape_of(block, jnp.bfloat16), ANY)
        scratch.update(collect_scratch("", *block))
        scratch["leaving"] = pltpu.VMEM(block, jnp.bfloat16)
        scratch["swap_sems"] = pltpu.SemaphoreType.DMA((2, PARTS))
    if same:
        scratch["grad_all"] = pltpu.VMEM((rows, length, 3 * wide), jnp.bfloat16)
    else:
        scratch["grad_queries"] = pltpu.VMEM((rows, length, wide), jnp.bfloat16)
        outs["grad_pairs"] = (shape_of((rows, length, 2 * wide), jnp.bfloat16), VMEM)
    scale = HD ** (-0.5)
    total = rows * heads
    size = 256

    def body(refs, moves):
        unpair = Unpair(refs["part"], refs["terms"], refs["unpair_sems"])
        out_work = None
        if out is not None:
            out_work = OutWork(
                collect_of(refs, "", "partial"),
                Swap(refs["leaving"], refs["out"], refs["swap_sems"]),
                refs.get("base"),
            )
        grad_queries = refs["grad_all"] if same else refs["grad_queries"]
        grad_pairs = refs["grad_all"] if same else refs["grad_pairs"]
        pair_refs = refs["queries"] if same else refs["pairs"]
        pair_out = wide if same else 0

        def form_grad_out(t):
            rows_of(refs["grad_out"], t, size)[...] = jnp.dot(
                rows_of(refs["branch"], t, size)[...],
                refs["weights"].at[:, pl.ds(out_place, wide)][...],
                preferred_element_type=jnp.float32,
            ).astype(jnp.bfloat16)

        def one(i):
            r, h = i // heads, i % heads
            queries_here = head_at(refs["queries"], r, h, query_at)[...]
            key_rows = head_at(pair_refs, r, h, pair_at)[...]
            value_rows = head_at(pair_refs, r, h, pair_at + wide)[...]
            grad_here = head_at(refs["grad_out"], r, h, 0)[...]
            probability = masked_probability(refs, r, queries_here, key_rows)
            grad_values = down(probability.astype(jnp.bfloat16), grad_here)
            grad_probs = across(grad_here, value_rows)
            inner = jnp.sum(probability * grad_probs, axis=-1, keepdims=True)
            grad_scores = (probability * (grad_probs - inner)).astype(jnp.bfloat16)
            query_terms = jnp.dot(grad_scores, key_rows, preferred_element_type=jnp.float32)
            key_terms = down(grad_scores, queries_here)
            head_at(grad_queries, r, h, 0)[...] = (query_terms * scale).astype(jnp.bfloat16)
            head_at(grad_pairs, r, h, pair_out)[...] = (key_terms * scale).astype(jnp.bfloat16)
            head_at(grad_pairs, r, h, pair_out + wide)[...] = grad_values.astype(jnp.bfloat16)

        def form_partial(t):
            columns = (query_place, 3 * wide if same else wide)
            rows_of(refs["input_partial"], t, size)[...] = across(
                rows_of(grad_queries, t, size)[...],
                refs["weights"].at[:, pl.ds(*columns)][...],
            ).astype(jnp.bfloat16)

        def written(i):
            return pltpu.make_async_copy(
                refs["stage"].at[i % 2],
                refs["weight_grads"].at[pl.ds(pl.multiple_of(i * size, size), size)],
                refs["stage_sems"].at[i % 2],
            )

        def form_grads(i):
            @pl.when(i >= 2)
            def _():
                written(i - 2).wait()

            at = pl.ds(pl.multiple_of(i * size, size), size)
            stage = refs["stage"].at[i % 2]

            def put(place, left, right):
                terms = right[...].reshape(rows * length, right.shape[-1])
                stage[:, place : place + right.shape[-1]] = down(left, terms).astype(jnp.bfloat16)

            put(query_place, refs["left0"].at[:, at][...], grad_queries)
            if not same:
                put(pair_place, refs["left1"].at[:, at][...], grad_pairs)
            if attended is not None:
                here = refs["branch"].at[:, :, at][...].reshape(rows * length, size)
                stage[:, out_place : out_place + wide] = down(here, refs["attended"][...]).astype(
                    jnp.bfloat16
                )
            written(i).start()

        def loop(count, work, stops=()):
            def step(i, carry):
                work(i)
                if out_work is not None:
                    for stop, k in stops:

                        @pl.when(i == stop)
                        def _(k=k):
                            out_work.leave_part(k)

                return carry

            lax.fori_loop(0, count, step, 0)

        moves.start("part", "partial", "branch", "weights", "queries", "pairs", "base")
        moves.start("left0", "left1", "attended")
        greet(True)
        moves.ready("part")
        unpair.start()
        moves.ready("partial")
        if out_work is not None:
            out_work.begin()
        moves.ready("branch", "weights")
        loop(rows * length // size, form_grad_out)
        if out_work is not None:
            out_work.forward()
        moves.ready("queries", "pairs", "base")
        loop(total, one, ((total - 1, 0),))
        moves.store("grad_pairs")
        moves.ready("left0", "left1", "attended")
        loop(width // size, form_grads, ((1, 1), (3, 2), (5, 3)))
        loop(rows * length // size, form_partial)
        moves.store("input_partial")
        if out_work is not None:
            out_work.end()
        unpair.finish()
        for i in (width // size - 2, width // size - 1):
            written(i).wait()
        moves.end()

    big = ("part", "partial", "branch", "weights", "queries", "pairs", "base")
    results = kernel_call(
        number,
        "attention_back",
        inputs,
        outs,
        scratch,
        body,
        lazy=big + ("left0", "left1", "attended"),
        eager=("grad_pairs", "input_partial"),
    )
    return (
        results["input_partial"],
        results["weight_grads"],
        results["terms"],
        results.get("grad_pairs"),
        results.get("out"),
    )


def attention_turn(number, lefts, weights, places, marks, stream, gain, done=None, beside=None):
    query_place, pair_place, out_place = places
    same = lefts[0] is lefts[1]
    rows, length, width = lefts[0].shape
    wide = weights.shape[1] // 4
    heads = wide // HD
    quarter = length // 4
    size = 256
    out_at = out_place if done is None else 0
    columns = None
    if done is not None:
        columns = {"weights": (out_place, wide)}
    elif stream is None:
        columns = {"weights": (0, 3 * wide)}
    inputs = {"weights": weights}
    outs, scratch = {}, {}
    if done is None:
        inputs.update(
            {
                "left0": lefts[0],
                "query_mark": marks[0],
                "key_mark": marks[1],
                "query_place": marks[2],
                "key_place": marks[3],
            }
        )
        outs["queries"] = (
            shape_of((rows, length, wide * (3 if same else 1)), jnp.bfloat16),
            VMEM,
        )
        outs["attended"] = (shape_of((rows, length, wide), jnp.bfloat16), VMEM)
        if not same:
            inputs["left1"] = lefts[1]
            outs["pairs"] = (shape_of((rows, length, 2 * wide), jnp.bfloat16), VMEM)
    else:
        inputs["attended"] = done
    if stream is not None:
        inputs["stream"] = stream
        inputs["gain"] = gain[None]
        outs["after"] = (shape_of(stream.shape, jnp.float32), VMEM)
        outs["gathered"] = gathered_out(rows, quarter, width)
        scratch.update(
            {
                **collect_scratch("", rows, quarter, width),
                "partial": pltpu.VMEM((rows, length, width), jnp.bfloat16),
                "normed": pltpu.VMEM((rows, quarter, width), jnp.bfloat16),
                "spread_sems": pltpu.SemaphoreType.DMA((7, PARTS)),
            }
        )
    if beside is not None:
        inputs["beside"] = beside
        outs["beside_gathered"] = gathered_out(rows, quarter, width)
        outs["beside_here"] = (shape_of((rows, quarter, width), jnp.bfloat16), VMEM)
        scratch["beside_sems"] = pltpu.SemaphoreType.DMA((7, PARTS))
        scratch["beside_swap_sems"] = pltpu.SemaphoreType.DMA((2, PARTS))

    def body(refs, moves):
        if stream is not None:
            collect_work = collect_of(refs, "", "partial")
            spread_work = Spread(refs["normed"], refs["gathered"], refs["spread_sems"])
        if beside is not None:
            swap = Swap(refs["beside"], refs["beside_here"], refs["beside_swap_sems"])
            beside_work = Spread(
                refs["beside_here"], refs["beside_gathered"], refs["beside_sems"]
            )
        if done is None:
            pair_refs = refs["queries"] if same else refs["pairs"]
        pair_at = wide if same else 0

        def loop(count, work):
            lax.fori_loop(0, count, lambda i, carry: (work(i), carry)[1], 0)

        def form(left, place, columns, target):
            def tile(t):
                rows_of(target, t, size)[...] = jnp.dot(
                    rows_of(left, t, size)[...],
                    refs["weights"].at[:, pl.ds(place, columns)][...],
                    preferred_element_type=jnp.float32,
                ).astype(jnp.bfloat16)

            loop(rows * length // size, tile)

        def one(i):
            r, h = i // heads, i % heads
            probability = masked_probability(
                refs,
                r,
                head_at(refs["queries"], r, h, 0)[...],
                head_at(pair_refs, r, h, pair_at)[...],
            ).astype(jnp.bfloat16)
            head_at(refs["attended"], r, h, 0)[...] = jnp.dot(
                probability,
                head_at(pair_refs, r, h, pair_at + wide)[...],
                preferred_element_type=jnp.float32,
            ).astype(jnp.bfloat16)

        def form_block(block):
            def tile(r):
                at = pl.ds(block * quarter, quarter)
                refs["partial"].at[r, at][...] = across(
                    refs["attended"].at[r, at][...],
                    refs["weights"].at[:, pl.ds(out_at, wide)][...],
                ).astype(jnp.bfloat16)

            loop(rows, tile)

        def norm_and_send(k):
            values = collect_work.at(refs["stream"], k, 0)[...].astype(
                jnp.float32
            ) + collect_work.total(k)
            collect_work.at(refs["after"], k, 0)[...] = values
            spread_work.src(k)[...] = normalize(values, refs["gain"][...]).astype(jnp.bfloat16)
            spread_work.start(k)

        def pass_on(first, last):
            if beside is not None:
                for k in range(first, last):
                    swap.arrive(k)
                    beside_work.start(k)

        moves.start("beside", "left1", "weights", "left0", "attended", "stream")
        if number is not None:
            greet(beside is not None)
        moves.ready("beside")
        if beside is not None:
            each(swap.start)
        moves.ready("left1", "weights")
        if done is None:
            if same:
                moves.ready("left0")
                form(refs["left0"], query_place, 3 * wide, refs["queries"])
            else:
                form(refs["left1"], pair_place, 2 * wide, refs["pairs"])
                pass_on(0, 1)
                moves.ready("left0")
                form(refs["left0"], query_place, wide, refs["queries"])
            pass_on(0 if same else 1, 2)
            moves.store("queries", "pairs")
            loop(rows * heads, one)
            moves.store("attended")
        pass_on(0 if done is not None else 2, PARTS)
        moves.store("beside_here")
        moves.ready("attended", "stream")
        if stream is not None:
            for block in (3, 2):
                form_block(block)
                collect_work.start_block(block - 2)
            form_block(1)
            each(collect_work.forward)
            form_block(0)
            if beside is not None:
                each(beside_work.relay)
            each(norm_and_send)
            moves.store("after")
            each(spread_work.relay)
            each(spread_work.finish)
            each(collect_work.finish)
        elif beside is not None:
            each(beside_work.relay)
        if beside is not None:
            each(beside_work.finish)
            each(swap.finish)
        moves.end()

    results = kernel_call(
        number,
        "attention_turn",
        inputs,
        outs,
        scratch,
        body,
        lazy=("beside", "left1", "weights", "left0", "attended", "stream"),
        eager=("queries", "pairs", "attended", "after", "beside_here"),
        columns=columns,
    )
    return tuple(
        results.get(name)
        for name in (
            "queries",
            "pairs",
            "attended",
            "after",
            "gathered",
            "beside_here",
            "beside_gathered",
        )
    )


class PlaneScatter:
    def __init__(self, grads, columns, taken, passing, crossed, part, sems):
        self.grads, self.columns, self.taken, self.passing = grads, columns, taken, passing
        self.crossed, self.part, self.sems = crossed, part, sems
        self.rows = grads.shape[0] // 4
        self.me = lax.axis_index("chip")

    def terms(self, chip, which):
        start, size = self.columns
        return self.grads.at[
            pl.ds(pl.multiple_of(chip * self.rows, self.rows), self.rows),
            pl.ds(start + which * (size // 2), size // 2),
        ]

    def copy(self, src, dst, axis, number):
        return pltpu.make_async_remote_copy(
            src,
            dst,
            self.sems.at[0, number],
            self.sems.at[1, number],
            device_id={"chip": across_plane(axis)},
            device_id_type=MESH,
        )

    def first(self, which, block):
        chip = 3 - self.me if block else across_plane(which)
        return self.copy(
            self.terms(chip, which), self.taken.at[which, block], which, 2 * which + block
        )

    def second(self, which):
        return self.copy(
            self.passing.at[which], self.crossed.at[which], 1 - which, 4 + which
        )

    def start(self):
        for block in (1, 0):
            for which in range(2):
                self.first(which, block).start()

    def pass_on(self, following):
        for which in range(2):
            self.first(which, 1).wait_recv()
        if following is not None:
            following.start()
        for which in range(2):
            self.passing.at[which][...] = (
                self.terms(across_plane(1 - which), which)[...].astype(jnp.float32)
                + self.taken.at[which, 1][...].astype(jnp.float32)
            ).astype(jnp.bfloat16)
            self.second(which).start()

    def total(self):
        half = self.columns[1] // 2
        for which in range(2):
            self.first(which, 0).wait_recv()
            self.second(which).wait_recv()
            self.part.at[:, pl.ds(which * half, half)][...] = (
                self.terms(self.me, which)[...].astype(jnp.float32)
                + self.taken.at[which, 0][...].astype(jnp.float32)
                + self.crossed.at[which][...].astype(jnp.float32)
            ).astype(jnp.bfloat16)

    def finish(self):
        for which in range(2):
            for block in range(2):
                self.first(which, block).wait_send()
            self.second(which).wait_send()


class SumEverywhere:
    def __init__(self, given, taken, sems):
        self.given, self.taken, self.sems = given, taken, sems
        chips = lax.axis_size("chip")
        core, zh, zp, chip = (lax.axis_index(axis) for axis in ("core", "zh", "zp", "chip"))
        self.partners = [{"core": 1 - core}]
        for bit in range(chips.bit_length() - 1):
            size = 2**bit
            self.partners.append({"chip": chip + size - 2 * size * (chip // size % 2)})
        self.partners += [{"zp": 1 - zp}, {"zh": 1 - zh}]
        self.steps = len(self.partners)
        self.sums = None

    def copy(self, step):
        return pltpu.make_async_remote_copy(
            self.given.at[step],
            self.taken.at[step],
            self.sems.at[0, step],
            self.sems.at[1, step],
            device_id=self.partners[step],
            device_id_type=MESH,
        )

    def begin(self, step):
        if step:
            self.given[step] = self.sums
        else:
            self.sums = self.given[0]
        self.copy(step).start()

    def end(self, step):
        self.copy(step).wait()
        self.sums = self.sums + self.taken[step]


def leave(number, partial, values, stream, gain, gain_sums, grads, part):
    rows, length, width = values.shape
    chips = lax.axis_size("chip")
    in_plane = chips == 4
    steps = 3 + chips.bit_length() - 1
    if not in_plane:
        grads = scatter_chips(grads)
    owned = grads.shape[0] // (4 if in_plane else 1)
    columns = grads.shape[1]
    size = 512
    pieces = columns // size if in_plane else 0

    def body(refs, moves):
        collect_work = collect_of(refs, "", "partial")
        swap = Swap(refs["leaving"], refs["out"], refs["swap_sems"])
        unpair = Unpair(refs["part"], refs["terms"], refs["unpair_sems"])
        if in_plane:
            scatters = [
                PlaneScatter(
                    refs["grads"],
                    (p * size, size),
                    refs["taken"].at[p],
                    refs["passing"].at[p],
                    refs["crossed"].at[p],
                    refs["summed"].at[p],
                    refs["plane_sems"].at[p],
                )
                for p in range(pieces)
            ]
            returns = [
                Unpair(
                    refs["summed"].at[p],
                    refs["grad_terms"].at[:, :, pl.ds(p * size, size)],
                    refs["return_sems"].at[p],
                )
                for p in range(pieces)
            ]
        else:
            scatters = []
            returns = [Unpair(refs["grads"], refs["grad_terms"], refs["return_sems"].at[0])]
        moves.start("part", "grads", "partial", "values", "stream")
        greet(True, True)
        moves.ready("part")
        unpair.start()
        moves.ready("partial")
        collect_work.start()
        moves.ready("grads")
        if scatters:
            scatters[0].start()
        each(collect_work.forward)
        if not in_plane:
            returns[0].start()
        moves.ready("values", "stream")
        refs["given"].at[0][1:3] = refs["gain_sums"][...]
        refs["gain_sum"][...] = jnp.zeros_like(refs["gain_sum"])

        def slope_and_send(k):
            slope, terms = norm_slope(
                collect_work.at(refs["values"], k, 0)[...].astype(jnp.float32),
                refs["gain"][...],
                collect_work.total(k),
            )
            sums = collect_work.at(refs["stream"], k, 0)[...] + slope
            swap.at(refs["leaving"], k)[...] = sums.astype(jnp.bfloat16)
            swap.start(k)
            refs["gain_sum"][...] += jnp.sum(terms, axis=0, keepdims=True)

        gain_work = SumEverywhere(refs["given"], refs["got"], refs["gain_sems"])
        last = gain_work.steps - 1
        turns = max(PARTS, len(scatters) + 1)
        for k in range(turns):
            if k < PARTS:
                slope_and_send(k)
            if k == PARTS - 1:
                refs["given"].at[0][0:1] = refs["gain_sum"][...]
                for step in range(last - 1):
                    gain_work.begin(step)
                    gain_work.end(step)
                gain_work.begin(last - 1)
            if k < len(scatters):
                scatters[k].pass_on(scatters[k + 1] if k + 1 < len(scatters) else None)
            if 0 < k <= len(scatters):
                scatters[k - 1].total()
                returns[k - 1].start()
        gain_work.end(last - 1)
        gain_work.begin(last)
        each(swap.arrive)
        each(swap.finish)
        each(collect_work.finish)
        unpair.finish()
        for scatter in scatters:
            scatter.finish()
        for back in returns:
            back.finish()
        gain_work.end(last)
        refs["totals"][...] = gain_work.sums

    scratch = {
        **collect_scratch("", rows, length, width),
        "leaving": pltpu.VMEM((rows, length, width), jnp.bfloat16),
        "swap_sems": pltpu.SemaphoreType.DMA((2, PARTS)),
        "unpair_sems": pltpu.SemaphoreType.DMA((4,)),
        "return_sems": pltpu.SemaphoreType.DMA((max(1, pieces), 4)),
        "gain_sum": pltpu.VMEM((1, width), jnp.float32),
        "given": pltpu.VMEM((steps, 3, width), jnp.float32),
        "got": pltpu.VMEM((steps, 3, width), jnp.float32),
        "gain_sems": pltpu.SemaphoreType.DMA((2, steps)),
    }
    if in_plane:
        scratch["taken"] = pltpu.VMEM((pieces, 2, 2, owned, size // 2), jnp.bfloat16)
        scratch["passing"] = pltpu.VMEM((pieces, 2, owned, size // 2), jnp.bfloat16)
        scratch["crossed"] = pltpu.VMEM((pieces, 2, owned, size // 2), jnp.bfloat16)
        scratch["summed"] = pltpu.VMEM((pieces, owned, size), jnp.bfloat16)
        scratch["plane_sems"] = pltpu.SemaphoreType.DMA((pieces, 2, 6))
    results = kernel_call(
        number,
        "leave",
        {
            "partial": partial,
            "values": values,
            "stream": stream,
            "gain": gain[None],
            "gain_sums": gain_sums,
            "grads": grads,
            "part": part,
        },
        {
            "out": (shape_of(values.shape, jnp.bfloat16), ANY),
            "totals": (shape_of((3, width), jnp.float32), VMEM),
            "terms": terms_out(part),
            "grad_terms": (shape_of((2, owned // 2, columns), jnp.bfloat16), ANY),
        },
        scratch,
        body,
        lazy=("part", "grads", "partial", "values", "stream"),
    )
    return results["out"], results["totals"], results["terms"], results["grad_terms"]


def summed(terms):
    return terms[0].astype(jnp.float32) + terms[1].astype(jnp.float32)


def project(left_side, right_side):
    return jnp.einsum("rtd,de->rte", left_side, right_side, preferred_element_type=jnp.float32)


def project_back(gradient, right_side):
    return jnp.einsum("rte,de->rtd", gradient, right_side, preferred_element_type=jnp.float32)


def weight_grad(left_side, gradient):
    return jnp.einsum("rtd,rte->de", left_side, gradient, preferred_element_type=jnp.float32)


def gelu_tanh(values):
    return jax.nn.gelu(values, approximate=True)


def shards(
    tokens,
    patches,
    seg_ids,
    seg_example,
    patch_owner,
    gain_self,
    self_query,
    self_key,
    self_value,
    self_out,
    gain_cross,
    cross_query,
    cross_key,
    cross_value,
    cross_out,
    gain_mlp,
    mlp_gate,
    mlp_up,
    mlp_down,
    cotangent,
):
    gains = jnp.stack([gain_self, gain_cross, gain_mlp]).astype(jnp.float32)
    onehot = (
        seg_ids[:, :, None] == lax.iota(jnp.int32, seg_example.shape[1])[None, None, :]
    ).astype(jnp.int32)
    example_of = jnp.sum(onehot * seg_example[:, None, :], axis=2)
    marks = jnp.concatenate([seg_ids, example_of, patch_owner], axis=0)
    rows = seg_ids.shape[0]
    length = seg_ids.shape[1]
    wide = self_query.shape[1]
    hidden_wide = mlp_gate.shape[1]
    local_tokens, marks, gains, normed_one, patch_rows, self_w, cross_pair = head(
        0,
        tokens,
        patches,
        marks,
        gains,
        (self_query, self_key, self_value, self_out.T),
        (cross_key, cross_value, cross_query, cross_out.T),
    )
    norm_one, norm_two, norm_three = gains[0], gains[1], gains[2]
    cross_w = gather_chips(cross_pair)
    mlp_moved = exchange(after(jnp.concatenate([mlp_gate, mlp_up], axis=1), normed_one))
    seg_here = relative(marks[:rows])
    example_here = relative(marks[rows : 2 * rows])
    owner_here = relative(marks[2 * rows :])
    positions = relative(lax.broadcasted_iota(jnp.int32, (1, length), 1))
    self_marks = (
        seg_here[:, :, None],
        seg_here[:, None, :],
        positions.reshape(length, 1),
        positions.reshape(1, length),
    )
    cross_marks = (
        example_here[:, :, None],
        owner_here[:, None, :],
        jnp.zeros((length, 1), jnp.int32),
        jnp.zeros((1, length), jnp.int32),
    )
    self_places = (0, wide, 3 * wide)
    self_lefts = (normed_one, normed_one)
    self_qkv, _, self_attended, _, _, _, _ = attention_turn(
        None, self_lefts, self_w, self_places, self_marks, None, None
    )
    mlp_pair = pair_up(after(mlp_moved, self_attended))
    mlp_in = gather_chips(mlp_pair)
    down_moved = exchange(after(mlp_down.T, mlp_pair))
    _, _, _, after_self, normed_two, _, _ = attention_turn(
        1,
        self_lefts,
        self_w,
        self_places,
        self_marks,
        local_tokens,
        norm_two,
        after(self_attended, mlp_pair),
    )
    down_pair = pair_up(after(down_moved, after_self))
    mlp_downw = gather_chips(down_pair)
    (
        cross_query_rows,
        cross_kv_rows,
        cross_mixed,
        after_cross,
        normed_three,
        local_grad,
        grad_rows,
    ) = attention_turn(
        2,
        (after(normed_two, down_pair), patch_rows),
        cross_w,
        (2 * wide, 0, 3 * wide),
        cross_marks,
        after_self,
        norm_three,
        None,
        cotangent,
    )
    both = project(normed_three, mlp_in)
    gate_pre = both[..., :hidden_wide]
    upward = both[..., hidden_wide:]
    activated, gelu_pull = jax.vjp(gelu_tanh, gate_pre)
    hidden = (activated * upward).astype(jnp.bfloat16)

    grad_down_w = weight_grad(grad_rows, hidden).astype(jnp.bfloat16)
    down_part = scatter_chips(grad_down_w)
    grad_hidden = project(after(grad_rows, grad_down_w), mlp_downw)
    grad_upward = (grad_hidden * activated).astype(jnp.bfloat16)
    grad_gate = gelu_pull(grad_hidden * upward)[0].astype(jnp.bfloat16)
    grad_both = jnp.concatenate([grad_gate, grad_upward], axis=2)
    partial_three = project_back(grad_both, mlp_in).astype(jnp.bfloat16)
    tokens_here = rows * length
    grad_mlp_w = weight_grad(normed_three, grad_both).astype(jnp.bfloat16)
    mlp_part = scatter_chips(grad_mlp_w)
    grad_cross_stream, cross_branch, part_three, result_partial = turn_back(
        3,
        after(partial_three, grad_mlp_w),
        after_cross,
        local_grad,
        norm_three,
        (ProductFill("result_", hidden.reshape(tokens_here, -1), mlp_downw, (0, hidden_wide)),),
    )
    partial_two, cross_grads, down_terms, grad_ckv, output = attention_back(
        4,
        cross_branch,
        cross_w,
        (2 * wide, 0, 3 * wide),
        (cross_query_rows, 0),
        (cross_kv_rows, 0),
        cross_marks,
        (normed_two, patch_rows),
        cross_mixed,
        (result_partial.reshape(rows, length, -1), after_cross),
        down_part,
    )
    down_sum = summed(down_terms).T
    cross_part = scatter_chips(cross_grads)
    grad_self_stream, self_branch, part_two, mlp_terms, patch_partial = turn_back(
        5,
        partial_two,
        after_self,
        grad_cross_stream,
        norm_two,
        (ProductFill("patch_", grad_ckv.reshape(tokens_here, -1), cross_w, (0, 2 * wide)),),
        mlp_part,
    )
    mlp_sum = summed(mlp_terms)
    grad_self_out = weight_grad(self_branch, self_attended).astype(jnp.bfloat16)
    self_out_part = scatter_chips(grad_self_out)
    partial_one, grad_self_in, cross_terms, _, grad_patches = attention_back(
        6,
        after(self_branch, grad_self_out),
        self_w,
        (0, wide, 3 * wide),
        (self_qkv, 0),
        (self_qkv, wide),
        self_marks,
        (normed_one, normed_one),
        None,
        (patch_partial.reshape(rows, length, -1), None),
        cross_part,
    )
    cross_sum = summed(cross_terms)
    grad_tokens, gain_sums, self_out_terms, self_terms = leave(
        7,
        partial_one,
        local_tokens,
        grad_self_stream,
        norm_one,
        jnp.concatenate([part_two, part_three]),
        grad_self_in,
        self_out_part,
    )
    held = gain_self.shape[0]
    place = lax.axis_index(("chip", "core")) * held
    gain_sums = lax.dynamic_slice_in_dim(gain_sums, place, held, axis=1)
    self_sum = summed(self_terms)
    return (
        output,
        grad_tokens.astype(jnp.float32),
        grad_patches.astype(jnp.float32),
        gain_sums[0],
        self_sum[:, :wide],
        self_sum[:, wide : 2 * wide],
        self_sum[:, 2 * wide :],
        summed(self_out_terms).T,
        gain_sums[1],
        cross_sum[:, 2 * wide : 3 * wide],
        cross_sum[:, :wide],
        cross_sum[:, wide : 2 * wide],
        cross_sum[:, 3 * wide :].T,
        gain_sums[2],
        mlp_sum[:, :hidden_wide],
        mlp_sum[:, hidden_wide:],
        down_sum,
    )


def solution(mesh):
    devices = mesh.devices.reshape(mesh.shape["dp"] // 2, 2, 2, mesh.shape["seq"] // 2)
    fine = Mesh(devices, AXES)
    dp = ("chip", "core")
    seq = ("zh", "zp")
    stream = P(dp, seq, None)
    rows = P(dp, None)
    inward = P(dp, seq)
    outward = P(seq, dp)
    vector = P(dp)
    block = (vector, inward, inward, inward, outward)
    weights = block + block + (vector, inward, inward, outward)
    return jax.shard_map(
        shards,
        mesh=fine,
        in_specs=(stream, stream, rows, rows, rows) + weights + (stream,),
        out_specs=(stream, stream, stream) + weights,
        check_vma=False,
    )
```

```python
import itertools

import jax
import jax.numpy as jnp
from jax import lax
from jax.experimental import pallas as pl
from jax.experimental.pallas import tpu as pltpu
from jax.sharding import Mesh
from jax.sharding import PartitionSpec as P

HD = 128


epsilon = 1e-06
masked_value = -1e30

AXES = ("chip", "core", "zh", "zp")


def moves(chips, source_of):
    pairs = []
    for chip, core, zh, zp in itertools.product(range(chips), range(2), range(2), range(2)):
        a, b, c, d = source_of(chip, core, zh, zp)
        pairs.append((((a * 2 + b) * 2 + c) * 2 + d, ((chip * 2 + core) * 2 + zh) * 2 + zp))
    return pairs


def permute(values, source_of):
    return lax.ppermute(values, AXES, moves(lax.axis_size("chip"), source_of))


def swapped(values):
    return permute(values, lambda chip, core, zh, zp: (chip, zh, core, zp))


def swapped_other(values):
    return permute(values, lambda chip, core, zh, zp: (chip, 1 - zh, core, zp))


def relative(values):
    rows, length = values.shape
    cut = values.reshape(rows, 2, 2, length // 4)
    cut = jnp.where(lax.axis_index("core") == 1, cut[:, ::-1], cut)
    cut = jnp.where(lax.axis_index("zp") == 1, cut[:, :, ::-1], cut)
    return cut.reshape(rows, length)


def after(values, *others):
    return lax.optimization_barrier((values,) + others)[0]


def exchange(shards_of):
    return swapped(shards_of), swapped_other(shards_of)


def pair_up(exchanged):
    first, second = exchanged
    low = lax.axis_index("zh") == 0
    return jnp.concatenate([jnp.where(low, first, second), jnp.where(low, second, first)], axis=0)


def gather_chips(pair):
    return lax.all_gather(pair, "chip", axis=0, tiled=True)


def scatter_chips(grads):
    return lax.psum_scatter(
        grads.astype(jnp.bfloat16), "chip", scatter_dimension=0, tiled=True
    )


def normalize(values, gain_vec):
    factor = lax.rsqrt(jnp.mean(values * values, axis=-1, keepdims=True) + epsilon)
    return values * factor * gain_vec


def norm_back(values, gain_vec, gradient):
    normed_value, pullback = jax.vjp(lambda inputs: normalize(inputs, gain_vec), values)
    return pullback(gradient)[0]


def gain_part(values, gradient):
    factor = lax.rsqrt(jnp.mean(values * values, axis=-1, keepdims=True) + epsilon)
    return jnp.sum(gradient * values * factor, axis=(0, 1))


MESH = pl.DeviceIdType.MESH
ANY = pl.BlockSpec(memory_space=pl.ANY)
VMEM = pl.BlockSpec(memory_space=pltpu.VMEM)
PARTS = 4


def across_plane(axis):
    chip = lax.axis_index("chip")
    x, y = chip % 2, chip // 2
    return y * 2 + 1 - x if axis == 0 else (1 - y) * 2 + x


def greet(everyone, plane=False):
    core, zh, zp = lax.axis_index("core"), lax.axis_index("zh"), lax.axis_index("zp")
    barrier = pltpu.get_barrier_semaphore()
    count = 0
    for a, b, c in itertools.product(range(2), range(2), range(2)):
        if (a, b, c) == (0, 0, 0) or (b and not everyone):
            continue
        pl.semaphore_signal(
            barrier,
            inc=1,
            device_id={"core": (core + a) % 2, "zh": (zh + b) % 2, "zp": (zp + c) % 2},
            device_id_type=MESH,
        )
        count += 1
    if plane:
        chips = lax.axis_size("chip")
        for a, b in itertools.product(range(1, chips), range(2)):
            pl.semaphore_signal(
                barrier,
                inc=1,
                device_id={
                    "chip": (lax.axis_index("chip") + a) % chips,
                    "core": (core + b) % 2,
                },
                device_id_type=MESH,
            )
            count += 1
    pl.semaphore_wait(barrier, count)


def to_core(src, dst, send, recv):
    return pltpu.make_async_remote_copy(
        src, dst, send, recv, device_id={"core": 1 - lax.axis_index("core")}, device_id_type=MESH
    )


def to_zp(src, dst, send, recv):
    return pltpu.make_async_remote_copy(
        src, dst, send, recv, device_id={"zp": 1 - lax.axis_index("zp")}, device_id_type=MESH
    )


def to_swapped(src, dst, send, recv):
    core, zh = lax.axis_index("core"), lax.axis_index("zh")
    return pltpu.make_async_remote_copy(
        src, dst, send, recv, device_id={"core": zh, "zh": core}, device_id_type=MESH
    )


class Exchange:
    def __init__(self, src, pair, sems):
        self.src, self.pair, self.sems = src, pair, sems
        self.core, self.zh = lax.axis_index("core"), lax.axis_index("zh")
        rows = src.shape[0]
        self.mine = pair.at[pl.ds(pl.multiple_of(self.core * rows, rows), rows)]
        self.slots = [pair.at[pl.ds(a * rows, rows)] for a in range(2)]

    def far(self):
        return pltpu.make_async_remote_copy(
            self.src,
            self.mine,
            self.sems.at[0],
            self.sems.at[2 + self.core],
            device_id={"core": self.zh, "zh": 1 - self.zh},
            device_id_type=MESH,
        )

    def near(self):
        return pltpu.make_async_remote_copy(
            self.src,
            self.mine,
            self.sems.at[1],
            self.sems.at[2 + self.core],
            device_id={"core": 1 - self.core},
            device_id_type=MESH,
        )

    def own(self):
        return pltpu.make_async_copy(self.src, self.mine, self.sems.at[2 + self.core])

    def start(self):
        self.far().start()

        @pl.when(self.core == self.zh)
        def _():
            self.own().start()

        @pl.when(self.core != self.zh)
        def _():
            self.near().start()

    def finish(self):
        self.far().wait_send()

        @pl.when(self.core != self.zh)
        def _():
            self.near().wait_send()

        for a in range(2):
            pltpu.make_async_copy(self.src, self.slots[a], self.sems.at[2 + a]).wait()


class Spread:
    def __init__(self, block, gathered, sems):
        self.block, self.gathered, self.sems = block, gathered, sems
        self.length = block.shape[1]
        self.step = 2 * self.length // PARTS

    def src(self, k):
        return self.block.at[k // (PARTS // 2), pl.ds(pl.multiple_of(k % (PARTS // 2) * self.step, self.step), self.step)]

    def dst(self, k, slot):
        return self.gathered.at[
            k // (PARTS // 2),
            pl.ds(
                pl.multiple_of(slot * self.length + k % (PARTS // 2) * self.step, self.step),
                self.step,
            ),
        ]

    def beside(self, k):
        return to_zp(self.src(k), self.dst(k, 1), self.sems.at[0, k], self.sems.at[1, k])

    def across(self, k):
        return to_core(self.src(k), self.dst(k, 2), self.sems.at[2, k], self.sems.at[3, k])

    def corner(self, k):
        return to_core(self.dst(k, 1), self.dst(k, 3), self.sems.at[4, k], self.sems.at[5, k])

    def own(self, k):
        return pltpu.make_async_copy(self.src(k), self.dst(k, 0), self.sems.at[6, k])

    def start(self, k):
        self.beside(k).start()
        self.across(k).start()
        self.own(k).start()

    def relay(self, k):
        self.beside(k).wait_recv()
        self.corner(k).start()

    def finish(self, k):
        self.beside(k).wait_send()
        self.across(k).wait()
        self.corner(k).wait()
        self.own(k).wait()


class Collect:
    def __init__(self, partial, arrived, outgoing, landed, sems):
        self.partial, self.arrived = partial, arrived
        self.outgoing, self.landed, self.sems = outgoing, landed, sems
        self.length = outgoing.shape[1]
        self.step = 2 * self.length // PARTS

    def at(self, ref, k, block):
        return ref.at[
            k // (PARTS // 2),
            pl.ds(
                pl.multiple_of(block * self.length + k % (PARTS // 2) * self.step, self.step),
                self.step,
            ),
        ]

    def crossing(self, k, block):
        return to_core(
            self.at(self.partial, k, 2 + block),
            self.at(self.arrived, k, block),
            self.sems.at[2 * block, k],
            self.sems.at[2 * block + 1, k],
        )

    def landing(self, k):
        return to_zp(
            self.at(self.outgoing, k, 0),
            self.at(self.landed, k, 0),
            self.sems.at[4, k],
            self.sems.at[5, k],
        )

    def start(self):
        for block in (1, 0):
            self.start_block(block)

    def start_block(self, block):
        for k in range(PARTS):
            self.crossing(k, block).start()

    def forward(self, k):
        self.crossing(k, 1).wait_recv()
        self.at(self.outgoing, k, 0)[...] = (
            self.at(self.partial, k, 1)[...].astype(jnp.float32)
            + self.at(self.arrived, k, 1)[...].astype(jnp.float32)
        ).astype(jnp.bfloat16)
        self.landing(k).start()

    def total(self, k):
        self.crossing(k, 0).wait_recv()
        self.landing(k).wait_recv()
        return (
            self.at(self.partial, k, 0)[...].astype(jnp.float32)
            + self.at(self.arrived, k, 0)[...].astype(jnp.float32)
        ) + self.at(self.landed, k, 0)[...].astype(jnp.float32)

    def finish(self, k):
        self.crossing(k, 0).wait_send()
        self.crossing(k, 1).wait_send()
        self.landing(k).wait_send()


class Unpair:
    def __init__(self, part, terms, sems):
        self.part, self.terms, self.sems = part, terms, sems
        self.core, self.zh = lax.axis_index("core"), lax.axis_index("zh")
        self.rows = part.shape[0] // 2

    def piece(self, p):
        return self.part.at[pl.ds(p * self.rows, self.rows)]

    def remote(self, p):
        return pltpu.make_async_remote_copy(
            self.piece(p),
            self.terms.at[self.zh],
            self.sems.at[p],
            self.sems.at[2 + self.zh],
            device_id={"core": p, "zh": self.core},
            device_id_type=MESH,
        )

    def own(self, p):
        return pltpu.make_async_copy(
            self.piece(p), self.terms.at[self.zh], self.sems.at[2 + self.zh]
        )

    def stays(self, p):
        return jnp.logical_and(self.core == p, self.zh == p)

    def start(self):
        for p in range(2):

            @pl.when(self.stays(p))
            def _(p=p):
                self.own(p).start()

            @pl.when(jnp.logical_not(self.stays(p)))
            def _(p=p):
                self.remote(p).start()

    def finish(self):
        for p in range(2):

            @pl.when(jnp.logical_not(self.stays(p)))
            def _(p=p):
                self.remote(p).wait_send()

            pltpu.make_async_copy(
                self.piece(p), self.terms.at[p], self.sems.at[2 + p]
            ).wait()


class Swap:
    def __init__(self, block, target, sems):
        self.block, self.target, self.sems = block, target, sems
        self.swaps = lax.axis_index("core") != lax.axis_index("zh")
        self.step = 2 * block.shape[1] // PARTS

    def at(self, ref, k):
        return ref.at[
            k // (PARTS // 2), pl.ds(pl.multiple_of(k % (PARTS // 2) * self.step, self.step), self.step)
        ]

    def remote(self, k):
        return to_swapped(
            self.at(self.block, k), self.at(self.target, k), self.sems.at[0, k], self.sems.at[1, k]
        )

    def own(self, k):
        return pltpu.make_async_copy(self.at(self.block, k), self.at(self.target, k), self.sems.at[1, k])

    def start(self, k):
        @pl.when(self.swaps)
        def _():
            self.remote(k).start()

        @pl.when(jnp.logical_not(self.swaps))
        def _():
            self.own(k).start()

    def arrive(self, k):
        self.own(k).wait()

    def finish(self, k):
        @pl.when(self.swaps)
        def _():
            self.remote(k).wait_send()


def each(body):
    lax.fori_loop(0, PARTS, lambda k, carry: (body(k), carry)[1], 0)


class Moves:
    def __init__(self, loads, stores):
        self.loads, self.stores, self.waited, self.going = loads, stores, set(), []

    def start(self, *names):
        for name in names:
            if name in self.loads:
                self.loads[name].start()

    def ready(self, *names):
        for name in names:
            if name in self.loads and name not in self.waited:
                self.waited.add(name)
                self.loads[name].wait()

    def store(self, *names):
        for name in names:
            if name in self.stores:
                self.stores[name].start()
                self.going.append(name)

    def end(self):
        for name in self.going:
            self.stores[name].wait()


def kernel_call(number, name, inputs, outs, scratch, body, lazy=(), eager=(), columns=None):
    columns = columns or {}
    lazy = [key for key in lazy if key in inputs]
    eager = [key for key in eager if key in outs]
    scratch = dict(scratch)
    for key in lazy:
        shape = inputs[key].shape
        if key in columns:
            shape = (shape[0], columns[key][1])
        scratch["lazy_" + key] = pltpu.VMEM(shape, inputs[key].dtype)
    for key in eager:
        scratch["eager_" + key] = pltpu.VMEM(outs[key][0].shape, outs[key][0].dtype)
    scratch["move_sems"] = pltpu.SemaphoreType.DMA((max(1, len(lazy) + len(eager)),))
    names = list(inputs) + list(outs) + list(scratch)

    def kernel(*given):
        refs = dict(zip(names, given))
        sems = refs["move_sems"]
        loads, stores = {}, {}
        for number, key in enumerate(lazy):
            here, source = refs["lazy_" + key], refs[key]
            if key in columns:
                source = source.at[:, pl.ds(*columns[key])]
            loads[key] = pltpu.make_async_copy(source, here, sems.at[number])
            refs[key] = here
        for number, key in enumerate(eager):
            here = refs["eager_" + key]
            stores[key] = pltpu.make_async_copy(here, refs[key], sems.at[len(lazy) + number])
            refs[key] = here
        body(refs, Moves(loads, stores))

    results = pl.pallas_call(
        kernel,
        out_shape=tuple(shape for shape, _ in outs.values()),
        in_specs=[ANY if key in lazy else VMEM for key in inputs],
        out_specs=tuple(ANY if key in eager else spec for key, (_, spec) in outs.items()),
        scratch_shapes=list(scratch.values()),
        compiler_params=pltpu.CompilerParams(
            collective_id=number,
            has_side_effects=number is not None,
            vmem_limit_bytes=61 * 1024 * 1024,
        ),
        name=name,
    )(*inputs.values())
    return dict(zip(outs, results))


def collect_scratch(tag, rows, length, width):
    return {
        tag + "arrived": pltpu.VMEM((rows, 2 * length, width), jnp.bfloat16),
        tag + "outgoing": pltpu.VMEM((rows, length, width), jnp.bfloat16),
        tag + "landed": pltpu.VMEM((rows, length, width), jnp.bfloat16),
        tag + "collect_sems": pltpu.SemaphoreType.DMA((6, PARTS)),
    }


def collect_of(refs, tag, partial):
    return Collect(
        refs[partial],
        refs[tag + "arrived"],
        refs[tag + "outgoing"],
        refs[tag + "landed"],
        refs[tag + "collect_sems"],
    )


def shape_of(shape, dtype):
    return jax.ShapeDtypeStruct(shape, dtype)


def gathered_out(rows, length, width):
    return (shape_of((rows, 4 * length, width), jnp.bfloat16), ANY)


def pair_out(shard):
    return (shape_of((2 * shard.shape[0], shard.shape[1]), shard.dtype), ANY)


def terms_out(part):
    return (shape_of((2, part.shape[0] // 2, part.shape[1]), part.dtype), ANY)


class PlaneGather:
    def __init__(self, whole, columns, sems):
        self.whole, self.columns, self.sems = whole, columns, sems
        self.rows = whole.shape[0] // 4

    def half(self, chip, which):
        start, size = self.columns
        return self.whole.at[
            pl.ds(pl.multiple_of(chip * self.rows, self.rows), self.rows),
            pl.ds(start + which * (size // 2), size // 2),
        ]

    def own(self, axis, which):
        ref = self.half(lax.axis_index("chip"), which)
        return self.copy(ref, axis, 2 * axis + which)

    def passed(self, which):
        ref = self.half(across_plane(which), which)
        return self.copy(ref, 1 - which, 4 + which)

    def copy(self, ref, axis, number):
        return pltpu.make_async_remote_copy(
            ref,
            ref,
            self.sems.at[0, number],
            self.sems.at[1, number],
            device_id={"chip": across_plane(axis)},
            device_id_type=MESH,
        )

    def start(self):
        for axis in range(2):
            self.own(axis, axis).start()
        for axis in range(2):
            self.own(axis, 1 - axis).start()

    def relay(self):
        for which in range(2):
            self.own(which, which).wait_recv()
            self.passed(which).start()

    def finish(self):
        for axis in range(2):
            self.own(axis, axis).wait_send()
            self.own(axis, 1 - axis).wait()
            self.passed(axis).wait()


class SwapWhole:
    def __init__(self, array, target, sems):
        self.array, self.target, self.sems = array, target, sems
        self.swaps = lax.axis_index("core") != lax.axis_index("zh")

    def remote(self):
        return to_swapped(self.array, self.target, self.sems.at[0], self.sems.at[1])

    def own(self):
        return pltpu.make_async_copy(self.array, self.target, self.sems.at[1])

    def start(self):
        @pl.when(self.swaps)
        def _():
            self.remote().start()

        @pl.when(jnp.logical_not(self.swaps))
        def _():
            self.own().start()

    def finish(self):
        self.own().wait()

        @pl.when(self.swaps)
        def _():
            self.remote().wait_send()


class GainGather:
    def __init__(self, own, slots, whole, sems):
        self.own, self.slots, self.whole, self.sems = own, slots, whole, sems
        self.chips = lax.axis_size("chip")
        self.chip, self.core = lax.axis_index("chip"), lax.axis_index("core")

    def others(self):
        for number in range(1, 2 * self.chips):
            yield number, (self.chip + number // 2) % self.chips, (self.core + number % 2) % 2

    def send(self, number, chip, core):
        return pltpu.make_async_remote_copy(
            self.own,
            self.slots.at[self.chip * 2 + self.core],
            self.sems.at[0, number],
            self.sems.at[1, self.chip * 2 + self.core],
            device_id={"chip": chip, "core": core},
            device_id_type=MESH,
        )

    def start(self):
        for other in self.others():
            self.send(*other).start()
        self.slots.at[self.chip * 2 + self.core][...] = self.own[...]

    def finish(self):
        for number, chip, core in self.others():
            self.send(number, chip, core).wait_send()
            place = chip * 2 + core
            pltpu.make_async_copy(self.own, self.slots.at[place], self.sems.at[1, place]).wait()
        held = self.own.shape[1]
        for place in range(2 * self.chips):
            self.whole[:, place * held : (place + 1) * held] = self.slots[place]


def head(number, block, beside, marks, gains, first, second):
    rows, length, width = block.shape
    depth, size = first[0].shape
    chips = lax.axis_size("chip")
    in_plane = chips == 4
    if not in_plane:
        gains = lax.all_gather(gains, ("chip", "core"), axis=1, tiled=True)

    def body(refs, moves):
        swap = Swap(refs["block"], refs["here"], refs["swap_sems"])
        marks_swap = SwapWhole(refs["marks"], refs["marks_here"], refs["marks_sems"])
        spread_work = Spread(refs["normed"], refs["gathered"], refs["spread_sems"])
        if in_plane:
            chip = lax.axis_index("chip")
            place = refs["whole"].at[pl.ds(pl.multiple_of(chip * 2 * depth, 2 * depth), 2 * depth)]
            gain_work = GainGather(
                refs["gains"], refs["gain_slots"], refs["gains_whole"], refs["gain_sems"]
            )
        else:
            place = refs["whole"]
        works = [
            Exchange(
                refs["first%d" % i],
                place.at[:, pl.ds(i * size, size)],
                refs["exchange_sems"].at[i],
            )
            for i in range(len(first))
        ]
        beside_swap = Swap(refs["beside"], refs["beside_here"], refs["beside_swap_sems"])
        beside_work = Spread(refs["beside_here"], refs["beside_gathered"], refs["beside_sems"])
        later = [
            Exchange(
                refs["second%d" % i],
                refs["pair"].at[:, pl.ds(i * size, size)],
                refs["exchange_sems"].at[len(first) + i],
            )
            for i in range(len(second))
        ]
        greet(True, in_plane)
        marks_swap.start()

        def norm_and_send(k):
            swap.arrive(k)
            values = swap.at(refs["here"], k)[...].astype(jnp.float32)
            spread_work.src(k)[...] = normalize(values, refs["gains_whole"][0:1, :]).astype(
                jnp.bfloat16
            )
            spread_work.start(k)

        planes = [
            PlaneGather(refs["whole"], (i * size, size), refs["plane_sems"].at[i])
            for i in range(len(first))
        ]
        last = len(works) - 1
        works[0].start()
        if in_plane:
            gain_work.start()
            gain_work.finish()
        else:
            refs["gains_whole"][...] = refs["gains"][...]
        for i, work in enumerate(works):
            work.finish()
            if in_plane:
                planes[i].start()
            if i < last:
                works[i + 1].start()
            if i == 0:
                each(swap.start)
            if i == last - 1:
                each(beside_swap.start)
            if in_plane and i:
                planes[i - 1].relay()
            if i == 1:
                each(norm_and_send)
            if i == last:
                each(spread_work.relay)

        def pass_on(k):
            beside_swap.arrive(k)
            beside_work.start(k)

        later[0].start()
        pass_on(0)
        pass_on(1)
        if in_plane:
            planes[last].relay()
        for k in range(2, PARTS):
            pass_on(k)
        for i, work in enumerate(later):
            if i + 1 < len(later):
                later[i + 1].start()
            if i == 1:
                each(beside_work.relay)
            work.finish()
        each(beside_work.finish)
        each(beside_swap.finish)
        each(spread_work.finish)
        each(swap.finish)
        if in_plane:
            for plane in planes:
                plane.finish()
        marks_swap.finish()

    whole_rows = 8 * depth if in_plane else 2 * depth
    results = kernel_call(
        number,
        "head",
        {
            "block": block,
            "beside": beside,
            "marks": marks,
            "gains": gains,
            **{"first%d" % i: shard for i, shard in enumerate(first)},
            **{"second%d" % i: shard for i, shard in enumerate(second)},
        },
        {
            "here": (shape_of(block.shape, block.dtype), VMEM),
            "marks_here": (shape_of(marks.shape, marks.dtype), VMEM),
            "gains_whole": (shape_of((gains.shape[0], width), jnp.float32), VMEM),
            "gathered": gathered_out(rows, length, width),
            "whole": (shape_of((whole_rows, len(first) * size), jnp.bfloat16), ANY),
            "beside_gathered": gathered_out(rows, length, width),
            "pair": (shape_of((2 * depth, len(second) * size), jnp.bfloat16), ANY),
        },
        {
            "normed": pltpu.VMEM((rows, length, width), jnp.bfloat16),
            "spread_sems": pltpu.SemaphoreType.DMA((7, PARTS)),
            "swap_sems": pltpu.SemaphoreType.DMA((2, PARTS)),
            "beside_here": pltpu.VMEM((rows, length, width), jnp.bfloat16),
            "beside_sems": pltpu.SemaphoreType.DMA((7, PARTS)),
            "beside_swap_sems": pltpu.SemaphoreType.DMA((2, PARTS)),
            "marks_sems": pltpu.SemaphoreType.DMA((2,)),
            "exchange_sems": pltpu.SemaphoreType.DMA((len(first) + len(second), 4)),
            "plane_sems": pltpu.SemaphoreType.DMA((len(first), 2, 6)),
            "gain_slots": pltpu.VMEM((2 * chips,) + gains.shape, jnp.float32),
            "gain_sems": pltpu.SemaphoreType.DMA((2, 2 * chips)),
        },
        body,
    )
    whole = results["whole"] if in_plane else gather_chips(results["whole"])
    return (
        results["here"],
        results["marks_here"],
        results["gains_whole"],
        results["gathered"],
        results["beside_gathered"],
        whole,
        results["pair"],
    )


class ProductFill:
    def __init__(self, tag, left, right, columns):
        self.tag = tag
        self.columns = {tag + "right": columns}
        rows = left.shape[0]
        self.size = 256
        self.tiles = rows // self.size
        self.inputs = {tag + "left": left, tag + "right": right}
        self.outs = {tag + "out": (shape_of((rows, right.shape[0]), jnp.bfloat16), VMEM)}
        self.scratch = {}

    def tile(self, refs, i):
        at = pl.ds(pl.multiple_of(i * self.size, self.size), self.size)
        refs[self.tag + "out"].at[at][...] = across(
            refs[self.tag + "left"].at[at][...],
            refs[self.tag + "right"][...],
        ).astype(jnp.bfloat16)

    def end(self, refs):
        pass


def fill_in(refs, fill, part, parts):
    if fill is not None:
        first, last = fill.tiles * part // parts, fill.tiles * (part + 1) // parts
        lax.fori_loop(first, last, lambda i, carry: (fill.tile(refs, i), carry)[1], 0)


def norm_slope(values, gain, gradient):
    factor = lax.rsqrt(jnp.mean(values * values, axis=-1, keepdims=True) + epsilon)
    scaled = gain * gradient
    inner = jnp.mean(scaled * values, axis=-1, keepdims=True)
    return factor * scaled - values * (factor * factor * factor * inner), gradient * values * factor


def turn_back(number, partial, values, stream, gain, fills, *parts):
    rows, length, width = values.shape
    first, second = (tuple(fills) + (None, None))[:2]

    def body(refs, moves):
        collect_work = collect_of(refs, "", "partial")
        spread_work = Spread(refs["branch"], refs["gathered"], refs["spread_sems"])
        works = [
            Unpair(refs["part%d" % i], refs["terms%d" % i], refs["unpair_sems"].at[i])
            for i in range(len(parts))
        ]
        part_names = ["part%d" % i for i in range(len(parts))]
        fill_names = [[*fill.inputs] for fill in fills]
        moves.start(*part_names, "partial", "values", "stream", *sum(fill_names, []))
        greet(bool(parts))
        moves.ready(*part_names)
        for work in works:
            work.start()
        moves.ready("partial")
        collect_work.start()
        each(collect_work.forward)
        refs["gain_sum"][...] = jnp.zeros_like(refs["gain_sum"])

        def slope_and_send(k):
            slope, terms = norm_slope(
                collect_work.at(refs["values"], k, 0)[...].astype(jnp.float32),
                refs["gain"][...],
                collect_work.total(k),
            )
            sums = collect_work.at(refs["stream"], k, 0)[...].astype(jnp.float32) + slope
            collect_work.at(refs["after"], k, 0)[...] = sums
            spread_work.src(k)[...] = sums.astype(jnp.bfloat16)
            spread_work.start(k)
            refs["gain_sum"][...] += jnp.sum(terms, axis=0, keepdims=True)

        moves.ready("values", "stream")
        moves.ready(*sum(fill_names[:1], []))
        if first is None:
            each(slope_and_send)
        else:
            for k in range(PARTS):
                fill_in(refs, first, k, PARTS)
                slope_and_send(k)
        moves.store("after")
        for fill in fills[:1]:
            moves.store(*fill.outs)
        moves.ready(*sum(fill_names[1:], []))
        fill_in(refs, second, 0, 1)
        for fill in fills[1:]:
            moves.store(*fill.outs)
        each(spread_work.relay)
        each(spread_work.finish)
        each(collect_work.finish)
        for work in works:
            work.finish()
        for fill in fills:
            fill.end(refs)
        moves.end()

    extra = {"inputs": {}, "outs": {}, "scratch": {}}
    for fill in fills:
        for kind, found in extra.items():
            found.update(getattr(fill, kind))
    results = kernel_call(
        number,
        "turn_back",
        {
            "partial": partial,
            "values": values,
            "stream": stream,
            "gain": gain[None],
            **{"part%d" % i: part for i, part in enumerate(parts)},
            **extra["inputs"],
        },
        {
            "after": (shape_of(values.shape, jnp.float32), VMEM),
            "gathered": gathered_out(rows, length, width),
            "gain_sum": (shape_of((1, width), jnp.float32), VMEM),
            **{"terms%d" % i: terms_out(part) for i, part in enumerate(parts)},
            **extra["outs"],
        },
        {
            **collect_scratch("", rows, length, width),
            "branch": pltpu.VMEM((rows, length, width), jnp.bfloat16),
            "spread_sems": pltpu.SemaphoreType.DMA((7, PARTS)),
            "unpair_sems": pltpu.SemaphoreType.DMA((max(1, len(parts)), 4)),
            **extra["scratch"],
        },
        body,
        lazy=("partial", "values", "stream")
        + tuple("part%d" % i for i in range(len(parts)))
        + tuple(extra["inputs"]),
        eager=("after",)
        + tuple(name for name, (_, spec) in extra["outs"].items() if spec is VMEM),
        columns={key: found for fill in fills for key, found in fill.columns.items()},
    )
    return (
        (results["after"], results["gathered"], results["gain_sum"])
        + tuple(results["terms%d" % i] for i in range(len(parts)))
        + tuple(results[name] for fill in fills for name in fill.outs)
    )


class OutWork:
    def __init__(self, collect_work, swap, base):
        self.collect_work, self.swap, self.base = collect_work, swap, base

    def begin(self):
        self.collect_work.start()

    def forward(self):
        each(self.collect_work.forward)

    def leave_part(self, k):
        total = self.collect_work.total(k)
        if self.base is not None:
            total = total + self.swap.at(self.base, k)[...]
        self.swap.at(self.swap.block, k)[...] = total.astype(jnp.bfloat16)
        self.swap.start(k)

    def end(self):
        each(self.swap.arrive)
        each(self.swap.finish)
        each(self.collect_work.finish)


def head_at(ref, r, h, offset):
    return ref.at[r, :, pl.ds(pl.multiple_of(offset + h * HD, HD), HD)]


def across(left, right):
    return lax.dot_general(
        left, right, (((1,), (1,)), ((), ())), preferred_element_type=jnp.float32
    )


def down(left, right):
    return lax.dot_general(
        left, right, (((0,), (0,)), ((), ())), preferred_element_type=jnp.float32
    )


def masked_probability(refs, r, queries, key_rows):
    scores = across(queries, key_rows) * HD ** (-0.5)
    allowed = jnp.logical_and(
        refs["query_mark"][r] == refs["key_mark"][r],
        refs["query_place"][...] >= refs["key_place"][...],
    )
    scores = jnp.where(allowed, scores, masked_value)
    shifted = jnp.exp(scores - jnp.max(scores, axis=-1, keepdims=True))
    return shifted / jnp.sum(shifted, axis=-1, keepdims=True)


def rows_of(ref, t, size):
    per_row = ref.shape[1] // size
    return ref.at[t // per_row, pl.ds(pl.multiple_of(t % per_row * size, size), size)]


def attention_back(
    number, branch, weights, places, queries, pairs, marks, lefts, attended, out, part
):
    query_place, pair_place, out_place = places
    (query_array, query_at), (pair_array, pair_at) = queries, pairs
    same = query_array is pair_array
    rows, length, width = branch.shape
    wide = weights.shape[1] // 4
    heads = wide // HD
    block = (rows, length // 4, width)
    flat = (rows * length, width)
    inputs = {
        "branch": branch,
        "weights": weights,
        "out_weights": weights,
        "queries": query_array,
        "query_mark": marks[0],
        "key_mark": marks[1],
        "query_place": marks[2],
        "key_place": marks[3],
        "left0": lefts[0].reshape(flat),
        "part": part,
    }
    if not same:
        inputs["pairs"] = pair_array
        inputs["left1"] = lefts[1].reshape(flat)
    if attended is not None:
        inputs["attended"] = attended.reshape(rows * length, wide)
    if out is not None:
        inputs["partial"] = out[0]
        if out[1] is not None:
            inputs["base"] = out[1]
    grad_columns = wide * (4 if attended is not None else 3)
    outs = {
        "input_partial": (shape_of((rows, length, width), jnp.bfloat16), VMEM),
        "weight_grads": (shape_of((width, grad_columns), jnp.bfloat16), ANY),
        "terms": terms_out(part),
    }
    scratch = {
        "grad_out": pltpu.VMEM((rows, length, wide), jnp.bfloat16),
        "stage": pltpu.VMEM((2, 256, grad_columns), jnp.bfloat16),
        "stage_sems": pltpu.SemaphoreType.DMA((2,)),
        "unpair_sems": pltpu.SemaphoreType.DMA((4,)),
    }
    if out is not None:
        outs["out"] = (shape_of(block, jnp.bfloat16), ANY)
        scratch.update(collect_scratch("", *block))
        scratch["leaving"] = pltpu.VMEM(block, jnp.bfloat16)
        scratch["swap_sems"] = pltpu.SemaphoreType.DMA((2, PARTS))
    if same:
        scratch["grad_all"] = pltpu.VMEM((rows, length, 3 * wide), jnp.bfloat16)
    else:
        scratch["grad_queries"] = pltpu.VMEM((rows, length, wide), jnp.bfloat16)
        outs["grad_pairs"] = (shape_of((rows, length, 2 * wide), jnp.bfloat16), VMEM)
    scale = HD ** (-0.5)
    total = rows * heads
    size = 256

    def body(refs, moves):
        unpair = Unpair(refs["part"], refs["terms"], refs["unpair_sems"])
        out_work = None
        if out is not None:
            out_work = OutWork(
                collect_of(refs, "", "partial"),
                Swap(refs["leaving"], refs["out"], refs["swap_sems"]),
                refs.get("base"),
            )
        grad_queries = refs["grad_all"] if same else refs["grad_queries"]
        grad_pairs = refs["grad_all"] if same else refs["grad_pairs"]
        pair_refs = refs["queries"] if same else refs["pairs"]
        pair_out = wide if same else 0

        def form_grad_out(t):
            rows_of(refs["grad_out"], t, size)[...] = jnp.dot(
                rows_of(refs["branch"], t, size)[...],
                refs["out_weights"][...],
                preferred_element_type=jnp.float32,
            ).astype(jnp.bfloat16)

        def one(i):
            r, h = i // heads, i % heads
            queries_here = head_at(refs["queries"], r, h, query_at)[...]
            key_rows = head_at(pair_refs, r, h, pair_at)[...]
            value_rows = head_at(pair_refs, r, h, pair_at + wide)[...]
            grad_here = head_at(refs["grad_out"], r, h, 0)[...]
            probability = masked_probability(refs, r, queries_here, key_rows)
            grad_values = down(probability.astype(jnp.bfloat16), grad_here)
            grad_probs = across(grad_here, value_rows)
            inner = jnp.sum(probability * grad_probs, axis=-1, keepdims=True)
            grad_scores = (probability * (grad_probs - inner)).astype(jnp.bfloat16)
            query_terms = jnp.dot(grad_scores, key_rows, preferred_element_type=jnp.float32)
            key_terms = down(grad_scores, queries_here)
            head_at(grad_queries, r, h, 0)[...] = (query_terms * scale).astype(jnp.bfloat16)
            head_at(grad_pairs, r, h, pair_out)[...] = (key_terms * scale).astype(jnp.bfloat16)
            head_at(grad_pairs, r, h, pair_out + wide)[...] = grad_values.astype(jnp.bfloat16)

        def form_partial(t):
            columns = (query_place, 3 * wide if same else wide)
            rows_of(refs["input_partial"], t, size)[...] = across(
                rows_of(grad_queries, t, size)[...],
                refs["weights"].at[:, pl.ds(*columns)][...],
            ).astype(jnp.bfloat16)

        def written(i):
            return pltpu.make_async_copy(
                refs["stage"].at[i % 2],
                refs["weight_grads"].at[pl.ds(pl.multiple_of(i * size, size), size)],
                refs["stage_sems"].at[i % 2],
            )

        def form_grads(i):
            @pl.when(i >= 2)
            def _():
                written(i - 2).wait()

            at = pl.ds(pl.multiple_of(i * size, size), size)
            stage = refs["stage"].at[i % 2]

            def put(place, left, right):
                terms = right[...].reshape(rows * length, right.shape[-1])
                stage[:, place : place + right.shape[-1]] = down(left, terms).astype(jnp.bfloat16)

            put(query_place, refs["left0"].at[:, at][...], grad_queries)
            if not same:
                put(pair_place, refs["left1"].at[:, at][...], grad_pairs)
            if attended is not None:
                here = refs["branch"].at[:, :, at][...].reshape(rows * length, size)
                stage[:, out_place : out_place + wide] = down(here, refs["attended"][...]).astype(
                    jnp.bfloat16
                )
            written(i).start()

        def loop(count, work, stops=()):
            def step(i, carry):
                work(i)
                if out_work is not None:
                    for stop, k in stops:

                        @pl.when(i == stop)
                        def _(k=k):
                            out_work.leave_part(k)

                return carry

            lax.fori_loop(0, count, step, 0)

        moves.start("part", "partial", "branch", "out_weights", "queries", "pairs", "base")
        moves.start("left0", "left1", "attended", "weights")
        greet(True)
        moves.ready("part")
        unpair.start()
        moves.ready("partial")
        if out_work is not None:
            out_work.begin()
        moves.ready("branch", "out_weights")
        loop(rows * length // size, form_grad_out)
        if out_work is not None:
            out_work.forward()
        moves.ready("queries", "pairs", "base")
        loop(total, one, ((total - 1, 0),))
        moves.store("grad_pairs")
        moves.ready("left0", "left1", "attended", "weights")
        loop(width // size, form_grads, ((1, 1), (3, 2), (5, 3)))
        loop(rows * length // size, form_partial)
        moves.store("input_partial")
        if out_work is not None:
            out_work.end()
        unpair.finish()
        for i in (width // size - 2, width // size - 1):
            written(i).wait()
        moves.end()

    big = ("part", "partial", "branch", "weights", "out_weights", "queries", "pairs", "base")
    results = kernel_call(
        number,
        "attention_back",
        inputs,
        outs,
        scratch,
        body,
        lazy=big + ("left0", "left1", "attended"),
        eager=("grad_pairs", "input_partial"),
        columns={"weights": (0, 3 * wide), "out_weights": (out_place, wide)},
    )
    return (
        results["input_partial"],
        results["weight_grads"],
        results["terms"],
        results.get("grad_pairs"),
        results.get("out"),
    )


def attention_turn(number, lefts, weights, places, marks, stream, gain, done=None, beside=None):
    query_place, pair_place, out_place = places
    same = lefts[0] is lefts[1]
    rows, length, width = lefts[0].shape
    wide = weights.shape[1] // 4
    heads = wide // HD
    quarter = length // 4
    size = 256
    out_at = out_place if done is None else 0
    columns = None
    if done is not None:
        columns = {"weights": (out_place, wide)}
    elif stream is None:
        columns = {"weights": (0, 3 * wide)}
    inputs = {"weights": weights}
    outs, scratch = {}, {}
    if done is None:
        inputs.update(
            {
                "left0": lefts[0],
                "query_mark": marks[0],
                "key_mark": marks[1],
                "query_place": marks[2],
                "key_place": marks[3],
            }
        )
        outs["queries"] = (
            shape_of((rows, length, wide * (3 if same else 1)), jnp.bfloat16),
            VMEM,
        )
        outs["attended"] = (shape_of((rows, length, wide), jnp.bfloat16), VMEM)
        if not same:
            inputs["left1"] = lefts[1]
            outs["pairs"] = (shape_of((rows, length, 2 * wide), jnp.bfloat16), VMEM)
    else:
        inputs["attended"] = done
    if stream is not None:
        inputs["stream"] = stream
        inputs["gain"] = gain[None]
        outs["after"] = (shape_of(stream.shape, jnp.float32), VMEM)
        outs["gathered"] = gathered_out(rows, quarter, width)
        scratch.update(
            {
                **collect_scratch("", rows, quarter, width),
                "partial": pltpu.VMEM((rows, length, width), jnp.bfloat16),
                "normed": pltpu.VMEM((rows, quarter, width), jnp.bfloat16),
                "spread_sems": pltpu.SemaphoreType.DMA((7, PARTS)),
            }
        )
    if beside is not None:
        inputs["beside"] = beside
        outs["beside_gathered"] = gathered_out(rows, quarter, width)
        outs["beside_here"] = (shape_of((rows, quarter, width), jnp.bfloat16), VMEM)
        scratch["beside_sems"] = pltpu.SemaphoreType.DMA((7, PARTS))
        scratch["beside_swap_sems"] = pltpu.SemaphoreType.DMA((2, PARTS))

    def body(refs, moves):
        if stream is not None:
            collect_work = collect_of(refs, "", "partial")
            spread_work = Spread(refs["normed"], refs["gathered"], refs["spread_sems"])
        if beside is not None:
            swap = Swap(refs["beside"], refs["beside_here"], refs["beside_swap_sems"])
            beside_work = Spread(
                refs["beside_here"], refs["beside_gathered"], refs["beside_sems"]
            )
        if done is None:
            pair_refs = refs["queries"] if same else refs["pairs"]
        pair_at = wide if same else 0

        def loop(count, work):
            lax.fori_loop(0, count, lambda i, carry: (work(i), carry)[1], 0)

        def form(left, place, columns, target):
            def tile(t):
                rows_of(target, t, size)[...] = jnp.dot(
                    rows_of(left, t, size)[...],
                    refs["weights"].at[:, pl.ds(place, columns)][...],
                    preferred_element_type=jnp.float32,
                ).astype(jnp.bfloat16)

            loop(rows * length // size, tile)

        def one(i):
            r, h = i // heads, i % heads
            probability = masked_probability(
                refs,
                r,
                head_at(refs["queries"], r, h, 0)[...],
                head_at(pair_refs, r, h, pair_at)[...],
            ).astype(jnp.bfloat16)
            head_at(refs["attended"], r, h, 0)[...] = jnp.dot(
                probability,
                head_at(pair_refs, r, h, pair_at + wide)[...],
                preferred_element_type=jnp.float32,
            ).astype(jnp.bfloat16)

        def form_block(block):
            def tile(r):
                at = pl.ds(block * quarter, quarter)
                refs["partial"].at[r, at][...] = across(
                    refs["attended"].at[r, at][...],
                    refs["weights"].at[:, pl.ds(out_at, wide)][...],
                ).astype(jnp.bfloat16)

            loop(rows, tile)

        def norm_and_send(k):
            values = collect_work.at(refs["stream"], k, 0)[...].astype(
                jnp.float32
            ) + collect_work.total(k)
            collect_work.at(refs["after"], k, 0)[...] = values
            spread_work.src(k)[...] = normalize(values, refs["gain"][...]).astype(jnp.bfloat16)
            spread_work.start(k)

        def pass_on(first, last):
            if beside is not None:
                for k in range(first, last):
                    swap.arrive(k)
                    beside_work.start(k)

        moves.start("beside", "left1", "weights", "left0", "attended", "stream")
        if number is not None:
            greet(beside is not None)
        moves.ready("beside")
        if beside is not None:
            each(swap.start)
        moves.ready("left1", "weights")
        if done is None:
            if same:
                moves.ready("left0")
                form(refs["left0"], query_place, 3 * wide, refs["queries"])
            else:
                form(refs["left1"], pair_place, 2 * wide, refs["pairs"])
                pass_on(0, 1)
                moves.ready("left0")
                form(refs["left0"], query_place, wide, refs["queries"])
            pass_on(0 if same else 1, 2)
            moves.store("queries", "pairs")
            loop(rows * heads, one)
            moves.store("attended")
        pass_on(0 if done is not None else 2, PARTS)
        moves.store("beside_here")
        moves.ready("attended", "stream")
        if stream is not None:
            for block in (3, 2):
                form_block(block)
                collect_work.start_block(block - 2)
            form_block(1)
            each(collect_work.forward)
            form_block(0)
            if beside is not None:
                each(beside_work.relay)
            each(norm_and_send)
            moves.store("after")
            each(spread_work.relay)
            each(spread_work.finish)
            each(collect_work.finish)
        elif beside is not None:
            each(beside_work.relay)
        if beside is not None:
            each(beside_work.finish)
            each(swap.finish)
        moves.end()

    results = kernel_call(
        number,
        "attention_turn",
        inputs,
        outs,
        scratch,
        body,
        lazy=("beside", "left1", "weights", "left0", "attended", "stream"),
        eager=("queries", "pairs", "attended", "after", "beside_here"),
        columns=columns,
    )
    return tuple(
        results.get(name)
        for name in (
            "queries",
            "pairs",
            "attended",
            "after",
            "gathered",
            "beside_here",
            "beside_gathered",
        )
    )


class PlaneScatter:
    def __init__(self, grads, columns, taken, passing, crossed, part, sems):
        self.grads, self.columns, self.taken, self.passing = grads, columns, taken, passing
        self.crossed, self.part, self.sems = crossed, part, sems
        self.rows = grads.shape[0] // 4
        self.me = lax.axis_index("chip")

    def terms(self, chip, which):
        start, size = self.columns
        return self.grads.at[
            pl.ds(pl.multiple_of(chip * self.rows, self.rows), self.rows),
            pl.ds(start + which * (size // 2), size // 2),
        ]

    def copy(self, src, dst, axis, number):
        return pltpu.make_async_remote_copy(
            src,
            dst,
            self.sems.at[0, number],
            self.sems.at[1, number],
            device_id={"chip": across_plane(axis)},
            device_id_type=MESH,
        )

    def first(self, which, block):
        chip = 3 - self.me if block else across_plane(which)
        return self.copy(
            self.terms(chip, which), self.taken.at[which, block], which, 2 * which + block
        )

    def second(self, which):
        return self.copy(
            self.passing.at[which], self.crossed.at[which], 1 - which, 4 + which
        )

    def start(self):
        for block in (1, 0):
            for which in range(2):
                self.first(which, block).start()

    def pass_on(self, following):
        for which in range(2):
            self.first(which, 1).wait_recv()
        if following is not None:
            following.start()
        for which in range(2):
            self.passing.at[which][...] = (
                self.terms(across_plane(1 - which), which)[...].astype(jnp.float32)
                + self.taken.at[which, 1][...].astype(jnp.float32)
            ).astype(jnp.bfloat16)
            self.second(which).start()

    def total(self):
        half = self.columns[1] // 2
        for which in range(2):
            self.first(which, 0).wait_recv()
            self.second(which).wait_recv()
            self.part.at[:, pl.ds(which * half, half)][...] = (
                self.terms(self.me, which)[...].astype(jnp.float32)
                + self.taken.at[which, 0][...].astype(jnp.float32)
                + self.crossed.at[which][...].astype(jnp.float32)
            ).astype(jnp.bfloat16)

    def finish(self):
        for which in range(2):
            for block in range(2):
                self.first(which, block).wait_send()
            self.second(which).wait_send()


class SumEverywhere:
    def __init__(self, given, taken, sems):
        self.given, self.taken, self.sems = given, taken, sems
        chips = lax.axis_size("chip")
        core, zh, zp, chip = (lax.axis_index(axis) for axis in ("core", "zh", "zp", "chip"))
        self.partners = [{"core": 1 - core}]
        for bit in range(chips.bit_length() - 1):
            size = 2**bit
            self.partners.append({"chip": chip + size - 2 * size * (chip // size % 2)})
        self.partners += [{"zp": 1 - zp}, {"zh": 1 - zh}]
        self.steps = len(self.partners)
        self.sums = None

    def copy(self, step):
        return pltpu.make_async_remote_copy(
            self.given.at[step],
            self.taken.at[step],
            self.sems.at[0, step],
            self.sems.at[1, step],
            device_id=self.partners[step],
            device_id_type=MESH,
        )

    def begin(self, step):
        if step:
            self.given[step] = self.sums
        else:
            self.sums = self.given[0]
        self.copy(step).start()

    def end(self, step):
        self.copy(step).wait()
        self.sums = self.sums + self.taken[step]


def leave(number, partial, values, stream, gain, gain_sums, grads, part):
    rows, length, width = values.shape
    chips = lax.axis_size("chip")
    in_plane = chips == 4
    steps = 3 + chips.bit_length() - 1
    if not in_plane:
        grads = scatter_chips(grads)
    owned = grads.shape[0] // (4 if in_plane else 1)
    columns = grads.shape[1]
    size = 512
    pieces = columns // size if in_plane else 0

    def body(refs, moves):
        collect_work = collect_of(refs, "", "partial")
        swap = Swap(refs["leaving"], refs["out"], refs["swap_sems"])
        unpair = Unpair(refs["part"], refs["terms"], refs["unpair_sems"])
        if in_plane:
            scatters = [
                PlaneScatter(
                    refs["grads"],
                    (p * size, size),
                    refs["taken"].at[p],
                    refs["passing"].at[p],
                    refs["crossed"].at[p],
                    refs["summed"].at[p],
                    refs["plane_sems"].at[p],
                )
                for p in range(pieces)
            ]
            returns = [
                Unpair(
                    refs["summed"].at[p],
                    refs["grad_terms"].at[:, :, pl.ds(p * size, size)],
                    refs["return_sems"].at[p],
                )
                for p in range(pieces)
            ]
        else:
            scatters = []
            returns = [Unpair(refs["grads"], refs["grad_terms"], refs["return_sems"].at[0])]
        moves.start("part", "grads", "partial", "values", "stream")
        greet(True, True)
        moves.ready("part")
        unpair.start()
        moves.ready("partial")
        collect_work.start()
        moves.ready("grads")
        if scatters:
            scatters[0].start()
        each(collect_work.forward)
        if not in_plane:
            returns[0].start()
        moves.ready("values", "stream")
        refs["given"].at[0][1:3] = refs["gain_sums"][...]
        refs["gain_sum"][...] = jnp.zeros_like(refs["gain_sum"])

        def slope_and_send(k):
            slope, terms = norm_slope(
                collect_work.at(refs["values"], k, 0)[...].astype(jnp.float32),
                refs["gain"][...],
                collect_work.total(k),
            )
            sums = collect_work.at(refs["stream"], k, 0)[...] + slope
            swap.at(refs["leaving"], k)[...] = sums.astype(jnp.bfloat16)
            swap.start(k)
            refs["gain_sum"][...] += jnp.sum(terms, axis=0, keepdims=True)

        gain_work = SumEverywhere(refs["given"], refs["got"], refs["gain_sems"])
        last = gain_work.steps - 1
        turns = max(PARTS, len(scatters) + 1)
        for k in range(turns):
            if k < PARTS:
                slope_and_send(k)
            if k == PARTS - 1:
                refs["given"].at[0][0:1] = refs["gain_sum"][...]
                for step in range(last - 1):
                    gain_work.begin(step)
                    gain_work.end(step)
                gain_work.begin(last - 1)
            if k < len(scatters):
                scatters[k].pass_on(scatters[k + 1] if k + 1 < len(scatters) else None)
            if 0 < k <= len(scatters):
                scatters[k - 1].total()
                returns[k - 1].start()
        gain_work.end(last - 1)
        gain_work.begin(last)
        each(swap.arrive)
        each(swap.finish)
        each(collect_work.finish)
        unpair.finish()
        for scatter in scatters:
            scatter.finish()
        for back in returns:
            back.finish()
        gain_work.end(last)
        refs["totals"][...] = gain_work.sums

    scratch = {
        **collect_scratch("", rows, length, width),
        "leaving": pltpu.VMEM((rows, length, width), jnp.bfloat16),
        "swap_sems": pltpu.SemaphoreType.DMA((2, PARTS)),
        "unpair_sems": pltpu.SemaphoreType.DMA((4,)),
        "return_sems": pltpu.SemaphoreType.DMA((max(1, pieces), 4)),
        "gain_sum": pltpu.VMEM((1, width), jnp.float32),
        "given": pltpu.VMEM((steps, 3, width), jnp.float32),
        "got": pltpu.VMEM((steps, 3, width), jnp.float32),
        "gain_sems": pltpu.SemaphoreType.DMA((2, steps)),
    }
    if in_plane:
        scratch["taken"] = pltpu.VMEM((pieces, 2, 2, owned, size // 2), jnp.bfloat16)
        scratch["passing"] = pltpu.VMEM((pieces, 2, owned, size // 2), jnp.bfloat16)
        scratch["crossed"] = pltpu.VMEM((pieces, 2, owned, size // 2), jnp.bfloat16)
        scratch["summed"] = pltpu.VMEM((pieces, owned, size), jnp.bfloat16)
        scratch["plane_sems"] = pltpu.SemaphoreType.DMA((pieces, 2, 6))
    results = kernel_call(
        number,
        "leave",
        {
            "partial": partial,
            "values": values,
            "stream": stream,
            "gain": gain[None],
            "gain_sums": gain_sums,
            "grads": grads,
            "part": part,
        },
        {
            "out": (shape_of(values.shape, jnp.bfloat16), ANY),
            "totals": (shape_of((3, width), jnp.float32), VMEM),
            "terms": terms_out(part),
            "grad_terms": (shape_of((2, owned // 2, columns), jnp.bfloat16), ANY),
        },
        scratch,
        body,
        lazy=("part", "grads", "partial", "values", "stream"),
    )
    return results["out"], results["totals"], results["terms"], results["grad_terms"]


def summed(terms):
    return terms[0].astype(jnp.float32) + terms[1].astype(jnp.float32)


def project(left_side, right_side):
    return jnp.einsum("rtd,de->rte", left_side, right_side, preferred_element_type=jnp.float32)


def project_back(gradient, right_side):
    return jnp.einsum("rte,de->rtd", gradient, right_side, preferred_element_type=jnp.float32)


def weight_grad(left_side, gradient):
    return jnp.einsum("rtd,rte->de", left_side, gradient, preferred_element_type=jnp.float32)


def gelu_tanh(values):
    return jax.nn.gelu(values, approximate=True)


def shards(
    tokens,
    patches,
    seg_ids,
    seg_example,
    patch_owner,
    gain_self,
    self_query,
    self_key,
    self_value,
    self_out,
    gain_cross,
    cross_query,
    cross_key,
    cross_value,
    cross_out,
    gain_mlp,
    mlp_gate,
    mlp_up,
    mlp_down,
    cotangent,
):
    gains = jnp.stack([gain_self, gain_cross, gain_mlp]).astype(jnp.float32)
    onehot = (
        seg_ids[:, :, None] == lax.iota(jnp.int32, seg_example.shape[1])[None, None, :]
    ).astype(jnp.int32)
    example_of = jnp.sum(onehot * seg_example[:, None, :], axis=2)
    marks = jnp.concatenate([seg_ids, example_of, patch_owner], axis=0)
    rows = seg_ids.shape[0]
    length = seg_ids.shape[1]
    wide = self_query.shape[1]
    hidden_wide = mlp_gate.shape[1]
    local_tokens, marks, gains, normed_one, patch_rows, self_w, cross_pair = head(
        0,
        tokens,
        patches,
        marks,
        gains,
        (self_query, self_key, self_value, self_out.T),
        (cross_key, cross_value, cross_query, cross_out.T),
    )
    norm_one, norm_two, norm_three = gains[0], gains[1], gains[2]
    cross_w = gather_chips(cross_pair)
    mlp_moved = exchange(after(jnp.concatenate([mlp_gate, mlp_up], axis=1), normed_one))
    seg_here = relative(marks[:rows])
    example_here = relative(marks[rows : 2 * rows])
    owner_here = relative(marks[2 * rows :])
    positions = relative(lax.broadcasted_iota(jnp.int32, (1, length), 1))
    self_marks = (
        seg_here[:, :, None],
        seg_here[:, None, :],
        positions.reshape(length, 1),
        positions.reshape(1, length),
    )
    cross_marks = (
        example_here[:, :, None],
        owner_here[:, None, :],
        jnp.zeros((length, 1), jnp.int32),
        jnp.zeros((1, length), jnp.int32),
    )
    self_places = (0, wide, 3 * wide)
    self_lefts = (normed_one, normed_one)
    self_qkv, _, self_attended, _, _, _, _ = attention_turn(
        None, self_lefts, self_w, self_places, self_marks, None, None
    )
    mlp_pair = pair_up(after(mlp_moved, self_attended))
    mlp_in = gather_chips(mlp_pair)
    down_moved = exchange(after(mlp_down.T, mlp_pair))
    _, _, _, after_self, normed_two, _, _ = attention_turn(
        1,
        self_lefts,
        self_w,
        self_places,
        self_marks,
        local_tokens,
        norm_two,
        after(self_attended, mlp_pair),
    )
    down_pair = pair_up(after(down_moved, after_self))
    mlp_downw = gather_chips(down_pair)
    (
        cross_query_rows,
        cross_kv_rows,
        cross_mixed,
        after_cross,
        normed_three,
        local_grad,
        grad_rows,
    ) = attention_turn(
        2,
        (after(normed_two, down_pair), patch_rows),
        cross_w,
        (2 * wide, 0, 3 * wide),
        cross_marks,
        after_self,
        norm_three,
        None,
        cotangent,
    )
    both = project(normed_three, mlp_in)
    gate_pre = both[..., :hidden_wide]
    upward = both[..., hidden_wide:]
    activated, gelu_pull = jax.vjp(gelu_tanh, gate_pre)
    hidden = (activated * upward).astype(jnp.bfloat16)

    grad_down_w = weight_grad(grad_rows, hidden).astype(jnp.bfloat16)
    down_part = scatter_chips(grad_down_w)
    grad_hidden = project(after(grad_rows, grad_down_w), mlp_downw)
    grad_upward = (grad_hidden * activated).astype(jnp.bfloat16)
    grad_gate = gelu_pull(grad_hidden * upward)[0].astype(jnp.bfloat16)
    grad_both = jnp.concatenate([grad_gate, grad_upward], axis=2)
    partial_three = project_back(grad_both, mlp_in).astype(jnp.bfloat16)
    tokens_here = rows * length
    grad_mlp_w = weight_grad(normed_three, grad_both).astype(jnp.bfloat16)
    mlp_part = scatter_chips(grad_mlp_w)
    grad_cross_stream, cross_branch, part_three, result_partial = turn_back(
        3,
        after(partial_three, grad_mlp_w),
        after_cross,
        local_grad,
        norm_three,
        (ProductFill("result_", hidden.reshape(tokens_here, -1), mlp_downw, (0, hidden_wide)),),
    )
    partial_two, cross_grads, down_terms, grad_ckv, output = attention_back(
        4,
        cross_branch,
        cross_w,
        (2 * wide, 0, 3 * wide),
        (cross_query_rows, 0),
        (cross_kv_rows, 0),
        cross_marks,
        (normed_two, patch_rows),
        cross_mixed,
        (result_partial.reshape(rows, length, -1), after_cross),
        down_part,
    )
    down_sum = summed(down_terms).T
    cross_part = scatter_chips(cross_grads)
    grad_self_stream, self_branch, part_two, mlp_terms, patch_partial = turn_back(
        5,
        partial_two,
        after_self,
        grad_cross_stream,
        norm_two,
        (ProductFill("patch_", grad_ckv.reshape(tokens_here, -1), cross_w, (0, 2 * wide)),),
        mlp_part,
    )
    mlp_sum = summed(mlp_terms)
    grad_self_out = weight_grad(self_branch, self_attended).astype(jnp.bfloat16)
    self_out_part = scatter_chips(grad_self_out)
    partial_one, grad_self_in, cross_terms, _, grad_patches = attention_back(
        6,
        after(self_branch, grad_self_out),
        self_w,
        (0, wide, 3 * wide),
        (self_qkv, 0),
        (self_qkv, wide),
        self_marks,
        (normed_one, normed_one),
        None,
        (patch_partial.reshape(rows, length, -1), None),
        cross_part,
    )
    cross_sum = summed(cross_terms)
    grad_tokens, gain_sums, self_out_terms, self_terms = leave(
        7,
        partial_one,
        local_tokens,
        grad_self_stream,
        norm_one,
        jnp.concatenate([part_two, part_three]),
        grad_self_in,
        self_out_part,
    )
    held = gain_self.shape[0]
    place = lax.axis_index(("chip", "core")) * held
    gain_sums = lax.dynamic_slice_in_dim(gain_sums, place, held, axis=1)
    self_sum = summed(self_terms)
    return (
        output,
        grad_tokens.astype(jnp.float32),
        grad_patches.astype(jnp.float32),
        gain_sums[0],
        self_sum[:, :wide],
        self_sum[:, wide : 2 * wide],
        self_sum[:, 2 * wide :],
        summed(self_out_terms).T,
        gain_sums[1],
        cross_sum[:, 2 * wide : 3 * wide],
        cross_sum[:, :wide],
        cross_sum[:, wide : 2 * wide],
        cross_sum[:, 3 * wide :].T,
        gain_sums[2],
        mlp_sum[:, :hidden_wide],
        mlp_sum[:, hidden_wide:],
        down_sum,
    )


def solution(mesh):
    devices = mesh.devices.reshape(mesh.shape["dp"] // 2, 2, 2, mesh.shape["seq"] // 2)
    fine = Mesh(devices, AXES)
    dp = ("chip", "core")
    seq = ("zh", "zp")
    stream = P(dp, seq, None)
    rows = P(dp, None)
    inward = P(dp, seq)
    outward = P(seq, dp)
    vector = P(dp)
    block = (vector, inward, inward, inward, outward)
    weights = block + block + (vector, inward, inward, outward)
    return jax.shard_map(
        shards,
        mesh=fine,
        in_specs=(stream, stream, rows, rows, rows) + weights + (stream,),
        out_specs=(stream, stream, stream) + weights,
        check_vma=False,
    )
```

```python
import itertools

import jax
import jax.numpy as jnp
from jax import lax
from jax.experimental import pallas as pl
from jax.experimental.pallas import tpu as pltpu
from jax.sharding import Mesh
from jax.sharding import PartitionSpec as P

HD = 128


epsilon = 1e-06
masked_value = -1e30

AXES = ("chip", "core", "zh", "zp")


def moves(chips, source_of):
    pairs = []
    for chip, core, zh, zp in itertools.product(range(chips), range(2), range(2), range(2)):
        a, b, c, d = source_of(chip, core, zh, zp)
        pairs.append((((a * 2 + b) * 2 + c) * 2 + d, ((chip * 2 + core) * 2 + zh) * 2 + zp))
    return pairs


def permute(values, source_of):
    return lax.ppermute(values, AXES, moves(lax.axis_size("chip"), source_of))


def swapped(values):
    return permute(values, lambda chip, core, zh, zp: (chip, zh, core, zp))


def swapped_other(values):
    return permute(values, lambda chip, core, zh, zp: (chip, 1 - zh, core, zp))


def relative(values):
    rows, length = values.shape
    cut = values.reshape(rows, 2, 2, length // 4)
    cut = jnp.where(lax.axis_index("core") == 1, cut[:, ::-1], cut)
    cut = jnp.where(lax.axis_index("zp") == 1, cut[:, :, ::-1], cut)
    return cut.reshape(rows, length)


def after(values, *others):
    return lax.optimization_barrier((values,) + others)[0]


def exchange(shards_of):
    return swapped(shards_of), swapped_other(shards_of)


def pair_up(exchanged):
    first, second = exchanged
    low = lax.axis_index("zh") == 0
    return jnp.concatenate([jnp.where(low, first, second), jnp.where(low, second, first)], axis=0)


def gather_chips(pair):
    return lax.all_gather(pair, "chip", axis=0, tiled=True)


def scatter_chips(grads):
    return lax.psum_scatter(
        grads.astype(jnp.bfloat16), "chip", scatter_dimension=0, tiled=True
    )


def normalize(values, gain_vec):
    factor = lax.rsqrt(jnp.mean(values * values, axis=-1, keepdims=True) + epsilon)
    return values * factor * gain_vec


def norm_back(values, gain_vec, gradient):
    normed_value, pullback = jax.vjp(lambda inputs: normalize(inputs, gain_vec), values)
    return pullback(gradient)[0]


def gain_part(values, gradient):
    factor = lax.rsqrt(jnp.mean(values * values, axis=-1, keepdims=True) + epsilon)
    return jnp.sum(gradient * values * factor, axis=(0, 1))


MESH = pl.DeviceIdType.MESH
ANY = pl.BlockSpec(memory_space=pl.ANY)
VMEM = pl.BlockSpec(memory_space=pltpu.VMEM)
PARTS = 4


def across_plane(axis):
    chip = lax.axis_index("chip")
    x, y = chip % 2, chip // 2
    return y * 2 + 1 - x if axis == 0 else (1 - y) * 2 + x


def greet(everyone, plane=False):
    core, zh, zp = lax.axis_index("core"), lax.axis_index("zh"), lax.axis_index("zp")
    barrier = pltpu.get_barrier_semaphore()
    count = 0
    for a, b, c in itertools.product(range(2), range(2), range(2)):
        if (a, b, c) == (0, 0, 0) or (b and not everyone):
            continue
        pl.semaphore_signal(
            barrier,
            inc=1,
            device_id={"core": (core + a) % 2, "zh": (zh + b) % 2, "zp": (zp + c) % 2},
            device_id_type=MESH,
        )
        count += 1
    if plane:
        chips = lax.axis_size("chip")
        for a, b in itertools.product(range(1, chips), range(2)):
            pl.semaphore_signal(
                barrier,
                inc=1,
                device_id={
                    "chip": (lax.axis_index("chip") + a) % chips,
                    "core": (core + b) % 2,
                },
                device_id_type=MESH,
            )
            count += 1
    pl.semaphore_wait(barrier, count)


def to_core(src, dst, send, recv):
    return pltpu.make_async_remote_copy(
        src, dst, send, recv, device_id={"core": 1 - lax.axis_index("core")}, device_id_type=MESH
    )


def to_zp(src, dst, send, recv):
    return pltpu.make_async_remote_copy(
        src, dst, send, recv, device_id={"zp": 1 - lax.axis_index("zp")}, device_id_type=MESH
    )


def to_swapped(src, dst, send, recv):
    core, zh = lax.axis_index("core"), lax.axis_index("zh")
    return pltpu.make_async_remote_copy(
        src, dst, send, recv, device_id={"core": zh, "zh": core}, device_id_type=MESH
    )


class Exchange:
    def __init__(self, src, pair, sems):
        self.src, self.pair, self.sems = src, pair, sems
        self.core, self.zh = lax.axis_index("core"), lax.axis_index("zh")
        rows = src.shape[0]
        self.mine = pair.at[pl.ds(pl.multiple_of(self.core * rows, rows), rows)]
        self.slots = [pair.at[pl.ds(a * rows, rows)] for a in range(2)]

    def far(self):
        return pltpu.make_async_remote_copy(
            self.src,
            self.mine,
            self.sems.at[0],
            self.sems.at[2 + self.core],
            device_id={"core": self.zh, "zh": 1 - self.zh},
            device_id_type=MESH,
        )

    def near(self):
        return pltpu.make_async_remote_copy(
            self.src,
            self.mine,
            self.sems.at[1],
            self.sems.at[2 + self.core],
            device_id={"core": 1 - self.core},
            device_id_type=MESH,
        )

    def own(self):
        return pltpu.make_async_copy(self.src, self.mine, self.sems.at[2 + self.core])

    def start(self):
        self.far().start()

        @pl.when(self.core == self.zh)
        def _():
            self.own().start()

        @pl.when(self.core != self.zh)
        def _():
            self.near().start()

    def finish(self):
        self.far().wait_send()

        @pl.when(self.core != self.zh)
        def _():
            self.near().wait_send()

        for a in range(2):
            pltpu.make_async_copy(self.src, self.slots[a], self.sems.at[2 + a]).wait()


class Spread:
    def __init__(self, block, gathered, sems):
        self.block, self.gathered, self.sems = block, gathered, sems
        self.length = block.shape[1]
        self.step = 2 * self.length // PARTS

    def src(self, k):
        return self.block.at[k // (PARTS // 2), pl.ds(pl.multiple_of(k % (PARTS // 2) * self.step, self.step), self.step)]

    def dst(self, k, slot):
        return self.gathered.at[
            k // (PARTS // 2),
            pl.ds(
                pl.multiple_of(slot * self.length + k % (PARTS // 2) * self.step, self.step),
                self.step,
            ),
        ]

    def beside(self, k):
        return to_zp(self.src(k), self.dst(k, 1), self.sems.at[0, k], self.sems.at[1, k])

    def across(self, k):
        return to_core(self.src(k), self.dst(k, 2), self.sems.at[2, k], self.sems.at[3, k])

    def corner(self, k):
        return to_core(self.dst(k, 1), self.dst(k, 3), self.sems.at[4, k], self.sems.at[5, k])

    def own(self, k):
        return pltpu.make_async_copy(self.src(k), self.dst(k, 0), self.sems.at[6, k])

    def start(self, k):
        self.beside(k).start()
        self.across(k).start()
        self.own(k).start()

    def relay(self, k):
        self.beside(k).wait_recv()
        self.corner(k).start()

    def finish(self, k):
        self.beside(k).wait_send()
        self.across(k).wait()
        self.corner(k).wait()
        self.own(k).wait()


class Collect:
    def __init__(self, partial, arrived, outgoing, landed, sems):
        self.partial, self.arrived = partial, arrived
        self.outgoing, self.landed, self.sems = outgoing, landed, sems
        self.length = outgoing.shape[1]
        self.step = 2 * self.length // PARTS

    def at(self, ref, k, block):
        return ref.at[
            k // (PARTS // 2),
            pl.ds(
                pl.multiple_of(block * self.length + k % (PARTS // 2) * self.step, self.step),
                self.step,
            ),
        ]

    def crossing(self, k, block):
        return to_core(
            self.at(self.partial, k, 2 + block),
            self.at(self.arrived, k, block),
            self.sems.at[2 * block, k],
            self.sems.at[2 * block + 1, k],
        )

    def landing(self, k):
        return to_zp(
            self.at(self.outgoing, k, 0),
            self.at(self.landed, k, 0),
            self.sems.at[4, k],
            self.sems.at[5, k],
        )

    def start(self):
        for block in (1, 0):
            self.start_block(block)

    def start_block(self, block):
        for k in range(PARTS):
            self.crossing(k, block).start()

    def forward(self, k):
        self.crossing(k, 1).wait_recv()
        self.at(self.outgoing, k, 0)[...] = (
            self.at(self.partial, k, 1)[...].astype(jnp.float32)
            + self.at(self.arrived, k, 1)[...].astype(jnp.float32)
        ).astype(jnp.bfloat16)
        self.landing(k).start()

    def total(self, k):
        self.crossing(k, 0).wait_recv()
        self.landing(k).wait_recv()
        return (
            self.at(self.partial, k, 0)[...].astype(jnp.float32)
            + self.at(self.arrived, k, 0)[...].astype(jnp.float32)
        ) + self.at(self.landed, k, 0)[...].astype(jnp.float32)

    def finish(self, k):
        self.crossing(k, 0).wait_send()
        self.crossing(k, 1).wait_send()
        self.landing(k).wait_send()


class Unpair:
    def __init__(self, part, terms, sems):
        self.part, self.terms, self.sems = part, terms, sems
        self.core, self.zh = lax.axis_index("core"), lax.axis_index("zh")
        self.rows = part.shape[0] // 2

    def piece(self, p):
        return self.part.at[pl.ds(p * self.rows, self.rows)]

    def remote(self, p):
        return pltpu.make_async_remote_copy(
            self.piece(p),
            self.terms.at[self.zh],
            self.sems.at[p],
            self.sems.at[2 + self.zh],
            device_id={"core": p, "zh": self.core},
            device_id_type=MESH,
        )

    def own(self, p):
        return pltpu.make_async_copy(
            self.piece(p), self.terms.at[self.zh], self.sems.at[2 + self.zh]
        )

    def stays(self, p):
        return jnp.logical_and(self.core == p, self.zh == p)

    def start(self):
        for p in range(2):

            @pl.when(self.stays(p))
            def _(p=p):
                self.own(p).start()

            @pl.when(jnp.logical_not(self.stays(p)))
            def _(p=p):
                self.remote(p).start()

    def finish(self):
        for p in range(2):

            @pl.when(jnp.logical_not(self.stays(p)))
            def _(p=p):
                self.remote(p).wait_send()

            pltpu.make_async_copy(
                self.piece(p), self.terms.at[p], self.sems.at[2 + p]
            ).wait()


class Swap:
    def __init__(self, block, target, sems):
        self.block, self.target, self.sems = block, target, sems
        self.swaps = lax.axis_index("core") != lax.axis_index("zh")
        self.step = 2 * block.shape[1] // PARTS

    def at(self, ref, k):
        return ref.at[
            k // (PARTS // 2), pl.ds(pl.multiple_of(k % (PARTS // 2) * self.step, self.step), self.step)
        ]

    def remote(self, k):
        return to_swapped(
            self.at(self.block, k), self.at(self.target, k), self.sems.at[0, k], self.sems.at[1, k]
        )

    def own(self, k):
        return pltpu.make_async_copy(self.at(self.block, k), self.at(self.target, k), self.sems.at[1, k])

    def start(self, k):
        @pl.when(self.swaps)
        def _():
            self.remote(k).start()

        @pl.when(jnp.logical_not(self.swaps))
        def _():
            self.own(k).start()

    def arrive(self, k):
        self.own(k).wait()

    def finish(self, k):
        @pl.when(self.swaps)
        def _():
            self.remote(k).wait_send()


def each(body):
    lax.fori_loop(0, PARTS, lambda k, carry: (body(k), carry)[1], 0)


class Moves:
    def __init__(self, loads, stores):
        self.loads, self.stores, self.waited, self.going = loads, stores, set(), []

    def start(self, *names):
        for name in names:
            if name in self.loads:
                self.loads[name].start()

    def ready(self, *names):
        for name in names:
            if name in self.loads and name not in self.waited:
                self.waited.add(name)
                self.loads[name].wait()

    def store(self, *names):
        for name in names:
            if name in self.stores:
                self.stores[name].start()
                self.going.append(name)

    def end(self):
        for name in self.going:
            self.stores[name].wait()


def kernel_call(number, name, inputs, outs, scratch, body, lazy=(), eager=(), columns=None):
    columns = columns or {}
    lazy = [key for key in lazy if key in inputs]
    eager = [key for key in eager if key in outs]
    scratch = dict(scratch)
    for key in lazy:
        shape = inputs[key].shape
        if key in columns:
            shape = (shape[0], columns[key][1])
        scratch["lazy_" + key] = pltpu.VMEM(shape, inputs[key].dtype)
    for key in eager:
        scratch["eager_" + key] = pltpu.VMEM(outs[key][0].shape, outs[key][0].dtype)
    scratch["move_sems"] = pltpu.SemaphoreType.DMA((max(1, len(lazy) + len(eager)),))
    names = list(inputs) + list(outs) + list(scratch)

    def kernel(*given):
        refs = dict(zip(names, given))
        sems = refs["move_sems"]
        loads, stores = {}, {}
        for number, key in enumerate(lazy):
            here, source = refs["lazy_" + key], refs[key]
            if key in columns:
                source = source.at[:, pl.ds(*columns[key])]
            loads[key] = pltpu.make_async_copy(source, here, sems.at[number])
            refs[key] = here
        for number, key in enumerate(eager):
            here = refs["eager_" + key]
            stores[key] = pltpu.make_async_copy(here, refs[key], sems.at[len(lazy) + number])
            refs[key] = here
        body(refs, Moves(loads, stores))

    results = pl.pallas_call(
        kernel,
        out_shape=tuple(shape for shape, _ in outs.values()),
        in_specs=[ANY if key in lazy else VMEM for key in inputs],
        out_specs=tuple(ANY if key in eager else spec for key, (_, spec) in outs.items()),
        scratch_shapes=list(scratch.values()),
        compiler_params=pltpu.CompilerParams(
            collective_id=number,
            has_side_effects=number is not None,
            vmem_limit_bytes=61 * 1024 * 1024,
        ),
        name=name,
    )(*inputs.values())
    return dict(zip(outs, results))


def collect_scratch(tag, rows, length, width):
    return {
        tag + "arrived": pltpu.VMEM((rows, 2 * length, width), jnp.bfloat16),
        tag + "outgoing": pltpu.VMEM((rows, length, width), jnp.bfloat16),
        tag + "landed": pltpu.VMEM((rows, length, width), jnp.bfloat16),
        tag + "collect_sems": pltpu.SemaphoreType.DMA((6, PARTS)),
    }


def collect_of(refs, tag, partial):
    return Collect(
        refs[partial],
        refs[tag + "arrived"],
        refs[tag + "outgoing"],
        refs[tag + "landed"],
        refs[tag + "collect_sems"],
    )


def shape_of(shape, dtype):
    return jax.ShapeDtypeStruct(shape, dtype)


def gathered_out(rows, length, width):
    return (shape_of((rows, 4 * length, width), jnp.bfloat16), ANY)


def pair_out(shard):
    return (shape_of((2 * shard.shape[0], shard.shape[1]), shard.dtype), ANY)


def terms_out(part):
    return (shape_of((2, part.shape[0] // 2, part.shape[1]), part.dtype), ANY)


class PlaneGather:
    def __init__(self, whole, columns, sems):
        self.whole, self.columns, self.sems = whole, columns, sems
        self.rows = whole.shape[0] // 4

    def half(self, chip, which):
        start, size = self.columns
        return self.whole.at[
            pl.ds(pl.multiple_of(chip * self.rows, self.rows), self.rows),
            pl.ds(start + which * (size // 2), size // 2),
        ]

    def own(self, axis, which):
        ref = self.half(lax.axis_index("chip"), which)
        return self.copy(ref, axis, 2 * axis + which)

    def passed(self, which):
        ref = self.half(across_plane(which), which)
        return self.copy(ref, 1 - which, 4 + which)

    def copy(self, ref, axis, number):
        return pltpu.make_async_remote_copy(
            ref,
            ref,
            self.sems.at[0, number],
            self.sems.at[1, number],
            device_id={"chip": across_plane(axis)},
            device_id_type=MESH,
        )

    def start(self):
        for axis in range(2):
            self.own(axis, axis).start()
        for axis in range(2):
            self.own(axis, 1 - axis).start()

    def relay(self):
        for which in range(2):
            self.own(which, which).wait_recv()
            self.passed(which).start()

    def finish(self):
        for axis in range(2):
            self.own(axis, axis).wait_send()
            self.own(axis, 1 - axis).wait()
            self.passed(axis).wait()


class SwapWhole:
    def __init__(self, array, target, sems):
        self.array, self.target, self.sems = array, target, sems
        self.swaps = lax.axis_index("core") != lax.axis_index("zh")

    def remote(self):
        return to_swapped(self.array, self.target, self.sems.at[0], self.sems.at[1])

    def own(self):
        return pltpu.make_async_copy(self.array, self.target, self.sems.at[1])

    def start(self):
        @pl.when(self.swaps)
        def _():
            self.remote().start()

        @pl.when(jnp.logical_not(self.swaps))
        def _():
            self.own().start()

    def finish(self):
        self.own().wait()

        @pl.when(self.swaps)
        def _():
            self.remote().wait_send()


class GainGather:
    def __init__(self, own, slots, whole, sems):
        self.own, self.slots, self.whole, self.sems = own, slots, whole, sems
        self.chips = lax.axis_size("chip")
        self.chip, self.core = lax.axis_index("chip"), lax.axis_index("core")

    def others(self):
        for number in range(1, 2 * self.chips):
            yield number, (self.chip + number // 2) % self.chips, (self.core + number % 2) % 2

    def send(self, number, chip, core):
        return pltpu.make_async_remote_copy(
            self.own,
            self.slots.at[self.chip * 2 + self.core],
            self.sems.at[0, number],
            self.sems.at[1, self.chip * 2 + self.core],
            device_id={"chip": chip, "core": core},
            device_id_type=MESH,
        )

    def start(self):
        for other in self.others():
            self.send(*other).start()
        self.slots.at[self.chip * 2 + self.core][...] = self.own[...]

    def finish(self):
        for number, chip, core in self.others():
            self.send(number, chip, core).wait_send()
            place = chip * 2 + core
            pltpu.make_async_copy(self.own, self.slots.at[place], self.sems.at[1, place]).wait()
        held = self.own.shape[1]
        for place in range(2 * self.chips):
            self.whole[:, place * held : (place + 1) * held] = self.slots[place]


def head(number, block, beside, marks, gains, first, second):
    rows, length, width = block.shape
    depth, size = first[0].shape
    chips = lax.axis_size("chip")
    in_plane = chips == 4
    if not in_plane:
        gains = lax.all_gather(gains, ("chip", "core"), axis=1, tiled=True)

    def body(refs, moves):
        swap = Swap(refs["block"], refs["here"], refs["swap_sems"])
        marks_swap = SwapWhole(refs["marks"], refs["marks_here"], refs["marks_sems"])
        spread_work = Spread(refs["normed"], refs["gathered"], refs["spread_sems"])
        if in_plane:
            chip = lax.axis_index("chip")
            place = refs["whole"].at[pl.ds(pl.multiple_of(chip * 2 * depth, 2 * depth), 2 * depth)]
            gain_work = GainGather(
                refs["gains"], refs["gain_slots"], refs["gains_whole"], refs["gain_sems"]
            )
        else:
            place = refs["whole"]
        works = [
            Exchange(
                refs["first%d" % i],
                place.at[:, pl.ds(i * size, size)],
                refs["exchange_sems"].at[i],
            )
            for i in range(len(first))
        ]
        beside_swap = Swap(refs["beside"], refs["beside_here"], refs["beside_swap_sems"])
        beside_work = Spread(refs["beside_here"], refs["beside_gathered"], refs["beside_sems"])
        later = [
            Exchange(
                refs["second%d" % i],
                refs["pair"].at[:, pl.ds(i * size, size)],
                refs["exchange_sems"].at[len(first) + i],
            )
            for i in range(len(second))
        ]
        greet(True, in_plane)
        marks_swap.start()

        def norm_and_send(k):
            swap.arrive(k)
            values = swap.at(refs["here"], k)[...].astype(jnp.float32)
            spread_work.src(k)[...] = normalize(values, refs["gains_whole"][0:1, :]).astype(
                jnp.bfloat16
            )
            spread_work.start(k)

        planes = [
            PlaneGather(refs["whole"], (i * size, size), refs["plane_sems"].at[i])
            for i in range(len(first))
        ]
        last = len(works) - 1
        works[0].start()
        if in_plane:
            gain_work.start()
            gain_work.finish()
        else:
            refs["gains_whole"][...] = refs["gains"][...]
        for i, work in enumerate(works):
            work.finish()
            if in_plane:
                planes[i].start()
            if i < last:
                works[i + 1].start()
            if i == 0:
                each(swap.start)
            if i == last - 1:
                each(beside_swap.start)
            if in_plane and i:
                planes[i - 1].relay()
            if i == 1:
                each(norm_and_send)
            if i == last:
                each(spread_work.relay)

        def pass_on(k):
            beside_swap.arrive(k)
            beside_work.start(k)

        later[0].start()
        pass_on(0)
        pass_on(1)
        if in_plane:
            planes[last].relay()
        for k in range(2, PARTS):
            pass_on(k)
        for i, work in enumerate(later):
            if i + 1 < len(later):
                later[i + 1].start()
            if i == 1:
                each(beside_work.relay)
            work.finish()
        each(beside_work.finish)
        each(beside_swap.finish)
        each(spread_work.finish)
        each(swap.finish)
        if in_plane:
            for plane in planes:
                plane.finish()
        marks_swap.finish()

    whole_rows = 8 * depth if in_plane else 2 * depth
    results = kernel_call(
        number,
        "head",
        {
            "block": block,
            "beside": beside,
            "marks": marks,
            "gains": gains,
            **{"first%d" % i: shard for i, shard in enumerate(first)},
            **{"second%d" % i: shard for i, shard in enumerate(second)},
        },
        {
            "here": (shape_of(block.shape, block.dtype), VMEM),
            "marks_here": (shape_of(marks.shape, marks.dtype), VMEM),
            "gains_whole": (shape_of((gains.shape[0], width), jnp.float32), VMEM),
            "gathered": gathered_out(rows, length, width),
            "whole": (shape_of((whole_rows, len(first) * size), jnp.bfloat16), ANY),
            "beside_gathered": gathered_out(rows, length, width),
            "pair": (shape_of((2 * depth, len(second) * size), jnp.bfloat16), ANY),
        },
        {
            "normed": pltpu.VMEM((rows, length, width), jnp.bfloat16),
            "spread_sems": pltpu.SemaphoreType.DMA((7, PARTS)),
            "swap_sems": pltpu.SemaphoreType.DMA((2, PARTS)),
            "beside_here": pltpu.VMEM((rows, length, width), jnp.bfloat16),
            "beside_sems": pltpu.SemaphoreType.DMA((7, PARTS)),
            "beside_swap_sems": pltpu.SemaphoreType.DMA((2, PARTS)),
            "marks_sems": pltpu.SemaphoreType.DMA((2,)),
            "exchange_sems": pltpu.SemaphoreType.DMA((len(first) + len(second), 4)),
            "plane_sems": pltpu.SemaphoreType.DMA((len(first), 2, 6)),
            "gain_slots": pltpu.VMEM((2 * chips,) + gains.shape, jnp.float32),
            "gain_sems": pltpu.SemaphoreType.DMA((2, 2 * chips)),
        },
        body,
    )
    whole = results["whole"] if in_plane else gather_chips(results["whole"])
    return (
        results["here"],
        results["marks_here"],
        results["gains_whole"],
        results["gathered"],
        results["beside_gathered"],
        whole,
        results["pair"],
    )


class ProductFill:
    def __init__(self, tag, left, right, columns):
        self.tag = tag
        self.columns = {tag + "right": columns}
        rows = left.shape[0]
        self.size = 256
        self.tiles = rows // self.size
        self.inputs = {tag + "left": left, tag + "right": right}
        self.outs = {tag + "out": (shape_of((rows, right.shape[0]), jnp.bfloat16), VMEM)}
        self.scratch = {}

    def tile(self, refs, i):
        at = pl.ds(pl.multiple_of(i * self.size, self.size), self.size)
        refs[self.tag + "out"].at[at][...] = across(
            refs[self.tag + "left"].at[at][...],
            refs[self.tag + "right"][...],
        ).astype(jnp.bfloat16)

    def end(self, refs):
        pass


def fill_in(refs, fill, part, parts):
    if fill is not None:
        first, last = fill.tiles * part // parts, fill.tiles * (part + 1) // parts
        lax.fori_loop(first, last, lambda i, carry: (fill.tile(refs, i), carry)[1], 0)


def norm_slope(values, gain, gradient):
    factor = lax.rsqrt(jnp.mean(values * values, axis=-1, keepdims=True) + epsilon)
    scaled = gain * gradient
    inner = jnp.mean(scaled * values, axis=-1, keepdims=True)
    return factor * scaled - values * (factor * factor * factor * inner), gradient * values * factor


def turn_back(number, partial, values, stream, gain, fills, *parts):
    rows, length, width = values.shape
    first, second = (tuple(fills) + (None, None))[:2]

    def body(refs, moves):
        collect_work = collect_of(refs, "", "partial")
        spread_work = Spread(refs["branch"], refs["gathered"], refs["spread_sems"])
        works = [
            Unpair(refs["part%d" % i], refs["terms%d" % i], refs["unpair_sems"].at[i])
            for i in range(len(parts))
        ]
        part_names = ["part%d" % i for i in range(len(parts))]
        fill_names = [[*fill.inputs] for fill in fills]
        moves.start(*part_names, "partial", "values", "stream", *sum(fill_names, []))
        greet(bool(parts))
        moves.ready(*part_names)
        for work in works:
            work.start()
        moves.ready("partial")
        collect_work.start()
        each(collect_work.forward)
        refs["gain_sum"][...] = jnp.zeros_like(refs["gain_sum"])

        def slope_and_send(k):
            slope, terms = norm_slope(
                collect_work.at(refs["values"], k, 0)[...].astype(jnp.float32),
                refs["gain"][...],
                collect_work.total(k),
            )
            sums = collect_work.at(refs["stream"], k, 0)[...].astype(jnp.float32) + slope
            collect_work.at(refs["after"], k, 0)[...] = sums
            spread_work.src(k)[...] = sums.astype(jnp.bfloat16)
            spread_work.start(k)
            refs["gain_sum"][...] += jnp.sum(terms, axis=0, keepdims=True)

        moves.ready("values", "stream")
        moves.ready(*sum(fill_names[:1], []))
        if first is None:
            each(slope_and_send)
        else:
            for k in range(PARTS):
                fill_in(refs, first, k, PARTS)
                slope_and_send(k)
        moves.store("after")
        for fill in fills[:1]:
            moves.store(*fill.outs)
        moves.ready(*sum(fill_names[1:], []))
        fill_in(refs, second, 0, 1)
        for fill in fills[1:]:
            moves.store(*fill.outs)
        each(spread_work.relay)
        each(spread_work.finish)
        each(collect_work.finish)
        for work in works:
            work.finish()
        for fill in fills:
            fill.end(refs)
        moves.end()

    extra = {"inputs": {}, "outs": {}, "scratch": {}}
    for fill in fills:
        for kind, found in extra.items():
            found.update(getattr(fill, kind))
    results = kernel_call(
        number,
        "turn_back",
        {
            "partial": partial,
            "values": values,
            "stream": stream,
            "gain": gain[None],
            **{"part%d" % i: part for i, part in enumerate(parts)},
            **extra["inputs"],
        },
        {
            "after": (shape_of(values.shape, jnp.float32), VMEM),
            "gathered": gathered_out(rows, length, width),
            "gain_sum": (shape_of((1, width), jnp.float32), VMEM),
            **{"terms%d" % i: terms_out(part) for i, part in enumerate(parts)},
            **extra["outs"],
        },
        {
            **collect_scratch("", rows, length, width),
            "branch": pltpu.VMEM((rows, length, width), jnp.bfloat16),
            "spread_sems": pltpu.SemaphoreType.DMA((7, PARTS)),
            "unpair_sems": pltpu.SemaphoreType.DMA((max(1, len(parts)), 4)),
            **extra["scratch"],
        },
        body,
        lazy=("partial", "values", "stream")
        + tuple("part%d" % i for i in range(len(parts)))
        + tuple(extra["inputs"]),
        eager=("after",)
        + tuple(name for name, (_, spec) in extra["outs"].items() if spec is VMEM),
        columns={key: found for fill in fills for key, found in fill.columns.items()},
    )
    return (
        (results["after"], results["gathered"], results["gain_sum"])
        + tuple(results["terms%d" % i] for i in range(len(parts)))
        + tuple(results[name] for fill in fills for name in fill.outs)
    )


class OutWork:
    def __init__(self, collect_work, swap, base):
        self.collect_work, self.swap, self.base = collect_work, swap, base

    def begin(self):
        self.collect_work.start()

    def forward(self):
        each(self.collect_work.forward)

    def leave_part(self, k):
        total = self.collect_work.total(k)
        if self.base is not None:
            total = total + self.swap.at(self.base, k)[...]
        self.swap.at(self.swap.block, k)[...] = total.astype(jnp.bfloat16)
        self.swap.start(k)

    def end(self):
        each(self.swap.arrive)
        each(self.swap.finish)
        each(self.collect_work.finish)


def head_at(ref, r, h, offset):
    return ref.at[r, :, pl.ds(pl.multiple_of(offset + h * HD, HD), HD)]


def across(left, right):
    return lax.dot_general(
        left, right, (((1,), (1,)), ((), ())), preferred_element_type=jnp.float32
    )


def down(left, right):
    return lax.dot_general(
        left, right, (((0,), (0,)), ((), ())), preferred_element_type=jnp.float32
    )


def masked_probability(refs, r, queries, key_rows):
    scores = across(queries, key_rows) * HD ** (-0.5)
    allowed = jnp.logical_and(
        refs["query_mark"][r] == refs["key_mark"][r],
        refs["query_place"][...] >= refs["key_place"][...],
    )
    scores = jnp.where(allowed, scores, masked_value)
    shifted = jnp.exp(scores - jnp.max(scores, axis=-1, keepdims=True))
    return shifted / jnp.sum(shifted, axis=-1, keepdims=True)


def rows_of(ref, t, size):
    per_row = ref.shape[1] // size
    return ref.at[t // per_row, pl.ds(pl.multiple_of(t % per_row * size, size), size)]


def attention_back(
    number, branch, weights, places, queries, pairs, marks, lefts, attended, out, part
):
    query_place, pair_place, out_place = places
    (query_array, query_at), (pair_array, pair_at) = queries, pairs
    same = query_array is pair_array
    rows, length, width = branch.shape
    wide = weights.shape[1] // 4
    heads = wide // HD
    block = (rows, length // 4, width)
    flat = (rows * length, width)
    inputs = {
        "branch": branch,
        "weights": weights,
        "out_weights": weights,
        "queries": query_array,
        "query_mark": marks[0],
        "key_mark": marks[1],
        "query_place": marks[2],
        "key_place": marks[3],
        "left0": lefts[0].reshape(flat),
        "part": part,
    }
    if not same:
        inputs["pairs"] = pair_array
        inputs["left1"] = lefts[1].reshape(flat)
    if attended is not None:
        inputs["attended"] = attended.reshape(rows * length, wide)
    if out is not None:
        inputs["partial"] = out[0]
        if out[1] is not None:
            inputs["base"] = out[1]
    grad_columns = wide * (4 if attended is not None else 3)
    outs = {
        "input_partial": (shape_of((rows, length, width), jnp.bfloat16), VMEM),
        "weight_grads": (shape_of((width, grad_columns), jnp.bfloat16), ANY),
        "terms": terms_out(part),
    }
    scratch = {
        "grad_out": pltpu.VMEM((rows, length, wide), jnp.bfloat16),
        "stage": pltpu.VMEM((2, 256, grad_columns), jnp.bfloat16),
        "stage_sems": pltpu.SemaphoreType.DMA((2,)),
        "unpair_sems": pltpu.SemaphoreType.DMA((4,)),
    }
    if out is not None:
        outs["out"] = (shape_of(block, jnp.bfloat16), ANY)
        scratch.update(collect_scratch("", *block))
        scratch["leaving"] = pltpu.VMEM(block, jnp.bfloat16)
        scratch["swap_sems"] = pltpu.SemaphoreType.DMA((2, PARTS))
    if same:
        scratch["grad_all"] = pltpu.VMEM((rows, length, 3 * wide), jnp.bfloat16)
    else:
        scratch["grad_queries"] = pltpu.VMEM((rows, length, wide), jnp.bfloat16)
        outs["grad_pairs"] = (shape_of((rows, length, 2 * wide), jnp.bfloat16), VMEM)
    scale = HD ** (-0.5)
    total = rows * heads
    size = 256

    def body(refs, moves):
        unpair = Unpair(refs["part"], refs["terms"], refs["unpair_sems"])
        out_work = None
        if out is not None:
            out_work = OutWork(
                collect_of(refs, "", "partial"),
                Swap(refs["leaving"], refs["out"], refs["swap_sems"]),
                refs.get("base"),
            )
        grad_queries = refs["grad_all"] if same else refs["grad_queries"]
        grad_pairs = refs["grad_all"] if same else refs["grad_pairs"]
        pair_refs = refs["queries"] if same else refs["pairs"]
        pair_out = wide if same else 0

        def form_grad_out(t):
            rows_of(refs["grad_out"], t, size)[...] = jnp.dot(
                rows_of(refs["branch"], t, size)[...],
                refs["out_weights"][...],
                preferred_element_type=jnp.float32,
            ).astype(jnp.bfloat16)

        def one(i):
            r, h = i // heads, i % heads
            queries_here = head_at(refs["queries"], r, h, query_at)[...]
            key_rows = head_at(pair_refs, r, h, pair_at)[...]
            value_rows = head_at(pair_refs, r, h, pair_at + wide)[...]
            grad_here = head_at(refs["grad_out"], r, h, 0)[...]
            probability = masked_probability(refs, r, queries_here, key_rows)
            grad_values = down(probability.astype(jnp.bfloat16), grad_here)
            grad_probs = across(grad_here, value_rows)
            inner = jnp.sum(probability * grad_probs, axis=-1, keepdims=True)
            grad_scores = (probability * (grad_probs - inner)).astype(jnp.bfloat16)
            query_terms = jnp.dot(grad_scores, key_rows, preferred_element_type=jnp.float32)
            key_terms = down(grad_scores, queries_here)
            head_at(grad_queries, r, h, 0)[...] = (query_terms * scale).astype(jnp.bfloat16)
            head_at(grad_pairs, r, h, pair_out)[...] = (key_terms * scale).astype(jnp.bfloat16)
            head_at(grad_pairs, r, h, pair_out + wide)[...] = grad_values.astype(jnp.bfloat16)

        def form_partial(t):
            columns = (query_place, 3 * wide if same else wide)
            rows_of(refs["input_partial"], t, size)[...] = across(
                rows_of(grad_queries, t, size)[...],
                refs["weights"].at[:, pl.ds(*columns)][...],
            ).astype(jnp.bfloat16)

        def written(i):
            return pltpu.make_async_copy(
                refs["stage"].at[i % 2],
                refs["weight_grads"].at[pl.ds(pl.multiple_of(i * size, size), size)],
                refs["stage_sems"].at[i % 2],
            )

        def form_grads(i):
            @pl.when(i >= 2)
            def _():
                written(i - 2).wait()

            at = pl.ds(pl.multiple_of(i * size, size), size)
            stage = refs["stage"].at[i % 2]

            def put(place, left, right):
                terms = right[...].reshape(rows * length, right.shape[-1])
                stage[:, place : place + right.shape[-1]] = down(left, terms).astype(jnp.bfloat16)

            put(query_place, refs["left0"].at[:, at][...], grad_queries)
            if not same:
                put(pair_place, refs["left1"].at[:, at][...], grad_pairs)
            if attended is not None:
                here = refs["branch"].at[:, :, at][...].reshape(rows * length, size)
                stage[:, out_place : out_place + wide] = down(here, refs["attended"][...]).astype(
                    jnp.bfloat16
                )
            written(i).start()

        def loop(count, work, stops=()):
            def step(i, carry):
                work(i)
                if out_work is not None:
                    for stop, k in stops:

                        @pl.when(i == stop)
                        def _(k=k):
                            out_work.leave_part(k)

                return carry

            lax.fori_loop(0, count, step, 0)

        moves.start("part", "partial", "branch", "out_weights", "queries", "pairs", "base")
        moves.start("left0", "left1", "attended", "weights")
        greet(True)
        moves.ready("part")
        unpair.start()
        moves.ready("partial")
        if out_work is not None:
            out_work.begin()
        moves.ready("branch", "out_weights")
        loop(rows * length // size, form_grad_out)
        if out_work is not None:
            out_work.forward()
        moves.ready("queries", "pairs", "base")
        loop(total, one, ((total - 1, 0),))
        moves.store("grad_pairs")
        moves.ready("left0", "left1", "attended", "weights")
        loop(width // size, form_grads, ((1, 1), (3, 2), (5, 3)))
        loop(rows * length // size, form_partial)
        moves.store("input_partial")
        if out_work is not None:
            out_work.end()
        unpair.finish()
        for i in (width // size - 2, width // size - 1):
            written(i).wait()
        moves.end()

    big = ("part", "partial", "branch", "weights", "out_weights", "queries", "pairs", "base")
    results = kernel_call(
        number,
        "attention_back",
        inputs,
        outs,
        scratch,
        body,
        lazy=big + ("left0", "left1", "attended"),
        eager=("grad_pairs", "input_partial"),
        columns={"weights": (0, 3 * wide), "out_weights": (out_place, wide)},
    )
    return (
        results["input_partial"],
        results["weight_grads"],
        results["terms"],
        results.get("grad_pairs"),
        results.get("out"),
    )


def attention_turn(number, lefts, weights, places, marks, stream, gain, done=None, beside=None):
    query_place, pair_place, out_place = places
    same = lefts[0] is lefts[1]
    rows, length, width = lefts[0].shape
    wide = weights.shape[1] // 4
    heads = wide // HD
    quarter = length // 4
    size = 256
    out_at = out_place if done is None else 0
    columns = None
    early = not same and done is None
    if early:
        columns = {"pair_weights": (pair_place, 2 * wide)}
    elif done is not None:
        columns = {"weights": (out_place, wide)}
    elif stream is None:
        columns = {"weights": (0, 3 * wide)}
    inputs = {"weights": weights}
    if early:
        inputs["pair_weights"] = weights
    outs, scratch = {}, {}
    if done is None:
        inputs.update(
            {
                "left0": lefts[0],
                "query_mark": marks[0],
                "key_mark": marks[1],
                "query_place": marks[2],
                "key_place": marks[3],
            }
        )
        outs["queries"] = (
            shape_of((rows, length, wide * (3 if same else 1)), jnp.bfloat16),
            VMEM,
        )
        outs["attended"] = (shape_of((rows, length, wide), jnp.bfloat16), VMEM)
        if not same:
            inputs["left1"] = lefts[1]
            outs["pairs"] = (shape_of((rows, length, 2 * wide), jnp.bfloat16), VMEM)
    else:
        inputs["attended"] = done
    if stream is not None:
        inputs["stream"] = stream
        inputs["gain"] = gain[None]
        outs["after"] = (shape_of(stream.shape, jnp.float32), VMEM)
        outs["gathered"] = gathered_out(rows, quarter, width)
        scratch.update(
            {
                **collect_scratch("", rows, quarter, width),
                "partial": pltpu.VMEM((rows, length, width), jnp.bfloat16),
                "normed": pltpu.VMEM((rows, quarter, width), jnp.bfloat16),
                "spread_sems": pltpu.SemaphoreType.DMA((7, PARTS)),
            }
        )
    if beside is not None:
        inputs["beside"] = beside
        outs["beside_gathered"] = gathered_out(rows, quarter, width)
        outs["beside_here"] = (shape_of((rows, quarter, width), jnp.bfloat16), VMEM)
        scratch["beside_sems"] = pltpu.SemaphoreType.DMA((7, PARTS))
        scratch["beside_swap_sems"] = pltpu.SemaphoreType.DMA((2, PARTS))

    def body(refs, moves):
        if stream is not None:
            collect_work = collect_of(refs, "", "partial")
            spread_work = Spread(refs["normed"], refs["gathered"], refs["spread_sems"])
        if beside is not None:
            swap = Swap(refs["beside"], refs["beside_here"], refs["beside_swap_sems"])
            beside_work = Spread(
                refs["beside_here"], refs["beside_gathered"], refs["beside_sems"]
            )
        if done is None:
            pair_refs = refs["queries"] if same else refs["pairs"]
        pair_at = wide if same else 0

        def loop(count, work):
            lax.fori_loop(0, count, lambda i, carry: (work(i), carry)[1], 0)

        def form(left, place, columns, target, source="weights"):
            def tile(t):
                rows_of(target, t, size)[...] = jnp.dot(
                    rows_of(left, t, size)[...],
                    refs[source].at[:, pl.ds(place, columns)][...],
                    preferred_element_type=jnp.float32,
                ).astype(jnp.bfloat16)

            loop(rows * length // size, tile)

        def one(i):
            r, h = i // heads, i % heads
            probability = masked_probability(
                refs,
                r,
                head_at(refs["queries"], r, h, 0)[...],
                head_at(pair_refs, r, h, pair_at)[...],
            ).astype(jnp.bfloat16)
            head_at(refs["attended"], r, h, 0)[...] = jnp.dot(
                probability,
                head_at(pair_refs, r, h, pair_at + wide)[...],
                preferred_element_type=jnp.float32,
            ).astype(jnp.bfloat16)

        def form_block(block):
            def tile(r):
                at = pl.ds(block * quarter, quarter)
                refs["partial"].at[r, at][...] = across(
                    refs["attended"].at[r, at][...],
                    refs["weights"].at[:, pl.ds(out_at, wide)][...],
                ).astype(jnp.bfloat16)

            loop(rows, tile)

        def norm_and_send(k):
            values = collect_work.at(refs["stream"], k, 0)[...].astype(
                jnp.float32
            ) + collect_work.total(k)
            collect_work.at(refs["after"], k, 0)[...] = values
            spread_work.src(k)[...] = normalize(values, refs["gain"][...]).astype(jnp.bfloat16)
            spread_work.start(k)

        def pass_on(first, last):
            if beside is not None:
                for k in range(first, last):
                    swap.arrive(k)
                    beside_work.start(k)

        moves.start("beside", "left1", "pair_weights", "weights", "left0", "attended", "stream")
        if number is not None:
            greet(beside is not None)
        moves.ready("beside")
        if beside is not None:
            each(swap.start)
        moves.ready("left1", "pair_weights")
        if not early:
            moves.ready("weights")
        if done is None:
            if same:
                moves.ready("left0")
                form(refs["left0"], query_place, 3 * wide, refs["queries"])
            else:
                form(refs["left1"], 0, 2 * wide, refs["pairs"], "pair_weights")
                pass_on(0, 1)
                moves.ready("left0", "weights")
                form(refs["left0"], query_place, wide, refs["queries"])
            pass_on(0 if same else 1, 2)
            moves.store("queries", "pairs")
            loop(rows * heads, one)
            moves.store("attended")
        pass_on(0 if done is not None else 2, PARTS)
        moves.store("beside_here")
        moves.ready("attended", "stream")
        if stream is not None:
            for block in (3, 2):
                form_block(block)
                collect_work.start_block(block - 2)
            form_block(1)
            each(collect_work.forward)
            form_block(0)
            if beside is not None:
                each(beside_work.relay)
            each(norm_and_send)
            moves.store("after")
            each(spread_work.relay)
            each(spread_work.finish)
            each(collect_work.finish)
        elif beside is not None:
            each(beside_work.relay)
        if beside is not None:
            each(beside_work.finish)
            each(swap.finish)
        moves.end()

    results = kernel_call(
        number,
        "attention_turn",
        inputs,
        outs,
        scratch,
        body,
        lazy=("beside", "left1", "pair_weights", "weights", "left0", "attended", "stream"),
        eager=("queries", "pairs", "attended", "after", "beside_here"),
        columns=columns,
    )
    return tuple(
        results.get(name)
        for name in (
            "queries",
            "pairs",
            "attended",
            "after",
            "gathered",
            "beside_here",
            "beside_gathered",
        )
    )


class PlaneScatter:
    def __init__(self, grads, columns, taken, passing, crossed, part, sems):
        self.grads, self.columns, self.taken, self.passing = grads, columns, taken, passing
        self.crossed, self.part, self.sems = crossed, part, sems
        self.rows = grads.shape[0] // 4
        self.me = lax.axis_index("chip")

    def terms(self, chip, which):
        start, size = self.columns
        return self.grads.at[
            pl.ds(pl.multiple_of(chip * self.rows, self.rows), self.rows),
            pl.ds(start + which * (size // 2), size // 2),
        ]

    def copy(self, src, dst, axis, number):
        return pltpu.make_async_remote_copy(
            src,
            dst,
            self.sems.at[0, number],
            self.sems.at[1, number],
            device_id={"chip": across_plane(axis)},
            device_id_type=MESH,
        )

    def first(self, which, block):
        chip = 3 - self.me if block else across_plane(which)
        return self.copy(
            self.terms(chip, which), self.taken.at[which, block], which, 2 * which + block
        )

    def second(self, which):
        return self.copy(
            self.passing.at[which], self.crossed.at[which], 1 - which, 4 + which
        )

    def start(self):
        for block in (1, 0):
            for which in range(2):
                self.first(which, block).start()

    def pass_on(self, following):
        for which in range(2):
            self.first(which, 1).wait_recv()
        if following is not None:
            following.start()
        for which in range(2):
            self.passing.at[which][...] = (
                self.terms(across_plane(1 - which), which)[...].astype(jnp.float32)
                + self.taken.at[which, 1][...].astype(jnp.float32)
            ).astype(jnp.bfloat16)
            self.second(which).start()

    def total(self):
        half = self.columns[1] // 2
        for which in range(2):
            self.first(which, 0).wait_recv()
            self.second(which).wait_recv()
            self.part.at[:, pl.ds(which * half, half)][...] = (
                self.terms(self.me, which)[...].astype(jnp.float32)
                + self.taken.at[which, 0][...].astype(jnp.float32)
                + self.crossed.at[which][...].astype(jnp.float32)
            ).astype(jnp.bfloat16)

    def finish(self):
        for which in range(2):
            for block in range(2):
                self.first(which, block).wait_send()
            self.second(which).wait_send()


class SumEverywhere:
    def __init__(self, given, taken, sems):
        self.given, self.taken, self.sems = given, taken, sems
        chips = lax.axis_size("chip")
        core, zh, zp, chip = (lax.axis_index(axis) for axis in ("core", "zh", "zp", "chip"))
        self.partners = [{"core": 1 - core}]
        for bit in range(chips.bit_length() - 1):
            size = 2**bit
            self.partners.append({"chip": chip + size - 2 * size * (chip // size % 2)})
        self.partners += [{"zp": 1 - zp}, {"zh": 1 - zh}]
        self.steps = len(self.partners)
        self.sums = None

    def copy(self, step):
        return pltpu.make_async_remote_copy(
            self.given.at[step],
            self.taken.at[step],
            self.sems.at[0, step],
            self.sems.at[1, step],
            device_id=self.partners[step],
            device_id_type=MESH,
        )

    def begin(self, step):
        if step:
            self.given[step] = self.sums
        else:
            self.sums = self.given[0]
        self.copy(step).start()

    def end(self, step):
        self.copy(step).wait()
        self.sums = self.sums + self.taken[step]


def leave(number, partial, values, stream, gain, gain_sums, grads, part):
    rows, length, width = values.shape
    chips = lax.axis_size("chip")
    in_plane = chips == 4
    steps = 3 + chips.bit_length() - 1
    if not in_plane:
        grads = scatter_chips(grads)
    owned = grads.shape[0] // (4 if in_plane else 1)
    columns = grads.shape[1]
    size = 512
    pieces = columns // size if in_plane else 0

    def body(refs, moves):
        collect_work = collect_of(refs, "", "partial")
        swap = Swap(refs["leaving"], refs["out"], refs["swap_sems"])
        unpair = Unpair(refs["part"], refs["terms"], refs["unpair_sems"])
        if in_plane:
            scatters = [
                PlaneScatter(
                    refs["grads"],
                    (p * size, size),
                    refs["taken"].at[p],
                    refs["passing"].at[p],
                    refs["crossed"].at[p],
                    refs["summed"].at[p],
                    refs["plane_sems"].at[p],
                )
                for p in range(pieces)
            ]
            returns = [
                Unpair(
                    refs["summed"].at[p],
                    refs["grad_terms"].at[:, :, pl.ds(p * size, size)],
                    refs["return_sems"].at[p],
                )
                for p in range(pieces)
            ]
        else:
            scatters = []
            returns = [Unpair(refs["grads"], refs["grad_terms"], refs["return_sems"].at[0])]
        moves.start("part", "grads", "partial", "values", "stream")
        greet(True, True)
        moves.ready("part")
        unpair.start()
        moves.ready("partial")
        collect_work.start()
        moves.ready("grads")
        if scatters:
            scatters[0].start()
        each(collect_work.forward)
        if not in_plane:
            returns[0].start()
        moves.ready("values", "stream")
        refs["given"].at[0][1:3] = refs["gain_sums"][...]
        refs["gain_sum"][...] = jnp.zeros_like(refs["gain_sum"])

        def slope_and_send(k):
            slope, terms = norm_slope(
                collect_work.at(refs["values"], k, 0)[...].astype(jnp.float32),
                refs["gain"][...],
                collect_work.total(k),
            )
            sums = collect_work.at(refs["stream"], k, 0)[...] + slope
            swap.at(refs["leaving"], k)[...] = sums.astype(jnp.bfloat16)
            swap.start(k)
            refs["gain_sum"][...] += jnp.sum(terms, axis=0, keepdims=True)

        gain_work = SumEverywhere(refs["given"], refs["got"], refs["gain_sems"])
        last = gain_work.steps - 1
        turns = max(PARTS, len(scatters) + 1)
        for k in range(turns):
            if k < PARTS:
                slope_and_send(k)
            if k == PARTS - 1:
                refs["given"].at[0][0:1] = refs["gain_sum"][...]
                for step in range(last - 1):
                    gain_work.begin(step)
                    gain_work.end(step)
                gain_work.begin(last - 1)
            if k < len(scatters):
                scatters[k].pass_on(scatters[k + 1] if k + 1 < len(scatters) else None)
            if 0 < k <= len(scatters):
                scatters[k - 1].total()
                returns[k - 1].start()
        gain_work.end(last - 1)
        gain_work.begin(last)
        each(swap.arrive)
        each(swap.finish)
        each(collect_work.finish)
        unpair.finish()
        for scatter in scatters:
            scatter.finish()
        for back in returns:
            back.finish()
        gain_work.end(last)
        refs["totals"][...] = gain_work.sums

    scratch = {
        **collect_scratch("", rows, length, width),
        "leaving": pltpu.VMEM((rows, length, width), jnp.bfloat16),
        "swap_sems": pltpu.SemaphoreType.DMA((2, PARTS)),
        "unpair_sems": pltpu.SemaphoreType.DMA((4,)),
        "return_sems": pltpu.SemaphoreType.DMA((max(1, pieces), 4)),
        "gain_sum": pltpu.VMEM((1, width), jnp.float32),
        "given": pltpu.VMEM((steps, 3, width), jnp.float32),
        "got": pltpu.VMEM((steps, 3, width), jnp.float32),
        "gain_sems": pltpu.SemaphoreType.DMA((2, steps)),
    }
    if in_plane:
        scratch["taken"] = pltpu.VMEM((pieces, 2, 2, owned, size // 2), jnp.bfloat16)
        scratch["passing"] = pltpu.VMEM((pieces, 2, owned, size // 2), jnp.bfloat16)
        scratch["crossed"] = pltpu.VMEM((pieces, 2, owned, size // 2), jnp.bfloat16)
        scratch["summed"] = pltpu.VMEM((pieces, owned, size), jnp.bfloat16)
        scratch["plane_sems"] = pltpu.SemaphoreType.DMA((pieces, 2, 6))
    results = kernel_call(
        number,
        "leave",
        {
            "partial": partial,
            "values": values,
            "stream": stream,
            "gain": gain[None],
            "gain_sums": gain_sums,
            "grads": grads,
            "part": part,
        },
        {
            "out": (shape_of(values.shape, jnp.bfloat16), ANY),
            "totals": (shape_of((3, width), jnp.float32), VMEM),
            "terms": terms_out(part),
            "grad_terms": (shape_of((2, owned // 2, columns), jnp.bfloat16), ANY),
        },
        scratch,
        body,
        lazy=("part", "grads", "partial", "values", "stream"),
    )
    return results["out"], results["totals"], results["terms"], results["grad_terms"]


def summed(terms):
    return terms[0].astype(jnp.float32) + terms[1].astype(jnp.float32)


def project(left_side, right_side):
    return jnp.einsum("rtd,de->rte", left_side, right_side, preferred_element_type=jnp.float32)


def project_back(gradient, right_side):
    return jnp.einsum("rte,de->rtd", gradient, right_side, preferred_element_type=jnp.float32)


def weight_grad(left_side, gradient):
    return jnp.einsum("rtd,rte->de", left_side, gradient, preferred_element_type=jnp.float32)


def gelu_tanh(values):
    return jax.nn.gelu(values, approximate=True)


def shards(
    tokens,
    patches,
    seg_ids,
    seg_example,
    patch_owner,
    gain_self,
    self_query,
    self_key,
    self_value,
    self_out,
    gain_cross,
    cross_query,
    cross_key,
    cross_value,
    cross_out,
    gain_mlp,
    mlp_gate,
    mlp_up,
    mlp_down,
    cotangent,
):
    gains = jnp.stack([gain_self, gain_cross, gain_mlp]).astype(jnp.float32)
    onehot = (
        seg_ids[:, :, None] == lax.iota(jnp.int32, seg_example.shape[1])[None, None, :]
    ).astype(jnp.int32)
    example_of = jnp.sum(onehot * seg_example[:, None, :], axis=2)
    marks = jnp.concatenate([seg_ids, example_of, patch_owner], axis=0)
    rows = seg_ids.shape[0]
    length = seg_ids.shape[1]
    wide = self_query.shape[1]
    hidden_wide = mlp_gate.shape[1]
    local_tokens, marks, gains, normed_one, patch_rows, self_w, cross_pair = head(
        0,
        tokens,
        patches,
        marks,
        gains,
        (self_query, self_key, self_value, self_out.T),
        (cross_key, cross_value, cross_query, cross_out.T),
    )
    norm_one, norm_two, norm_three = gains[0], gains[1], gains[2]
    cross_w = gather_chips(cross_pair)
    mlp_moved = exchange(after(jnp.concatenate([mlp_gate, mlp_up], axis=1), normed_one))
    seg_here = relative(marks[:rows])
    example_here = relative(marks[rows : 2 * rows])
    owner_here = relative(marks[2 * rows :])
    positions = relative(lax.broadcasted_iota(jnp.int32, (1, length), 1))
    self_marks = (
        seg_here[:, :, None],
        seg_here[:, None, :],
        positions.reshape(length, 1),
        positions.reshape(1, length),
    )
    cross_marks = (
        example_here[:, :, None],
        owner_here[:, None, :],
        jnp.zeros((length, 1), jnp.int32),
        jnp.zeros((1, length), jnp.int32),
    )
    self_places = (0, wide, 3 * wide)
    self_lefts = (normed_one, normed_one)
    self_qkv, _, self_attended, _, _, _, _ = attention_turn(
        None, self_lefts, self_w, self_places, self_marks, None, None
    )
    mlp_pair = pair_up(after(mlp_moved, self_attended))
    mlp_in = gather_chips(mlp_pair)
    down_moved = exchange(after(mlp_down.T, mlp_pair))
    _, _, _, after_self, normed_two, _, _ = attention_turn(
        1,
        self_lefts,
        self_w,
        self_places,
        self_marks,
        local_tokens,
        norm_two,
        after(self_attended, mlp_pair),
    )
    down_pair = pair_up(after(down_moved, after_self))
    mlp_downw = gather_chips(down_pair)
    (
        cross_query_rows,
        cross_kv_rows,
        cross_mixed,
        after_cross,
        normed_three,
        local_grad,
        grad_rows,
    ) = attention_turn(
        2,
        (after(normed_two, down_pair), patch_rows),
        cross_w,
        (2 * wide, 0, 3 * wide),
        cross_marks,
        after_self,
        norm_three,
        None,
        cotangent,
    )
    both = project(normed_three, mlp_in)
    gate_pre = both[..., :hidden_wide]
    upward = both[..., hidden_wide:]
    activated, gelu_pull = jax.vjp(gelu_tanh, gate_pre)
    hidden = (activated * upward).astype(jnp.bfloat16)

    grad_down_w = weight_grad(grad_rows, hidden).astype(jnp.bfloat16)
    down_part = scatter_chips(grad_down_w)
    grad_hidden = project(after(grad_rows, grad_down_w), mlp_downw)
    grad_upward = (grad_hidden * activated).astype(jnp.bfloat16)
    grad_gate = gelu_pull(grad_hidden * upward)[0].astype(jnp.bfloat16)
    grad_both = jnp.concatenate([grad_gate, grad_upward], axis=2)
    partial_three = project_back(grad_both, mlp_in).astype(jnp.bfloat16)
    tokens_here = rows * length
    grad_mlp_w = weight_grad(normed_three, grad_both).astype(jnp.bfloat16)
    mlp_part = scatter_chips(grad_mlp_w)
    grad_cross_stream, cross_branch, part_three, result_partial = turn_back(
        3,
        after(partial_three, grad_mlp_w),
        after_cross,
        local_grad,
        norm_three,
        (ProductFill("result_", hidden.reshape(tokens_here, -1), mlp_downw, (0, hidden_wide)),),
    )
    partial_two, cross_grads, down_terms, grad_ckv, output = attention_back(
        4,
        cross_branch,
        cross_w,
        (2 * wide, 0, 3 * wide),
        (cross_query_rows, 0),
        (cross_kv_rows, 0),
        cross_marks,
        (normed_two, patch_rows),
        cross_mixed,
        (result_partial.reshape(rows, length, -1), after_cross),
        down_part,
    )
    down_sum = summed(down_terms).T
    cross_part = scatter_chips(cross_grads)
    grad_self_stream, self_branch, part_two, mlp_terms, patch_partial = turn_back(
        5,
        partial_two,
        after_self,
        grad_cross_stream,
        norm_two,
        (ProductFill("patch_", grad_ckv.reshape(tokens_here, -1), cross_w, (0, 2 * wide)),),
        mlp_part,
    )
    mlp_sum = summed(mlp_terms)
    grad_self_out = weight_grad(self_branch, self_attended).astype(jnp.bfloat16)
    self_out_part = scatter_chips(grad_self_out)
    partial_one, grad_self_in, cross_terms, _, grad_patches = attention_back(
        6,
        after(self_branch, grad_self_out),
        self_w,
        (0, wide, 3 * wide),
        (self_qkv, 0),
        (self_qkv, wide),
        self_marks,
        (normed_one, normed_one),
        None,
        (patch_partial.reshape(rows, length, -1), None),
        cross_part,
    )
    cross_sum = summed(cross_terms)
    grad_tokens, gain_sums, self_out_terms, self_terms = leave(
        7,
        partial_one,
        local_tokens,
        grad_self_stream,
        norm_one,
        jnp.concatenate([part_two, part_three]),
        grad_self_in,
        self_out_part,
    )
    held = gain_self.shape[0]
    place = lax.axis_index(("chip", "core")) * held
    gain_sums = lax.dynamic_slice_in_dim(gain_sums, place, held, axis=1)
    self_sum = summed(self_terms)
    return (
        output,
        grad_tokens.astype(jnp.float32),
        grad_patches.astype(jnp.float32),
        gain_sums[0],
        self_sum[:, :wide],
        self_sum[:, wide : 2 * wide],
        self_sum[:, 2 * wide :],
        summed(self_out_terms).T,
        gain_sums[1],
        cross_sum[:, 2 * wide : 3 * wide],
        cross_sum[:, :wide],
        cross_sum[:, wide : 2 * wide],
        cross_sum[:, 3 * wide :].T,
        gain_sums[2],
        mlp_sum[:, :hidden_wide],
        mlp_sum[:, hidden_wide:],
        down_sum,
    )


def solution(mesh):
    devices = mesh.devices.reshape(mesh.shape["dp"] // 2, 2, 2, mesh.shape["seq"] // 2)
    fine = Mesh(devices, AXES)
    dp = ("chip", "core")
    seq = ("zh", "zp")
    stream = P(dp, seq, None)
    rows = P(dp, None)
    inward = P(dp, seq)
    outward = P(seq, dp)
    vector = P(dp)
    block = (vector, inward, inward, inward, outward)
    weights = block + block + (vector, inward, inward, outward)
    return jax.shard_map(
        shards,
        mesh=fine,
        in_specs=(stream, stream, rows, rows, rows) + weights + (stream,),
        out_specs=(stream, stream, stream) + weights,
        check_vma=False,
    )
```
